32 devices in a mesh: dp: 4 (over x, core), fsdp: 8 (over z, y).
Axes of the slice: x: 2, y: 2, z: 4, core: 2. Of those that a mesh axis runs over, the one named last changes fastest.
Arguments:
- patches: bfloat16 [25600, 1024], P(('dp', 'fsdp')), may hold values from -6 to 6
- cotangent: bfloat16 [25600, 1024], P(('dp', 'fsdp')), may hold values from -6 to 6
- window_rows: int32 [25600], P(('dp', 'fsdp')), may hold values from 0 to 799, as said below
- rel_index: int32 [100, 100], replicated, may hold values from 0 to 360, as said below
- params: float32 [12619776], P(('dp', 'fsdp')), as said below
- first_moment: float32 [12619776], P(('dp', 'fsdp')), may hold values from -6 to 6
- second_moment: float32 [12619776], P(('dp', 'fsdp')), may hold values from 0.001 to 0.05
- learn_rate: float32 [], replicated, may hold values from 0.05 to 0.5
- step_count: int32 [], replicated, may hold values from 10 to 1999
Outputs:
- activations: bfloat16 [25600, 1024], P(('dp', 'fsdp'))
- input_grad: bfloat16 [25600, 1024], P(('dp', 'fsdp'))
- group_rms: float32 [13], replicated
- params_new: float32 [12619776], P(('dp', 'fsdp'))
- first_new: float32 [12619776], P(('dp', 'fsdp'))
- second_new: float32 [12619776], P(('dp', 'fsdp'))
The draws below stay inside these ranges and needn't reach their ends.
Inputs may be any that keep to these rules, and one draw needn't show every extreme that they name: `window_rows`: each aligned block of 800 entries is a permutation of 0 to 799. rel_index[i, j] depends only on the difference of the positions of patches i and j in a 10 x 10 window (row-major), and distinct differences have distinct rows. `params`: finite parameters in the layout of the steps.
All inputs are finite; a program needn't handle non-finite values.
Results may differ from the reference program's by a relative error of at most 0.014.
The reference program's roundings to bfloat16 on the way count: a program that leaves them out, or rounds other values in their place, can miss the bound.
Values may be sent and summed in bfloat16 or wider, within the bound.
No kernel may reach another device: no remote copies, remote signals or barrier semaphores. Data moves between devices by JAX's collectives and lax.ppermute only.
A program may use at most 384 MiB of HBM per device.

```python
import math
import jax
import jax.numpy as jnp
from jax import lax

D = 1024
HEADS = 32
HEAD_DIM = 32
FF = 4096
WSIDE = 10
WIN_DEV = 8
WT = 100
TABLE_ROWS = 361
TOK_DEV = 800
TOKENS = 25600
RAW = 12607776
PARAMS = 12619776


def rough_draw(subkey, entries):
    return jax.random.normal(subkey, (entries,), jnp.float32)


def rising(entries):
    return 0.6 + 1.2 * jnp.arange(entries, dtype=jnp.float32) / entries


def draw_params(key, part):

    def segment_draw(index, entries, factor):
        return rough_draw(jax.random.fold_in(key, index), entries) * factor
    mix_scale = jnp.concatenate([jnp.ones((2 * D,), jnp.float32), rising(D)])
    parts_list = [rising(D) * (1.0 + 0.1 * segment_draw(1, D, 1.0)), segment_draw(2, D, 0.2), (segment_draw(3, D * 3 * D, D ** (-0.5)).reshape(D, 3 * D) * mix_scale[None, :]).reshape(-1), segment_draw(4, 3 * D, 0.2), segment_draw(5, TABLE_ROWS * HEADS, 1.0), segment_draw(6, D * D, 3.0 * D ** (-0.5)), segment_draw(7, D, 0.2), rising(D) * (1.0 + 0.1 * segment_draw(8, D, 1.0)), segment_draw(9, D, 0.2), (segment_draw(10, D * FF, D ** (-0.5)).reshape(D, FF) * rising(FF)[None, :]).reshape(-1), segment_draw(11, FF, 0.2), segment_draw(12, FF * D, 1.5 * FF ** (-0.5)), segment_draw(13, D, 0.2), segment_draw(14, PARAMS - RAW, 0.02)]
    return jnp.concatenate(parts_list).astype(jnp.float32)


def draw_window_rows(key, part):
    block_count = TOKENS // TOK_DEV
    subkeys = jax.random.split(key, block_count)
    orders = jax.vmap(lambda subkey: jax.random.permutation(subkey, TOK_DEV))(subkeys)
    return orders.reshape(TOKENS).astype(jnp.int32)


def draw_rel_index(key, part):
    cell_ids = jnp.arange(WT, dtype=jnp.int32)
    row_pos = cell_ids // WSIDE
    col_pos = cell_ids % WSIDE
    offset_code = (row_pos[:, None] - row_pos[None, :] + WSIDE - 1) * (2 * WSIDE - 1) + (col_pos[:, None] - col_pos[None, :] + WSIDE - 1)
    row_order = jax.random.permutation(key, TABLE_ROWS).astype(jnp.int32)
    return row_order[offset_code].astype(jnp.int32)


def shard_levels(stream_key, dims, shards, low, largest):
    def one(dim, shards_of):
        steps = jax.random.uniform(jax.random.fold_in(jax.random.fold_in(stream_key, 6), dim), (shards_of,), jnp.float32, low / len(shards), largest / len(shards))
        return jnp.repeat(jnp.exp(steps), dims[dim] // shards_of).reshape((-1,) + (1,) * (len(dims) - dim - 1))

    factor_of = one(*shards[0])
    for cut in shards[1:]:
        factor_of = factor_of * one(*cut)
    return factor_of


def normal_values(stream_key, shape, width, most, cuts=(), kind=jnp.bfloat16):
    values = width * jax.random.normal(stream_key, shape, jnp.float32)
    if cuts:
        values = values * shard_levels(stream_key, shape, cuts, -0.22, 0.18)
    return jnp.clip(values, -most, most).astype(kind)


def setup_inputs(seed: int = 0) -> dict:
    streams_of = jax.random.split(jax.random.key(seed), 10)
    patches = normal_values(streams_of[0], (TOKENS, D), 1.0, 6.0, ((0, 32),))
    cotangent = normal_values(streams_of[1], (TOKENS, D), 1.0, 6.0, ((0, 32),))
    window_rows = draw_window_rows(jax.random.fold_in(streams_of[9], 71), 0)
    rel_index = draw_rel_index(jax.random.fold_in(streams_of[9], 71), 0)
    params = draw_params(jax.random.fold_in(streams_of[9], 71), 0)
    first_moment = normal_values(streams_of[5], (PARAMS,), 0.5, 6.0, ((0, 32),), jnp.float32)
    second_moment = jnp.clip(jnp.exp(math.log(0.05) - 3.912023 * jax.random.uniform(streams_of[6], (PARAMS,), jnp.float32) ** shard_levels(streams_of[6], (PARAMS,), ((0, 32),), -0.2, 0.2)), 0.001, 0.05)
    learn_rate = jnp.clip(jnp.exp(jax.random.uniform(streams_of[7], (), jnp.float32, math.log(0.05), math.log(0.5))), 0.05, 0.5)
    step_count = jax.random.randint(streams_of[8], (), 10, 2000).astype(jnp.int32)
    return dict(patches=patches, cotangent=cotangent, window_rows=window_rows, rel_index=rel_index, params=params, first_moment=first_moment, second_moment=second_moment, learn_rate=learn_rate, step_count=step_count)


@jax.custom_vjp
def low(v):
    return lax.optimization_barrier(v.astype(jnp.bfloat16)).astype(jnp.float32)

@jax.custom_vjp
def low_back(v):
    return v

def low_keep(v):
    return (low(v), None)

def low_pass(kept, grad):
    return (grad,)

def back_keep(v):
    return (v, None)

def back_low(kept, grad):
    return (low(grad),)
low.defvjp(low_keep, low_pass)
low_back.defvjp(back_keep, back_low)

def tensor_shapes():
    return [(D,), (D,), (D, 3 * D), (3 * D,), (TABLE_ROWS, HEADS), (D, D), (D,), (D,), (D,), (D, FF), (FF,), (FF, D), (D,)]

def unpack(flat_vector):
    pieces = []
    offset = 0
    for layout in tensor_shapes():
        entries = math.prod(layout)
        pieces.append(flat_vector[offset:offset + entries].reshape(layout))
        offset += entries
    return pieces

def norm_forward(inputs, norm_gain, norm_shift):
    center = inputs - lax.optimization_barrier(jnp.mean(inputs, axis=-1, keepdims=True))
    spread = lax.optimization_barrier(jnp.mean(center * center, axis=-1, keepdims=True))
    return center * lax.rsqrt(spread + 1e-05) * norm_gain + norm_shift

def block_forward(pieces, inputs, rel_index):
    attn_gain, attn_shift, mix_weight, mix_bias, bias_table, out_weight, out_bias, mlp_gain, mlp_shift, expand_weight, expand_bias, shrink_weight, shrink_bias = pieces
    highest = lax.Precision.HIGHEST
    windows = inputs.shape[0]
    rows_in = inputs.reshape(windows * WT, D)
    normed = low(norm_forward(rows_in, attn_gain, attn_shift))
    mixed_rows = low_back(jnp.dot(normed, mix_weight, precision=highest) + mix_bias)
    queries = low(mixed_rows[:, :D] * HEAD_DIM ** (-0.5)).reshape(windows, WT, HEADS, HEAD_DIM)
    keys_low = low(mixed_rows[:, D:2 * D]).reshape(windows, WT, HEADS, HEAD_DIM)
    values_low = low(mixed_rows[:, 2 * D:]).reshape(windows, WT, HEADS, HEAD_DIM)
    table_bias = jnp.transpose(bias_table[rel_index], (2, 0, 1))
    scores = low_back(jnp.einsum('nqhd,nkhd->nhqk', queries, keys_low, precision=highest) + table_bias[None])
    attn_probs = jax.nn.softmax(scores, axis=-1)
    probs_low = low(attn_probs)
    context = jnp.einsum('nhqk,nkhd->nqhd', probs_low, values_low, precision=highest).reshape(windows * WT, D)
    attended = low(low_back(context))
    branch = low_back(jnp.dot(attended, out_weight, precision=highest) + out_bias)
    middle = rows_in + branch
    second = low(norm_forward(middle, mlp_gain, mlp_shift))
    hidden_pre = low_back(jnp.dot(second, expand_weight, precision=highest) + expand_bias)
    hidden = low(jax.nn.gelu(hidden_pre, approximate=False))
    closing = low_back(jnp.dot(hidden, shrink_weight, precision=highest) + shrink_bias)
    return (middle + closing).reshape(windows, WT, D)

def windows_per_step():
    per_step = WIN_DEV
    while per_step * 2 * WT <= 4096 and TOKENS // WT % (per_step * 2) == 0:
        per_step = per_step * 2
    return per_step

def reference(patches, cotangent, window_rows, rel_index, params, first_moment, second_moment, learn_rate, step_count):
    wide = lax.optimization_barrier(params.astype(jnp.bfloat16)).astype(jnp.float32)
    pieces = unpack(wide)
    block_start = jnp.arange(TOKENS, dtype=jnp.int32) // TOK_DEV * TOK_DEV
    sources = block_start + window_rows.astype(jnp.int32)
    rows_in = patches[sources].astype(jnp.float32)
    cot_rows = cotangent[sources].astype(jnp.float32)
    per_step = windows_per_step()
    step_total = TOKENS // (WT * per_step)
    group_rows = rows_in.reshape(step_total, per_step, WT, D)
    group_cots = cot_rows.reshape(step_total, per_step, WT, D)

    def one_group(running, blocks):
        rows_now, cots_now = blocks
        outputs_now, pullback = jax.vjp(lambda weights_now, inputs_now: block_forward(weights_now, inputs_now, rel_index), pieces, rows_now)
        group_grads, input_grads = pullback(cots_now)
        updated = [total_grad + fresh_grad for total_grad, fresh_grad in zip(running, group_grads)]
        return (updated, (outputs_now, input_grads))
    initial = [jnp.zeros(layout, jnp.float32) for layout in tensor_shapes()]
    summed, (outputs_all, input_all) = lax.scan(one_group, initial, (group_rows, group_cots))
    result = outputs_all.reshape(TOKENS, D)
    input_rows = input_all.reshape(TOKENS, D)
    activations = jnp.zeros((TOKENS, D), jnp.float32).at[sources].set(result).astype(jnp.bfloat16)
    input_grad = jnp.zeros((TOKENS, D), jnp.float32).at[sources].set(input_rows).astype(jnp.bfloat16)
    grad = jnp.concatenate([piece_grad.reshape(-1) for piece_grad in summed] + [jnp.zeros((PARAMS - RAW,), jnp.float32)])
    scaled = grad / jnp.sqrt(jnp.float32(TOKENS))
    rms_list = []
    offset = 0
    for layout in tensor_shapes():
        entries = math.prod(layout)
        segment = scaled[offset:offset + entries]
        rms_list.append(jnp.sqrt(jnp.sum(segment * segment) / jnp.float32(entries)))
        offset += entries
    group_rms = jnp.stack(rms_list)
    first_new = 0.9 * first_moment + 0.1 * scaled
    second_new = 0.999 * second_moment + 0.001 * scaled * scaled
    step_float = step_count.astype(jnp.float32)
    first_fix = 1.0 - jnp.power(jnp.float32(0.9), step_float)
    second_fix = 1.0 - jnp.power(jnp.float32(0.999), step_float)
    update = first_new / first_fix / (jnp.sqrt(second_new / second_fix) + 1e-08) + 0.05 * params
    params_new = params - learn_rate * update
    return (activations, input_grad, group_rms, params_new, first_new, second_new)
```

```python
from functools import partial
import math

import jax
import jax.numpy as jnp
from jax import lax
from jax.experimental import pallas as pl
from jax.experimental.pallas import tpu as pltpu
from jax.sharding import PartitionSpec as P

D = 1024
HEADS = 32
HEAD_DIM = 32
FF = 4096
WT = 100
TABLE_ROWS = 361
RAW = 12607776
LANES = 128
AXES = ("dp", "fsdp")
BF16 = jnp.bfloat16
F32 = jnp.float32
VMEM_LIMIT = 60 << 20

SHAPES = [
    (D,),
    (D,),
    (D, 3 * D),
    (3 * D,),
    (TABLE_ROWS, HEADS),
    (D, D),
    (D,),
    (D,),
    (D,),
    (D, FF),
    (FF,),
    (FF, D),
    (D,),
]
STARTS = [0]
for _shape in SHAPES:
    STARTS.append(STARTS[-1] + math.prod(_shape))

SPLIT = STARTS[5]
LIFT = (-SPLIT) % LANES


def p_row(position):
    lifted = position + (LIFT if position >= SPLIT else 0)
    assert lifted % LANES == 0
    return lifted // LANES


SPLIT_ROW = p_row(SPLIT)
END_ROW = p_row(RAW)


def round_up(value, step):
    return -(-value // step) * step


class Geometry:
    def __init__(self, dp, fsdp, shard_len):
        assert dp == 4 and shard_len % LANES == 0 and fsdp % 2 == 0
        self.dp, self.fsdp = dp, fsdp
        self.devices = dp * fsdp
        self.line = fsdp // 2
        assert self.line & (self.line - 1) == 0
        self.rows = shard_len // LANES
        first, last = p_row(STARTS[3]) // self.rows, (SPLIT_ROW - 1) // self.rows
        table_first = (STARTS[4] // LANES) // self.rows
        assert last - table_first in (0, 1) and first >= 0
        self.spill_from, self.spill_to = last, table_first
        self.spill = SPLIT_ROW - self.rows * last if last != table_first else 0
        self.spill_pad = round_up(self.spill, 8)
        self.half = round_up(-(-(self.rows + 1 + self.spill) // 2), 16)
        self.slot = 2 * self.half
        tiles = self.slot // 16
        self.step = 16 * max(t for t in range(1, 13) if tiles % t == 0)
        self.bit_x, self.bit_core, self.bit_y = 2 * fsdp, fsdp, 1

    def permute(self, value, mask_core0, mask_core1):
        pairs = []
        for index in range(self.devices):
            core = (index // self.fsdp) % 2
            pairs.append((index, index ^ (mask_core1 if core else mask_core0)))
        return lax.ppermute(value, AXES, pairs)

    def core_swap(self, value):
        return self.permute(value, self.bit_core, self.bit_core)


def prepare_kernel(geo, me_ref, shard_ref, spill_ref, out_ref, pad_ref):
    rows = geo.rows
    base = me_ref[0] * rows
    pad_ref[0:8, :] = jnp.zeros((8, LANES), F32)
    pad_ref[8 : 8 + rows, :] = shard_ref[...]
    tail = geo.slot + 16 - (8 + rows)
    pad_ref[8 + rows : geo.slot + 16, :] = jnp.zeros((tail, LANES), F32)
    step = geo.step

    def body(i, _):
        r0 = pl.multiple_of(i * step, 8)
        here = pad_ref[pl.ds(r0 + 8, step), :]
        above = pad_ref[pl.ds(r0 + 7, step), :]
        lane = lax.broadcasted_iota(jnp.int32, (step, LANES), 1)
        row = lax.broadcasted_iota(jnp.int32, (step, LANES), 0)
        flat = (base + r0 + row) * LANES + lane
        moved = jnp.where(
            lane >= LIFT, pltpu.roll(here, LIFT, 1), pltpu.roll(above, LIFT, 1)
        )
        value = jnp.where(flat < SPLIT, here, jnp.where(flat >= SPLIT + LIFT, moved, 0.0))
        out_ref[pl.ds(r0, step), :] = value.astype(BF16)
        return 0

    lax.fori_loop(0, geo.slot // step, body, 0)
    if geo.spill:

        @pl.when(me_ref[0] == geo.spill_to)
        def _():
            lane = lax.broadcasted_iota(jnp.int32, (geo.spill_pad, LANES), 1)
            row = lax.broadcasted_iota(jnp.int32, (geo.spill_pad, LANES), 0)
            flat = (geo.rows * geo.spill_from + row) * LANES + lane
            pad_ref[0 : geo.spill_pad, :] = jnp.where(flat < SPLIT, spill_ref[...], 0.0)
            top = (rows // 16) * 16
            over = rows - top
            span = round_up(over + geo.spill_pad, 16)
            pad_ref[geo.spill_pad : geo.spill_pad + 16, :] = jnp.zeros((16, LANES), F32)
            lower = out_ref[top : top + 16, :].astype(F32)
            head = lax.broadcasted_iota(jnp.int32, (16, LANES), 0)
            for r in range(0, span, 16):
                if r == 0:
                    shifted = pltpu.roll(pad_ref[0:16, :], over, 0)
                    block = jnp.where(head < over, lower, shifted)
                else:
                    block = pad_ref[r - over : r - over + 16, :]
                if top + r + 16 <= geo.slot:
                    out_ref[top + r : top + r + 16, :] = block.astype(BF16)


def prepare(geo, me, shard, spill):
    spec = pl.BlockSpec(memory_space=pltpu.VMEM)
    return pl.pallas_call(
        partial(prepare_kernel, geo),
        out_shape=jax.ShapeDtypeStruct((geo.slot, LANES), BF16),
        in_specs=[pl.BlockSpec(memory_space=pltpu.SMEM), spec, spec],
        out_specs=spec,
        scratch_shapes=[pltpu.VMEM((geo.slot + 16, LANES), F32)],
        compiler_params=pltpu.CompilerParams(vmem_limit_bytes=VMEM_LIMIT),
        name="prepare_share",
    )(me, shard, spill)


def place(geo, me_ref, device, half):
    y = device % 2
    z = (device // 2) % geo.line
    x = device // (2 * geo.fsdp)
    rel_x = x ^ me_ref[1]
    rel_z = z ^ me_ref[3]
    rel_y = y ^ me_ref[4]
    mine = half == me_ref[2]
    first, second = (rel_x, rel_y) if half == 0 else (rel_y, rel_x)
    return mine, second, first * geo.line + rel_z


def on_arrays(geo, me_ref, phases, device, half, action):
    mine, second, at = place(geo, me_ref, device, half)
    phase = (device // geo.fsdp) % 2
    for slot_index, group in enumerate(phases):
        for own in range(2):
            for late in range(2):
                number = slot_index * 4 + (1 - own) * 2 + late
                cond = (mine if own else jnp.logical_not(mine)) & (second == late)
                if len(phases) > 1:
                    cond = cond & (phase == group)

                @pl.when(cond)
                def _(number=number):
                    action(number, at)


class Region:
    def __init__(self, geo, row0, count, parts, full_end=False):
        self.row0, self.count, self.parts = row0, count, parts
        self.low = max(row0 - 1, 0) // geo.rows
        last = row0 + count - 1
        self.high = last // geo.rows
        if row0 == 0:
            self.high = geo.spill_to if geo.spill else self.high
        if full_end:
            self.high = geo.devices - 1
        self.slots = self.high - self.low + 1
        self.offset = row0 - geo.rows * self.low
        self.scratch_rows = round_up(geo.rows * (self.slots - 1) + geo.slot, 16)
        groups = sorted({(d // geo.fsdp) % 2 for d in range(self.low, self.high + 1)})
        self.phases = groups


def regions(geo):
    def mat(index):
        depth, width = SHAPES[index]
        return ("mat", p_row(STARTS[index]), depth, width // LANES)

    def vec(first, last):
        start, stop = p_row(STARTS[first]), -(-(STARTS[last]) // LANES)
        if STARTS[last] > SPLIT:
            stop = p_row(STARTS[last])
        return ("vec", start, stop - start)

    table = ("vec", STARTS[4] // LANES, SPLIT_ROW - STARTS[4] // LANES)
    r_mix, r_out, r_exp, r_shr = (p_row(STARTS[i]) for i in (2, 5, 9, 11))
    return [
        Region(geo, 0, r_out, [vec(0, 2), mat(2), vec(3, 4), table]),
        Region(geo, r_out, r_exp - r_out, [mat(5), vec(6, 9)]),
        Region(geo, r_exp, r_shr - r_exp, [mat(9), vec(10, 11)]),
        Region(geo, r_shr, END_ROW - r_shr, [mat(11), vec(12, 13)], full_end=True),
    ]


def unpack_kernel(geo, region, me_ref, *refs):
    arrays = 4 * len(region.phases)
    srcs = refs[:arrays]
    outs = refs[arrays : arrays + len(region.parts)]
    flat_ref, slot_ref, sems = refs[arrays + len(region.parts) :]

    def fetch(step):
        device = region.low + step
        buf = lax.rem(step, 2)
        for half in range(2):

            def start(number, at, half=half):
                pltpu.make_async_copy(
                    srcs[number].at[at],
                    slot_ref.at[buf, pl.ds(half * geo.half, geo.half)],
                    sems.at[buf, half],
                ).start()

            on_arrays(geo, me_ref, region.phases, device, half, start)

    fetch(0)

    def slot_body(step, carry):
        @pl.when(step + 1 < region.slots)
        def _():
            fetch(step + 1)

        buf = lax.rem(step, 2)
        for half in range(2):
            pltpu.make_async_copy(
                srcs[0].at[0],
                slot_ref.at[buf, pl.ds(half * geo.half, geo.half)],
                sems.at[buf, half],
            ).wait()
        base = step * geo.rows

        def rows_body(i, _):
            r0 = pl.multiple_of(i * geo.step, 16)
            flat_ref[pl.ds(base + r0, geo.step), :] = slot_ref[buf, pl.ds(r0, geo.step), :].astype(F32)
            return 0

        lax.fori_loop(0, geo.slot // geo.step, rows_body, 0)
        flat_ref[pl.ds(base, 1), :] = flat_ref[pl.ds(base, 1), :] + carry
        return flat_ref[pl.ds(base + geo.rows, 1), :]

    lax.fori_loop(0, region.slots, slot_body, jnp.zeros((1, LANES), F32))

    for part, out_ref in zip(region.parts, outs):
        at = region.offset + part[1] - region.row0
        if part[0] == "vec":
            out_ref[...] = flat_ref[at : at + part[2], :]
        else:
            _, _, depth, cols = part
            block = 16 if cols > 8 else 64

            def mat_body(i, _, at=at, cols=cols, block=block, out_ref=out_ref):
                i0 = pl.multiple_of(i * block, block)
                for c in range(cols):
                    out_ref[pl.ds(i0, block), c * LANES : (c + 1) * LANES] = flat_ref[
                        pl.ds(at + i0 * cols + c, block, stride=cols), :
                    ].astype(BF16)
                return 0

            lax.fori_loop(0, depth // block, mat_body, 0)


def part_shape(part):
    if part[0] == "vec":
        return jax.ShapeDtypeStruct((part[2], LANES), F32)
    return jax.ShapeDtypeStruct((part[2], part[3] * LANES), BF16)


def unpack(geo, region, me, gathered):
    vmem = pl.BlockSpec(memory_space=pltpu.VMEM)
    operands = [array for group in region.phases for array in gathered[group]]
    return pl.pallas_call(
        partial(unpack_kernel, geo, region),
        out_shape=[part_shape(part) for part in region.parts],
        in_specs=[pl.BlockSpec(memory_space=pltpu.SMEM)]
        + [pl.BlockSpec(memory_space=pl.ANY)] * len(operands),
        out_specs=[vmem] * len(region.parts),
        scratch_shapes=[
            pltpu.VMEM((region.scratch_rows, LANES), F32),
            pltpu.VMEM((2, geo.slot, LANES), BF16),
            pltpu.SemaphoreType.DMA((2, 2)),
        ],
        compiler_params=pltpu.CompilerParams(vmem_limit_bytes=VMEM_LIMIT),
        cost_estimate=pl.CostEstimate(
            flops=0, bytes_accessed=4 * LANES * region.count, transcendentals=0
        ),
        name="unpack_weights",
    )(me, *operands)


def pack_kernel(geo, region, shared, grid_steps, kb, cols, fresh, me_ref, a_ref, b_ref, *refs):
    vecs = sum(part[0] == "vec" for part in region.parts)
    arrays = 4 * len(region.phases)
    vec_refs = refs[:vecs]
    refs = refs[vecs:]
    if not fresh:
        refs = refs[arrays:]
    outs = refs[:arrays]
    flat_ref, left_ref, slot_ref, old_ref, sems, old_sem = refs[arrays:]
    step = pl.program_id(0)

    @pl.when(step == 0)
    def _():
        def clear(start, stop):
            span = 64
            while start < stop:
                size = min(span, stop - start)
                flat_ref[start : start + size, :] = jnp.zeros((size, LANES), F32)
                start += size

        clear(0, region.offset)
        clear(region.offset + region.count, region.scratch_rows)
        numbers = iter(range(vecs))
        for part in region.parts:
            if part[0] == "vec":
                at = region.offset + part[1] - region.row0
                flat_ref[at : at + part[2], :] = vec_refs[next(numbers)][...]

    mat = [part for part in region.parts if part[0] == "mat"][0]
    at = region.offset + mat[1] - region.row0
    left_ref[...] = a_ref[...].T
    chunk = 4

    def panel(j, _):
        c0 = j * chunk
        res = jnp.dot(
            left_ref[...],
            b_ref[:, pl.ds(pl.multiple_of(c0 * LANES, LANES), chunk * LANES)],
            preferred_element_type=F32,
        )
        for c in range(chunk):
            flat_ref[pl.ds(at + step * (kb * cols) + c0 + c, kb, stride=cols), :] = res[
                :, c * LANES : (c + 1) * LANES
            ]
        return 0

    lax.fori_loop(0, cols // chunk, panel, 0)

    @pl.when(step == grid_steps - 1)
    def _():
        def send(index, half, parity, start):
            def action(number, at_slot):
                copy = pltpu.make_async_copy(
                    slot_ref.at[parity, half], outs[number].at[at_slot], sems.at[parity, half]
                )
                copy.start()

            if start:
                on_arrays(geo, me_ref, region.phases, region.low + index, half, action)
            else:
                pltpu.make_async_copy(
                    slot_ref.at[parity, half], outs[0].at[0], sems.at[parity, half]
                ).wait()

        if shared:
            for half in range(2):

                def action(number, at_slot, half=half):
                    pltpu.make_async_copy(
                        outs[number].at[at_slot], old_ref.at[half], old_sem.at[half]
                    ).start()

                on_arrays(geo, me_ref, region.phases, region.high, half, action)
            for half in range(2):
                pltpu.make_async_copy(outs[0].at[0], old_ref.at[half], old_sem.at[half]).wait()

        def slot_body(index, _):
            parity = lax.rem(index, 2)
            for half in range(2):

                @pl.when(index >= 2)
                def _(half=half):
                    send(index, half, parity, False)

                base = index * geo.rows + half * geo.half
                stride = geo.step if geo.half % geo.step == 0 else 16
                is_last = index == region.slots - 1

                def rows_body(i, _, half=half, base=base):
                    r0 = pl.multiple_of(i * stride, 16)
                    value = flat_ref[pl.ds(base + r0, stride), :]
                    slot_ref[parity, half, pl.ds(r0, stride), :] = value.astype(BF16)
                    return 0

                def rows_add(i, _, half=half, base=base):
                    r0 = pl.multiple_of(i * stride, 16)
                    value = flat_ref[pl.ds(base + r0, stride), :]
                    value = value + old_ref[half, pl.ds(r0, stride), :].astype(F32)
                    slot_ref[parity, half, pl.ds(r0, stride), :] = value.astype(BF16)
                    return 0

                if shared:

                    @pl.when(is_last)
                    def _(rows_add=rows_add):
                        lax.fori_loop(0, geo.half // stride, rows_add, 0)

                    @pl.when(jnp.logical_not(is_last))
                    def _(rows_body=rows_body):
                        lax.fori_loop(0, geo.half // stride, rows_body, 0)
                else:
                    lax.fori_loop(0, geo.half // stride, rows_body, 0)
                send(index, half, parity, True)
            return 0

        lax.fori_loop(0, region.slots, slot_body, 0)
        for index in range(max(0, region.slots - 2), region.slots):
            for half in range(2):
                send(index, half, index % 2, False)


def pack(geo, region, me, left, right, vectors, previous, shared):
    tokens, depth = left.shape
    width = right.shape[1]
    cols = width // LANES
    kb = 256
    steps = depth // kb
    arrays = [previous.get(group) for group in region.phases]
    fresh_groups = [entry is None for entry in arrays]
    slot_shape = jax.ShapeDtypeStruct((2 * geo.line, geo.half, LANES), BF16)
    count = 4 * len(region.phases)
    operands = [me, left, right] + vectors
    specs = [
        pl.BlockSpec(memory_space=pltpu.SMEM),
        pl.BlockSpec((tokens, kb), lambda k: (0, k)),
        pl.BlockSpec((tokens, width), lambda k: (0, 0), pipeline_mode=pl.Buffered(1)),
    ] + [pl.BlockSpec(vector.shape, lambda k: (0, 0)) for vector in vectors]
    aliases = {}
    fresh = all(fresh_groups)
    if not fresh:
        for position, entry in enumerate(arrays):
            for number in range(4):
                if entry is None:
                    operands.append(jnp.zeros(slot_shape.shape, BF16))
                else:
                    operands.append(entry[number])
                specs.append(pl.BlockSpec(memory_space=pl.ANY))
                aliases[len(operands) - 1] = position * 4 + number
    results = pl.pallas_call(
        partial(pack_kernel, geo, region, shared, steps, kb, cols, fresh),
        grid=(steps,),
        out_shape=[slot_shape] * count,
        in_specs=specs,
        out_specs=[pl.BlockSpec(memory_space=pl.ANY)] * count,
        scratch_shapes=[
            pltpu.VMEM((region.scratch_rows, LANES), F32),
            pltpu.VMEM((kb, tokens), BF16),
            pltpu.VMEM((2, 2, geo.half, LANES), BF16),
            pltpu.VMEM((2, geo.half, LANES), BF16),
            pltpu.SemaphoreType.DMA((2, 2)),
            pltpu.SemaphoreType.DMA((2,)),
        ],
        input_output_aliases=aliases,
        compiler_params=pltpu.CompilerParams(vmem_limit_bytes=VMEM_LIMIT),
        cost_estimate=pl.CostEstimate(
            flops=2 * tokens * depth * width,
            bytes_accessed=2 * depth * width,
            transcendentals=0,
        ),
        name="weight_grad_pack",
    )(*operands)
    updated = dict(previous)
    for position, group in enumerate(region.phases):
        updated[group] = results[position * 4 : position * 4 + 4]
    return updated


def line_masks(geo):
    if geo.line == 4:
        return [[2, 4, 6]]
    return [[2 << bit] for bit in range(geo.line.bit_length() - 1)]


def gather_group(geo, half_share):
    held = half_share[None]
    for masks in line_masks(geo):
        held = jnp.concatenate([held] + [geo.permute(held, mask, mask) for mask in masks], axis=0)
    across = geo.permute(held, geo.bit_x, geo.bit_y)
    near = jnp.concatenate([held, across], axis=0)
    far = geo.permute(near, geo.bit_y, geo.bit_x)
    return [near, far, geo.core_swap(near), geo.core_swap(far)]


def reduce_group(geo, keep_near, keep_far, send_near, send_far):
    got_far = geo.core_swap(send_far)
    got_near = geo.core_swap(send_near)
    far = (keep_far.astype(F32) + got_far.astype(F32)).astype(BF16)
    from_far = geo.permute(far, geo.bit_y, geo.bit_x)
    near = keep_near.astype(F32) + got_near.astype(F32) + from_far.astype(F32)
    count = geo.line
    from_across = geo.permute(near[count:].astype(BF16), geo.bit_x, geo.bit_y)
    held = near[:count] + from_across.astype(F32)
    for masks in reversed(line_masks(geo)):
        block = held.shape[0] // (len(masks) + 1)
        total = held[:block]
        for number, mask in enumerate(masks):
            part = held[(number + 1) * block : (number + 2) * block].astype(BF16)
            total = total + geo.permute(part, mask, mask).astype(F32)
        held = total
    return held[0]


def update_kernel(geo, me_ref, coef_ref, grad_ref, params_ref, first_ref, second_ref, *outs):
    params_out, first_out, second_out, sums_ref = outs
    rows = geo.rows
    base = me_ref[0] * rows
    span = 64
    steps = -(-rows // span)
    tensors = len(SHAPES)
    scale, first_fix, second_fix, rate = (coef_ref[i] for i in range(4))
    sums_ref[...] = jnp.zeros((16, LANES), F32)

    def body(i, _):
        r0 = jnp.minimum(i * span, rows - span)
        skip = i * span - r0
        here = grad_ref[pl.ds(r0, span), :]
        below = grad_ref[pl.ds(r0 + 1, span), :]
        lane = lax.broadcasted_iota(jnp.int32, (span, LANES), 1)
        row = lax.broadcasted_iota(jnp.int32, (span, LANES), 0)
        flat = (base + r0 + row) * LANES + lane
        moved = jnp.where(
            lane < LANES - LIFT,
            pltpu.roll(here, LANES - LIFT, 1),
            pltpu.roll(below, LANES - LIFT, 1),
        )
        grad = jnp.where(flat < SPLIT, here, moved)
        scaled = grad * scale
        first_new = 0.9 * first_ref[pl.ds(r0, span), :] + 0.1 * scaled
        second_new = 0.999 * second_ref[pl.ds(r0, span), :] + 0.001 * scaled * scaled
        params = params_ref[pl.ds(r0, span), :]
        update = first_new / first_fix / (jnp.sqrt(second_new / second_fix) + 1e-08) + 0.05 * params
        params_out[pl.ds(r0, span), :] = params - rate * update
        first_out[pl.ds(r0, span), :] = first_new
        second_out[pl.ds(r0, span), :] = second_new
        squares = jnp.where(row >= skip, scaled * scaled, 0.0)
        low = (base + r0) * LANES
        high = (base + r0 + span) * LANES
        for t in range(tensors):

            @pl.when((low < STARTS[t + 1]) & (high > STARTS[t]))
            def _(t=t):
                inside = (flat >= STARTS[t]) & (flat < STARTS[t + 1])
                part = jnp.where(inside, squares, 0.0)
                sums_ref[t : t + 1, :] += jnp.sum(part, axis=0, keepdims=True)

        return 0

    lax.fori_loop(0, steps, body, 0)


def update_step(geo, me, coef, grad, params, first, second):
    vmem = pl.BlockSpec(memory_space=pltpu.VMEM)
    smem = pl.BlockSpec(memory_space=pltpu.SMEM)
    rows = jax.ShapeDtypeStruct((geo.rows, LANES), F32)
    return pl.pallas_call(
        partial(update_kernel, geo),
        out_shape=[rows, rows, rows, jax.ShapeDtypeStruct((16, LANES), F32)],
        in_specs=[smem, smem, vmem, vmem, vmem, vmem],
        out_specs=[vmem] * 4,
        compiler_params=pltpu.CompilerParams(vmem_limit_bytes=VMEM_LIMIT),
        name="moments_update",
    )(me, coef, grad, params, first, second)


def norm_forward(inputs, norm_gain, norm_shift):
    center = inputs - jnp.mean(inputs, axis=-1, keepdims=True)
    spread = jnp.mean(center * center, axis=-1, keepdims=True)
    return center * lax.rsqrt(spread + 1e-05) * norm_gain + norm_shift


def contract_last(left_side, right_side):
    return lax.dot_general(
        left_side, right_side, (((1,), (1,)), ((), ())), preferred_element_type=F32
    )


def attention_scores(queries, keys_low, table_bias):
    raw_scores = jnp.einsum("nqhd,nkhd->nhqk", queries, keys_low, preferred_element_type=F32)
    return raw_scores + table_bias[None]


def local(
    patches,
    cotangent,
    window_rows,
    rel_index,
    params,
    first_moment,
    second_moment,
    learn_rate,
    step_count,
):
    tok_rows = patches.shape[0]
    windows = tok_rows // WT
    geo = Geometry(lax.axis_size("dp"), lax.axis_size("fsdp"), params.shape[0])
    me_flat = lax.axis_index(AXES)
    core = lax.axis_index("dp") % 2
    me = jnp.stack(
        [
            me_flat,
            lax.axis_index("dp") // 2,
            core,
            lax.axis_index("fsdp") // 2,
            lax.axis_index("fsdp") % 2,
        ]
    ).astype(jnp.int32)
    shard = params.reshape(geo.rows, LANES)
    if geo.spill:
        spill = lax.ppermute(shard[: geo.spill_pad], AXES, [(geo.spill_from, geo.spill_to)])
    else:
        spill = jnp.zeros((8, LANES), F32)
    share = prepare(geo, me, shard, spill).reshape(2, geo.half, LANES)
    mine = lax.dynamic_index_in_dim(share, core, 0, keepdims=False)
    other = geo.core_swap(lax.dynamic_index_in_dim(share, 1 - core, 0, keepdims=False))
    gathered = {
        0: gather_group(geo, jnp.where(core == 0, mine, other)),
        1: gather_group(geo, jnp.where(core == 0, other, mine)),
    }
    region_list = regions(geo)
    vec1, mix_weight, mix_rows, table_rows = unpack(geo, region_list[0], me, gathered)
    out_weight, vec3 = unpack(geo, region_list[1], me, gathered)
    expand_weight, expand_rows = unpack(geo, region_list[2], me, gathered)
    shrink_weight, shrink_rows = unpack(geo, region_list[3], me, gathered)
    attn_gain = vec1[:8].reshape(D)
    attn_shift = vec1[8:].reshape(D)
    mix_bias = mix_rows.reshape(3 * D)
    bias_table = table_rows.reshape(-1)[: TABLE_ROWS * HEADS].reshape(TABLE_ROWS, HEADS)
    out_bias, mlp_gain, mlp_shift = (vec3[8 * i : 8 * i + 8].reshape(D) for i in range(3))
    expand_bias = expand_rows.reshape(FF)
    shrink_bias = shrink_rows.reshape(D)

    rows_in = patches[window_rows].astype(F32)
    cot_rows = cotangent[window_rows].astype(F32)
    flat_ids = rel_index.reshape(-1)
    picker = (flat_ids[:, None] == jnp.arange(TABLE_ROWS, dtype=jnp.int32)[None, :]).astype(BF16)
    bias_rows = jnp.dot(picker, bias_table.astype(BF16), preferred_element_type=F32)
    table_bias = bias_rows.T.reshape(HEADS, WT, WT)
    normed_f, first_pull = jax.vjp(norm_forward, rows_in, attn_gain, attn_shift)
    normed = normed_f.astype(BF16)
    mixed_rows = jnp.dot(normed, mix_weight, preferred_element_type=F32) + mix_bias
    queries = (
        (mixed_rows[:, :D] * HEAD_DIM ** (-0.5))
        .astype(BF16)
        .reshape(windows, WT, HEADS, HEAD_DIM)
    )
    keys_low = mixed_rows[:, D : 2 * D].astype(BF16).reshape(windows, WT, HEADS, HEAD_DIM)
    values_low = mixed_rows[:, 2 * D :].astype(BF16).reshape(windows, WT, HEADS, HEAD_DIM)
    scores = attention_scores(queries, keys_low, table_bias)
    row_max = jnp.max(scores, axis=-1, keepdims=True)
    exponent = jnp.exp(scores - row_max)
    row_total = jnp.sum(exponent, axis=-1, keepdims=True)
    attn_probs = exponent / row_total
    log_total = row_max + jnp.log(row_total)
    context = jnp.einsum(
        "nhqk,nkhd->nqhd", attn_probs.astype(BF16), values_low, preferred_element_type=F32
    )
    attended = context.reshape(tok_rows, D).astype(BF16)
    middle = rows_in + jnp.dot(attended, out_weight, preferred_element_type=F32) + out_bias
    second_f, second_pull = jax.vjp(norm_forward, middle, mlp_gain, mlp_shift)
    second = second_f.astype(BF16)
    hidden_pre = jnp.dot(second, expand_weight, preferred_element_type=F32) + expand_bias
    hidden = jax.nn.gelu(hidden_pre, approximate=False).astype(BF16)
    result = middle + jnp.dot(hidden, shrink_weight, preferred_element_type=F32) + shrink_bias
    activations = jnp.zeros((tok_rows, D), BF16).at[window_rows].set(result.astype(BF16))

    slots = {}
    grad_out = cot_rows.astype(BF16)
    shrink_bias_grad = jnp.sum(grad_out.astype(F32), axis=0)
    slots = pack(
        geo, region_list[3], me, hidden, grad_out, [shrink_bias_grad.reshape(-1, LANES)], slots, False
    )
    hidden_grad = contract_last(grad_out, shrink_weight)
    gelu_pull = jax.vjp(partial(jax.nn.gelu, approximate=False), hidden_pre)[1]
    pre_grad = gelu_pull(hidden_grad)[0].astype(BF16)
    expand_bias_grad = jnp.sum(pre_grad.astype(F32), axis=0)
    slots = pack(
        geo,
        region_list[2],
        me,
        second,
        pre_grad,
        [expand_bias_grad.reshape(-1, LANES)],
        slots,
        region_list[2].high == region_list[3].low,
    )
    second_grad = contract_last(pre_grad, expand_weight)
    middle_part, mlp_gain_grad, mlp_shift_grad = second_pull(second_grad)
    middle_grad = cot_rows + middle_part
    branch_grad = middle_grad.astype(BF16)
    out_bias_grad = jnp.sum(branch_grad.astype(F32), axis=0)
    vec3_grad = jnp.concatenate([out_bias_grad, mlp_gain_grad, mlp_shift_grad]).reshape(-1, LANES)
    slots = pack(
        geo,
        region_list[1],
        me,
        attended,
        branch_grad,
        [vec3_grad],
        slots,
        region_list[1].high == region_list[2].low,
    )
    context_grad = (
        contract_last(branch_grad, out_weight).astype(BF16).reshape(windows, WT, HEADS, HEAD_DIM)
    )
    again_scores = attention_scores(queries, keys_low, table_bias)
    again_probs = jnp.exp(again_scores - log_total)
    probs_low = again_probs.astype(BF16)
    values_grad = jnp.einsum(
        "nhqk,nqhd->nkhd", probs_low, context_grad, preferred_element_type=F32
    )
    probs_grad = jnp.einsum(
        "nqhd,nkhd->nhqk", context_grad, values_low, preferred_element_type=F32
    )
    scores_grad = (
        again_probs * (probs_grad - jnp.sum(again_probs * probs_grad, axis=-1, keepdims=True))
    ).astype(BF16)
    query_grad = jnp.einsum(
        "nhqk,nkhd->nqhd", scores_grad, keys_low, preferred_element_type=F32
    ) * HEAD_DIM ** (-0.5)
    key_grad = jnp.einsum("nhqk,nqhd->nkhd", scores_grad, queries, preferred_element_type=F32)
    mixed_grad = jnp.concatenate(
        [
            query_grad.reshape(tok_rows, D),
            key_grad.reshape(tok_rows, D),
            values_grad.reshape(tok_rows, D),
        ],
        axis=1,
    ).astype(BF16)
    bias_sum = jnp.sum(scores_grad.astype(F32), axis=0).reshape(HEADS, WT * WT)
    picker_full = (flat_ids[:, None] == jnp.arange(TABLE_ROWS, dtype=jnp.int32)[None, :]).astype(F32)
    table_grad = lax.dot_general(
        picker_full,
        bias_sum,
        (((0,), (1,)), ((), ())),
        precision=lax.Precision.HIGHEST,
        preferred_element_type=F32,
    )
    mix_bias_grad = jnp.sum(mixed_grad.astype(F32), axis=0)
    normed_grad = contract_last(mixed_grad, mix_weight)
    input_part, attn_gain_grad, attn_shift_grad = first_pull(normed_grad)
    input_rows = (middle_grad + input_part).astype(BF16)
    input_grad = jnp.zeros((tok_rows, D), BF16).at[window_rows].set(input_rows)
    vec1_grad = jnp.concatenate([attn_gain_grad, attn_shift_grad]).reshape(-1, LANES)
    table_pad = region_list[0].parts[3][2] * LANES - TABLE_ROWS * HEADS
    table_vec = jnp.pad(table_grad.reshape(-1), (0, table_pad)).reshape(-1, LANES)
    slots = pack(
        geo,
        region_list[0],
        me,
        normed,
        mixed_grad,
        [vec1_grad, mix_bias_grad.reshape(-1, LANES), table_vec],
        slots,
        region_list[0].high == region_list[1].low,
    )

    sums = [reduce_group(geo, *slots[group]) for group in range(2)]
    stay = jnp.where(core == 0, sums[0], sums[1])
    leave = geo.core_swap(jnp.where(core == 0, sums[1], sums[0]))
    owned = jnp.where(
        core == 0,
        jnp.concatenate([stay, leave], axis=0),
        jnp.concatenate([leave, stay], axis=0),
    )
    if geo.spill:
        extra = lax.ppermute(
            owned[geo.rows : geo.rows + geo.spill], AXES, [(geo.spill_to, geo.spill_from)]
        )
        owned = owned + jnp.pad(extra, ((0, geo.slot - geo.spill), (0, 0)))
    step_float = step_count.astype(F32)
    coef = jnp.stack(
        [
            1.0 / jnp.sqrt(F32(tok_rows * geo.devices)),
            1.0 - jnp.power(F32(0.9), step_float),
            1.0 - jnp.power(F32(0.999), step_float),
            learn_rate,
        ]
    )
    params_new, first_new, second_new, squares = update_step(
        geo,
        me,
        coef,
        owned,
        shard,
        first_moment.reshape(geo.rows, LANES),
        second_moment.reshape(geo.rows, LANES),
    )
    group_total = lax.psum(jnp.sum(squares, axis=1)[: len(SHAPES)], AXES)
    entry_counts = jnp.array([math.prod(shape) for shape in SHAPES], F32)
    group_rms = jnp.sqrt(group_total / entry_counts)
    return (
        activations,
        input_grad,
        group_rms,
        params_new.reshape(-1),
        first_new.reshape(-1),
        second_new.reshape(-1),
    )


def solution(mesh):
    placed = (
        P(AXES, None),
        P(AXES, None),
        P(AXES),
        P(),
        P(AXES),
        P(AXES),
        P(AXES),
        P(),
        P(),
    )
    return jax.shard_map(
        local,
        mesh=mesh,
        in_specs=placed,
        out_specs=(P(AXES, None), P(AXES, None), P(), P(AXES), P(AXES), P(AXES)),
        check_vma=False,
    )
```

```python
from functools import partial
import math

import jax
import jax.numpy as jnp
from jax import lax
from jax.experimental import pallas as pl
from jax.experimental.pallas import tpu as pltpu
from jax.sharding import PartitionSpec as P

D = 1024
HEADS = 32
HEAD_DIM = 32
FF = 4096
WT = 100
WP = 104
TABLE_ROWS = 361
RAW = 12607776
LANES = 128
QUAD = LANES // HEAD_DIM
AXES = ("dp", "fsdp")
BF16 = jnp.bfloat16
F32 = jnp.float32
VMEM_LIMIT = 62 << 20

SHAPES = [
    (D,),
    (D,),
    (D, 3 * D),
    (3 * D,),
    (TABLE_ROWS, HEADS),
    (D, D),
    (D,),
    (D,),
    (D,),
    (D, FF),
    (FF,),
    (FF, D),
    (D,),
]
STARTS = [0]
for _shape in SHAPES:
    STARTS.append(STARTS[-1] + math.prod(_shape))

SPLIT = STARTS[5]
LIFT = (-SPLIT) % LANES


def p_row(position):
    lifted = position + (LIFT if position >= SPLIT else 0)
    assert lifted % LANES == 0
    return lifted // LANES


MIX_ROW, OUT_ROW, EXPAND_ROW, SHRINK_ROW = (p_row(STARTS[i]) for i in (2, 5, 9, 11))
SPLIT_ROW = p_row(SPLIT)
TAIL_ROW = p_row(STARTS[3])
TABLE_ROW = STARTS[4] // LANES
END_ROW = p_row(RAW)
HEAD_ROWS = MIX_ROW
LATE_TAIL = SPLIT_ROW - TAIL_ROW
LATE_ROWS = -(-(HEAD_ROWS + LATE_TAIL) // 8) * 8


def round_up(value, step):
    return -(-value // step) * step


def vmem():
    return pl.BlockSpec(memory_space=pltpu.VMEM)


def smem():
    return pl.BlockSpec(memory_space=pltpu.SMEM)


def anywhere():
    return pl.BlockSpec(memory_space=pl.ANY)


def params_of(**more):
    return pltpu.CompilerParams(vmem_limit_bytes=VMEM_LIMIT, **more)


def cost(flops, bytes_accessed, transcendentals=0):
    return pl.CostEstimate(
        flops=int(flops), bytes_accessed=int(bytes_accessed), transcendentals=int(transcendentals)
    )


def nn(left, right):
    return jnp.dot(left, right, preferred_element_type=F32)


def nt(left, right):
    return lax.dot_general(left, right, (((1,), (1,)), ((), ())), preferred_element_type=F32)


class Geometry:
    def __init__(self, dp, fsdp, shard_len):
        assert dp == 4 and shard_len % LANES == 0 and fsdp % 2 == 0
        self.fsdp = fsdp
        self.devices = dp * fsdp
        self.line = fsdp // 2
        assert self.line & (self.line - 1) == 0
        self.rows = shard_len // LANES
        first, last = TABLE_ROW // self.rows, (SPLIT_ROW - 1) // self.rows
        assert last - first in (0, 1)
        self.spill_from, self.spill_to = last, first
        self.spill = SPLIT_ROW - self.rows * last if last != first else 0
        self.quarter = round_up(-(-(self.rows + 16 + self.spill) // 4), 8)
        self.slot = 4 * self.quarter
        assert self.slot % 16 == 0
        tiles = self.slot // 16
        self.chunk = max(t for t in range(1, 13) if tiles % t == 0)
        self.bit_x, self.bit_core, self.bit_y = 2 * fsdp, fsdp, 1

    def base(self, device):
        return (device * self.rows) // 16 * 16

    def permute(self, value, mask_core0, mask_core1):
        pairs = []
        for index in range(self.devices):
            core = (index // self.fsdp) % 2
            pairs.append((index, index ^ (mask_core1 if core else mask_core0)))
        return lax.ppermute(value, AXES, pairs)

    def core_swap(self, value):
        return self.permute(value, self.bit_core, self.bit_core)


def prepare_kernel(geo, me_ref, shard_ref, spill_ref, out_ref, pad_ref):
    rows, slot = geo.rows, geo.slot
    base = me_ref[0] * rows
    shift = lax.rem(base, 16)
    pad_ref[0:32, :] = jnp.zeros((32, LANES), F32)
    pad_ref[16 + rows : slot + 32, :] = jnp.zeros((slot + 16 - rows, LANES), F32)
    whole = rows // 64

    def place_body(i, _):
        r0 = i * 64
        pad_ref[pl.ds(16 + shift + r0, 64), :] = shard_ref[pl.ds(pl.multiple_of(r0, 64), 64), :]
        return 0

    lax.fori_loop(0, whole, place_body, 0)
    rest = rows - whole * 64
    if rest:
        pad_ref[pl.ds(16 + shift + whole * 64, rest), :] = shard_ref[whole * 64 : rows, :]
    if geo.spill:
        count = geo.spill

        @pl.when(me_ref[0] == geo.spill_to)
        def _():
            lane = lax.broadcasted_iota(jnp.int32, (count, LANES), 1)
            row = lax.broadcasted_iota(jnp.int32, (count, LANES), 0)
            flat = (rows * geo.spill_from + row) * LANES + lane
            at = 16 + rows * geo.spill_from - geo.base(geo.spill_to)
            pad_ref[at : at + count, :] = jnp.where(flat < SPLIT, spill_ref[0:count, :], 0.0)

    step = 16 * geo.chunk

    def body(i, _):
        r0 = pl.multiple_of(i * step, 16)
        here = pad_ref[pl.ds(r0 + 16, step), :]
        above = pad_ref[pl.ds(r0 + 15, step), :]
        lane = lax.broadcasted_iota(jnp.int32, (step, LANES), 1)
        row = lax.broadcasted_iota(jnp.int32, (step, LANES), 0)
        flat = (base - shift + r0 + row) * LANES + lane
        moved = jnp.where(lane >= LIFT, pltpu.roll(here, LIFT, 1), pltpu.roll(above, LIFT, 1))
        value = jnp.where(flat < SPLIT, here, jnp.where(flat >= SPLIT + LIFT, moved, 0.0))
        out_ref[pl.ds(r0, step), :] = value.astype(BF16)
        return 0

    lax.fori_loop(0, slot // step, body, 0)


def prepare(geo, me, shard, spill):
    return pl.pallas_call(
        partial(prepare_kernel, geo),
        out_shape=jax.ShapeDtypeStruct((geo.slot, LANES), BF16),
        in_specs=[smem(), vmem(), vmem()],
        out_specs=vmem(),
        scratch_shapes=[pltpu.VMEM((geo.slot + 32, LANES), F32)],
        compiler_params=params_of(),
        name="prepare_share",
    )(me, shard, spill)


def on_arrays(geo, me_ref, groups, device, quarter, action):
    quarter_x, quarter_core = quarter // 2, quarter % 2
    rel_x = quarter_x ^ me_ref[1]
    rel_z = (lax.rem(device, geo.fsdp) // 2) ^ me_ref[3]
    rel_y = lax.rem(device, 2) ^ me_ref[4]
    mine = me_ref[2] == quarter_core
    first, last = (rel_x, rel_y) if quarter_core == 0 else (rel_y, rel_x)
    at = first * geo.line + rel_z
    for position, group in enumerate(groups):
        for own in range(2):
            for late in range(2):
                number = position * 4 + (1 - own) * 2 + late
                cond = (mine if own else jnp.logical_not(mine)) & (last == late)
                if len(groups) > 1:
                    cond = cond & (device // geo.fsdp == group)

                @pl.when(cond)
                def _(number=number):
                    action(number, at)


class Region:
    def __init__(self, geo, row0, row1, matrix, vectors, span=None, high=None):
        self.row0, self.row1 = row0, row1
        self.mat_row, self.depth, self.cols = matrix
        self.start, self.stop = span or (0, self.depth)
        self.vectors = vectors
        self.low = max(row0 - 1, 0) // geo.rows
        self.high = (row1 - 1) // geo.rows if high is None else high
        self.slots = self.high - self.low + 1
        self.origin = geo.base(self.low)
        self.pitch = 17 if self.cols % 32 == 0 else 16
        self.stride = self.cols * self.pitch // 16
        self.scratch_tiles = (geo.base(self.high) + geo.slot - self.origin) // 16
        self.groups = sorted({d // geo.fsdp for d in range(self.low, self.high + 1)})

    def address(self, row):
        rel = row - self.origin
        return rel if self.pitch == 16 else rel + rel // 16

    def scratch(self):
        return pltpu.VMEM((self.scratch_tiles * self.pitch, LANES), F32)


def copy_rows(region, ref, row, count, move):
    done = 0
    while done < count:
        size = min(count - done, 16 - (row + done - region.origin) % 16)
        if region.pitch == 16:
            size = count - done
        move(region.address(row + done), done, size)
        done += size


def unpack_kernel(geo, region, block, aliased, me_ref, *refs):
    arrays = 4 * len(region.groups)
    srcs, refs = refs[:arrays], refs[arrays:]
    if aliased:
        refs = refs[1:]
    weight_ref, refs = refs[0], refs[1:]
    vec_refs, refs = refs[: len(region.vectors)], refs[len(region.vectors) :]
    flat_ref, slot_ref, stage_ref, sems, out_sem = refs
    quarter, pitch, cols = geo.quarter, region.pitch, region.cols
    total = (region.stop - region.start) // block

    def fetch(step):
        device = region.low + step
        buf = lax.rem(step, 2)
        for q in range(4):

            def start(number, at, q=q):
                pltpu.make_async_copy(
                    srcs[number].at[at],
                    slot_ref.at[buf, pl.ds(q * quarter, quarter)],
                    sems.at[buf, q],
                ).start()

            on_arrays(geo, me_ref, region.groups, device, q, start)

    fetch(0)

    def slot_body(step, carry):
        tile_carry, done = carry

        @pl.when(step + 1 < region.slots)
        def _():
            fetch(step + 1)

        buf = lax.rem(step, 2)
        for q in range(4):
            pltpu.make_async_copy(
                srcs[0].at[0], slot_ref.at[buf, pl.ds(q * quarter, quarter)], sems.at[buf, q]
            ).wait()
        device = region.low + step
        first_tile = geo.base(device) // 16 - region.origin // 16
        next_row = (device + 1) * geo.rows // 16 * 16
        next_tile = next_row // 16 - region.origin // 16

        def rows_body(i, _):
            t0 = i * geo.chunk
            r0 = pl.multiple_of(t0 * 16, 16)
            if pitch == 16:
                to = pl.multiple_of((first_tile + t0) * 16, 16)
                flat_ref[pl.ds(to, geo.chunk * 16), :] = slot_ref[
                    buf, pl.ds(r0, geo.chunk * 16), :
                ].astype(F32)
            else:
                for t in range(geo.chunk):
                    flat_ref[pl.ds((first_tile + t0 + t) * pitch, 16), :] = slot_ref[
                        buf, pl.ds(r0 + t * 16, 16), :
                    ].astype(F32)
            return 0

        lax.fori_loop(0, geo.slot // 16 // geo.chunk, rows_body, 0)
        seam = pl.ds(first_tile * pitch, 16)
        flat_ref[seam, :] = flat_ref[seam, :] + tile_carry
        complete = jnp.maximum(next_row - region.mat_row - region.start * cols, 0) // (block * cols)
        complete = jnp.where(step == region.slots - 1, total, jnp.minimum(complete, total))

        def mat_body(i, _):
            to = pl.multiple_of(i * block, block)
            row = i * (block * region.stride)
            for c in range(cols):
                at = region.address(region.mat_row + region.start * cols + c)
                stage_ref[pl.ds(to, block), c * LANES : (c + 1) * LANES] = flat_ref[
                    pl.ds(at + row, block, stride=region.stride), :
                ].astype(BF16)
            pltpu.make_async_copy(
                stage_ref.at[pl.ds(to, block)],
                weight_ref.at[pl.ds(region.start + to, block)],
                out_sem,
            ).start()
            return 0

        lax.fori_loop(done, complete, mat_body, 0)
        return flat_ref[pl.ds(next_tile * pitch, 16), :], complete

    lax.fori_loop(0, region.slots, slot_body, (jnp.zeros((16, LANES), F32), jnp.int32(0)))
    for (row, count), out_ref in zip(region.vectors, vec_refs):

        def move(at, done, size, out_ref=out_ref):
            out_ref[done : done + size, :] = flat_ref[at : at + size, :]

        copy_rows(region, flat_ref, row, count, move)
    pltpu.make_async_copy(
        stage_ref, weight_ref.at[pl.ds(region.start, region.stop - region.start)], out_sem
    ).wait()


def unpack(geo, region, me, gathered, weight=None):
    operands = [me] + [array for group in region.groups for array in gathered[group]]
    specs = [smem()] + [anywhere()] * (len(operands) - 1)
    aliases = {}
    if weight is not None:
        operands.append(weight)
        specs.append(anywhere())
        aliases = {len(operands) - 1: 0}
    height = region.stop - region.start
    return pl.pallas_call(
        partial(unpack_kernel, geo, region, 64 if region.cols <= 8 else 16, weight is not None),
        out_shape=[jax.ShapeDtypeStruct((region.depth, region.cols * LANES), BF16)]
        + [jax.ShapeDtypeStruct((count, LANES), F32) for _, count in region.vectors],
        in_specs=specs,
        out_specs=[anywhere()] + [vmem()] * len(region.vectors),
        scratch_shapes=[
            region.scratch(),
            pltpu.VMEM((2, geo.slot, LANES), BF16),
            pltpu.VMEM((height, region.cols * LANES), BF16),
            pltpu.SemaphoreType.DMA((2, 4)),
            pltpu.SemaphoreType.DMA(()),
        ],
        input_output_aliases=aliases,
        compiler_params=params_of(),
        cost_estimate=cost(0, 8 * LANES * height * region.cols),
        name="unpack_weights",
    )(*operands)


def clear_rows(region, flat_ref):
    filled = sorted(
        [(region.mat_row, region.mat_row + region.depth * region.cols)]
        + [(row, row + count) for row, count in region.vectors]
    )
    edges = [region.origin] + [edge for run in filled for edge in run]
    edges.append(region.origin + 16 * region.scratch_tiles)
    for start, stop in zip(edges[::2], edges[1::2]):
        if stop > start:

            def move(at, done, size):
                for r in range(0, size, 64):
                    span = min(64, size - r)
                    flat_ref[at + r : at + r + span, :] = jnp.zeros((span, LANES), F32)

            copy_rows(region, flat_ref, start, stop - start, move)


def emit_slots(geo, region, shared, me_ref, flat_ref, slot_ref, old_ref, sems, old_sem, outs):
    quarter, pitch = geo.quarter, region.pitch

    def send(index, parity, start):
        for q in range(4):

            def action(number, at, q=q):
                pltpu.make_async_copy(
                    slot_ref.at[parity, pl.ds(q * quarter, quarter)],
                    outs[number].at[at],
                    sems.at[parity, q],
                ).start()

            if start:
                on_arrays(geo, me_ref, region.groups, region.low + index, q, action)
            else:
                pltpu.make_async_copy(
                    slot_ref.at[parity, pl.ds(q * quarter, quarter)],
                    outs[0].at[0],
                    sems.at[parity, q],
                ).wait()

    if shared:
        for q in range(4):

            def action(number, at, q=q):
                pltpu.make_async_copy(
                    outs[number].at[at], old_ref.at[pl.ds(q * quarter, quarter)], old_sem.at[q]
                ).start()

            on_arrays(geo, me_ref, region.groups, region.high, q, action)
        for q in range(4):
            pltpu.make_async_copy(
                outs[0].at[0], old_ref.at[pl.ds(q * quarter, quarter)], old_sem.at[q]
            ).wait()

    def slot_body(index, _):
        parity = lax.rem(index, 2)

        @pl.when(index >= 2)
        def _():
            send(index, parity, False)

        first_tile = geo.base(region.low + index) // 16 - region.origin // 16

        def convert(add):
            def rows_body(i, _):
                t0 = i * geo.chunk
                r0 = pl.multiple_of(t0 * 16, 16)
                for t in range(geo.chunk):
                    value = flat_ref[pl.ds((first_tile + t0 + t) * pitch, 16), :]
                    here = pl.ds(r0 + t * 16, 16)
                    if add:
                        value = value + old_ref[here, :].astype(F32)
                    slot_ref[parity, here, :] = value.astype(BF16)
                return 0

            lax.fori_loop(0, geo.slot // 16 // geo.chunk, rows_body, 0)

        if shared:
            last = index == region.slots - 1
            pl.when(last)(lambda: convert(True))
            pl.when(jnp.logical_not(last))(lambda: convert(False))
        else:
            convert(False)
        send(index, parity, True)
        return 0

    lax.fori_loop(0, region.slots, slot_body, 0)
    for index in range(max(0, region.slots - 2), region.slots):
        send(index, index % 2, False)


def emit_scratch(geo, region):
    return [
        region.scratch(),
        pltpu.VMEM((2, geo.slot, LANES), BF16),
        pltpu.VMEM((geo.slot, LANES), BF16),
        pltpu.SemaphoreType.DMA((2, 4)),
        pltpu.SemaphoreType.DMA((4,)),
    ]


def store_columns(region, flat_ref, row0, first_col, values):
    height = values.shape[0]
    for c in range(values.shape[1] // LANES):
        at = region.address(region.mat_row + first_col + c) + row0 * region.stride
        flat_ref[pl.ds(at, height, stride=region.stride), :] = values[
            :, c * LANES : (c + 1) * LANES
        ]


def with_slots(geo, region, slots, operands, specs):
    shape = jax.ShapeDtypeStruct((2 * geo.line, geo.quarter, LANES), BF16)
    aliases = {}
    count = 0
    for position, group in enumerate(region.groups):
        for number in range(4):
            if group in slots:
                operands.append(slots[group][number])
                specs.append(anywhere())
                aliases[len(operands) - 1] = position * 4 + number
                count += 1
    return [shape] * (4 * len(region.groups)), aliases, count


def updated_slots(region, slots, results):
    merged = dict(slots)
    for position, group in enumerate(region.groups):
        merged[group] = results[position * 4 : position * 4 + 4]
    return merged


def pack_kernel(geo, region, shared, grid_steps, height, skip, me_ref, a_ref, b_ref, *refs):
    vec_refs, refs = refs[: len(region.vectors)], refs[len(region.vectors) + skip :]
    arrays = 4 * len(region.groups)
    outs = refs[:arrays]
    flat_ref, slot_ref, old_ref, sems, old_sem, left_ref = refs[arrays:]
    step = pl.program_id(0)

    @pl.when(step == 0)
    def _():
        clear_rows(region, flat_ref)
        for (row, count), vec_ref in zip(region.vectors, vec_refs):

            def move(at, done, size, vec_ref=vec_ref):
                flat_ref[at : at + size, :] = vec_ref[done : done + size, :]

            copy_rows(region, flat_ref, row, count, move)

    left_ref[...] = a_ref[...].T

    def panel(j, _):
        lanes = pl.ds(pl.multiple_of(j * 512, 512), 512)
        store_columns(region, flat_ref, step * height, j * 4, nn(left_ref[...], b_ref[:, lanes]))
        return 0

    lax.fori_loop(0, region.cols // 4, panel, 0)

    @pl.when(step == grid_steps - 1)
    def _():
        emit_slots(
            geo, region, shared, me_ref, flat_ref, slot_ref, old_ref, sems, old_sem, outs
        )


def pack(geo, region, me, left, right, vectors, slots, shared):
    tokens = left.shape[0]
    height = 256
    steps = region.depth // height
    width = region.cols * LANES
    operands = [me, left, right] + vectors
    specs = [
        smem(),
        pl.BlockSpec((tokens, height), lambda k: (0, k)),
        pl.BlockSpec((tokens, width), lambda k: (0, 0), pipeline_mode=pl.Buffered(1)),
    ] + [pl.BlockSpec(vector.shape, lambda k: (0, 0)) for vector in vectors]
    shapes, aliases, skip = with_slots(geo, region, slots, operands, specs)
    results = pl.pallas_call(
        partial(pack_kernel, geo, region, shared, steps, height, skip),
        grid=(steps,),
        out_shape=shapes,
        in_specs=specs,
        out_specs=[anywhere()] * len(shapes),
        scratch_shapes=emit_scratch(geo, region) + [pltpu.VMEM((height, tokens), BF16)],
        input_output_aliases=aliases,
        compiler_params=params_of(),
        cost_estimate=cost(2 * tokens * region.depth * width, 2 * region.depth * width),
        name="weight_grad_pack",
    )(*operands)
    return updated_slots(region, slots, results)


def line_masks(geo):
    if geo.line == 4:
        return [[2, 4, 6]]
    return [[2 << bit] for bit in range(geo.line.bit_length() - 1)]


def spread_quarters(geo, share, dp_index):
    pieces = [lax.dynamic_index_in_dim(share, dp_index, 0, keepdims=False)]
    for offset in (1, 2, 3):
        piece = lax.dynamic_index_in_dim(share, dp_index ^ offset, 0, keepdims=False)
        mask = offset * geo.fsdp
        pieces.append(geo.permute(piece, mask, mask))
    stacked = jnp.stack(pieces)
    return [
        lax.dynamic_index_in_dim(stacked, dp_index ^ group, 0, keepdims=False)
        for group in range(4)
    ]


def gather_group(geo, piece):
    held = piece[None]
    for masks in line_masks(geo):
        held = jnp.concatenate([held] + [geo.permute(held, mask, mask) for mask in masks], axis=0)
    across = geo.permute(held, geo.bit_x, geo.bit_y)
    near = jnp.concatenate([held, across], axis=0)
    far = geo.permute(near, geo.bit_y, geo.bit_x)
    return [near, far, geo.core_swap(near), geo.core_swap(far)]


def reduce_group(geo, keep_near, keep_far, send_near, send_far):
    got_far = geo.core_swap(send_far)
    got_near = geo.core_swap(send_near)
    far = (keep_far.astype(F32) + got_far.astype(F32)).astype(BF16)
    from_far = geo.permute(far, geo.bit_y, geo.bit_x)
    near = keep_near.astype(F32) + got_near.astype(F32) + from_far.astype(F32)
    count = geo.line
    from_across = geo.permute(near[count:].astype(BF16), geo.bit_x, geo.bit_y)
    held = near[:count] + from_across.astype(F32)
    for masks in reversed(line_masks(geo)):
        block = held.shape[0] // (len(masks) + 1)
        total = held[:block]
        for number, mask in enumerate(masks):
            part = held[(number + 1) * block : (number + 2) * block].astype(BF16)
            total = total + geo.permute(part, mask, mask).astype(F32)
        held = total
    return held[0]


def collect_quarters(geo, sums, dp_index):
    stacked = jnp.stack(sums)
    pieces = [lax.dynamic_index_in_dim(stacked, dp_index, 0, keepdims=False)]
    for offset in (1, 2, 3):
        piece = lax.dynamic_index_in_dim(stacked, dp_index ^ offset, 0, keepdims=False)
        mask = offset * geo.fsdp
        pieces.append(geo.permute(piece, mask, mask))
    return pieces


def sum_everywhere(geo, value):
    mask = 1
    while mask < geo.devices:
        value = value + geo.permute(value, mask, mask)
        mask *= 2
    return value


def tensor_sums(sums_ref, squares, flat, low, high, tensors):
    for t in tensors:

        @pl.when((low < STARTS[t + 1]) & (high > STARTS[t]))
        def _(t=t):
            inside = (flat >= STARTS[t]) & (flat < STARTS[t + 1])
            part = jnp.where(inside, squares, 0.0)
            sums_ref[t : t + 1, :] += jnp.sum(part, axis=0, keepdims=True)


def squares_kernel(geo, me_ref, *refs):
    sums_ref = refs[-1]
    sums_ref[...] = jnp.zeros((16, LANES), F32)
    span = 8 * max(t for t in range(1, 13) if geo.quarter // 8 % t == 0)
    dp_index = me_ref[1] * 2 + me_ref[2]
    for group in range(4):
        device = group * geo.fsdp + me_ref[3] * 2 + me_ref[4]
        share = geo.rows * LANES
        base = device * geo.rows
        first = base - lax.rem(base, 16) + dp_index * geo.quarter

        def body(i, _, group=group, base=base, first=first):
            r0 = pl.multiple_of(i * span, 8)
            value = refs[group][pl.ds(r0, span), :]
            lane = lax.broadcasted_iota(jnp.int32, (span, LANES), 1)
            row = lax.broadcasted_iota(jnp.int32, (span, LANES), 0)
            lifted = (first + r0 + row) * LANES + lane
            flat = jnp.where(lifted < SPLIT, lifted, lifted - LIFT)
            owned = (flat >= base * LANES) & (flat < base * LANES + share)
            low = (first + r0) * LANES - LIFT
            high = (first + r0 + span) * LANES
            squares = jnp.where(owned, value * value, 0.0)
            tensor_sums(sums_ref, squares, flat, low, high, (2,) + tuple(range(5, 13)))
            return 0

        lax.fori_loop(0, geo.quarter // span, body, 0)


def square_sums(geo, me, sums):
    return pl.pallas_call(
        partial(squares_kernel, geo),
        out_shape=jax.ShapeDtypeStruct((16, LANES), F32),
        in_specs=[smem()] + [vmem()] * 4,
        out_specs=vmem(),
        compiler_params=params_of(),
        name="square_sums",
    )(me, *sums)


def update_kernel(geo, me_ref, coef_ref, q0, q1, q2, q3, late_ref, p_ref, m_ref, v_ref, *outs):
    params_out, first_out, second_out, grad_ref = outs
    rows, quarter = geo.rows, geo.quarter
    base = me_ref[0] * rows
    shift = lax.rem(base, 16)
    dp_index = me_ref[1] * 2 + me_ref[2]
    margin = 128
    for offset, ref in enumerate((q0, q1, q2, q3)):
        to = pl.multiple_of(margin + (dp_index ^ offset) * quarter, 8)
        grad_ref[pl.ds(to, quarter), :] = ref[...]
    for row, count, at in ((0, HEAD_ROWS, 0), (TAIL_ROW, LATE_TAIL, HEAD_ROWS)):

        @pl.when((base < row + count) & (base + rows > row))
        def _(row=row, count=count, at=at):
            lane = lax.broadcasted_iota(jnp.int32, (count, LANES), 1)
            p_rows = lax.broadcasted_iota(jnp.int32, (count, LANES), 0) + row
            before = p_rows * LANES + lane < SPLIT
            to = jnp.clip(margin + shift + row - base, 0, margin + geo.slot)
            here = pl.ds(to, count)
            late = late_ref[at : at + count, :]
            grad_ref[here, :] = jnp.where(before, late, grad_ref[here, :])

    span = 64
    scale, first_fix, second_fix, rate = (coef_ref[i] for i in range(4))

    def body(i, _):
        r0 = jnp.minimum(i * span, rows - span)
        here = grad_ref[pl.ds(margin + shift + r0, span), :]
        below = grad_ref[pl.ds(margin + shift + r0 + 1, span), :]
        lane = lax.broadcasted_iota(jnp.int32, (span, LANES), 1)
        row = lax.broadcasted_iota(jnp.int32, (span, LANES), 0)
        flat = (base + r0 + row) * LANES + lane
        back = LANES - LIFT
        moved = jnp.where(lane < back, pltpu.roll(here, back, 1), pltpu.roll(below, back, 1))
        scaled = jnp.where(flat < SPLIT, here, moved) * scale
        at = pl.ds(r0, span)
        first_new = 0.9 * m_ref[at, :] + 0.1 * scaled
        second_new = 0.999 * v_ref[at, :] + 0.001 * scaled * scaled
        params = p_ref[at, :]
        update = first_new / first_fix / (jnp.sqrt(second_new / second_fix) + 1e-08) + 0.05 * params
        params_out[at, :] = params - rate * update
        first_out[at, :] = first_new
        second_out[at, :] = second_new
        return 0

    lax.fori_loop(0, -(-rows // span), body, 0)


def update_step(geo, me, coef, quarters, late, params, first, second):
    rows = jax.ShapeDtypeStruct((geo.rows, LANES), F32)
    return pl.pallas_call(
        partial(update_kernel, geo),
        out_shape=[rows, rows, rows],
        in_specs=[smem(), smem()] + [vmem()] * 8,
        out_specs=[vmem()] * 3,
        scratch_shapes=[pltpu.VMEM((geo.slot + 384, LANES), F32)],
        compiler_params=params_of(),
        name="moments_update",
    )(me, coef, *quarters, late, params, first, second)


def row_blocks(tokens):
    return tokens // 4 if tokens % 64 == 0 else tokens


def permute_in_kernel(rows_ref, patches_ref, cot_ref, x_ref, g_ref):
    arrivals = patches_ref.shape[0]
    lane = lax.broadcasted_iota(jnp.int32, (WP, arrivals), 1)
    pick = jnp.where(rows_ref[...] == lane, 1.0, 0.0).astype(BF16)
    x_ref[...] = nn(pick, patches_ref[...]).astype(BF16)
    g_ref[...] = nn(pick, cot_ref[...]).astype(BF16)


def permute_in(row_ids, patches, cotangent):
    tokens = row_ids.shape[0]
    whole = pl.BlockSpec(patches.shape, lambda i: (0, 0))
    part = pl.BlockSpec((WP, D), lambda i: (i, 0))
    shape = jax.ShapeDtypeStruct((tokens, D), BF16)
    return pl.pallas_call(
        permute_in_kernel,
        grid=(tokens // WP,),
        out_shape=[shape, shape],
        in_specs=[pl.BlockSpec((WP, 1), lambda i: (i, 0)), whole, whole],
        out_specs=[part, part],
        compiler_params=params_of(),
        cost_estimate=cost(4 * tokens * tokens * D, 8 * tokens * D),
        name="window_order",
    )(row_ids, patches, cotangent)


def permute_out_kernel(rows_ref, x_ref, out_ref):
    count = out_ref.shape[0]
    arrival = lax.broadcasted_iota(jnp.int32, (count, rows_ref.shape[1]), 0)
    pick = jnp.where(rows_ref[...] == arrival + pl.program_id(0) * count, 1.0, 0.0).astype(BF16)
    out_ref[...] = nn(pick, x_ref[...]).astype(BF16)


def permute_out(row_ids, values, arrivals):
    tokens = values.shape[0]
    block = 160 if arrivals % 160 == 0 else arrivals
    return pl.pallas_call(
        permute_out_kernel,
        grid=(arrivals // block,),
        out_shape=jax.ShapeDtypeStruct((arrivals, D), BF16),
        in_specs=[
            pl.BlockSpec((1, tokens), lambda i: (0, 0)),
            pl.BlockSpec((tokens, D), lambda i: (0, 0)),
        ],
        out_specs=pl.BlockSpec((block, D), lambda i: (i, 0)),
        compiler_params=params_of(),
        cost_estimate=cost(2 * tokens * arrivals * D, 4 * tokens * D),
        name="arrival_order",
    )(row_ids, values)


def normalized(x):
    center = x - jnp.mean(x, axis=-1, keepdims=True)
    spread = jnp.mean(center * center, axis=-1, keepdims=True)
    inverse = lax.rsqrt(spread + 1e-05)
    return center * inverse, inverse


def normalized_back(e, xhat, inverse):
    mean = jnp.mean(e, axis=-1, keepdims=True)
    along = jnp.mean(e * xhat, axis=-1, keepdims=True)
    return (e - mean - xhat * along) * inverse


def mix_kernel(x_ref, gain_ref, shift_ref, w_ref, b_ref, normed_ref, mixed_ref):
    step = pl.program_id(0)
    tokens = x_ref.shape[0]

    @pl.when(step == 0)
    def _():
        def body(i, _):
            rows = pl.ds(pl.multiple_of(i * 16, 16), 16)
            xhat, _ = normalized(x_ref[rows, :].astype(F32))
            normed_ref[rows, :] = (xhat * gain_ref[...] + shift_ref[...]).astype(BF16)
            return 0

        lax.fori_loop(0, tokens // 16, body, 0, unroll=4)

    mixed = nn(normed_ref[...], w_ref[...]) + b_ref[...]
    scale = jnp.where(step < D // w_ref.shape[1], F32(HEAD_DIM ** (-0.5)), F32(1.0))
    mixed_ref[...] = (mixed * scale).astype(BF16)


def mix(x, gain, shift, weight, bias):
    tokens = x.shape[0]
    width = 512
    rows = pl.BlockSpec((tokens, D), lambda j: (0, 0))
    vec = pl.BlockSpec((1, D), lambda j: (0, 0))
    return pl.pallas_call(
        mix_kernel,
        grid=(3 * D // width,),
        out_shape=[
            jax.ShapeDtypeStruct((tokens, D), BF16),
            jax.ShapeDtypeStruct((tokens, 3 * D), BF16),
        ],
        in_specs=[
            rows,
            vec,
            vec,
            pl.BlockSpec((D, width), lambda j: (0, j)),
            pl.BlockSpec((1, width), lambda j: (0, j)),
        ],
        out_specs=[rows, pl.BlockSpec((tokens, width), lambda j: (0, j))],
        compiler_params=params_of(),
        cost_estimate=cost(6 * tokens * D * D, 6 * D * D + 8 * tokens * D),
        name="mix_rows",
    )(x, gain, shift, weight, bias)


def bias_kernel(ids_ref, table_ref, out_ref):
    entries = table_ref.shape[1]

    def body(j, _):
        entry = lax.broadcasted_iota(jnp.int32, (entries, LANES), 0)
        pick = jnp.where(ids_ref[pl.ds(j, 1), :] == entry, 1.0, 0.0).astype(BF16)
        out_ref[:, pl.ds(j, 1), :] = nn(table_ref[...], pick).reshape(HEADS, 1, LANES)
        return 0

    lax.fori_loop(0, WT, body, 0, unroll=4)
    for j in range(WT, WP):
        out_ref[:, j : j + 1, :] = jnp.full((HEADS, 1, LANES), -1e30, F32)


def score_bias(ids, table):
    return pl.pallas_call(
        bias_kernel,
        out_shape=jax.ShapeDtypeStruct((HEADS, WP, LANES), F32),
        in_specs=[vmem(), vmem()],
        out_specs=vmem(),
        compiler_params=params_of(),
        cost_estimate=cost(2 * HEADS * WP * LANES * 384, 4 * HEADS * WP * LANES),
        name="score_bias",
    )(ids, table)


def bias_back_kernel(ids_ref, sums_ref, out_ref):
    entries = out_ref.shape[0]
    out_ref[...] = jnp.zeros(out_ref.shape, F32)

    def body(j, _):
        lane = lax.broadcasted_iota(jnp.int32, (HEADS, LANES), 1)
        row = jnp.where(lane < WT, sums_ref[:, pl.ds(j, 1), :].reshape(HEADS, LANES), 0.0)
        high = row.astype(BF16)
        rest = row - high.astype(F32)
        middle = rest.astype(BF16)
        low = (rest - middle.astype(F32)).astype(BF16)
        parts = jnp.concatenate([high, middle, low], axis=0)
        entry = lax.broadcasted_iota(jnp.int32, (entries, LANES), 0)
        pick = jnp.where(ids_ref[pl.ds(j, 1), :] == entry, 1.0, 0.0).astype(BF16)
        out_ref[...] += nt(pick, parts)
        return 0

    lax.fori_loop(0, WT, body, 0, unroll=4)


def score_bias_back(ids, sums, entries):
    parts = pl.pallas_call(
        bias_back_kernel,
        out_shape=jax.ShapeDtypeStruct((entries, 3 * HEADS), F32),
        in_specs=[vmem(), vmem()],
        out_specs=vmem(),
        compiler_params=params_of(),
        cost_estimate=cost(6 * HEADS * WP * LANES * 384, 4 * HEADS * WP * LANES),
        name="score_bias_back",
    )(ids, sums)
    return parts[:, :HEADS] + parts[:, HEADS : 2 * HEADS] + parts[:, 2 * HEADS :]


def pad_rows(x, rows):
    return jnp.concatenate([x, jnp.zeros((rows - x.shape[0], x.shape[1]), x.dtype)], axis=0)


def one_head(x, head):
    lane = lax.broadcasted_iota(jnp.int32, x.shape, 1)
    return jnp.where(lane // HEAD_DIM == head, x, jnp.zeros_like(x))


def by_head(x):
    return jnp.concatenate([one_head(x, head) for head in range(QUAD)], axis=0)


def attention_kernel(q_ref, k_ref, v_ref, bias_ref, out_ref, log_ref):
    def block(b, _):
        lanes = pl.ds(pl.multiple_of(b * LANES, LANES), LANES)
        queries = pad_rows(q_ref[:, lanes], LANES)
        scores = nt(by_head(k_ref[:, lanes]), queries)
        values = v_ref[:, lanes].astype(F32).T.astype(BF16)
        parts = []
        for head in range(QUAD):
            s = scores[head * WP : (head + 1) * WP] + bias_ref[b * QUAD + head]
            top = jnp.max(s, axis=0, keepdims=True)
            e = jnp.exp(s - top)
            total = jnp.sum(e, axis=0, keepdims=True)
            probs = (e * (1.0 / total)).astype(BF16)
            log_ref[0, pl.ds(b * QUAD + head, 1), :] = top + jnp.log(total)
            parts.append(nn(values[head * HEAD_DIM : (head + 1) * HEAD_DIM], probs))
        context = jnp.concatenate(parts, axis=0).T
        out_ref[:, lanes] = context[:WP].astype(BF16)
        return 0

    lax.fori_loop(0, HEADS // QUAD, block, 0, unroll=4)


def attention(mixed, bias):
    windows = mixed.shape[0] // WP

    def third(c):
        return pl.BlockSpec((WP, D), lambda i, c=c: (i, c))

    return pl.pallas_call(
        attention_kernel,
        grid=(windows,),
        out_shape=[
            jax.ShapeDtypeStruct((windows * WP, D), BF16),
            jax.ShapeDtypeStruct((windows, HEADS, LANES), F32),
        ],
        in_specs=[third(0), third(1), third(2), pl.BlockSpec(bias.shape, lambda i: (0, 0, 0))],
        out_specs=[third(0), pl.BlockSpec((1, HEADS, LANES), lambda i: (i, 0, 0))],
        compiler_params=params_of(),
        cost_estimate=cost(12e9, 8 * windows * WP * D, windows * HEADS * WP * LANES),
        name="attention",
    )(mixed, mixed, mixed, bias)


def attention_back_kernel(
    q_ref, k_ref, v_ref, g_ref, bias_ref, log_ref, out_ref, acc_ref, column_ref
):
    @pl.when(pl.program_id(0) == 0)
    def _():
        acc_ref[...] = jnp.zeros(acc_ref.shape, F32)
        column_ref[...] = jnp.zeros(column_ref.shape, F32)

    def put(third, b, value):
        lanes = pl.ds(pl.multiple_of(third * D + b * LANES, LANES), LANES)
        low = value.astype(BF16)
        out_ref[:, lanes] = low
        column_ref[0:1, lanes] += jnp.sum(low.astype(F32), axis=0, keepdims=True)

    def block(b, _):
        lanes = pl.ds(pl.multiple_of(b * LANES, LANES), LANES)
        queries = pad_rows(q_ref[:, lanes], LANES)
        grads = pad_rows(g_ref[:, lanes], LANES)
        keys = k_ref[:, lanes]
        scores = nt(by_head(keys), queries)
        probs_grads = nt(by_head(v_ref[:, lanes]), grads)
        keys_t = keys.astype(F32).T.astype(BF16)
        query_parts, probs_parts, score_parts = [], [], []
        for head in range(QUAD):
            span = slice(head * WP, (head + 1) * WP)
            s = scores[span] + bias_ref[b * QUAD + head]
            probs = jnp.exp(s - log_ref[0, pl.ds(b * QUAD + head, 1), :])
            probs_grad = probs_grads[span]
            along = jnp.sum(probs * probs_grad, axis=0, keepdims=True)
            score_grad = (probs * (probs_grad - along)).astype(BF16)
            acc_ref[b * QUAD + head] += score_grad.astype(F32)
            probs_parts.append(probs.astype(BF16))
            score_parts.append(score_grad)
            query_parts.append(nn(keys_t[head * HEAD_DIM : (head + 1) * HEAD_DIM], score_grad))
        put(2, b, nn(jnp.concatenate(probs_parts, axis=1), by_head(grads)))
        put(1, b, nn(jnp.concatenate(score_parts, axis=1), by_head(queries)))
        put(0, b, jnp.concatenate(query_parts, axis=0).T[:WP] * HEAD_DIM ** (-0.5))
        return 0

    lax.fori_loop(0, HEADS // QUAD, block, 0, unroll=4)


def attention_back(mixed, grads, bias, logs):
    windows = mixed.shape[0] // WP

    def third(c):
        return pl.BlockSpec((WP, D), lambda i, c=c: (i, c))

    fixed = pl.BlockSpec(bias.shape, lambda i: (0, 0, 0))
    return pl.pallas_call(
        attention_back_kernel,
        grid=(windows,),
        out_shape=[
            jax.ShapeDtypeStruct((windows * WP, 3 * D), BF16),
            jax.ShapeDtypeStruct(bias.shape, F32),
            jax.ShapeDtypeStruct((8, 3 * D), F32),
        ],
        in_specs=[
            third(0),
            third(1),
            third(2),
            third(0),
            fixed,
            pl.BlockSpec((1, HEADS, LANES), lambda i: (i, 0, 0)),
        ],
        out_specs=[
            pl.BlockSpec((WP, 3 * D), lambda i: (i, 0)),
            fixed,
            pl.BlockSpec((8, 3 * D), lambda i: (0, 0)),
        ],
        compiler_params=params_of(),
        cost_estimate=cost(25e9, 16 * windows * WP * D, windows * HEADS * WP * LANES),
        name="attention_back",
    )(mixed, mixed, mixed, grads, bias, logs)


def middle_kernel(x_ref, a_ref, w_ref, b_ref, gain_ref, shift_ref, middle_ref, second_ref):
    middle = x_ref[...].astype(F32) + nn(a_ref[...], w_ref[...]) + b_ref[...]
    middle_ref[...] = middle
    xhat, _ = normalized(middle)
    second_ref[...] = (xhat * gain_ref[...] + shift_ref[...]).astype(BF16)


def middle_rows(x, attended, weight, bias, gain, shift):
    tokens = x.shape[0]
    block = row_blocks(tokens)
    rows = pl.BlockSpec((block, D), lambda i: (i, 0))
    vec = pl.BlockSpec((1, D), lambda i: (0, 0))
    return pl.pallas_call(
        middle_kernel,
        grid=(tokens // block,),
        out_shape=[
            jax.ShapeDtypeStruct((tokens, D), F32),
            jax.ShapeDtypeStruct((tokens, D), BF16),
        ],
        in_specs=[rows, rows, pl.BlockSpec((D, D), lambda i: (0, 0)), vec, vec, vec],
        out_specs=[rows, rows],
        compiler_params=params_of(),
        cost_estimate=cost(2 * tokens * D * D, 10 * tokens * D),
        name="middle_rows",
    )(x, attended, weight, bias, gain, shift)


def mlp_up_kernel(geo, region, shared, steps, skip, me_ref, s_ref, g_ref, w_ref, b_ref, *refs):
    vec_ref, refs = refs[0], refs[1 + skip :]
    hidden_ref, slope_ref, refs = refs[0], refs[1], refs[2:]
    arrays = 4 * len(region.groups)
    outs = refs[:arrays]
    flat_ref, slot_ref, old_ref, sems, old_sem = refs[arrays:]
    step = pl.program_id(0)
    height = w_ref.shape[1]

    @pl.when(step == 0)
    def _():
        clear_rows(region, flat_ref)
        ((row, count),) = region.vectors

        def move(at, done, size):
            flat_ref[at : at + size, :] = vec_ref[done : done + size, :]

        copy_rows(region, flat_ref, row, count, move)

    tokens = s_ref.shape[0]
    block = row_blocks(tokens)
    for r in range(0, tokens, block):
        rows = slice(r, r + block)
        u = nn(s_ref[rows, :], w_ref[...]) + b_ref[...]
        below = 0.5 * (1.0 + lax.erf(u * F32(math.sqrt(0.5))))
        density = jnp.exp(-0.5 * u * u) * F32(1.0 / math.sqrt(2.0 * math.pi))
        hidden_ref[rows, :] = (u * below).astype(BF16)
        slope_ref[rows, :] = below + u * density
    left = hidden_ref[...].T
    for j in range(0, D, 512):
        store_columns(
            region, flat_ref, step * height, j // LANES, nn(left, g_ref[:, j : j + 512])
        )

    @pl.when(step == steps - 1)
    def _():
        emit_slots(
            geo, region, shared, me_ref, flat_ref, slot_ref, old_ref, sems, old_sem, outs
        )


def mlp_up(geo, region, me, second, grad_out, weight, bias, vector, slots, shared):
    tokens = second.shape[0]
    height = 256
    steps = FF // height
    rows = pl.BlockSpec((tokens, D), lambda k: (0, 0), pipeline_mode=pl.Buffered(1))
    columns = pl.BlockSpec((tokens, height), lambda k: (0, k))
    operands = [me, second, grad_out, weight, bias, vector]
    specs = [
        smem(),
        rows,
        rows,
        pl.BlockSpec((D, height), lambda k: (0, k)),
        pl.BlockSpec((1, height), lambda k: (0, k)),
        pl.BlockSpec(vector.shape, lambda k: (0, 0)),
    ]
    shapes, aliases, skip = with_slots(geo, region, slots, operands, specs)
    results = pl.pallas_call(
        partial(mlp_up_kernel, geo, region, shared, steps, skip),
        grid=(steps,),
        out_shape=[
            jax.ShapeDtypeStruct((tokens, FF), BF16),
            jax.ShapeDtypeStruct((tokens, FF), F32),
        ]
        + shapes,
        in_specs=specs,
        out_specs=[columns, columns] + [anywhere()] * len(shapes),
        scratch_shapes=emit_scratch(geo, region),
        input_output_aliases={key: value + 2 for key, value in aliases.items()},
        compiler_params=params_of(),
        cost_estimate=cost(4 * tokens * D * FF, 4 * D * FF + 6 * tokens * FF),
        name="mlp_up",
    )(*operands)
    return results[0], results[1], updated_slots(region, slots, results[2:])


def mlp_down_kernel(geo, region, shared, steps, skip, me_ref, *refs):
    (h_ref, slope_ref, s_ref, g_ref, up_ref, down_ref, m_ref, b_ref) = refs[:8]
    refs = refs[8 + skip :]
    result_ref, grad_ref, refs = refs[0], refs[1], refs[2:]
    arrays = 4 * len(region.groups)
    outs = refs[:arrays]
    flat_ref, slot_ref, old_ref, sems, old_sem, left_ref, sum_ref, pre_ref = refs[arrays:]
    step = pl.program_id(0)
    tokens = s_ref.shape[0]
    block = row_blocks(tokens)
    width = h_ref.shape[1]

    @pl.when(step == 0)
    def _():
        clear_rows(region, flat_ref)
        left_ref[...] = s_ref[...].T
        sum_ref[...] = jnp.zeros(sum_ref.shape, F32)
        grad_ref[...] = jnp.zeros(grad_ref.shape, F32)

    column = jnp.zeros((1, width), F32)
    for r in range(0, tokens, block):
        rows = slice(r, r + block)
        pre = (nt(g_ref[rows, :], down_ref[...]) * slope_ref[rows, :]).astype(BF16)
        pre_ref[rows, :] = pre
        column = column + jnp.sum(pre.astype(F32), axis=0, keepdims=True)
        sum_ref[rows, :] += nn(h_ref[rows, :], down_ref[...])
        grad_ref[rows, :] += nt(pre, up_ref[...])
    cols = width // LANES
    ((vec_row, _),) = region.vectors
    for c in range(cols):
        at = region.address(vec_row + step * cols + c)
        flat_ref[pl.ds(at, 1), :] = column[:, c * LANES : (c + 1) * LANES]
    for r in range(0, D, 256):
        store_columns(
            region, flat_ref, r, step * cols, nn(left_ref[r : r + 256, :], pre_ref[...])
        )

    @pl.when(step == steps - 1)
    def _():
        for r in range(0, tokens, block):
            rows = slice(r, r + block)
            result_ref[rows, :] = (sum_ref[rows, :] + m_ref[rows, :] + b_ref[...]).astype(BF16)
        emit_slots(
            geo, region, shared, me_ref, flat_ref, slot_ref, old_ref, sems, old_sem, outs
        )


def mlp_down(geo, region, me, hidden, slope, second, grad_out, up, down, middle, bias, slots, shared):
    tokens = second.shape[0]
    width = 256
    steps = FF // width
    rows = pl.BlockSpec((tokens, D), lambda k: (0, 0), pipeline_mode=pl.Buffered(1))
    columns = pl.BlockSpec((tokens, width), lambda k: (0, k))
    operands = [me, hidden, slope, second, grad_out, up, down, middle, bias]
    specs = [
        smem(),
        columns,
        columns,
        rows,
        rows,
        pl.BlockSpec((D, width), lambda k: (0, k)),
        pl.BlockSpec((width, D), lambda k: (k, 0)),
        rows,
        pl.BlockSpec((1, D), lambda k: (0, 0)),
    ]
    shapes, aliases, skip = with_slots(geo, region, slots, operands, specs)
    whole = pl.BlockSpec((tokens, D), lambda k: (0, 0))
    results = pl.pallas_call(
        partial(mlp_down_kernel, geo, region, shared, steps, skip),
        grid=(steps,),
        out_shape=[
            jax.ShapeDtypeStruct((tokens, D), BF16),
            jax.ShapeDtypeStruct((tokens, D), F32),
        ]
        + shapes,
        in_specs=specs,
        out_specs=[whole, whole] + [anywhere()] * len(shapes),
        scratch_shapes=emit_scratch(geo, region)
        + [
            pltpu.VMEM((D, tokens), BF16),
            pltpu.VMEM((tokens, D), F32),
            pltpu.VMEM((tokens, width), BF16),
        ],
        input_output_aliases={key: value + 2 for key, value in aliases.items()},
        compiler_params=params_of(),
        cost_estimate=cost(8 * tokens * D * FF, 6 * D * FF + 6 * tokens * FF),
        name="mlp_down",
    )(*operands)
    return results[0], results[1], updated_slots(region, slots, results[2:])


def middle_back_kernel(s_ref, m_ref, g_ref, gain_ref, w_ref, mg_ref, bg_ref, cg_ref, vec_ref):
    @pl.when(pl.program_id(0) == 0)
    def _():
        vec_ref[...] = jnp.zeros(vec_ref.shape, F32)

    grad = s_ref[...]
    xhat, inverse = normalized(m_ref[...])
    middle_grad = g_ref[...].astype(F32) + normalized_back(grad * gain_ref[...], xhat, inverse)
    branch = middle_grad.astype(BF16)
    mg_ref[...] = middle_grad
    bg_ref[...] = branch
    cg_ref[...] = nt(branch, w_ref[...]).astype(BF16)
    vec_ref[0:1, :] += jnp.sum(branch.astype(F32), axis=0, keepdims=True)
    vec_ref[1:2, :] += jnp.sum(grad * xhat, axis=0, keepdims=True)
    vec_ref[2:3, :] += jnp.sum(grad, axis=0, keepdims=True)


def middle_back(second_grad, middle, grad_out, gain, weight):
    tokens = middle.shape[0]
    block = row_blocks(tokens)
    rows = pl.BlockSpec((block, D), lambda i: (i, 0))
    low = jax.ShapeDtypeStruct((tokens, D), BF16)
    return pl.pallas_call(
        middle_back_kernel,
        grid=(tokens // block,),
        out_shape=[
            jax.ShapeDtypeStruct((tokens, D), F32),
            low,
            low,
            jax.ShapeDtypeStruct((8, D), F32),
        ],
        in_specs=[
            rows,
            rows,
            rows,
            pl.BlockSpec((1, D), lambda i: (0, 0)),
            pl.BlockSpec((D, D), lambda i: (0, 0)),
        ],
        out_specs=[rows, rows, rows, pl.BlockSpec((8, D), lambda i: (0, 0))],
        compiler_params=params_of(),
        cost_estimate=cost(2 * tokens * D * D, 18 * tokens * D),
        name="middle_back",
    )(second_grad, middle, grad_out, gain, weight)


def first_back_kernel(mixed_ref, w_ref, x_ref, mg_ref, gain_ref, out_ref, vec_ref):
    @pl.when(pl.program_id(0) == 0)
    def _():
        vec_ref[...] = jnp.zeros(vec_ref.shape, F32)

    grad = nt(mixed_ref[...], w_ref[...])
    xhat, inverse = normalized(x_ref[...].astype(F32))
    inner = normalized_back(grad * gain_ref[...], xhat, inverse)
    out_ref[...] = (mg_ref[...] + inner).astype(BF16)
    vec_ref[0:1, :] += jnp.sum(grad * xhat, axis=0, keepdims=True)
    vec_ref[1:2, :] += jnp.sum(grad, axis=0, keepdims=True)


def first_back(mixed_grad, weight, x, middle_grad, gain):
    tokens = x.shape[0]
    block = row_blocks(tokens)
    rows = pl.BlockSpec((block, D), lambda i: (i, 0))
    return pl.pallas_call(
        first_back_kernel,
        grid=(tokens // block,),
        out_shape=[
            jax.ShapeDtypeStruct((tokens, D), BF16),
            jax.ShapeDtypeStruct((8, D), F32),
        ],
        in_specs=[
            pl.BlockSpec((block, 3 * D), lambda i: (i, 0)),
            pl.BlockSpec((D, 3 * D), lambda i: (0, 0), pipeline_mode=pl.Buffered(1)),
            rows,
            rows,
            pl.BlockSpec((1, D), lambda i: (0, 0)),
        ],
        out_specs=[rows, pl.BlockSpec((8, D), lambda i: (0, 0))],
        compiler_params=params_of(),
        cost_estimate=cost(6 * tokens * D * D, 6 * D * D + 14 * tokens * D),
        name="first_back",
    )(mixed_grad, weight, x, middle_grad, gain)


def split_span(geo, row, depth, cols, block):
    group = (row // geo.rows) // geo.fsdp
    edge = (group + 1) * geo.fsdp * geo.rows // 16 * 16
    inside = max(0, (edge - row) // cols) // block * block
    return min(depth, inside)


def local(
    patches,
    cotangent,
    window_rows,
    rel_index,
    params,
    first_moment,
    second_moment,
    learn_rate,
    step_count,
):
    arrivals = patches.shape[0]
    windows = arrivals // WT
    geo = Geometry(lax.axis_size("dp"), lax.axis_size("fsdp"), params.shape[0])
    dp_index = lax.axis_index("dp")
    fsdp_index = lax.axis_index("fsdp")
    me = jnp.stack(
        [lax.axis_index(AXES), dp_index // 2, dp_index % 2, fsdp_index // 2, fsdp_index % 2]
    ).astype(jnp.int32)

    shard = params.reshape(geo.rows, LANES)
    if geo.spill:
        spill = lax.ppermute(
            shard[: round_up(geo.spill, 8)], AXES, [(geo.spill_from, geo.spill_to)]
        )
    else:
        spill = jnp.zeros((8, LANES), F32)
    share = prepare(geo, me, shard, spill).reshape(4, geo.quarter, LANES)
    pieces = spread_quarters(geo, share, dp_index)
    gathered = {group: gather_group(geo, pieces[group]) for group in range(4)}

    mix_matrix = (MIX_ROW, D, 3 * D // LANES)
    out_matrix = (OUT_ROW, D, D // LANES)
    expand_matrix = (EXPAND_ROW, D, FF // LANES)
    shrink_matrix = (SHRINK_ROW, FF, D // LANES)
    out_end = p_row(STARTS[6])
    expand_end = p_row(STARTS[10])
    shrink_end = p_row(STARTS[12])
    mix_vectors = [(0, 8), (8, 8), (TAIL_ROW, TABLE_ROW - TAIL_ROW), (TABLE_ROW, SPLIT_ROW - TABLE_ROW)]
    out_vectors = [(out_end + 8 * i, 8) for i in range(3)]
    expand_vectors = [(expand_end, FF // LANES)]
    shrink_vectors = [(shrink_end, 8)]

    first = Region(
        geo, 0, OUT_ROW, mix_matrix, mix_vectors, high=geo.spill_to if geo.spill else None
    )
    mix_weight, attn_gain, attn_shift, mix_bias, table_rows = unpack(geo, first, me, gathered)
    out_weight, out_bias, mlp_gain, mlp_shift = unpack(
        geo, Region(geo, OUT_ROW, EXPAND_ROW, out_matrix, out_vectors), me, gathered
    )

    def in_two(matrix, vectors, end, block):
        row, depth, cols = matrix
        edge = split_span(geo, row, depth, cols, block)
        weight = None
        if 0 < edge < depth:
            part = Region(geo, row, row + edge * cols, matrix, [], span=(0, edge))
            (weight,) = unpack(geo, part, me, gathered)
            rest = Region(geo, row + edge * cols, end, matrix, vectors, span=(edge, depth))
            return unpack(geo, rest, me, gathered, weight)
        return unpack(geo, Region(geo, row, end, matrix, vectors), me, gathered)

    expand_weight, expand_bias = in_two(expand_matrix, expand_vectors, SHRINK_ROW, 16)
    shrink_weight, shrink_bias = in_two(shrink_matrix, shrink_vectors, END_ROW, 64)

    def line_of(rows):
        return rows.reshape(1, -1)

    entries = round_up(TABLE_ROWS, 16)
    table = table_rows.reshape(-1)[: TABLE_ROWS * HEADS].reshape(TABLE_ROWS, HEADS).T
    table = jnp.pad(table, ((0, 0), (0, entries - TABLE_ROWS))).astype(BF16)
    ids = jnp.pad(rel_index.T, ((0, WP - WT), (0, LANES - WT)), constant_values=-1)
    bias = score_bias(ids, table)

    row_ids = jnp.pad(
        window_rows.reshape(windows, WT), ((0, 0), (0, WP - WT)), constant_values=-1
    ).reshape(windows * WP)
    x, grad_out = permute_in(row_ids[:, None], patches, cotangent)
    normed, mixed = mix(x, line_of(attn_gain), line_of(attn_shift), mix_weight, line_of(mix_bias))
    attended, logs = attention(mixed, bias)
    middle, second = middle_rows(
        x, attended, out_weight, line_of(out_bias), line_of(mlp_gain), line_of(mlp_shift)
    )

    shrink_region = Region(
        geo, SHRINK_ROW, END_ROW, shrink_matrix, shrink_vectors, high=geo.devices - 1
    )
    expand_region = Region(geo, EXPAND_ROW, SHRINK_ROW, expand_matrix, expand_vectors)
    out_region = Region(geo, OUT_ROW, EXPAND_ROW, out_matrix, out_vectors)
    mix_region = Region(geo, 0, TAIL_ROW, mix_matrix, [])
    slots = {}
    shrink_bias_grad = jnp.sum(grad_out.astype(F32), axis=0).reshape(-1, LANES)
    hidden, slope, slots = mlp_up(
        geo,
        shrink_region,
        me,
        second,
        grad_out,
        expand_weight,
        line_of(expand_bias),
        shrink_bias_grad,
        slots,
        False,
    )
    result, second_grad, slots = mlp_down(
        geo,
        expand_region,
        me,
        hidden,
        slope,
        second,
        grad_out,
        expand_weight,
        shrink_weight,
        middle,
        line_of(shrink_bias),
        slots,
        expand_region.high == shrink_region.low,
    )
    middle_grad, branch_grad, context_grad, middle_vec = middle_back(
        second_grad, middle, grad_out, line_of(mlp_gain), out_weight
    )
    slots = pack(
        geo,
        out_region,
        me,
        attended,
        branch_grad,
        [middle_vec[i].reshape(8, LANES) for i in range(3)],
        slots,
        out_region.high == expand_region.low,
    )
    mixed_grad, score_sums, column_sums = attention_back(mixed, context_grad, bias, logs)
    slots = pack(
        geo, mix_region, me, normed, mixed_grad, [], slots, mix_region.high == out_region.low
    )
    sums = [reduce_group(geo, *slots[group]) for group in (3, 2, 1, 0)][::-1]
    input_rows, first_vec = first_back(
        mixed_grad, mix_weight, x, middle_grad, line_of(attn_gain)
    )
    activations = permute_out(row_ids[None], result, arrivals)
    input_grad = permute_out(row_ids[None], input_rows, arrivals)

    table_grad = score_bias_back(ids, score_sums, entries)[:TABLE_ROWS]
    table_pad = (SPLIT_ROW - TABLE_ROW) * LANES - TABLE_ROWS * HEADS
    late = jnp.concatenate(
        [
            first_vec[:2].reshape(HEAD_ROWS, LANES),
            column_sums[0].reshape(-1, LANES),
            jnp.pad(table_grad.reshape(-1), (0, table_pad)).reshape(-1, LANES),
        ],
        axis=0,
    )
    late = jnp.pad(late, ((0, LATE_ROWS - late.shape[0]), (0, 0)))
    late = sum_everywhere(geo, late)

    squares = sum_everywhere(geo, jnp.sum(square_sums(geo, me, sums), axis=1)[None])
    scale = 1.0 / jnp.sqrt(F32(arrivals * geo.devices))
    edges = [0, 8, HEAD_ROWS, HEAD_ROWS + TABLE_ROW - TAIL_ROW, LATE_ROWS]
    late_squares = [jnp.sum(late[a:b] * late[a:b]) for a, b in zip(edges, edges[1:])]
    totals = [squares[0, t] for t in range(len(SHAPES))]
    for number, t in enumerate((0, 1, 3, 4)):
        totals[t] = late_squares[number]
    entry_counts = jnp.array([math.prod(shape) for shape in SHAPES], F32)
    group_rms = jnp.sqrt(jnp.stack(totals) * (scale * scale) / entry_counts)

    step_float = step_count.astype(F32)
    coef = jnp.stack(
        [
            scale,
            1.0 - jnp.power(F32(0.9), step_float),
            1.0 - jnp.power(F32(0.999), step_float),
            learn_rate,
        ]
    )
    params_new, first_new, second_new = update_step(
        geo,
        me,
        coef,
        collect_quarters(geo, sums, dp_index),
        late,
        shard,
        first_moment.reshape(geo.rows, LANES),
        second_moment.reshape(geo.rows, LANES),
    )
    return (
        activations,
        input_grad,
        group_rms,
        params_new.reshape(-1),
        first_new.reshape(-1),
        second_new.reshape(-1),
    )


def solution(mesh):
    placed = (
        P(AXES, None),
        P(AXES, None),
        P(AXES),
        P(),
        P(AXES),
        P(AXES),
        P(AXES),
        P(),
        P(),
    )
    return jax.shard_map(
        local,
        mesh=mesh,
        in_specs=placed,
        out_specs=(P(AXES, None), P(AXES, None), P(), P(AXES), P(AXES), P(AXES)),
        check_vma=False,
    )
```

```python
from functools import partial
import math

import jax
import jax.numpy as jnp
from jax import lax
from jax.experimental import pallas as pl
from jax.experimental.pallas import tpu as pltpu
from jax.sharding import PartitionSpec as P

D = 1024
HEADS = 32
HEAD_DIM = 32
FF = 4096
WT = 100
WP = 104
TABLE_ROWS = 361
RAW = 12607776
LANES = 128
QUAD = LANES // HEAD_DIM
AXES = ("dp", "fsdp")
BF16 = jnp.bfloat16
F32 = jnp.float32
VMEM_LIMIT = 62 << 20

SHAPES = [
    (D,),
    (D,),
    (D, 3 * D),
    (3 * D,),
    (TABLE_ROWS, HEADS),
    (D, D),
    (D,),
    (D,),
    (D,),
    (D, FF),
    (FF,),
    (FF, D),
    (D,),
]
STARTS = [0]
for _shape in SHAPES:
    STARTS.append(STARTS[-1] + math.prod(_shape))

SPLIT = STARTS[5]
LIFT = (-SPLIT) % LANES


def p_row(position):
    lifted = position + (LIFT if position >= SPLIT else 0)
    assert lifted % LANES == 0
    return lifted // LANES


MIX_ROW, OUT_ROW, EXPAND_ROW, SHRINK_ROW = (p_row(STARTS[i]) for i in (2, 5, 9, 11))
SPLIT_ROW = p_row(SPLIT)
TAIL_ROW = p_row(STARTS[3])
TABLE_ROW = STARTS[4] // LANES
END_ROW = p_row(RAW)
HEAD_ROWS = MIX_ROW
LATE_TAIL = SPLIT_ROW - TAIL_ROW
LATE_ROWS = -(-(HEAD_ROWS + LATE_TAIL) // 8) * 8


def round_up(value, step):
    return -(-value // step) * step


def vmem():
    return pl.BlockSpec(memory_space=pltpu.VMEM)


def smem():
    return pl.BlockSpec(memory_space=pltpu.SMEM)


def anywhere():
    return pl.BlockSpec(memory_space=pl.ANY)


def params_of(**more):
    return pltpu.CompilerParams(vmem_limit_bytes=VMEM_LIMIT, **more)


COST_SCALE = 20


def cost(flops, bytes_accessed, transcendentals=0):
    return pl.CostEstimate(
        flops=int(COST_SCALE * flops),
        bytes_accessed=int(COST_SCALE * bytes_accessed),
        transcendentals=int(transcendentals),
    )


def nn(left, right):
    return jnp.dot(left, right, preferred_element_type=F32)


def nt(left, right):
    return lax.dot_general(left, right, (((1,), (1,)), ((), ())), preferred_element_type=F32)


class Geometry:
    def __init__(self, dp, fsdp, shard_len):
        assert dp == 4 and shard_len % LANES == 0 and fsdp % 2 == 0
        self.fsdp = fsdp
        self.devices = dp * fsdp
        self.line = fsdp // 2
        assert self.line & (self.line - 1) == 0
        self.rows = shard_len // LANES
        first, last = TABLE_ROW // self.rows, (SPLIT_ROW - 1) // self.rows
        assert last - first in (0, 1)
        self.spill_from, self.spill_to = last, first
        self.spill = SPLIT_ROW - self.rows * last if last != first else 0
        self.quarter = round_up(-(-(self.rows + 16 + self.spill) // 4), 8)
        self.slot = 4 * self.quarter
        assert self.slot % 16 == 0
        tiles = self.slot // 16
        self.chunk = max(t for t in range(1, 13) if tiles % t == 0)
        self.bit_x, self.bit_core, self.bit_y = 2 * fsdp, fsdp, 1

    def base(self, device):
        return (device * self.rows) // 16 * 16

    def permute(self, value, mask_core0, mask_core1):
        pairs = []
        for index in range(self.devices):
            core = (index // self.fsdp) % 2
            pairs.append((index, index ^ (mask_core1 if core else mask_core0)))
        return lax.ppermute(value, AXES, pairs)

    def core_swap(self, value):
        return self.permute(value, self.bit_core, self.bit_core)


def prepare_kernel(geo, me_ref, shard_ref, spill_ref, out_ref, pad_ref):
    rows, slot = geo.rows, geo.slot
    base = me_ref[0] * rows
    shift = lax.rem(base, 16)
    pad_ref[0:32, :] = jnp.zeros((32, LANES), F32)
    pad_ref[16 + rows : slot + 32, :] = jnp.zeros((slot + 16 - rows, LANES), F32)
    whole = rows // 64

    def place_body(i, _):
        r0 = i * 64
        pad_ref[pl.ds(16 + shift + r0, 64), :] = shard_ref[pl.ds(pl.multiple_of(r0, 64), 64), :]
        return 0

    lax.fori_loop(0, whole, place_body, 0)
    rest = rows - whole * 64
    if rest:
        pad_ref[pl.ds(16 + shift + whole * 64, rest), :] = shard_ref[whole * 64 : rows, :]
    if geo.spill:
        count = geo.spill

        @pl.when(me_ref[0] == geo.spill_to)
        def _():
            lane = lax.broadcasted_iota(jnp.int32, (count, LANES), 1)
            row = lax.broadcasted_iota(jnp.int32, (count, LANES), 0)
            flat = (rows * geo.spill_from + row) * LANES + lane
            at = 16 + rows * geo.spill_from - geo.base(geo.spill_to)
            pad_ref[at : at + count, :] = jnp.where(flat < SPLIT, spill_ref[0:count, :], 0.0)

    step = 16 * geo.chunk

    def body(i, _):
        r0 = pl.multiple_of(i * step, 16)
        here = pad_ref[pl.ds(r0 + 16, step), :]
        above = pad_ref[pl.ds(r0 + 15, step), :]
        lane = lax.broadcasted_iota(jnp.int32, (step, LANES), 1)
        row = lax.broadcasted_iota(jnp.int32, (step, LANES), 0)
        flat = (base - shift + r0 + row) * LANES + lane
        moved = jnp.where(lane >= LIFT, pltpu.roll(here, LIFT, 1), pltpu.roll(above, LIFT, 1))
        value = jnp.where(flat < SPLIT, here, jnp.where(flat >= SPLIT + LIFT, moved, 0.0))
        out_ref[pl.ds(r0, step), :] = value.astype(BF16)
        return 0

    lax.fori_loop(0, slot // step, body, 0)


def prepare(geo, me, shard, spill):
    return pl.pallas_call(
        partial(prepare_kernel, geo),
        out_shape=jax.ShapeDtypeStruct((geo.slot, LANES), BF16),
        in_specs=[smem(), vmem(), vmem()],
        out_specs=vmem(),
        scratch_shapes=[pltpu.VMEM((geo.slot + 32, LANES), F32)],
        compiler_params=params_of(),
        name="prepare_share",
    )(me, shard, spill)


def spot(geo, me_ref, device, own, quarter_x):
    core = me_ref[2] if own else 1 - me_ref[2]
    rel_x = quarter_x ^ me_ref[1]
    rel_z = (lax.rem(device, geo.fsdp) // 2) ^ me_ref[3]
    rel_y = lax.rem(device, 2) ^ me_ref[4]
    straight = core == 0
    first = jnp.where(straight, rel_x, rel_y)
    late = jnp.where(straight, rel_y, rel_x)
    return quarter_x * 2 + core, late, first * geo.line + rel_z


def by_group(geo, groups, device, action):
    if len(groups) == 1:
        action(0)
        return
    for position, group in enumerate(groups):
        pl.when(device // geo.fsdp == group)(partial(action, position))


class Region:
    def __init__(self, geo, row0, row1, matrix, vectors, span=None, high=None):
        self.row0, self.row1 = row0, row1
        self.mat_row, self.depth, self.cols = matrix
        self.start, self.stop = span or (0, self.depth)
        self.vectors = vectors
        self.low = max(row0 - 1, 0) // geo.rows
        self.high = (row1 - 1) // geo.rows if high is None else high
        self.slots = self.high - self.low + 1
        self.origin = geo.base(self.low)
        self.pitch = 17 if self.cols % 32 == 0 else 16
        self.stride = self.cols * self.pitch // 16
        self.scratch_tiles = (geo.base(self.high) + geo.slot - self.origin) // 16
        self.groups = sorted({d // geo.fsdp for d in range(self.low, self.high + 1)})

    def address(self, row):
        rel = row - self.origin
        return rel if self.pitch == 16 else rel + rel // 16

    def scratch(self):
        return pltpu.VMEM((self.scratch_tiles * self.pitch, LANES), F32)


def copy_rows(region, ref, row, count, move):
    done = 0
    while done < count:
        size = min(count - done, 16 - (row + done - region.origin) % 16)
        if region.pitch == 16:
            size = count - done
        move(region.address(row + done), done, size)
        done += size


def unpack_kernel(geo, region, block, aliased, me_ref, *refs):
    arrays = 4 * len(region.groups)
    srcs, refs = refs[:arrays], refs[arrays:]
    if aliased:
        refs = refs[1:]
    weight_ref, refs = refs[0], refs[1:]
    vec_refs, refs = refs[: len(region.vectors)], refs[len(region.vectors) :]
    flat_ref, slot_ref, stage_ref, sems, out_sem = refs
    quarter, pitch, cols = geo.quarter, region.pitch, region.cols
    total = (region.stop - region.start) // block

    def fetch(step):
        device = region.low + step
        buf = lax.rem(step, 2)

        def from_group(position):
            for own in range(2):
                for quarter_x in range(2):
                    q, late, at = spot(geo, me_ref, device, own, quarter_x)
                    to = pl.ds(pl.multiple_of(q * quarter, 8), quarter)
                    for side in range(2):
                        src = srcs[position * 4 + (1 - own) * 2 + side]

                        @pl.when(late == side)
                        def _(src=src, at=at, to=to, own=own, quarter_x=quarter_x):
                            pltpu.make_async_copy(
                                src.at[at],
                                slot_ref.at[buf, to],
                                sems.at[buf, own * 2 + quarter_x],
                            ).start()

        by_group(geo, region.groups, device, from_group)

    fetch(0)

    def slot_body(step, carry):
        tile_carry, done = carry

        @pl.when(step + 1 < region.slots)
        def _():
            fetch(step + 1)

        buf = lax.rem(step, 2)
        for number in range(4):
            pltpu.make_async_copy(
                srcs[0].at[0], slot_ref.at[buf, pl.ds(0, quarter)], sems.at[buf, number]
            ).wait()
        device = region.low + step
        first_tile = geo.base(device) // 16 - region.origin // 16
        next_row = (device + 1) * geo.rows // 16 * 16
        next_tile = next_row // 16 - region.origin // 16

        def rows_body(i, _):
            t0 = i * geo.chunk
            r0 = pl.multiple_of(t0 * 16, 16)
            if pitch == 16:
                to = pl.multiple_of((first_tile + t0) * 16, 16)
                flat_ref[pl.ds(to, geo.chunk * 16), :] = slot_ref[
                    buf, pl.ds(r0, geo.chunk * 16), :
                ].astype(F32)
            else:
                for t in range(geo.chunk):
                    flat_ref[pl.ds((first_tile + t0 + t) * pitch, 16), :] = slot_ref[
                        buf, pl.ds(r0 + t * 16, 16), :
                    ].astype(F32)
            return 0

        lax.fori_loop(0, geo.slot // 16 // geo.chunk, rows_body, 0)
        seam = pl.ds(first_tile * pitch, 16)
        flat_ref[seam, :] = flat_ref[seam, :] + tile_carry
        complete = jnp.maximum(next_row - region.mat_row - region.start * cols, 0) // (block * cols)
        complete = jnp.where(step == region.slots - 1, total, jnp.minimum(complete, total))

        def mat_body(i, _):
            to = pl.multiple_of(i * block, block)
            row = i * (block * region.stride)
            for c in range(cols):
                at = region.address(region.mat_row + region.start * cols + c)
                stage_ref[pl.ds(to, block), c * LANES : (c + 1) * LANES] = flat_ref[
                    pl.ds(at + row, block, stride=region.stride), :
                ].astype(BF16)
            pltpu.make_async_copy(
                stage_ref.at[pl.ds(to, block)],
                weight_ref.at[pl.ds(region.start + to, block)],
                out_sem,
            ).start()
            return 0

        lax.fori_loop(done, complete, mat_body, 0)
        return flat_ref[pl.ds(next_tile * pitch, 16), :], complete

    lax.fori_loop(0, region.slots, slot_body, (jnp.zeros((16, LANES), F32), jnp.int32(0)))
    for (row, count), out_ref in zip(region.vectors, vec_refs):

        def move(at, done, size, out_ref=out_ref):
            out_ref[done : done + size, :] = flat_ref[at : at + size, :]

        copy_rows(region, flat_ref, row, count, move)
    pltpu.make_async_copy(
        stage_ref, weight_ref.at[pl.ds(region.start, region.stop - region.start)], out_sem
    ).wait()


def unpack(geo, region, me, gathered, weight=None):
    operands = [me] + [array for group in region.groups for array in gathered[group]]
    specs = [smem()] + [anywhere()] * (len(operands) - 1)
    aliases = {}
    if weight is not None:
        operands.append(weight)
        specs.append(anywhere())
        aliases = {len(operands) - 1: 0}
    height = region.stop - region.start
    return pl.pallas_call(
        partial(unpack_kernel, geo, region, 64 if region.cols <= 8 else 16, weight is not None),
        out_shape=[jax.ShapeDtypeStruct((region.depth, region.cols * LANES), BF16)]
        + [jax.ShapeDtypeStruct((count, LANES), F32) for _, count in region.vectors],
        in_specs=specs,
        out_specs=[anywhere()] + [vmem()] * len(region.vectors),
        scratch_shapes=[
            region.scratch(),
            pltpu.VMEM((2, geo.slot, LANES), BF16),
            pltpu.VMEM((height, region.cols * LANES), BF16),
            pltpu.SemaphoreType.DMA((2, 4)),
            pltpu.SemaphoreType.DMA(()),
        ],
        input_output_aliases=aliases,
        compiler_params=params_of(),
        cost_estimate=cost(0, 8 * LANES * height * region.cols),
        name="unpack_weights",
    )(*operands)


def clear_rows(region, flat_ref):
    filled = sorted(
        [(region.mat_row, region.mat_row + region.depth * region.cols)]
        + [(row, row + count) for row, count in region.vectors]
    )
    edges = [region.origin] + [edge for run in filled for edge in run]
    edges.append(region.origin + 16 * region.scratch_tiles)
    for start, stop in zip(edges[::2], edges[1::2]):
        if stop > start:

            def move(at, done, size):
                for r in range(0, size, 64):
                    span = min(64, size - r)
                    flat_ref[at + r : at + r + span, :] = jnp.zeros((span, LANES), F32)

            copy_rows(region, flat_ref, start, stop - start, move)


class Emitter:
    def __init__(self, geo, region, shared, me_ref, outs, flat_ref, slot_ref, old_ref, sems, old_sem):
        self.geo, self.region, self.shared, self.me_ref = geo, region, shared, me_ref
        self.outs, self.flat_ref, self.slot_ref, self.old_ref = outs, flat_ref, slot_ref, old_ref
        self.sems, self.old_sem = sems, old_sem

    def copies(self, device, action):
        geo = self.geo
        count = 2 * geo.line

        def to_group(position):
            for own in range(2):
                for quarter_x in range(2):
                    q, late, at = spot(geo, self.me_ref, device, own, quarter_x)
                    rows = pl.ds(pl.multiple_of(q * geo.quarter, 8), geo.quarter)
                    action(
                        self.outs[position * 2 + 1 - own].at[late * count + at],
                        rows,
                        own * 2 + quarter_x,
                    )

        by_group(geo, self.region.groups, device, to_group)

    def begin(self):
        clear_rows(self.region, self.flat_ref)
        if self.shared:
            def action(place, rows, number):
                pltpu.make_async_copy(
                    place, self.old_ref.at[rows], self.old_sem.at[number]
                ).start()

            self.copies(self.region.high, action)

    def wait(self, parity):
        for number in range(4):
            pltpu.make_async_copy(
                self.slot_ref.at[parity, pl.ds(0, self.geo.quarter)],
                self.outs[0].at[0],
                self.sems.at[parity, number],
            ).wait()

    def slots_before(self, row):
        ready = (row - 1) // self.geo.rows - self.region.low
        return jnp.clip(ready, 0, self.region.slots)

    def emit(self, start, stop):
        geo, region, pitch = self.geo, self.region, self.region.pitch

        def slot_body(index, _):
            parity = lax.rem(index, 2)
            pl.when(index >= 2)(lambda: self.wait(parity))
            first_tile = geo.base(region.low + index) // 16 - region.origin // 16

            def convert(add):
                def rows_body(i, _):
                    t0 = i * geo.chunk
                    r0 = pl.multiple_of(t0 * 16, 16)
                    for t in range(geo.chunk):
                        value = self.flat_ref[pl.ds((first_tile + t0 + t) * pitch, 16), :]
                        here = pl.ds(r0 + t * 16, 16)
                        if add:
                            value = value + self.old_ref[here, :].astype(F32)
                        self.slot_ref[parity, here, :] = value.astype(BF16)
                    return 0

                lax.fori_loop(0, geo.slot // 16 // geo.chunk, rows_body, 0)

            if self.shared:
                last = index == region.slots - 1

                @pl.when(last)
                def _():
                    for number in range(4):
                        pltpu.make_async_copy(
                            self.outs[0].at[0],
                            self.old_ref.at[pl.ds(0, geo.quarter)],
                            self.old_sem.at[number],
                        ).wait()
                    convert(True)

                pl.when(jnp.logical_not(last))(lambda: convert(False))
            else:
                convert(False)

            def action(place, rows, number):
                pltpu.make_async_copy(
                    self.slot_ref.at[parity, rows], place, self.sems.at[parity, number]
                ).start()

            self.copies(region.low + index, action)
            return 0

        lax.fori_loop(start, stop, slot_body, 0)

    def finish(self):
        for index in range(max(0, self.region.slots - 2), self.region.slots):
            self.wait(index % 2)


def emit_scratch(geo, region):
    return [
        region.scratch(),
        pltpu.VMEM((2, geo.slot, LANES), BF16),
        pltpu.VMEM((geo.slot, LANES), BF16),
        pltpu.SemaphoreType.DMA((2, 4)),
        pltpu.SemaphoreType.DMA((4,)),
    ]


def store_columns(region, flat_ref, row0, first_col, values):
    height = values.shape[0]
    for c in range(values.shape[1] // LANES):
        at = region.address(region.mat_row + first_col + c) + row0 * region.stride
        flat_ref[pl.ds(at, height, stride=region.stride), :] = values[
            :, c * LANES : (c + 1) * LANES
        ]


def with_slots(geo, region, slots, operands, specs):
    shape = jax.ShapeDtypeStruct((4 * geo.line, geo.quarter, LANES), BF16)
    aliases = {}
    for position, group in enumerate(region.groups):
        for number in range(2):
            if group in slots:
                operands.append(slots[group][number])
                specs.append(anywhere())
                aliases[len(operands) - 1] = position * 2 + number
    return [shape] * (2 * len(region.groups)), aliases, len(aliases)


def updated_slots(region, slots, results):
    merged = dict(slots)
    for position, group in enumerate(region.groups):
        merged[group] = results[position * 2 : position * 2 + 2]
    return merged


def pack_kernel(geo, region, shared, grid_steps, height, skip, me_ref, a_ref, b_ref, *refs):
    vec_refs, refs = refs[: len(region.vectors)], refs[len(region.vectors) + skip :]
    arrays = 2 * len(region.groups)
    *scratch, left_ref = refs[arrays:]
    emitter = Emitter(geo, region, shared, me_ref, refs[:arrays], *scratch)
    flat_ref = emitter.flat_ref
    step = pl.program_id(0)

    @pl.when(step == 0)
    def _():
        emitter.begin()
        for (row, count), vec_ref in zip(region.vectors, vec_refs):

            def move(at, done, size, vec_ref=vec_ref):
                flat_ref[at : at + size, :] = vec_ref[done : done + size, :]

            copy_rows(region, flat_ref, row, count, move)

    left_ref[...] = a_ref[...].T

    def panel(j, _):
        lanes = pl.ds(pl.multiple_of(j * 512, 512), 512)
        store_columns(region, flat_ref, step * height, j * 4, nn(left_ref[...], b_ref[:, lanes]))
        return 0

    lax.fori_loop(0, region.cols // 4, panel, 0)
    emit_rows(emitter, step, grid_steps, height)


def emit_rows(emitter, step, grid_steps, height):
    region = emitter.region
    span = height * region.cols
    before = emitter.slots_before(region.mat_row + step * span)
    after = emitter.slots_before(region.mat_row + (step + 1) * span)
    last = step == grid_steps - 1
    emitter.emit(jnp.where(step == 0, 0, before), jnp.where(last, region.slots, after))
    pl.when(last)(emitter.finish)


def pack(geo, region, me, left, right, vectors, slots, shared):
    tokens = left.shape[0]
    height = 256
    steps = region.depth // height
    width = region.cols * LANES
    operands = [me, left, right] + vectors
    specs = [
        smem(),
        pl.BlockSpec((tokens, height), lambda k: (0, k)),
        pl.BlockSpec((tokens, width), lambda k: (0, 0), pipeline_mode=pl.Buffered(1)),
    ] + [pl.BlockSpec(vector.shape, lambda k: (0, 0)) for vector in vectors]
    shapes, aliases, skip = with_slots(geo, region, slots, operands, specs)
    results = pl.pallas_call(
        partial(pack_kernel, geo, region, shared, steps, height, skip),
        grid=(steps,),
        out_shape=shapes,
        in_specs=specs,
        out_specs=[anywhere()] * len(shapes),
        scratch_shapes=emit_scratch(geo, region) + [pltpu.VMEM((height, tokens), BF16)],
        input_output_aliases=aliases,
        compiler_params=params_of(),
        cost_estimate=cost(2 * tokens * region.depth * width, 2 * region.depth * width),
        name="weight_grad_pack",
    )(*operands)
    return updated_slots(region, slots, results)


def line_masks(geo):
    if geo.line == 4:
        return [[2, 4, 6]]
    return [[2 << bit] for bit in range(geo.line.bit_length() - 1)]


def after(value, *others):
    return lax.optimization_barrier((value,) + others)[0]


def spread_quarters(geo, share, dp_index):
    pieces = [lax.dynamic_index_in_dim(share, dp_index, 0, keepdims=False)]
    for offset in (1, 2, 3):
        piece = lax.dynamic_index_in_dim(share, dp_index ^ offset, 0, keepdims=False)
        mask = offset * geo.fsdp
        pieces.append(geo.permute(piece, mask, mask))
    return pieces


class Gather:
    def __init__(self, geo, piece):
        self.geo, self.held = geo, piece[None]

    def line(self, *deps):
        held = after(self.held, *deps)
        for masks in line_masks(self.geo):
            moved = [self.geo.permute(held, mask, mask) for mask in masks]
            held = jnp.concatenate([held] + moved, axis=0)
        self.held = held

    def across(self, *deps):
        held = after(self.held, *deps)
        self.near = jnp.concatenate(
            [held, self.geo.permute(held, self.geo.bit_x, self.geo.bit_y)], axis=0
        )

    def last(self, *deps):
        near = after(self.near, *deps)
        self.far = self.geo.permute(near, self.geo.bit_y, self.geo.bit_x)
        self.near_other = self.geo.core_swap(near)

    def finish(self, *deps):
        far = after(self.far, *deps)
        return [self.near, far, self.near_other, self.geo.core_swap(far)]


class Reduction:
    def __init__(self, geo, slots):
        self.geo = geo
        self.keep, send = slots
        self.got = geo.core_swap(send)

    def last(self, *deps):
        count = 2 * self.geo.line
        got = after(self.got, *deps)
        far = (self.keep[count:].astype(F32) + got[count:].astype(F32)).astype(BF16)
        self.from_far = self.geo.permute(far, self.geo.bit_y, self.geo.bit_x)
        self.got = got
        return far

    def across(self, *deps):
        count = 2 * self.geo.line
        from_far = after(self.from_far, *deps)
        near = self.keep[:count].astype(F32) + self.got[:count].astype(F32) + from_far.astype(F32)
        count = self.geo.line
        moved = near[count:].astype(BF16)
        self.from_across = self.geo.permute(moved, self.geo.bit_x, self.geo.bit_y)
        self.near = near[:count]
        return moved

    def line(self, *deps):
        held = self.near + after(self.from_across, *deps).astype(F32)
        stages = line_masks(self.geo)[::-1]
        for masks in stages[:-1]:
            held = self.add_line(held, masks)[0]
        self.held, self.parts = self.send_line(held, stages[-1])
        return self.held

    def send_line(self, held, masks):
        block = held.shape[0] // (len(masks) + 1)
        parts = [
            self.geo.permute(
                held[(number + 1) * block : (number + 2) * block].astype(BF16), mask, mask
            )
            for number, mask in enumerate(masks)
        ]
        return held[:block], parts

    def add_line(self, held, masks):
        held, parts = self.send_line(held, masks)
        for part in parts:
            held = held + part.astype(F32)
        return held, None

    def total(self, *deps):
        total = self.held
        for part in self.parts:
            total = total + after(part, *deps).astype(F32)
        return total[0]


def collect_early(geo, sums, dp_index):
    mine = [jnp.where(dp_index == group, sums[group], 0.0) for group in (1, 2, 3)]
    pieces = [mine[0] + mine[1] + mine[2]]
    for offset in (1, 2, 3):
        target = dp_index ^ offset
        piece = jnp.where(target == 1, sums[1], jnp.where(target == 2, sums[2], sums[3]))
        pairs = [
            (dp * geo.fsdp + i, (dp ^ offset) * geo.fsdp + i)
            for dp in range(4)
            for i in range(geo.fsdp)
            if dp != offset
        ]
        pieces.append(lax.ppermute(piece, AXES, pairs))
    return pieces


def collect_late(geo, total, dp_index):
    pieces = [jnp.where(dp_index == 0, total, 0.0)]
    for offset in (1, 2, 3):
        pairs = [(offset * geo.fsdp + i, i) for i in range(geo.fsdp)]
        pieces.append(lax.ppermute(total, AXES, pairs))
    return pieces


def sum_everywhere(geo, value):
    mask = 1
    while mask < geo.devices:
        value = value + geo.permute(value, mask, mask)
        mask *= 2
    return value


def tensor_sums(sums_ref, squares, flat, low, high, tensors):
    for t in tensors:

        @pl.when((low < STARTS[t + 1]) & (high > STARTS[t]))
        def _(t=t):
            inside = (flat >= STARTS[t]) & (flat < STARTS[t + 1])
            part = jnp.where(inside, squares, 0.0)
            sums_ref[t : t + 1, :] += jnp.sum(part, axis=0, keepdims=True)


def squares_kernel(geo, groups, me_ref, *refs):
    sums_ref = refs[-1]
    sums_ref[...] = jnp.zeros((16, LANES), F32)
    span = 8 * max(t for t in range(1, 13) if geo.quarter // 8 % t == 0)
    dp_index = me_ref[1] * 2 + me_ref[2]
    for position, group in enumerate(groups):
        device = group * geo.fsdp + me_ref[3] * 2 + me_ref[4]
        share = geo.rows * LANES
        base = device * geo.rows
        first = base - lax.rem(base, 16) + dp_index * geo.quarter

        def body(i, _, position=position, base=base, first=first):
            r0 = pl.multiple_of(i * span, 8)
            value = refs[position][pl.ds(r0, span), :]
            lane = lax.broadcasted_iota(jnp.int32, (span, LANES), 1)
            row = lax.broadcasted_iota(jnp.int32, (span, LANES), 0)
            lifted = (first + r0 + row) * LANES + lane
            flat = jnp.where(lifted < SPLIT, lifted, lifted - LIFT)
            owned = (flat >= base * LANES) & (flat < base * LANES + share)
            low = (first + r0) * LANES - LIFT
            high = (first + r0 + span) * LANES
            squares = jnp.where(owned, value * value, 0.0)
            tensor_sums(sums_ref, squares, flat, low, high, (2,) + tuple(range(5, 13)))
            return 0

        lax.fori_loop(0, geo.quarter // span, body, 0)


def square_sums(geo, me, groups, sums):
    return pl.pallas_call(
        partial(squares_kernel, geo, groups),
        out_shape=jax.ShapeDtypeStruct((16, LANES), F32),
        in_specs=[smem()] + [vmem()] * len(sums),
        out_specs=vmem(),
        compiler_params=params_of(),
        name="square_sums",
    )(me, *sums)


def update_kernel(geo, me_ref, coef_ref, *refs):
    quarters, (late_ref, p_ref, m_ref, v_ref), outs = refs[:8], refs[8:12], refs[12:]
    params_out, first_out, second_out, grad_ref = outs
    rows, quarter = geo.rows, geo.quarter
    base = me_ref[0] * rows
    shift = lax.rem(base, 16)
    dp_index = me_ref[1] * 2 + me_ref[2]
    margin = 128
    for offset in range(4):
        to = pl.multiple_of(margin + (dp_index ^ offset) * quarter, 8)
        grad_ref[pl.ds(to, quarter), :] = quarters[offset][...] + quarters[4 + offset][...]
    for row, count, at in ((0, HEAD_ROWS, 0), (TAIL_ROW, LATE_TAIL, HEAD_ROWS)):

        @pl.when((base < row + count) & (base + rows > row))
        def _(row=row, count=count, at=at):
            lane = lax.broadcasted_iota(jnp.int32, (count, LANES), 1)
            p_rows = lax.broadcasted_iota(jnp.int32, (count, LANES), 0) + row
            before = p_rows * LANES + lane < SPLIT
            to = jnp.clip(margin + shift + row - base, 0, margin + geo.slot)
            here = pl.ds(to, count)
            late = late_ref[at : at + count, :]
            grad_ref[here, :] = jnp.where(before, late, grad_ref[here, :])

    span = 64
    scale, first_fix, second_fix, rate = (coef_ref[i] for i in range(4))

    def body(i, _):
        r0 = jnp.minimum(i * span, rows - span)
        here = grad_ref[pl.ds(margin + shift + r0, span), :]
        below = grad_ref[pl.ds(margin + shift + r0 + 1, span), :]
        lane = lax.broadcasted_iota(jnp.int32, (span, LANES), 1)
        row = lax.broadcasted_iota(jnp.int32, (span, LANES), 0)
        flat = (base + r0 + row) * LANES + lane
        back = LANES - LIFT
        moved = jnp.where(lane < back, pltpu.roll(here, back, 1), pltpu.roll(below, back, 1))
        scaled = jnp.where(flat < SPLIT, here, moved) * scale
        at = pl.ds(r0, span)
        first_new = 0.9 * m_ref[at, :] + 0.1 * scaled
        second_new = 0.999 * v_ref[at, :] + 0.001 * scaled * scaled
        params = p_ref[at, :]
        update = first_new / first_fix / (jnp.sqrt(second_new / second_fix) + 1e-08) + 0.05 * params
        params_out[at, :] = params - rate * update
        first_out[at, :] = first_new
        second_out[at, :] = second_new
        return 0

    lax.fori_loop(0, -(-rows // span), body, 0)


def update_step(geo, me, coef, quarters, late, params, first, second):
    rows = jax.ShapeDtypeStruct((geo.rows, LANES), F32)
    return pl.pallas_call(
        partial(update_kernel, geo),
        out_shape=[rows, rows, rows],
        in_specs=[smem(), smem()] + [vmem()] * 12,
        out_specs=[vmem()] * 3,
        scratch_shapes=[pltpu.VMEM((geo.slot + 384, LANES), F32)],
        compiler_params=params_of(),
        name="moments_update",
    )(me, coef, *quarters, late, params, first, second)


def row_blocks(tokens):
    return tokens // 4 if tokens % 64 == 0 else tokens


def permute_in_kernel(rows_ref, patches_ref, cot_ref, x_ref, g_ref):
    arrivals = patches_ref.shape[0]
    lane = lax.broadcasted_iota(jnp.int32, (WP, arrivals), 1)
    pick = jnp.where(rows_ref[...] == lane, 1.0, 0.0).astype(BF16)
    x_ref[...] = nn(pick, patches_ref[...]).astype(BF16)
    g_ref[...] = nn(pick, cot_ref[...]).astype(BF16)


def permute_in(row_ids, patches, cotangent):
    tokens = row_ids.shape[0]
    whole = pl.BlockSpec(patches.shape, lambda i: (0, 0))
    part = pl.BlockSpec((WP, D), lambda i: (i, 0))
    shape = jax.ShapeDtypeStruct((tokens, D), BF16)
    return pl.pallas_call(
        permute_in_kernel,
        grid=(tokens // WP,),
        out_shape=[shape, shape],
        in_specs=[pl.BlockSpec((WP, 1), lambda i: (i, 0)), whole, whole],
        out_specs=[part, part],
        compiler_params=params_of(),
        cost_estimate=cost(4 * tokens * tokens * D, 8 * tokens * D),
        name="window_order",
    )(row_ids, patches, cotangent)


def permute_out_kernel(rows_ref, x_ref, out_ref):
    count = out_ref.shape[0]
    arrival = lax.broadcasted_iota(jnp.int32, (count, rows_ref.shape[1]), 0)
    pick = jnp.where(rows_ref[...] == arrival + pl.program_id(0) * count, 1.0, 0.0).astype(BF16)
    out_ref[...] = nn(pick, x_ref[...]).astype(BF16)


def permute_out(row_ids, values, arrivals):
    tokens = values.shape[0]
    block = 160 if arrivals % 160 == 0 else arrivals
    return pl.pallas_call(
        permute_out_kernel,
        grid=(arrivals // block,),
        out_shape=jax.ShapeDtypeStruct((arrivals, D), BF16),
        in_specs=[
            pl.BlockSpec((1, tokens), lambda i: (0, 0)),
            pl.BlockSpec((tokens, D), lambda i: (0, 0)),
        ],
        out_specs=pl.BlockSpec((block, D), lambda i: (i, 0)),
        compiler_params=params_of(),
        cost_estimate=cost(2 * tokens * arrivals * D, 4 * tokens * D),
        name="arrival_order",
    )(row_ids, values)


def normalized(x):
    center = x - jnp.mean(x, axis=-1, keepdims=True)
    spread = jnp.mean(center * center, axis=-1, keepdims=True)
    inverse = lax.rsqrt(spread + 1e-05)
    return center * inverse, inverse


def normalized_back(e, xhat, inverse):
    mean = jnp.mean(e, axis=-1, keepdims=True)
    along = jnp.mean(e * xhat, axis=-1, keepdims=True)
    return (e - mean - xhat * along) * inverse


def mix_kernel(x_ref, gain_ref, shift_ref, w_ref, b_ref, normed_ref, mixed_ref):
    step = pl.program_id(0)
    tokens = x_ref.shape[0]

    @pl.when(step == 0)
    def _():
        def body(i, _):
            rows = pl.ds(pl.multiple_of(i * 16, 16), 16)
            xhat, _ = normalized(x_ref[rows, :].astype(F32))
            normed_ref[rows, :] = (xhat * gain_ref[...] + shift_ref[...]).astype(BF16)
            return 0

        lax.fori_loop(0, tokens // 16, body, 0, unroll=4)

    mixed = nn(normed_ref[...], w_ref[...]) + b_ref[...]
    scale = jnp.where(step < D // w_ref.shape[1], F32(HEAD_DIM ** (-0.5)), F32(1.0))
    mixed_ref[...] = (mixed * scale).astype(BF16)


def mix(x, gain, shift, weight, bias):
    tokens = x.shape[0]
    width = 512
    rows = pl.BlockSpec((tokens, D), lambda j: (0, 0))
    vec = pl.BlockSpec((1, D), lambda j: (0, 0))
    return pl.pallas_call(
        mix_kernel,
        grid=(3 * D // width,),
        out_shape=[
            jax.ShapeDtypeStruct((tokens, D), BF16),
            jax.ShapeDtypeStruct((tokens, 3 * D), BF16),
        ],
        in_specs=[
            rows,
            vec,
            vec,
            pl.BlockSpec((D, width), lambda j: (0, j)),
            pl.BlockSpec((1, width), lambda j: (0, j)),
        ],
        out_specs=[rows, pl.BlockSpec((tokens, width), lambda j: (0, j))],
        compiler_params=params_of(),
        cost_estimate=cost(6 * tokens * D * D, 6 * D * D + 8 * tokens * D),
        name="mix_rows",
    )(x, gain, shift, weight, bias)


def bias_kernel(ids_ref, table_ref, out_ref):
    entries = table_ref.shape[1]

    def body(j, _):
        entry = lax.broadcasted_iota(jnp.int32, (entries, LANES), 0)
        pick = jnp.where(ids_ref[pl.ds(j, 1), :] == entry, 1.0, 0.0).astype(BF16)
        out_ref[:, pl.ds(j, 1), :] = nn(table_ref[...], pick).reshape(HEADS, 1, LANES)
        return 0

    lax.fori_loop(0, WT, body, 0, unroll=4)
    for j in range(WT, WP):
        out_ref[:, j : j + 1, :] = jnp.full((HEADS, 1, LANES), -1e30, F32)


def score_bias(ids, table):
    return pl.pallas_call(
        bias_kernel,
        out_shape=jax.ShapeDtypeStruct((HEADS, WP, LANES), F32),
        in_specs=[vmem(), vmem()],
        out_specs=vmem(),
        compiler_params=params_of(),
        cost_estimate=cost(2 * HEADS * WP * LANES * 384, 4 * HEADS * WP * LANES),
        name="score_bias",
    )(ids, table)


def bias_back_kernel(ids_ref, sums_ref, out_ref):
    entries = out_ref.shape[0]
    out_ref[...] = jnp.zeros(out_ref.shape, F32)

    def body(j, _):
        lane = lax.broadcasted_iota(jnp.int32, (HEADS, LANES), 1)
        row = jnp.where(lane < WT, sums_ref[:, pl.ds(j, 1), :].reshape(HEADS, LANES), 0.0)
        high = row.astype(BF16)
        rest = row - high.astype(F32)
        middle = rest.astype(BF16)
        low = (rest - middle.astype(F32)).astype(BF16)
        parts = jnp.concatenate([high, middle, low], axis=0)
        entry = lax.broadcasted_iota(jnp.int32, (entries, LANES), 0)
        pick = jnp.where(ids_ref[pl.ds(j, 1), :] == entry, 1.0, 0.0).astype(BF16)
        out_ref[...] += nt(pick, parts)
        return 0

    lax.fori_loop(0, WT, body, 0, unroll=4)


def score_bias_back(ids, sums, entries):
    parts = pl.pallas_call(
        bias_back_kernel,
        out_shape=jax.ShapeDtypeStruct((entries, 3 * HEADS), F32),
        in_specs=[vmem(), vmem()],
        out_specs=vmem(),
        compiler_params=params_of(),
        cost_estimate=cost(6 * HEADS * WP * LANES * 384, 4 * HEADS * WP * LANES),
        name="score_bias_back",
    )(ids, sums)
    return parts[:, :HEADS] + parts[:, HEADS : 2 * HEADS] + parts[:, 2 * HEADS :]


def pad_rows(x, rows):
    return jnp.concatenate([x, jnp.zeros((rows - x.shape[0], x.shape[1]), x.dtype)], axis=0)


def one_head(x, head):
    lane = lax.broadcasted_iota(jnp.int32, x.shape, 1)
    return jnp.where(lane // HEAD_DIM == head, x, jnp.zeros_like(x))


def by_head(x):
    return jnp.concatenate([one_head(x, head) for head in range(QUAD)], axis=0)


def attention_kernel(q_ref, k_ref, v_ref, bias_ref, out_ref, log_ref):
    def block(b, _):
        lanes = pl.ds(pl.multiple_of(b * LANES, LANES), LANES)
        queries = pad_rows(q_ref[:, lanes], LANES)
        scores = nt(by_head(k_ref[:, lanes]), queries)
        values = v_ref[:, lanes].astype(F32).T.astype(BF16)
        parts = []
        for head in range(QUAD):
            s = scores[head * WP : (head + 1) * WP] + bias_ref[b * QUAD + head]
            top = jnp.max(s, axis=0, keepdims=True)
            e = jnp.exp(s - top)
            total = jnp.sum(e, axis=0, keepdims=True)
            probs = (e * (1.0 / total)).astype(BF16)
            log_ref[0, pl.ds(b * QUAD + head, 1), :] = top + jnp.log(total)
            parts.append(nn(values[head * HEAD_DIM : (head + 1) * HEAD_DIM], probs))
        context = jnp.concatenate(parts, axis=0).T
        out_ref[:, lanes] = context[:WP].astype(BF16)
        return 0

    lax.fori_loop(0, HEADS // QUAD, block, 0, unroll=4)


def attention(mixed, bias):
    windows = mixed.shape[0] // WP

    def third(c):
        return pl.BlockSpec((WP, D), lambda i, c=c: (i, c))

    return pl.pallas_call(
        attention_kernel,
        grid=(windows,),
        out_shape=[
            jax.ShapeDtypeStruct((windows * WP, D), BF16),
            jax.ShapeDtypeStruct((windows, HEADS, LANES), F32),
        ],
        in_specs=[third(0), third(1), third(2), pl.BlockSpec(bias.shape, lambda i: (0, 0, 0))],
        out_specs=[third(0), pl.BlockSpec((1, HEADS, LANES), lambda i: (i, 0, 0))],
        compiler_params=params_of(),
        cost_estimate=cost(12e9, 8 * windows * WP * D, windows * HEADS * WP * LANES),
        name="attention",
    )(mixed, mixed, mixed, bias)


def attention_back_kernel(
    q_ref, k_ref, v_ref, g_ref, bias_ref, log_ref, out_ref, acc_ref, column_ref
):
    @pl.when(pl.program_id(0) == 0)
    def _():
        acc_ref[...] = jnp.zeros(acc_ref.shape, F32)
        column_ref[...] = jnp.zeros(column_ref.shape, F32)

    def put(third, b, value):
        lanes = pl.ds(pl.multiple_of(third * D + b * LANES, LANES), LANES)
        low = value.astype(BF16)
        out_ref[:, lanes] = low
        column_ref[0:1, lanes] += jnp.sum(low.astype(F32), axis=0, keepdims=True)

    def block(b, _):
        lanes = pl.ds(pl.multiple_of(b * LANES, LANES), LANES)
        queries = pad_rows(q_ref[:, lanes], LANES)
        grads = pad_rows(g_ref[:, lanes], LANES)
        keys = k_ref[:, lanes]
        scores = nt(by_head(keys), queries)
        probs_grads = nt(by_head(v_ref[:, lanes]), grads)
        keys_t = keys.astype(F32).T.astype(BF16)
        query_parts, probs_parts, score_parts = [], [], []
        for head in range(QUAD):
            span = slice(head * WP, (head + 1) * WP)
            s = scores[span] + bias_ref[b * QUAD + head]
            probs = jnp.exp(s - log_ref[0, pl.ds(b * QUAD + head, 1), :])
            probs_grad = probs_grads[span]
            along = jnp.sum(probs * probs_grad, axis=0, keepdims=True)
            score_grad = (probs * (probs_grad - along)).astype(BF16)
            acc_ref[b * QUAD + head] += score_grad.astype(F32)
            probs_parts.append(probs.astype(BF16))
            score_parts.append(score_grad)
            query_parts.append(nn(keys_t[head * HEAD_DIM : (head + 1) * HEAD_DIM], score_grad))
        put(2, b, nn(jnp.concatenate(probs_parts, axis=1), by_head(grads)))
        put(1, b, nn(jnp.concatenate(score_parts, axis=1), by_head(queries)))
        put(0, b, jnp.concatenate(query_parts, axis=0).T[:WP] * HEAD_DIM ** (-0.5))
        return 0

    lax.fori_loop(0, HEADS // QUAD, block, 0, unroll=4)


def attention_back(mixed, grads, bias, logs):
    windows = mixed.shape[0] // WP

    def third(c):
        return pl.BlockSpec((WP, D), lambda i, c=c: (i, c))

    fixed = pl.BlockSpec(bias.shape, lambda i: (0, 0, 0))
    return pl.pallas_call(
        attention_back_kernel,
        grid=(windows,),
        out_shape=[
            jax.ShapeDtypeStruct((windows * WP, 3 * D), BF16),
            jax.ShapeDtypeStruct(bias.shape, F32),
            jax.ShapeDtypeStruct((8, 3 * D), F32),
        ],
        in_specs=[
            third(0),
            third(1),
            third(2),
            third(0),
            fixed,
            pl.BlockSpec((1, HEADS, LANES), lambda i: (i, 0, 0)),
        ],
        out_specs=[
            pl.BlockSpec((WP, 3 * D), lambda i: (i, 0)),
            fixed,
            pl.BlockSpec((8, 3 * D), lambda i: (0, 0)),
        ],
        compiler_params=params_of(),
        cost_estimate=cost(25e9, 16 * windows * WP * D, windows * HEADS * WP * LANES),
        name="attention_back",
    )(mixed, mixed, mixed, grads, bias, logs)


def middle_kernel(x_ref, a_ref, w_ref, b_ref, gain_ref, shift_ref, middle_ref, second_ref):
    middle = x_ref[...].astype(F32) + nn(a_ref[...], w_ref[...]) + b_ref[...]
    middle_ref[...] = middle
    xhat, _ = normalized(middle)
    second_ref[...] = (xhat * gain_ref[...] + shift_ref[...]).astype(BF16)


def middle_rows(x, attended, weight, bias, gain, shift):
    tokens = x.shape[0]
    block = row_blocks(tokens)
    rows = pl.BlockSpec((block, D), lambda i: (i, 0))
    vec = pl.BlockSpec((1, D), lambda i: (0, 0))
    return pl.pallas_call(
        middle_kernel,
        grid=(tokens // block,),
        out_shape=[
            jax.ShapeDtypeStruct((tokens, D), F32),
            jax.ShapeDtypeStruct((tokens, D), BF16),
        ],
        in_specs=[rows, rows, pl.BlockSpec((D, D), lambda i: (0, 0)), vec, vec, vec],
        out_specs=[rows, rows],
        compiler_params=params_of(),
        cost_estimate=cost(2 * tokens * D * D, 10 * tokens * D),
        name="middle_rows",
    )(x, attended, weight, bias, gain, shift)


def mlp_up_kernel(geo, region, shared, steps, skip, me_ref, s_ref, g_ref, w_ref, b_ref, *refs):
    vec_ref, refs = refs[0], refs[1 + skip :]
    hidden_ref, slope_ref, refs = refs[0], refs[1], refs[2:]
    arrays = 2 * len(region.groups)
    *scratch, held_ref = refs[arrays:]
    emitter = Emitter(geo, region, shared, me_ref, refs[:arrays], *scratch)
    flat_ref = emitter.flat_ref
    step = pl.program_id(0)
    height = w_ref.shape[1]

    @pl.when(step == 0)
    def _():
        emitter.begin()
        ((row, count),) = region.vectors

        def move(at, done, size):
            flat_ref[at : at + size, :] = vec_ref[done : done + size, :]

        copy_rows(region, flat_ref, row, count, move)

    block = jnp.maximum(step - 1, 0)
    left = held_ref[lax.rem(step + 1, 2)].T
    u = nn(s_ref[...], w_ref[...]) + b_ref[...]
    below = 0.5 * (1.0 + lax.erf(u * F32(math.sqrt(0.5))))
    density = jnp.exp(-0.5 * u * u) * F32(1.0 / math.sqrt(2.0 * math.pi))
    hidden = (u * below).astype(BF16)
    for j in range(0, D, 512):
        store_columns(
            region, flat_ref, block * height, j // LANES, nn(left, g_ref[:, j : j + 512])
        )
    hidden_ref[...] = hidden
    slope_ref[...] = below + u * density
    held_ref[lax.rem(step, 2)] = hidden
    pl.when(step > 0)(lambda: emit_rows(emitter, step - 1, steps, height))


def mlp_up(geo, region, me, second, grad_out, weight, bias, vector, slots, shared):
    tokens = second.shape[0]
    height = 256
    steps = FF // height
    last = steps - 1
    rows = pl.BlockSpec((tokens, D), lambda k: (0, 0), pipeline_mode=pl.Buffered(1))
    columns = pl.BlockSpec((tokens, height), lambda k: (0, jnp.minimum(k, last)))
    operands = [me, second, grad_out, weight, bias, vector]
    specs = [
        smem(),
        rows,
        rows,
        pl.BlockSpec((D, height), lambda k: (0, jnp.minimum(k, last))),
        pl.BlockSpec((1, height), lambda k: (0, jnp.minimum(k, last))),
        pl.BlockSpec(vector.shape, lambda k: (0, 0)),
    ]
    shapes, aliases, skip = with_slots(geo, region, slots, operands, specs)
    results = pl.pallas_call(
        partial(mlp_up_kernel, geo, region, shared, steps, skip),
        grid=(steps + 1,),
        out_shape=[
            jax.ShapeDtypeStruct((tokens, FF), BF16),
            jax.ShapeDtypeStruct((tokens, FF), F32),
        ]
        + shapes,
        in_specs=specs,
        out_specs=[columns, columns] + [anywhere()] * len(shapes),
        scratch_shapes=emit_scratch(geo, region) + [pltpu.VMEM((2, tokens, height), BF16)],
        input_output_aliases={key: value + 2 for key, value in aliases.items()},
        compiler_params=params_of(),
        cost_estimate=cost(4 * tokens * D * FF, 4 * D * FF + 6 * tokens * FF),
        name="mlp_up",
    )(*operands)
    return results[0], results[1], updated_slots(region, slots, results[2:])


def mlp_down_kernel(geo, region, shared, steps, skip, me_ref, *refs):
    (h_ref, slope_ref, s_ref, g_ref, up_ref, down_ref, m_ref, b_ref) = refs[:8]
    refs = refs[8 + skip :]
    result_ref, grad_ref, refs = refs[0], refs[1], refs[2:]
    arrays = 2 * len(region.groups)
    *scratch, left_ref, sum_ref = refs[arrays:]
    emitter = Emitter(geo, region, shared, me_ref, refs[:arrays], *scratch)
    flat_ref = emitter.flat_ref
    step = pl.program_id(0)
    width = h_ref.shape[1]

    @pl.when(step == 0)
    def _():
        emitter.begin()
        left_ref[...] = s_ref[...].T
        sum_ref[...] = jnp.zeros(sum_ref.shape, F32)
        grad_ref[...] = jnp.zeros(grad_ref.shape, F32)

    pre = (nt(g_ref[...], down_ref[...]) * slope_ref[...]).astype(BF16)
    column = jnp.sum(pre.astype(F32), axis=0, keepdims=True)
    sum_ref[...] += nn(h_ref[...], down_ref[...])
    grad_ref[...] += nt(pre, up_ref[...])
    cols = width // LANES
    ((vec_row, _),) = region.vectors
    for c in range(cols):
        at = region.address(vec_row + step * cols + c)
        flat_ref[pl.ds(at, 1), :] = column[:, c * LANES : (c + 1) * LANES]
    for r in range(0, D, 256):
        store_columns(region, flat_ref, r, step * cols, nn(left_ref[r : r + 256, :], pre))

    @pl.when(step == steps - 1)
    def _():
        result_ref[...] = (sum_ref[...] + m_ref[...] + b_ref[...]).astype(BF16)
        emitter.emit(0, region.slots)
        emitter.finish()


def mlp_down(geo, region, me, hidden, slope, second, grad_out, up, down, middle, bias, slots, shared):
    tokens = second.shape[0]
    width = 512
    steps = FF // width
    rows = pl.BlockSpec((tokens, D), lambda k: (0, 0), pipeline_mode=pl.Buffered(1))
    columns = pl.BlockSpec((tokens, width), lambda k: (0, k))
    operands = [me, hidden, slope, second, grad_out, up, down, middle, bias]
    specs = [
        smem(),
        columns,
        columns,
        rows,
        rows,
        pl.BlockSpec((D, width), lambda k: (0, k)),
        pl.BlockSpec((width, D), lambda k: (k, 0)),
        rows,
        pl.BlockSpec((1, D), lambda k: (0, 0)),
    ]
    shapes, aliases, skip = with_slots(geo, region, slots, operands, specs)
    whole = pl.BlockSpec((tokens, D), lambda k: (0, 0))
    results = pl.pallas_call(
        partial(mlp_down_kernel, geo, region, shared, steps, skip),
        grid=(steps,),
        out_shape=[
            jax.ShapeDtypeStruct((tokens, D), BF16),
            jax.ShapeDtypeStruct((tokens, D), F32),
        ]
        + shapes,
        in_specs=specs,
        out_specs=[whole, whole] + [anywhere()] * len(shapes),
        scratch_shapes=emit_scratch(geo, region)
        + [
            pltpu.VMEM((D, tokens), BF16),
            pltpu.VMEM((tokens, D), F32),
        ],
        input_output_aliases={key: value + 2 for key, value in aliases.items()},
        compiler_params=params_of(),
        cost_estimate=cost(8 * tokens * D * FF, 6 * D * FF + 6 * tokens * FF),
        name="mlp_down",
    )(*operands)
    return results[0], results[1], updated_slots(region, slots, results[2:])


def middle_back_kernel(s_ref, m_ref, g_ref, gain_ref, w_ref, mg_ref, bg_ref, cg_ref, vec_ref):
    @pl.when(pl.program_id(0) == 0)
    def _():
        vec_ref[...] = jnp.zeros(vec_ref.shape, F32)

    grad = s_ref[...]
    xhat, inverse = normalized(m_ref[...])
    middle_grad = g_ref[...].astype(F32) + normalized_back(grad * gain_ref[...], xhat, inverse)
    branch = middle_grad.astype(BF16)
    mg_ref[...] = middle_grad
    bg_ref[...] = branch
    cg_ref[...] = nt(branch, w_ref[...]).astype(BF16)
    vec_ref[0:1, :] += jnp.sum(branch.astype(F32), axis=0, keepdims=True)
    vec_ref[1:2, :] += jnp.sum(grad * xhat, axis=0, keepdims=True)
    vec_ref[2:3, :] += jnp.sum(grad, axis=0, keepdims=True)


def middle_back(second_grad, middle, grad_out, gain, weight):
    tokens = middle.shape[0]
    block = row_blocks(tokens)
    rows = pl.BlockSpec((block, D), lambda i: (i, 0))
    low = jax.ShapeDtypeStruct((tokens, D), BF16)
    return pl.pallas_call(
        middle_back_kernel,
        grid=(tokens // block,),
        out_shape=[
            jax.ShapeDtypeStruct((tokens, D), F32),
            low,
            low,
            jax.ShapeDtypeStruct((8, D), F32),
        ],
        in_specs=[
            rows,
            rows,
            rows,
            pl.BlockSpec((1, D), lambda i: (0, 0)),
            pl.BlockSpec((D, D), lambda i: (0, 0)),
        ],
        out_specs=[rows, rows, rows, pl.BlockSpec((8, D), lambda i: (0, 0))],
        compiler_params=params_of(),
        cost_estimate=cost(2 * tokens * D * D, 18 * tokens * D),
        name="middle_back",
    )(second_grad, middle, grad_out, gain, weight)


def first_back_kernel(mixed_ref, w_ref, x_ref, mg_ref, gain_ref, out_ref, vec_ref):
    @pl.when(pl.program_id(0) == 0)
    def _():
        vec_ref[...] = jnp.zeros(vec_ref.shape, F32)

    grad = nt(mixed_ref[...], w_ref[...])
    xhat, inverse = normalized(x_ref[...].astype(F32))
    inner = normalized_back(grad * gain_ref[...], xhat, inverse)
    out_ref[...] = (mg_ref[...] + inner).astype(BF16)
    vec_ref[0:1, :] += jnp.sum(grad * xhat, axis=0, keepdims=True)
    vec_ref[1:2, :] += jnp.sum(grad, axis=0, keepdims=True)


def first_back(mixed_grad, weight, x, middle_grad, gain):
    tokens = x.shape[0]
    block = row_blocks(tokens)
    rows = pl.BlockSpec((block, D), lambda i: (i, 0))
    return pl.pallas_call(
        first_back_kernel,
        grid=(tokens // block,),
        out_shape=[
            jax.ShapeDtypeStruct((tokens, D), BF16),
            jax.ShapeDtypeStruct((8, D), F32),
        ],
        in_specs=[
            pl.BlockSpec((block, 3 * D), lambda i: (i, 0)),
            pl.BlockSpec((D, 3 * D), lambda i: (0, 0), pipeline_mode=pl.Buffered(1)),
            rows,
            rows,
            pl.BlockSpec((1, D), lambda i: (0, 0)),
        ],
        out_specs=[rows, pl.BlockSpec((8, D), lambda i: (0, 0))],
        compiler_params=params_of(),
        cost_estimate=cost(6 * tokens * D * D, 6 * D * D + 14 * tokens * D),
        name="first_back",
    )(mixed_grad, weight, x, middle_grad, gain)


def split_span(geo, row, depth, cols, block):
    group = (row // geo.rows) // geo.fsdp
    edge = (group + 1) * geo.fsdp * geo.rows // 16 * 16
    inside = max(0, (edge - row) // cols) // block * block
    return min(depth, inside)


def local(
    patches,
    cotangent,
    window_rows,
    rel_index,
    params,
    first_moment,
    second_moment,
    learn_rate,
    step_count,
):
    arrivals = patches.shape[0]
    windows = arrivals // WT
    geo = Geometry(lax.axis_size("dp"), lax.axis_size("fsdp"), params.shape[0])
    dp_index = lax.axis_index("dp")
    fsdp_index = lax.axis_index("fsdp")
    me = jnp.stack(
        [lax.axis_index(AXES), dp_index // 2, dp_index % 2, fsdp_index // 2, fsdp_index % 2]
    ).astype(jnp.int32)

    shard = params.reshape(geo.rows, LANES)
    if geo.spill:
        spill = lax.ppermute(
            shard[: round_up(geo.spill, 8)], AXES, [(geo.spill_from, geo.spill_to)]
        )
    else:
        spill = jnp.zeros((8, LANES), F32)
    share = prepare(geo, me, shard, spill).reshape(4, geo.quarter, LANES)
    row_ids = jnp.pad(
        window_rows.reshape(windows, WT), ((0, 0), (0, WP - WT)), constant_values=-1
    ).reshape(windows * WP)
    stacked = jnp.stack(spread_quarters(geo, share, dp_index))
    x, grad_out = permute_in(after(row_ids, stacked)[:, None], patches, cotangent)
    gathers = []
    for group in range(4):
        piece = lax.dynamic_index_in_dim(stacked, dp_index ^ group, 0, keepdims=False)
        gathers.append(Gather(geo, piece))
    gathers[0].line()
    gathers[0].across(x)
    gathers[1].line(gathers[0].held)
    gathers[0].last()
    gathers[1].across()
    gathers[2].line(gathers[1].held)
    gathered = {0: gathers[0].finish()}

    mix_matrix = (MIX_ROW, D, 3 * D // LANES)
    out_matrix = (OUT_ROW, D, D // LANES)
    expand_matrix = (EXPAND_ROW, D, FF // LANES)
    shrink_matrix = (SHRINK_ROW, FF, D // LANES)
    out_end = p_row(STARTS[6])
    expand_end = p_row(STARTS[10])
    shrink_end = p_row(STARTS[12])
    mix_vectors = [(0, 8), (8, 8), (TAIL_ROW, TABLE_ROW - TAIL_ROW), (TABLE_ROW, SPLIT_ROW - TABLE_ROW)]
    out_vectors = [(out_end + 8 * i, 8) for i in range(3)]
    expand_vectors = [(expand_end, FF // LANES)]
    shrink_vectors = [(shrink_end, 8)]

    first = Region(
        geo, 0, OUT_ROW, mix_matrix, mix_vectors, high=geo.spill_to if geo.spill else None
    )
    mix_weight, attn_gain, attn_shift, mix_bias, table_rows = unpack(geo, first, me, gathered)
    gathers[1].last(mix_weight)
    gathers[3].line(gathers[2].held, mix_weight)
    gathers[2].across(mix_weight)

    def line_of(rows):
        return rows.reshape(1, -1)

    entries = round_up(TABLE_ROWS, 16)
    table = table_rows.reshape(-1)[: TABLE_ROWS * HEADS].reshape(TABLE_ROWS, HEADS).T
    table = jnp.pad(table, ((0, 0), (0, entries - TABLE_ROWS))).astype(BF16)
    ids = jnp.pad(rel_index.T, ((0, WP - WT), (0, LANES - WT)), constant_values=-1)
    bias = score_bias(ids, table)

    gathers[3].across(bias)
    normed, mixed = mix(
        after(x, bias, gathers[2].near),
        line_of(attn_gain),
        line_of(attn_shift),
        mix_weight,
        line_of(mix_bias),
    )
    gathered[1] = gathers[1].finish(mixed)
    gathers[2].last(mixed)
    attended, logs = attention(after(mixed, gathers[3].near), bias)
    gathers[3].last(attended)
    gathered[2] = gathers[2].finish(attended)
    out_weight, out_bias, mlp_gain, mlp_shift = unpack(
        geo, Region(geo, OUT_ROW, EXPAND_ROW, out_matrix, out_vectors), me, gathered
    )

    def in_two(matrix, vectors, end, block):
        row, depth, cols = matrix
        edge = split_span(geo, row, depth, cols, block)
        weight = None
        if 0 < edge < depth:
            part = Region(geo, row, row + edge * cols, matrix, [], span=(0, edge))
            (weight,) = unpack(geo, part, me, gathered)
            rest = Region(geo, row + edge * cols, end, matrix, vectors, span=(edge, depth))
            return unpack(geo, rest, me, gathered, weight)
        return unpack(geo, Region(geo, row, end, matrix, vectors), me, gathered)

    expand_weight, expand_bias = in_two(expand_matrix, expand_vectors, SHRINK_ROW, 16)

    middle, second = middle_rows(
        x, attended, out_weight, line_of(out_bias), line_of(mlp_gain), line_of(mlp_shift)
    )

    gathered[3] = gathers[3].finish(second)

    shrink_region = Region(
        geo, SHRINK_ROW, END_ROW, shrink_matrix, shrink_vectors, high=geo.devices - 1
    )
    expand_region = Region(geo, EXPAND_ROW, SHRINK_ROW, expand_matrix, expand_vectors)
    out_region = Region(geo, OUT_ROW, EXPAND_ROW, out_matrix, out_vectors)
    mix_region = Region(geo, 0, TAIL_ROW, mix_matrix, [])
    slots = {}
    shrink_bias_grad = jnp.sum(grad_out.astype(F32), axis=0).reshape(-1, LANES)
    hidden, slope, slots = mlp_up(
        geo,
        shrink_region,
        me,
        second,
        grad_out,
        expand_weight,
        line_of(expand_bias),
        shrink_bias_grad,
        slots,
        False,
    )
    reductions = {3: Reduction(geo, slots[3])}
    shrink_weight, shrink_bias = in_two(shrink_matrix, shrink_vectors, END_ROW, 64)
    sent = reductions[3].last(shrink_weight)
    result, second_grad, slots = mlp_down(
        geo,
        expand_region,
        me,
        after(hidden, sent),
        slope,
        second,
        grad_out,
        expand_weight,
        shrink_weight,
        middle,
        line_of(shrink_bias),
        slots,
        expand_region.high == shrink_region.low,
    )
    reductions[2] = Reduction(geo, slots[2])
    sent = reductions[3].across(second_grad)
    middle_grad, branch_grad, context_grad, middle_vec = middle_back(
        after(second_grad, sent), middle, grad_out, line_of(mlp_gain), out_weight
    )
    sent = [reductions[2].last(context_grad), reductions[3].line(context_grad)]
    slots = pack(
        geo,
        out_region,
        me,
        attended,
        after(branch_grad, *sent),
        [middle_vec[i].reshape(8, LANES) for i in range(3)],
        slots,
        out_region.high == expand_region.low,
    )
    reductions[1] = Reduction(geo, slots[1])
    mixed_grad, score_sums, column_sums = attention_back(
        mixed, after(context_grad, slots[1][0]), bias, logs
    )
    sent = [reductions[2].across(mixed_grad), reductions[1].last(mixed_grad)]
    sums = {3: reductions[3].total(mixed_grad)}
    slots = pack(
        geo,
        mix_region,
        me,
        normed,
        after(mixed_grad, *sent),
        [],
        slots,
        mix_region.high == out_region.low,
    )
    packed = slots[0][0]
    reductions[0] = Reduction(geo, slots[0])
    sent = [reductions[2].line(packed), reductions[1].across(packed)]
    activations = permute_out(row_ids[None], after(result, packed, *sent), arrivals)
    sent = reductions[0].last(activations)
    input_rows, first_vec = first_back(
        after(mixed_grad, sent), mix_weight, x, middle_grad, line_of(attn_gain)
    )
    sent = reductions[1].line(input_rows)
    sums[2] = reductions[2].total(input_rows)
    table_grad = score_bias_back(ids, after(score_sums, sent), entries)[:TABLE_ROWS]
    sent = reductions[0].across(table_grad)

    table_pad = (SPLIT_ROW - TABLE_ROW) * LANES - TABLE_ROWS * HEADS
    late = jnp.concatenate(
        [
            first_vec[:2].reshape(HEAD_ROWS, LANES),
            column_sums[0].reshape(-1, LANES),
            jnp.pad(table_grad.reshape(-1), (0, table_pad)).reshape(-1, LANES),
        ],
        axis=0,
    )
    late = after(jnp.pad(late, ((0, LATE_ROWS - late.shape[0]), (0, 0))), sent)
    late = sum_everywhere(geo, late)
    sums[1] = reductions[1].total(sent)
    input_grad = permute_out(row_ids[None], after(input_rows, sent), arrivals)
    sent = reductions[0].line(input_grad)
    early = collect_early(geo, sums, dp_index)
    squares = square_sums(geo, me, (1, 2, 3), [after(sums[1], sent), sums[2], sums[3]])
    sums[0] = reductions[0].total(late, squares)
    squares = squares + square_sums(geo, me, (0,), [sums[0]])
    squares = sum_everywhere(geo, jnp.sum(squares, axis=1)[None])
    scale = 1.0 / jnp.sqrt(F32(arrivals * geo.devices))
    edges = [0, 8, HEAD_ROWS, HEAD_ROWS + TABLE_ROW - TAIL_ROW, LATE_ROWS]
    late_squares = [jnp.sum(late[a:b] * late[a:b]) for a, b in zip(edges, edges[1:])]
    totals = [squares[0, t] for t in range(len(SHAPES))]
    for number, t in enumerate((0, 1, 3, 4)):
        totals[t] = late_squares[number]
    entry_counts = jnp.array([math.prod(shape) for shape in SHAPES], F32)
    group_rms = jnp.sqrt(jnp.stack(totals) * (scale * scale) / entry_counts)

    step_float = step_count.astype(F32)
    coef = jnp.stack(
        [
            scale,
            1.0 - jnp.power(F32(0.9), step_float),
            1.0 - jnp.power(F32(0.999), step_float),
            learn_rate,
        ]
    )
    params_new, first_new, second_new = update_step(
        geo,
        me,
        coef,
        early + collect_late(geo, sums[0], dp_index),
        late,
        shard,
        first_moment.reshape(geo.rows, LANES),
        second_moment.reshape(geo.rows, LANES),
    )
    return (
        activations,
        input_grad,
        group_rms,
        params_new.reshape(-1),
        first_new.reshape(-1),
        second_new.reshape(-1),
    )


def solution(mesh):
    placed = (
        P(AXES, None),
        P(AXES, None),
        P(AXES),
        P(),
        P(AXES),
        P(AXES),
        P(AXES),
        P(),
        P(),
    )
    return jax.shard_map(
        local,
        mesh=mesh,
        in_specs=placed,
        out_specs=(P(AXES, None), P(AXES, None), P(), P(AXES), P(AXES), P(AXES)),
        check_vma=False,
    )
```

```python
from functools import partial
import math

import jax
import jax.numpy as jnp
from jax import lax
from jax.experimental import pallas as pl
from jax.experimental.pallas import tpu as pltpu
from jax.sharding import PartitionSpec as P

D = 1024
HEADS = 32
HEAD_DIM = 32
FF = 4096
WT = 100
WP = 104
TABLE_ROWS = 361
RAW = 12607776
LANES = 128
QUAD = LANES // HEAD_DIM
AXES = ("dp", "fsdp")
BF16 = jnp.bfloat16
F32 = jnp.float32
VMEM_LIMIT = 62 << 20

SHAPES = [
    (D,),
    (D,),
    (D, 3 * D),
    (3 * D,),
    (TABLE_ROWS, HEADS),
    (D, D),
    (D,),
    (D,),
    (D,),
    (D, FF),
    (FF,),
    (FF, D),
    (D,),
]
STARTS = [0]
for _shape in SHAPES:
    STARTS.append(STARTS[-1] + math.prod(_shape))

SPLIT = STARTS[5]
LIFT = (-SPLIT) % LANES


def p_row(position):
    lifted = position + (LIFT if position >= SPLIT else 0)
    assert lifted % LANES == 0
    return lifted // LANES


MIX_ROW, OUT_ROW, EXPAND_ROW, SHRINK_ROW = (p_row(STARTS[i]) for i in (2, 5, 9, 11))
SPLIT_ROW = p_row(SPLIT)
TAIL_ROW = p_row(STARTS[3])
TABLE_ROW = STARTS[4] // LANES
END_ROW = p_row(RAW)
HEAD_ROWS = MIX_ROW
LATE_TAIL = SPLIT_ROW - TAIL_ROW
LATE_ROWS = -(-(HEAD_ROWS + LATE_TAIL) // 8) * 8


def round_up(value, step):
    return -(-value // step) * step


def vmem():
    return pl.BlockSpec(memory_space=pltpu.VMEM)


def smem():
    return pl.BlockSpec(memory_space=pltpu.SMEM)


def anywhere():
    return pl.BlockSpec(memory_space=pl.ANY)


def params_of(**more):
    return pltpu.CompilerParams(vmem_limit_bytes=VMEM_LIMIT, **more)


COST_SCALE = 200


def cost(flops, bytes_accessed, transcendentals=0):
    return pl.CostEstimate(
        flops=int(COST_SCALE * flops),
        bytes_accessed=int(COST_SCALE * bytes_accessed),
        transcendentals=int(transcendentals),
    )


def nn(left, right):
    return jnp.dot(left, right, preferred_element_type=F32)


def nt(left, right):
    return lax.dot_general(left, right, (((1,), (1,)), ((), ())), preferred_element_type=F32)


class Geometry:
    def __init__(self, dp, fsdp, shard_len):
        assert dp == 4 and shard_len % LANES == 0 and fsdp % 2 == 0
        self.fsdp = fsdp
        self.devices = dp * fsdp
        self.line = fsdp // 2
        assert self.line & (self.line - 1) == 0
        self.rows = shard_len // LANES
        first, last = TABLE_ROW // self.rows, (SPLIT_ROW - 1) // self.rows
        assert last - first in (0, 1)
        self.spill_from, self.spill_to = last, first
        self.spill = SPLIT_ROW - self.rows * last if last != first else 0
        self.quarter = round_up(-(-(self.rows + 16 + self.spill) // 4), 8)
        self.slot = 4 * self.quarter
        assert self.slot % 16 == 0
        tiles = self.slot // 16
        self.chunk = max(t for t in range(1, 34) if tiles % t == 0)
        self.bit_x, self.bit_core, self.bit_y = 2 * fsdp, fsdp, 1

    def base(self, device):
        return (device * self.rows) // 16 * 16

    def permute(self, value, mask_core0, mask_core1):
        pairs = []
        for index in range(self.devices):
            core = (index // self.fsdp) % 2
            pairs.append((index, index ^ (mask_core1 if core else mask_core0)))
        return lax.ppermute(value, AXES, pairs)

    def core_swap(self, value):
        return self.permute(value, self.bit_core, self.bit_core)


def prepare_kernel(geo, me_ref, shard_ref, spill_ref, out_ref, pad_ref):
    rows, slot = geo.rows, geo.slot
    base = me_ref[0] * rows
    shift = lax.rem(base, 16)
    pad_ref[0:32, :] = jnp.zeros((32, LANES), F32)
    pad_ref[16 + rows : slot + 32, :] = jnp.zeros((slot + 16 - rows, LANES), F32)
    whole = rows // 64

    def place_body(i, _):
        r0 = i * 64
        pad_ref[pl.ds(16 + shift + r0, 64), :] = shard_ref[pl.ds(pl.multiple_of(r0, 64), 64), :]
        return 0

    lax.fori_loop(0, whole, place_body, 0)
    rest = rows - whole * 64
    if rest:
        pad_ref[pl.ds(16 + shift + whole * 64, rest), :] = shard_ref[whole * 64 : rows, :]
    if geo.spill:
        count = geo.spill

        @pl.when(me_ref[0] == geo.spill_to)
        def _():
            lane = lax.broadcasted_iota(jnp.int32, (count, LANES), 1)
            row = lax.broadcasted_iota(jnp.int32, (count, LANES), 0)
            flat = (rows * geo.spill_from + row) * LANES + lane
            at = 16 + rows * geo.spill_from - geo.base(geo.spill_to)
            pad_ref[at : at + count, :] = jnp.where(flat < SPLIT, spill_ref[0:count, :], 0.0)

    step = 16 * geo.chunk

    def body(i, _):
        r0 = pl.multiple_of(i * step, 16)
        here = pad_ref[pl.ds(r0 + 16, step), :]
        above = pad_ref[pl.ds(r0 + 15, step), :]
        lane = lax.broadcasted_iota(jnp.int32, (step, LANES), 1)
        row = lax.broadcasted_iota(jnp.int32, (step, LANES), 0)
        flat = (base - shift + r0 + row) * LANES + lane
        moved = jnp.where(lane >= LIFT, pltpu.roll(here, LIFT, 1), pltpu.roll(above, LIFT, 1))
        value = jnp.where(flat < SPLIT, here, jnp.where(flat >= SPLIT + LIFT, moved, 0.0))
        out_ref[pl.ds(r0, step), :] = value.astype(BF16)
        return 0

    lax.fori_loop(0, slot // step, body, 0)


def prepare(geo, me, shard, spill):
    return pl.pallas_call(
        partial(prepare_kernel, geo),
        out_shape=jax.ShapeDtypeStruct((geo.slot, LANES), BF16),
        in_specs=[smem(), vmem(), vmem()],
        out_specs=vmem(),
        scratch_shapes=[pltpu.VMEM((geo.slot + 32, LANES), F32)],
        compiler_params=params_of(),
        name="prepare_share",
    )(me, shard, spill)


GATHER_PHASES = ((0,), (1,), (2,), (3,))
REDUCE_PHASES = ((0,), (1,), (2,), (3,))


def phase_of(phases, group):
    return [number for number, groups in enumerate(phases) if group in groups][0]


def spot(geo, me_ref, device, own, quarter_x, groups):
    core = me_ref[2] if own else 1 - me_ref[2]
    rel_x = quarter_x ^ me_ref[1]
    rel_z = (lax.rem(device, geo.fsdp) // 2) ^ me_ref[3]
    rel_y = lax.rem(device, 2) ^ me_ref[4]
    straight = core == 0
    first = jnp.where(straight, rel_x, rel_y)
    late = jnp.where(straight, rel_y, rel_x)
    at = (first * geo.line + rel_z) * len(groups) + device // geo.fsdp - groups[0]
    return quarter_x * 2 + core, late, at


def by_phase(geo, phases, numbers, device, action):
    if len(numbers) == 1:
        action(0, phases[numbers[0]])
        return
    group = device // geo.fsdp
    for position, number in enumerate(numbers):
        groups = phases[number]
        pl.when((group >= groups[0]) & (group <= groups[-1]))(partial(action, position, groups))


class Region:
    def __init__(self, geo, row0, row1, matrix, vectors, span=None, high=None):
        self.row0, self.row1 = row0, row1
        self.mat_row, self.depth, self.cols = matrix
        self.start, self.stop = span or (0, self.depth)
        self.vectors = vectors
        self.low = max(row0 - 1, 0) // geo.rows
        self.high = (row1 - 1) // geo.rows if high is None else high
        self.slots = self.high - self.low + 1
        self.origin = geo.base(self.low)
        self.pitch = 17 if self.cols % 32 == 0 else 16
        self.stride = self.cols * self.pitch // 16
        self.scratch_tiles = (geo.base(self.high) + geo.slot - self.origin) // 16
        groups = {d // geo.fsdp for d in range(self.low, self.high + 1)}
        self.gather = sorted({phase_of(GATHER_PHASES, group) for group in groups})
        self.reduce = sorted({phase_of(REDUCE_PHASES, group) for group in groups})

    def address(self, row):
        rel = row - self.origin
        return rel if self.pitch == 16 else rel + rel // 16

    def scratch(self):
        return pltpu.VMEM((self.scratch_tiles * self.pitch, LANES), F32)


def copy_rows(region, ref, row, count, move):
    done = 0
    while done < count:
        size = min(count - done, 16 - (row + done - region.origin) % 16)
        if region.pitch == 16:
            size = count - done
        move(region.address(row + done), done, size)
        done += size


def unpack_kernel(geo, region, block, aliased, me_ref, *refs):
    arrays = 4 * len(region.gather)
    srcs, refs = refs[:arrays], refs[arrays:]
    if aliased:
        refs = refs[1:]
    weight_ref, refs = refs[0], refs[1:]
    vec_refs, refs = refs[: len(region.vectors)], refs[len(region.vectors) :]
    flat_ref, slot_ref, stage_ref, sems, out_sem = refs
    quarter, pitch, cols = geo.quarter, region.pitch, region.cols
    total = (region.stop - region.start) // block

    def fetch(step):
        device = region.low + step
        buf = lax.rem(step, 2)

        def from_phase(position, groups):
            for own in range(2):
                for quarter_x in range(2):
                    q, late, at = spot(geo, me_ref, device, own, quarter_x, groups)
                    to = pl.ds(pl.multiple_of(q * quarter, 8), quarter)
                    for side in range(2):
                        src = srcs[position * 4 + (1 - own) * 2 + side]

                        @pl.when(late == side)
                        def _(src=src, at=at, to=to, own=own, quarter_x=quarter_x):
                            pltpu.make_async_copy(
                                src.at[at],
                                slot_ref.at[buf, to],
                                sems.at[buf, own * 2 + quarter_x],
                            ).start()

        by_phase(geo, GATHER_PHASES, region.gather, device, from_phase)

    fetch(0)

    def slot_body(step, carry):
        tile_carry, done = carry

        @pl.when(step + 1 < region.slots)
        def _():
            fetch(step + 1)

        buf = lax.rem(step, 2)
        for number in range(4):
            pltpu.make_async_copy(
                srcs[0].at[0], slot_ref.at[buf, pl.ds(0, quarter)], sems.at[buf, number]
            ).wait()
        device = region.low + step
        first_tile = geo.base(device) // 16 - region.origin // 16
        next_row = (device + 1) * geo.rows // 16 * 16
        next_tile = next_row // 16 - region.origin // 16

        def rows_body(i, _):
            t0 = i * geo.chunk
            r0 = pl.multiple_of(t0 * 16, 16)
            if pitch == 16:
                to = pl.multiple_of((first_tile + t0) * 16, 16)
                flat_ref[pl.ds(to, geo.chunk * 16), :] = slot_ref[
                    buf, pl.ds(r0, geo.chunk * 16), :
                ].astype(F32)
            else:
                for t in range(geo.chunk):
                    flat_ref[pl.ds((first_tile + t0 + t) * pitch, 16), :] = slot_ref[
                        buf, pl.ds(r0 + t * 16, 16), :
                    ].astype(F32)
            return 0

        lax.fori_loop(0, geo.slot // 16 // geo.chunk, rows_body, 0)
        seam = pl.ds(first_tile * pitch, 16)
        flat_ref[seam, :] = flat_ref[seam, :] + tile_carry
        complete = jnp.maximum(next_row - region.mat_row - region.start * cols, 0) // (block * cols)
        complete = jnp.where(step == region.slots - 1, total, jnp.minimum(complete, total))

        def mat_body(i, _):
            to = pl.multiple_of(i * block, block)
            row = i * (block * region.stride)
            for c in range(cols):
                at = region.address(region.mat_row + region.start * cols + c)
                stage_ref[pl.ds(to, block), c * LANES : (c + 1) * LANES] = flat_ref[
                    pl.ds(at + row, block, stride=region.stride), :
                ].astype(BF16)
            pltpu.make_async_copy(
                stage_ref.at[pl.ds(to, block)],
                weight_ref.at[pl.ds(region.start + to, block)],
                out_sem,
            ).start()
            return 0

        lax.fori_loop(done, complete, mat_body, 0)
        return flat_ref[pl.ds(next_tile * pitch, 16), :], complete

    lax.fori_loop(0, region.slots, slot_body, (jnp.zeros((16, LANES), F32), jnp.int32(0)))
    for (row, count), out_ref in zip(region.vectors, vec_refs):

        def move(at, done, size, out_ref=out_ref):
            out_ref[done : done + size, :] = flat_ref[at : at + size, :]

        copy_rows(region, flat_ref, row, count, move)
    pltpu.make_async_copy(
        stage_ref, weight_ref.at[pl.ds(region.start, region.stop - region.start)], out_sem
    ).wait()


def unpack(geo, region, me, gathered, weight=None):
    operands = [me] + [array for phase in region.gather for array in gathered[phase]]
    specs = [smem()] + [anywhere()] * (len(operands) - 1)
    aliases = {}
    if weight is not None:
        operands.append(weight)
        specs.append(anywhere())
        aliases = {len(operands) - 1: 0}
    height = region.stop - region.start
    return pl.pallas_call(
        partial(unpack_kernel, geo, region, 64 if region.cols <= 8 else 16, weight is not None),
        out_shape=[jax.ShapeDtypeStruct((region.depth, region.cols * LANES), BF16)]
        + [jax.ShapeDtypeStruct((count, LANES), F32) for _, count in region.vectors],
        in_specs=specs,
        out_specs=[anywhere()] + [vmem()] * len(region.vectors),
        scratch_shapes=[
            region.scratch(),
            pltpu.VMEM((2, geo.slot, LANES), BF16),
            pltpu.VMEM((height, region.cols * LANES), BF16),
            pltpu.SemaphoreType.DMA((2, 4)),
            pltpu.SemaphoreType.DMA(()),
        ],
        input_output_aliases=aliases,
        compiler_params=params_of(),
        cost_estimate=cost(0, 8 * LANES * height * region.cols),
        name="unpack_weights",
    )(*operands)


def clear_rows(region, flat_ref):
    filled = sorted(
        [(region.mat_row, region.mat_row + region.depth * region.cols)]
        + [(row, row + count) for row, count in region.vectors]
    )
    edges = [region.origin] + [edge for run in filled for edge in run]
    edges.append(region.origin + 16 * region.scratch_tiles)
    for start, stop in zip(edges[::2], edges[1::2]):
        if stop > start:

            def move(at, done, size):
                for r in range(0, size, 64):
                    span = min(64, size - r)
                    flat_ref[at + r : at + r + span, :] = jnp.zeros((span, LANES), F32)

            copy_rows(region, flat_ref, start, stop - start, move)


class Emitter:
    def __init__(self, geo, region, shared, me_ref, outs, flat_ref, slot_ref, old_ref, sems, old_sem):
        self.geo, self.region, self.shared, self.me_ref = geo, region, shared, me_ref
        self.outs, self.flat_ref, self.slot_ref, self.old_ref = outs, flat_ref, slot_ref, old_ref
        self.sems, self.old_sem = sems, old_sem

    def copies(self, device, action):
        geo = self.geo

        def to_phase(position, groups):
            count = 2 * geo.line * len(groups)
            for own in range(2):
                for quarter_x in range(2):
                    q, late, at = spot(geo, self.me_ref, device, own, quarter_x, groups)
                    rows = pl.ds(pl.multiple_of(q * geo.quarter, 8), geo.quarter)
                    action(
                        self.outs[position * 2 + 1 - own].at[late * count + at],
                        rows,
                        own * 2 + quarter_x,
                    )

        by_phase(geo, REDUCE_PHASES, self.region.reduce, device, to_phase)

    def begin(self):
        clear_rows(self.region, self.flat_ref)
        if self.shared:
            def action(place, rows, number):
                pltpu.make_async_copy(
                    place, self.old_ref.at[rows], self.old_sem.at[number]
                ).start()

            self.copies(self.region.high, action)

    def wait(self, parity):
        for number in range(4):
            pltpu.make_async_copy(
                self.slot_ref.at[parity, pl.ds(0, self.geo.quarter)],
                self.outs[0].at[0],
                self.sems.at[parity, number],
            ).wait()

    def slots_before(self, row):
        ready = (row - 1) // self.geo.rows - self.region.low
        return jnp.clip(ready, 0, self.region.slots)

    def emit(self, start, stop):
        geo, region, pitch = self.geo, self.region, self.region.pitch

        def slot_body(index, _):
            parity = lax.rem(index, 2)
            pl.when(index >= 2)(lambda: self.wait(parity))
            first_tile = geo.base(region.low + index) // 16 - region.origin // 16

            def convert(add):
                def rows_body(i, _):
                    t0 = i * geo.chunk
                    r0 = pl.multiple_of(t0 * 16, 16)
                    run = 1 if pitch > 16 else geo.chunk
                    for t in range(0, geo.chunk, run):
                        row = (first_tile + t0 + t) * pitch
                        row = pl.multiple_of(row, 16) if pitch == 16 else row
                        value = self.flat_ref[pl.ds(row, run * 16), :]
                        here = pl.ds(r0 + t * 16, run * 16)
                        if add:
                            value = value + self.old_ref[here, :].astype(F32)
                        self.slot_ref[parity, here, :] = value.astype(BF16)
                    return 0

                lax.fori_loop(0, geo.slot // 16 // geo.chunk, rows_body, 0)

            if self.shared:
                last = index == region.slots - 1

                @pl.when(last)
                def _():
                    for number in range(4):
                        pltpu.make_async_copy(
                            self.outs[0].at[0],
                            self.old_ref.at[pl.ds(0, geo.quarter)],
                            self.old_sem.at[number],
                        ).wait()
                    convert(True)

                pl.when(jnp.logical_not(last))(lambda: convert(False))
            else:
                convert(False)

            def action(place, rows, number):
                pltpu.make_async_copy(
                    self.slot_ref.at[parity, rows], place, self.sems.at[parity, number]
                ).start()

            self.copies(region.low + index, action)
            return 0

        lax.fori_loop(start, stop, slot_body, 0)

    def finish(self):
        for index in range(max(0, self.region.slots - 2), self.region.slots):
            self.wait(index % 2)


def emit_scratch(geo, region):
    return [
        region.scratch(),
        pltpu.VMEM((2, geo.slot, LANES), BF16),
        pltpu.VMEM((geo.slot, LANES), BF16),
        pltpu.SemaphoreType.DMA((2, 4)),
        pltpu.SemaphoreType.DMA((4,)),
    ]


def store_columns(region, flat_ref, row0, first_col, values):
    height = values.shape[0]
    for c in range(values.shape[1] // LANES):
        at = region.address(region.mat_row + first_col + c) + row0 * region.stride
        flat_ref[pl.ds(at, height, stride=region.stride), :] = values[
            :, c * LANES : (c + 1) * LANES
        ]


def with_slots(geo, region, slots, operands, specs):
    shapes = []
    aliases = {}
    for position, phase in enumerate(region.reduce):
        count = 4 * geo.line * len(REDUCE_PHASES[phase])
        for number in range(2):
            shapes.append(jax.ShapeDtypeStruct((count, geo.quarter, LANES), BF16))
            if phase in slots:
                operands.append(slots[phase][number])
                specs.append(anywhere())
                aliases[len(operands) - 1] = position * 2 + number
    return shapes, aliases, len(aliases)


def updated_slots(region, slots, results):
    merged = dict(slots)
    for position, phase in enumerate(region.reduce):
        merged[phase] = results[position * 2 : position * 2 + 2]
    return merged


def pack_kernel(geo, region, shared, grid_steps, skip, me_ref, a_ref, b_ref, *refs):
    vec_refs, refs = refs[: len(region.vectors)], refs[len(region.vectors) + skip :]
    arrays = 2 * len(region.reduce)
    *scratch, left_ref = refs[arrays:]
    emitter = Emitter(geo, region, shared, me_ref, refs[:arrays], *scratch)
    flat_ref = emitter.flat_ref
    step = pl.program_id(0)

    @pl.when(step == 0)
    def _():
        emitter.begin()
        for (row, count), vec_ref in zip(region.vectors, vec_refs):

            def move(at, done, size, vec_ref=vec_ref):
                flat_ref[at : at + size, :] = vec_ref[done : done + size, :]

            copy_rows(region, flat_ref, row, count, move)

        for r in range(0, region.depth, 256):
            left_ref[r : r + 256, :] = a_ref[:, r : r + 256].T

    width = b_ref.shape[1]
    store_columns(
        region, flat_ref, 0, step * (width // LANES), nn(left_ref[...], b_ref[...])
    )

    @pl.when(step == grid_steps - 1)
    def _():
        emitter.emit(0, region.slots)
        emitter.finish()


def emit_rows(emitter, step, grid_steps, height):
    region = emitter.region
    span = height * region.cols
    before = emitter.slots_before(region.mat_row + step * span)
    after = emitter.slots_before(region.mat_row + (step + 1) * span)
    last = step == grid_steps - 1
    emitter.emit(jnp.where(step == 0, 0, before), jnp.where(last, region.slots, after))
    pl.when(last)(emitter.finish)


def pack(geo, region, me, left, right, vectors, slots, shared):
    tokens = left.shape[0]
    width = 512
    steps = region.cols * LANES // width
    operands = [me, left, right] + vectors
    specs = [
        smem(),
        pl.BlockSpec((tokens, region.depth), lambda k: (0, 0), pipeline_mode=pl.Buffered(1)),
        pl.BlockSpec((tokens, width), lambda k: (0, k)),
    ] + [pl.BlockSpec(vector.shape, lambda k: (0, 0)) for vector in vectors]
    shapes, aliases, skip = with_slots(geo, region, slots, operands, specs)
    results = pl.pallas_call(
        partial(pack_kernel, geo, region, shared, steps, skip),
        grid=(steps,),
        out_shape=shapes,
        in_specs=specs,
        out_specs=[anywhere()] * len(shapes),
        scratch_shapes=emit_scratch(geo, region) + [pltpu.VMEM((region.depth, tokens), BF16)],
        input_output_aliases=aliases,
        compiler_params=params_of(),
        cost_estimate=cost(
            2 * tokens * region.depth * width * steps, 2 * region.depth * width * steps
        ),
        name="weight_grad_pack",
    )(*operands)
    return updated_slots(region, slots, results)


def line_masks(geo):
    if geo.line == 4:
        return [[2, 4, 6]]
    return [[2 << bit] for bit in range(geo.line.bit_length() - 1)]


def after(value, *others):
    return lax.optimization_barrier((value,) + others)[0]


def spread_quarters(geo, share, dp_index):
    pieces = [lax.dynamic_index_in_dim(share, dp_index, 0, keepdims=False)]
    for offset in (1, 2, 3):
        piece = lax.dynamic_index_in_dim(share, dp_index ^ offset, 0, keepdims=False)
        mask = offset * geo.fsdp
        pieces.append(geo.permute(piece, mask, mask))
    return pieces


def light():
    return pl.CostEstimate(flops=1024, bytes_accessed=1024, transcendentals=0)


def join_kernel(*refs):
    out_ref = refs[-1]
    start = 0
    for ref in refs[:-1]:
        out_ref[start : start + ref.shape[0]] = ref[...]
        start += ref.shape[0]


def join(parts):
    count = sum(part.shape[0] for part in parts)
    return pl.pallas_call(
        join_kernel,
        out_shape=jax.ShapeDtypeStruct((count,) + parts[0].shape[1:], parts[0].dtype),
        in_specs=[vmem()] * len(parts),
        out_specs=vmem(),
        compiler_params=params_of(),
        cost_estimate=light(),
        name="join",
    )(*parts)


class Gather:
    def __init__(self, geo, pieces):
        self.geo, self.held = geo, pieces

    def line(self, *deps):
        held = after(self.held, *deps)
        stages = line_masks(self.geo)
        for masks in stages[:-1]:
            moved = [self.geo.permute(held, mask, mask) for mask in masks]
            held = jnp.concatenate([held] + moved, axis=0)
        self.held = held
        self.moved = [self.geo.permute(held, mask, mask) for mask in stages[-1]]

    def joined(self, *deps):
        self.held = join([self.held] + [after(part, *deps) for part in self.moved])
        return self.held

    def across(self, *deps):
        self.moved = self.geo.permute(
            after(self.held, *deps), self.geo.bit_x, self.geo.bit_y
        )

    def last(self, *deps):
        self.near = join([self.held, after(self.moved, *deps)])
        self.moved = self.geo.permute(self.near, self.geo.bit_y, self.geo.bit_x)
        self.near_other = self.geo.core_swap(self.near)
        return self.near

    def finish(self, *deps):
        far = after(self.moved, *deps)
        return [self.near, far, after(self.near_other, *deps), self.geo.core_swap(far)]


def add_far_kernel(keep_ref, got_ref, out_ref):
    out_ref[...] = (keep_ref[...].astype(F32) + got_ref[...].astype(F32)).astype(BF16)


def add_near_kernel(keep_ref, got_ref, far_ref, kept_ref, moved_ref):
    total = keep_ref[...].astype(F32) + got_ref[...].astype(F32) + far_ref[...].astype(F32)
    half = kept_ref.shape[0]
    kept_ref[...] = total[:half]
    moved_ref[...] = total[half:].astype(BF16)


def add_line_kernel(near_ref, across_ref, own_ref, *moved_refs):
    own = own_ref.shape[0]
    own_ref[...] = near_ref[:own] + across_ref[:own].astype(F32)
    for number, ref in enumerate(moved_refs):
        rows = slice((number + 1) * own, (number + 2) * own)
        ref[...] = (near_ref[rows] + across_ref[rows].astype(F32)).astype(BF16)


def add_total_kernel(own_ref, *refs):
    total = own_ref[...]
    for ref in refs[:-1]:
        total = total + ref[...].astype(F32)
    refs[-1][...] = total


class Reduction:
    def __init__(self, geo, slots, phase):
        self.geo = geo
        self.count = geo.line * len(REDUCE_PHASES[phase])
        self.keep, send = slots
        self.got = geo.core_swap(send)
        self.block = (1, geo.quarter, LANES)

    def call(self, kernel, out_shape, **more):
        return pl.pallas_call(
            kernel,
            out_shape=out_shape,
            compiler_params=params_of(),
            cost_estimate=light(),
            name="add_terms",
            **more,
        )

    def shape(self, count, dtype):
        return jax.ShapeDtypeStruct((count,) + self.block[1:], dtype)

    def last(self, *deps):
        count = 2 * self.count
        got = after(self.got, *deps)
        later = pl.BlockSpec((count,) + self.block[1:], lambda i: (1, 0, 0))
        far = self.call(
            add_far_kernel,
            self.shape(count, BF16),
            grid=(1,),
            in_specs=[later, later],
            out_specs=vmem(),
        )(self.keep, got)
        self.from_far = self.geo.permute(far, self.geo.bit_y, self.geo.bit_x)
        self.got = got
        return far

    def across(self, *deps):
        count = self.count
        part = pl.BlockSpec((2 * count,) + self.block[1:], lambda i: (0, 0, 0))
        self.near, moved = self.call(
            add_near_kernel,
            [self.shape(count, F32), self.shape(count, BF16)],
            grid=(1,),
            in_specs=[part, part, part],
            out_specs=[vmem(), vmem()],
        )(self.keep, self.got, after(self.from_far, *deps))
        self.from_across = self.geo.permute(moved, self.geo.bit_x, self.geo.bit_y)
        return moved

    def line(self, *deps):
        near, received = self.near, after(self.from_across, *deps)
        stages = line_masks(self.geo)[::-1]
        for masks in stages:
            own = near.shape[0] // (len(masks) + 1)
            near, *parts = self.call(
                add_line_kernel,
                [self.shape(own, F32)] + [self.shape(own, BF16)] * len(masks),
                in_specs=[vmem(), vmem()],
                out_specs=[vmem()] * (len(masks) + 1),
            )(near, received)
            moved = [self.geo.permute(part, mask, mask) for part, mask in zip(parts, masks)]
            if masks is not stages[-1]:
                (received,) = moved
        self.near, self.parts = near, moved
        return near

    def total(self, *deps):
        parts = [after(part, *deps) for part in self.parts]
        return self.call(
            add_total_kernel,
            self.shape(self.near.shape[0], F32),
            in_specs=[vmem()] * (1 + len(parts)),
            out_specs=vmem(),
        )(self.near, *parts)


def collect_quarters(geo, sums, dp_index):
    def of_group(group):
        low = jnp.where(group == 0, sums[0], sums[1])
        return jnp.where(group < 2, low, jnp.where(group == 2, sums[2], sums[3]))

    pieces = [of_group(dp_index)]
    for offset in (1, 2, 3):
        mask = offset * geo.fsdp
        pieces.append(geo.permute(of_group(dp_index ^ offset).astype(BF16), mask, mask))
    return pieces


def sum_everywhere(geo, value, start=0, stop=None):
    bits = geo.devices.bit_length() - 1
    for bit in range(start, bits if stop is None else stop):
        value = value + geo.permute(value, 1 << bit, 1 << bit)
    return value


def tensor_sums(sums_ref, squares, flat, low, high, tensors):
    for t in tensors:

        @pl.when((low < STARTS[t + 1]) & (high > STARTS[t]))
        def _(t=t):
            inside = (flat >= STARTS[t]) & (flat < STARTS[t + 1])
            part = jnp.where(inside, squares, 0.0)
            sums_ref[t : t + 1, :] += jnp.sum(part, axis=0, keepdims=True)


def squares_kernel(geo, groups, me_ref, *refs):
    sums_ref = refs[-1]
    sums_ref[...] = jnp.zeros((16, LANES), F32)
    span = 8 * max(t for t in range(1, 13) if geo.quarter // 8 % t == 0)
    dp_index = me_ref[1] * 2 + me_ref[2]
    places = [(number, at, g) for number, part in enumerate(groups) for at, g in enumerate(part)]
    for number, at, group in places:
        device = group * geo.fsdp + me_ref[3] * 2 + me_ref[4]
        share = geo.rows * LANES
        base = device * geo.rows
        first = base - lax.rem(base, 16) + dp_index * geo.quarter

        def body(i, _, number=number, at=at, base=base, first=first):
            r0 = pl.multiple_of(i * span, 8)
            value = refs[number][at, pl.ds(r0, span), :]
            lane = lax.broadcasted_iota(jnp.int32, (span, LANES), 1)
            row = lax.broadcasted_iota(jnp.int32, (span, LANES), 0)
            lifted = (first + r0 + row) * LANES + lane
            flat = jnp.where(lifted < SPLIT, lifted, lifted - LIFT)
            owned = (flat >= base * LANES) & (flat < base * LANES + share)
            low = (first + r0) * LANES - LIFT
            high = (first + r0 + span) * LANES
            squares = jnp.where(owned, value * value, 0.0)
            tensor_sums(sums_ref, squares, flat, low, high, (2,) + tuple(range(5, 13)))
            return 0

        lax.fori_loop(0, geo.quarter // span, body, 0)


def square_sums(geo, me, groups, sums):
    return pl.pallas_call(
        partial(squares_kernel, geo, groups),
        out_shape=jax.ShapeDtypeStruct((16, LANES), F32),
        in_specs=[smem()] + [vmem()] * len(sums),
        out_specs=vmem(),
        compiler_params=params_of(),
        cost_estimate=light(),
        name="square_sums",
    )(me, *sums)


def update_kernel(geo, me_ref, coef_ref, *refs):
    quarters, (late_ref, p_ref, m_ref, v_ref), outs = refs[:4], refs[4:8], refs[8:]
    params_out, first_out, second_out, grad_ref = outs
    rows, quarter = geo.rows, geo.quarter
    base = me_ref[0] * rows
    shift = lax.rem(base, 16)
    dp_index = me_ref[1] * 2 + me_ref[2]
    margin = 128
    for offset in range(4):
        to = pl.multiple_of(margin + (dp_index ^ offset) * quarter, 8)
        grad_ref[pl.ds(to, quarter), :] = quarters[offset][...].astype(F32)
    for row, count, at in ((0, HEAD_ROWS, 0), (TAIL_ROW, LATE_TAIL, HEAD_ROWS)):

        @pl.when((base < row + count) & (base + rows > row))
        def _(row=row, count=count, at=at):
            lane = lax.broadcasted_iota(jnp.int32, (count, LANES), 1)
            p_rows = lax.broadcasted_iota(jnp.int32, (count, LANES), 0) + row
            before = p_rows * LANES + lane < SPLIT
            to = jnp.clip(margin + shift + row - base, 0, margin + geo.slot)
            here = pl.ds(to, count)
            late = late_ref[at : at + count, :]
            grad_ref[here, :] = jnp.where(before, late, grad_ref[here, :])

    span = 64
    scale, first_fix, second_fix, rate = (coef_ref[i] for i in range(4))

    def body(i, _):
        r0 = jnp.minimum(i * span, rows - span)
        here = grad_ref[pl.ds(margin + shift + r0, span), :]
        below = grad_ref[pl.ds(margin + shift + r0 + 1, span), :]
        lane = lax.broadcasted_iota(jnp.int32, (span, LANES), 1)
        row = lax.broadcasted_iota(jnp.int32, (span, LANES), 0)
        flat = (base + r0 + row) * LANES + lane
        back = LANES - LIFT
        moved = jnp.where(lane < back, pltpu.roll(here, back, 1), pltpu.roll(below, back, 1))
        scaled = jnp.where(flat < SPLIT, here, moved) * scale
        at = pl.ds(r0, span)
        first_new = 0.9 * m_ref[at, :] + 0.1 * scaled
        second_new = 0.999 * v_ref[at, :] + 0.001 * scaled * scaled
        params = p_ref[at, :]
        update = first_new / first_fix / (jnp.sqrt(second_new / second_fix) + 1e-08) + 0.05 * params
        params_out[at, :] = params - rate * update
        first_out[at, :] = first_new
        second_out[at, :] = second_new
        return 0

    lax.fori_loop(0, -(-rows // span), body, 0)


def update_step(geo, me, coef, quarters, late, params, first, second):
    rows = jax.ShapeDtypeStruct((geo.rows, LANES), F32)
    return pl.pallas_call(
        partial(update_kernel, geo),
        out_shape=[rows, rows, rows],
        in_specs=[smem(), smem()] + [vmem()] * 8,
        out_specs=[vmem()] * 3,
        scratch_shapes=[pltpu.VMEM((geo.slot + 384, LANES), F32)],
        compiler_params=params_of(),
        name="moments_update",
    )(me, coef, *quarters, late, params, first, second)


def row_blocks(tokens):
    return tokens // 4 if tokens % 64 == 0 else tokens


def permute_in_kernel(rows_ref, values_ref, *refs):
    arrivals = values_ref.shape[0]
    lane = lax.broadcasted_iota(jnp.int32, (WP, arrivals), 1)
    pick = jnp.where(rows_ref[...] == lane, 1.0, 0.0).astype(BF16)
    refs[-1][...] = nn(pick, values_ref[...]).astype(BF16)


def permute_in(row_ids, values, start, stop, before=None):
    tokens = row_ids.shape[0]
    operands = [row_ids, values]
    specs = [
        pl.BlockSpec((WP, 1), lambda i: (i + start, 0)),
        pl.BlockSpec(values.shape, lambda i: (0, 0)),
    ]
    if before is not None:
        operands.append(before)
        specs.append(anywhere())
    return pl.pallas_call(
        permute_in_kernel,
        grid=(stop - start,),
        out_shape=jax.ShapeDtypeStruct((tokens, D), BF16),
        in_specs=specs,
        out_specs=pl.BlockSpec((WP, D), lambda i: (i + start, 0)),
        input_output_aliases={} if before is None else {2: 0},
        compiler_params=params_of(),
        cost_estimate=cost(tokens * tokens * D, 2 * tokens * D),
        name="window_order",
    )(*operands)


def permute_out_kernel(rows_ref, x_ref, out_ref):
    count = out_ref.shape[0]
    arrival = lax.broadcasted_iota(jnp.int32, (count, rows_ref.shape[1]), 0)
    pick = jnp.where(rows_ref[...] == arrival + pl.program_id(0) * count, 1.0, 0.0).astype(BF16)
    out_ref[...] = nn(pick, x_ref[...]).astype(BF16)


def permute_out(row_ids, values, arrivals):
    tokens = values.shape[0]
    block = 160 if arrivals % 160 == 0 else arrivals
    return pl.pallas_call(
        permute_out_kernel,
        grid=(arrivals // block,),
        out_shape=jax.ShapeDtypeStruct((arrivals, D), BF16),
        in_specs=[
            pl.BlockSpec((1, tokens), lambda i: (0, 0)),
            pl.BlockSpec((tokens, D), lambda i: (0, 0)),
        ],
        out_specs=pl.BlockSpec((block, D), lambda i: (i, 0)),
        compiler_params=params_of(),
        cost_estimate=cost(2 * tokens * arrivals * D, 4 * tokens * D),
        name="arrival_order",
    )(row_ids, values)


def normalized(x):
    center = x - jnp.mean(x, axis=-1, keepdims=True)
    spread = jnp.mean(center * center, axis=-1, keepdims=True)
    inverse = lax.rsqrt(spread + 1e-05)
    return center * inverse, inverse


def normalized_back(e, xhat, inverse):
    mean = jnp.mean(e, axis=-1, keepdims=True)
    along = jnp.mean(e * xhat, axis=-1, keepdims=True)
    return (e - mean - xhat * along) * inverse


def mix_kernel(x_ref, gain_ref, shift_ref, w_ref, b_ref, normed_ref, mixed_ref):
    step = pl.program_id(0)
    tokens = x_ref.shape[0]

    @pl.when(step == 0)
    def _():
        def body(i, _):
            rows = pl.ds(pl.multiple_of(i * 16, 16), 16)
            xhat, _ = normalized(x_ref[rows, :].astype(F32))
            normed_ref[rows, :] = (xhat * gain_ref[...] + shift_ref[...]).astype(BF16)
            return 0

        lax.fori_loop(0, tokens // 16, body, 0, unroll=4)

    mixed = nn(normed_ref[...], w_ref[...]) + b_ref[...]
    scale = jnp.where(step < D // w_ref.shape[1], F32(HEAD_DIM ** (-0.5)), F32(1.0))
    mixed_ref[...] = (mixed * scale).astype(BF16)


def mix(x, gain, shift, weight, bias):
    tokens = x.shape[0]
    width = 512
    rows = pl.BlockSpec((tokens, D), lambda j: (0, 0))
    vec = pl.BlockSpec((1, D), lambda j: (0, 0))
    return pl.pallas_call(
        mix_kernel,
        grid=(3 * D // width,),
        out_shape=[
            jax.ShapeDtypeStruct((tokens, D), BF16),
            jax.ShapeDtypeStruct((tokens, 3 * D), BF16),
        ],
        in_specs=[
            rows,
            vec,
            vec,
            pl.BlockSpec((D, width), lambda j: (0, j)),
            pl.BlockSpec((1, width), lambda j: (0, j)),
        ],
        out_specs=[rows, pl.BlockSpec((tokens, width), lambda j: (0, j))],
        compiler_params=params_of(),
        cost_estimate=cost(6 * tokens * D * D, 6 * D * D + 8 * tokens * D),
        name="mix_rows",
    )(x, gain, shift, weight, bias)


def bias_kernel(ids_ref, table_ref, out_ref):
    entries = table_ref.shape[1]

    def body(j, _):
        entry = lax.broadcasted_iota(jnp.int32, (entries, LANES), 0)
        pick = jnp.where(ids_ref[pl.ds(j, 1), :] == entry, 1.0, 0.0).astype(BF16)
        out_ref[:, pl.ds(j, 1), :] = nn(table_ref[...], pick).reshape(HEADS, 1, LANES)
        return 0

    lax.fori_loop(0, WT, body, 0, unroll=4)
    for j in range(WT, WP):
        out_ref[:, j : j + 1, :] = jnp.full((HEADS, 1, LANES), -1e30, F32)


def score_bias(ids, table):
    return pl.pallas_call(
        bias_kernel,
        out_shape=jax.ShapeDtypeStruct((HEADS, WP, LANES), F32),
        in_specs=[vmem(), vmem()],
        out_specs=vmem(),
        compiler_params=params_of(),
        cost_estimate=cost(2 * HEADS * WP * LANES * 384, 4 * HEADS * WP * LANES),
        name="score_bias",
    )(ids, table)


def bias_back_kernel(ids_ref, sums_ref, out_ref):
    entries = out_ref.shape[0]
    out_ref[...] = jnp.zeros(out_ref.shape, F32)
    lane = lax.broadcasted_iota(jnp.int32, (HEADS, LANES), 1)
    entry = lax.broadcasted_iota(jnp.int32, (entries, LANES), 0)
    together = 4

    def body(i, _):
        rows, picks = [], []
        for number in range(together):
            j = i * together + number
            row = sums_ref[:, pl.ds(j, 1), :].reshape(HEADS, LANES)
            rows.append(jnp.where(lane < WT, row, 0.0))
            picks.append(jnp.where(ids_ref[pl.ds(j, 1), :] == entry, 1.0, 0.0).astype(BF16))
        row = jnp.concatenate(rows, axis=1)
        high = row.astype(BF16)
        rest = row - high.astype(F32)
        middle = rest.astype(BF16)
        low = (rest - middle.astype(F32)).astype(BF16)
        parts = jnp.concatenate([high, middle, low], axis=0)
        out_ref[...] += nt(jnp.concatenate(picks, axis=1), parts)
        return 0

    lax.fori_loop(0, WT // together, body, 0)


def score_bias_back(ids, sums, entries):
    parts = pl.pallas_call(
        bias_back_kernel,
        out_shape=jax.ShapeDtypeStruct((entries, 3 * HEADS), F32),
        in_specs=[vmem(), vmem()],
        out_specs=vmem(),
        compiler_params=params_of(),
        cost_estimate=cost(6 * HEADS * WP * LANES * 384, 4 * HEADS * WP * LANES),
        name="score_bias_back",
    )(ids, sums)
    return parts[:, :HEADS] + parts[:, HEADS : 2 * HEADS] + parts[:, 2 * HEADS :]


def pad_rows(x, rows):
    return jnp.concatenate([x, jnp.zeros((rows - x.shape[0], x.shape[1]), x.dtype)], axis=0)


def one_head(x, head):
    lane = lax.broadcasted_iota(jnp.int32, x.shape, 1)
    return jnp.where(lane // HEAD_DIM == head, x, jnp.zeros_like(x))


def by_head(x):
    return jnp.concatenate([one_head(x, head) for head in range(QUAD)], axis=0)


def attention_kernel(q_ref, k_ref, v_ref, bias_ref, out_ref, log_ref):
    def block(b, _):
        lanes = pl.ds(pl.multiple_of(b * LANES, LANES), LANES)
        queries = pad_rows(q_ref[:, lanes], LANES)
        scores = nt(by_head(k_ref[:, lanes]), queries)
        values = v_ref[:, lanes].astype(F32).T.astype(BF16)
        parts = []
        for head in range(QUAD):
            s = scores[head * WP : (head + 1) * WP] + bias_ref[b * QUAD + head]
            top = jnp.max(s, axis=0, keepdims=True)
            e = jnp.exp(s - top)
            total = jnp.sum(e, axis=0, keepdims=True)
            probs = (e * (1.0 / total)).astype(BF16)
            log_ref[0, pl.ds(b * QUAD + head, 1), :] = top + jnp.log(total)
            parts.append(nn(values[head * HEAD_DIM : (head + 1) * HEAD_DIM], probs))
        context = jnp.concatenate(parts, axis=0).T
        out_ref[:, lanes] = context[:WP].astype(BF16)
        return 0

    lax.fori_loop(0, HEADS // QUAD, block, 0, unroll=4)


def attention(mixed, bias):
    windows = mixed.shape[0] // WP

    def third(c):
        return pl.BlockSpec((WP, D), lambda i, c=c: (i, c))

    return pl.pallas_call(
        attention_kernel,
        grid=(windows,),
        out_shape=[
            jax.ShapeDtypeStruct((windows * WP, D), BF16),
            jax.ShapeDtypeStruct((windows, HEADS, LANES), F32),
        ],
        in_specs=[third(0), third(1), third(2), pl.BlockSpec(bias.shape, lambda i: (0, 0, 0))],
        out_specs=[third(0), pl.BlockSpec((1, HEADS, LANES), lambda i: (i, 0, 0))],
        compiler_params=params_of(),
        cost_estimate=cost(12e9, 8 * windows * WP * D, windows * HEADS * WP * LANES),
        name="attention",
    )(mixed, mixed, mixed, bias)


def attention_back_kernel(
    more, q_ref, k_ref, v_ref, g_ref, bias_ref, log_ref, *refs
):
    out_ref, acc_ref, column_ref = refs[-3:]

    @pl.when(pl.program_id(0) == 0)
    def _():
        if more:
            acc_ref[...] = refs[0][...]
            column_ref[...] = refs[1][...]
        else:
            acc_ref[...] = jnp.zeros(acc_ref.shape, F32)
            column_ref[...] = jnp.zeros(column_ref.shape, F32)

    def put(third, b, value):
        lanes = pl.ds(pl.multiple_of(third * D + b * LANES, LANES), LANES)
        low = value.astype(BF16)
        out_ref[:, lanes] = low
        column_ref[0:1, lanes] += jnp.sum(low.astype(F32), axis=0, keepdims=True)

    def block(b, _):
        lanes = pl.ds(pl.multiple_of(b * LANES, LANES), LANES)
        queries = pad_rows(q_ref[:, lanes], LANES)
        grads = pad_rows(g_ref[:, lanes], LANES)
        keys = k_ref[:, lanes]
        scores = nt(by_head(keys), queries)
        probs_grads = nt(by_head(v_ref[:, lanes]), grads)
        keys_t = keys.astype(F32).T.astype(BF16)
        query_parts, probs_parts, score_parts = [], [], []
        for head in range(QUAD):
            span = slice(head * WP, (head + 1) * WP)
            s = scores[span] + bias_ref[b * QUAD + head]
            probs = jnp.exp(s - log_ref[0, pl.ds(b * QUAD + head, 1), :])
            probs_grad = probs_grads[span]
            along = jnp.sum(probs * probs_grad, axis=0, keepdims=True)
            score_grad = (probs * (probs_grad - along)).astype(BF16)
            acc_ref[b * QUAD + head] += score_grad.astype(F32)
            probs_parts.append(probs.astype(BF16))
            score_parts.append(score_grad)
            query_parts.append(nn(keys_t[head * HEAD_DIM : (head + 1) * HEAD_DIM], score_grad))
        put(2, b, nn(jnp.concatenate(probs_parts, axis=1), by_head(grads)))
        put(1, b, nn(jnp.concatenate(score_parts, axis=1), by_head(queries)))
        put(0, b, jnp.concatenate(query_parts, axis=0).T[:WP] * HEAD_DIM ** (-0.5))
        return 0

    lax.fori_loop(0, HEADS // QUAD, block, 0, unroll=4)


def attention_back(mixed, grads, bias, logs, start, stop, before=None):
    rows = mixed.shape[0]

    def third(c):
        return pl.BlockSpec((WP, D), lambda i, c=c: (i + start, c))

    fixed = pl.BlockSpec(bias.shape, lambda i: (0, 0, 0))
    columns = pl.BlockSpec((8, 3 * D), lambda i: (0, 0))
    operands = [mixed, mixed, mixed, grads, bias, logs]
    specs = [
        third(0),
        third(1),
        third(2),
        third(0),
        fixed,
        pl.BlockSpec((1, HEADS, LANES), lambda i: (i + start, 0, 0)),
    ]
    aliases = {}
    if before is not None:
        operands += [before[1], before[2], before[0]]
        specs += [fixed, columns, anywhere()]
        aliases = {8: 0}
    return pl.pallas_call(
        partial(attention_back_kernel, before is not None),
        grid=(stop - start,),
        out_shape=[
            jax.ShapeDtypeStruct((rows, 3 * D), BF16),
            jax.ShapeDtypeStruct(bias.shape, F32),
            jax.ShapeDtypeStruct((8, 3 * D), F32),
        ],
        in_specs=specs,
        out_specs=[pl.BlockSpec((WP, 3 * D), lambda i: (i + start, 0)), fixed, columns],
        input_output_aliases=aliases,
        compiler_params=params_of(),
        cost_estimate=cost(
            3e9 * (stop - start), 16 * (stop - start) * WP * D, HEADS * WP * LANES
        ),
        name="attention_back",
    )(*operands)


def middle_kernel(x_ref, a_ref, w_ref, b_ref, gain_ref, shift_ref, middle_ref, second_ref):
    middle = x_ref[...].astype(F32) + nn(a_ref[...], w_ref[...]) + b_ref[...]
    middle_ref[...] = middle
    xhat, _ = normalized(middle)
    second_ref[...] = (xhat * gain_ref[...] + shift_ref[...]).astype(BF16)


def middle_rows(x, attended, weight, bias, gain, shift):
    tokens = x.shape[0]
    block = row_blocks(tokens)
    rows = pl.BlockSpec((block, D), lambda i: (i, 0))
    vec = pl.BlockSpec((1, D), lambda i: (0, 0))
    return pl.pallas_call(
        middle_kernel,
        grid=(tokens // block,),
        out_shape=[
            jax.ShapeDtypeStruct((tokens, D), F32),
            jax.ShapeDtypeStruct((tokens, D), BF16),
        ],
        in_specs=[rows, rows, pl.BlockSpec((D, D), lambda i: (0, 0)), vec, vec, vec],
        out_specs=[rows, rows],
        compiler_params=params_of(),
        cost_estimate=cost(2 * tokens * D * D, 10 * tokens * D),
        name="middle_rows",
    )(x, attended, weight, bias, gain, shift)


def mlp_up_kernel(geo, region, shared, steps, skip, me_ref, s_ref, g_ref, w_ref, b_ref, *refs):
    vec_ref, refs = refs[0], refs[1 + skip :]
    hidden_ref, slope_ref, refs = refs[0], refs[1], refs[2:]
    arrays = 2 * len(region.reduce)
    *scratch, held_ref = refs[arrays:]
    emitter = Emitter(geo, region, shared, me_ref, refs[:arrays], *scratch)
    flat_ref = emitter.flat_ref
    step = pl.program_id(0)
    height = w_ref.shape[1]

    @pl.when(step == 0)
    def _():
        emitter.begin()
        ((row, count),) = region.vectors

        def move(at, done, size):
            flat_ref[at : at + size, :] = vec_ref[done : done + size, :]

        copy_rows(region, flat_ref, row, count, move)

    block = jnp.maximum(step - 1, 0)
    left = held_ref[lax.rem(step + 1, 2)].T
    u = nn(s_ref[...], w_ref[...]) + b_ref[...]
    below = 0.5 * (1.0 + lax.erf(u * F32(math.sqrt(0.5))))
    density = jnp.exp(-0.5 * u * u) * F32(1.0 / math.sqrt(2.0 * math.pi))
    hidden = (u * below).astype(BF16)
    for j in range(0, D, 512):
        store_columns(
            region, flat_ref, block * height, j // LANES, nn(left, g_ref[:, j : j + 512])
        )
    hidden_ref[...] = hidden
    slope_ref[...] = below + u * density
    held_ref[lax.rem(step, 2)] = hidden
    pl.when(step > 0)(lambda: emit_rows(emitter, step - 1, steps, height))


def mlp_up(geo, region, me, second, grad_out, weight, bias, vector, slots, shared):
    tokens = second.shape[0]
    height = 512
    steps = FF // height
    last = steps - 1
    rows = pl.BlockSpec((tokens, D), lambda k: (0, 0), pipeline_mode=pl.Buffered(1))
    columns = pl.BlockSpec((tokens, height), lambda k: (0, jnp.minimum(k, last)))
    operands = [me, second, grad_out, weight, bias, vector]
    specs = [
        smem(),
        rows,
        rows,
        pl.BlockSpec((D, height), lambda k: (0, jnp.minimum(k, last))),
        pl.BlockSpec((1, height), lambda k: (0, jnp.minimum(k, last))),
        pl.BlockSpec(vector.shape, lambda k: (0, 0)),
    ]
    shapes, aliases, skip = with_slots(geo, region, slots, operands, specs)
    results = pl.pallas_call(
        partial(mlp_up_kernel, geo, region, shared, steps, skip),
        grid=(steps + 1,),
        out_shape=[
            jax.ShapeDtypeStruct((tokens, FF), BF16),
            jax.ShapeDtypeStruct((tokens, FF), F32),
        ]
        + shapes,
        in_specs=specs,
        out_specs=[columns, columns] + [anywhere()] * len(shapes),
        scratch_shapes=emit_scratch(geo, region) + [pltpu.VMEM((2, tokens, height), BF16)],
        input_output_aliases={key: value + 2 for key, value in aliases.items()},
        compiler_params=params_of(),
        cost_estimate=cost(4 * tokens * D * FF, 4 * D * FF + 6 * tokens * FF),
        name="mlp_up",
    )(*operands)
    return results[0], results[1], updated_slots(region, slots, results[2:])


def mlp_down_kernel(geo, region, shared, steps, skip, me_ref, *refs):
    (h_ref, slope_ref, s_ref, g_ref, up_ref, down_ref, m_ref, b_ref) = refs[:8]
    refs = refs[8 + skip :]
    result_ref, grad_ref, refs = refs[0], refs[1], refs[2:]
    arrays = 2 * len(region.reduce)
    *scratch, left_ref, sum_ref = refs[arrays:]
    emitter = Emitter(geo, region, shared, me_ref, refs[:arrays], *scratch)
    flat_ref = emitter.flat_ref
    step = pl.program_id(0)
    width = h_ref.shape[1]

    @pl.when(step == 0)
    def _():
        emitter.begin()
        left_ref[...] = s_ref[...].T
        sum_ref[...] = jnp.zeros(sum_ref.shape, F32)
        grad_ref[...] = jnp.zeros(grad_ref.shape, F32)

    pre = (nt(g_ref[...], down_ref[...]) * slope_ref[...]).astype(BF16)
    column = jnp.sum(pre.astype(F32), axis=0, keepdims=True)
    sum_ref[...] += nn(h_ref[...], down_ref[...])
    grad_ref[...] += nt(pre, up_ref[...])
    cols = width // LANES
    ((vec_row, _),) = region.vectors
    for c in range(cols):
        at = region.address(vec_row + step * cols + c)
        flat_ref[pl.ds(at, 1), :] = column[:, c * LANES : (c + 1) * LANES]
    store_columns(region, flat_ref, 0, step * cols, nn(left_ref[...], pre))

    @pl.when(step == steps - 1)
    def _():
        result_ref[...] = (sum_ref[...] + m_ref[...] + b_ref[...]).astype(BF16)
        emitter.emit(0, region.slots)
        emitter.finish()


def mlp_down(geo, region, me, hidden, slope, second, grad_out, up, down, middle, bias, slots, shared):
    tokens = second.shape[0]
    width = 512
    steps = FF // width
    rows = pl.BlockSpec((tokens, D), lambda k: (0, 0), pipeline_mode=pl.Buffered(1))
    columns = pl.BlockSpec((tokens, width), lambda k: (0, k))
    operands = [me, hidden, slope, second, grad_out, up, down, middle, bias]
    specs = [
        smem(),
        columns,
        columns,
        rows,
        rows,
        pl.BlockSpec((D, width), lambda k: (0, k)),
        pl.BlockSpec((width, D), lambda k: (k, 0)),
        rows,
        pl.BlockSpec((1, D), lambda k: (0, 0)),
    ]
    shapes, aliases, skip = with_slots(geo, region, slots, operands, specs)
    whole = pl.BlockSpec((tokens, D), lambda k: (0, 0))
    results = pl.pallas_call(
        partial(mlp_down_kernel, geo, region, shared, steps, skip),
        grid=(steps,),
        out_shape=[
            jax.ShapeDtypeStruct((tokens, D), BF16),
            jax.ShapeDtypeStruct((tokens, D), F32),
        ]
        + shapes,
        in_specs=specs,
        out_specs=[whole, whole] + [anywhere()] * len(shapes),
        scratch_shapes=emit_scratch(geo, region)
        + [
            pltpu.VMEM((D, tokens), BF16),
            pltpu.VMEM((tokens, D), F32),
        ],
        input_output_aliases={key: value + 2 for key, value in aliases.items()},
        compiler_params=params_of(),
        cost_estimate=cost(8 * tokens * D * FF, 6 * D * FF + 6 * tokens * FF),
        name="mlp_down",
    )(*operands)
    return results[0], results[1], updated_slots(region, slots, results[2:])


def middle_back_kernel(s_ref, m_ref, g_ref, gain_ref, w_ref, mg_ref, bg_ref, cg_ref, vec_ref):
    @pl.when(pl.program_id(0) == 0)
    def _():
        vec_ref[...] = jnp.zeros(vec_ref.shape, F32)

    grad = s_ref[...]
    xhat, inverse = normalized(m_ref[...])
    middle_grad = g_ref[...].astype(F32) + normalized_back(grad * gain_ref[...], xhat, inverse)
    branch = middle_grad.astype(BF16)
    mg_ref[...] = middle_grad
    bg_ref[...] = branch
    cg_ref[...] = nt(branch, w_ref[...]).astype(BF16)
    vec_ref[0:1, :] += jnp.sum(branch.astype(F32), axis=0, keepdims=True)
    vec_ref[1:2, :] += jnp.sum(grad * xhat, axis=0, keepdims=True)
    vec_ref[2:3, :] += jnp.sum(grad, axis=0, keepdims=True)


def middle_back(second_grad, middle, grad_out, gain, weight):
    tokens = middle.shape[0]
    block = row_blocks(tokens)
    rows = pl.BlockSpec((block, D), lambda i: (i, 0))
    low = jax.ShapeDtypeStruct((tokens, D), BF16)
    return pl.pallas_call(
        middle_back_kernel,
        grid=(tokens // block,),
        out_shape=[
            jax.ShapeDtypeStruct((tokens, D), F32),
            low,
            low,
            jax.ShapeDtypeStruct((8, D), F32),
        ],
        in_specs=[
            rows,
            rows,
            rows,
            pl.BlockSpec((1, D), lambda i: (0, 0)),
            pl.BlockSpec((D, D), lambda i: (0, 0)),
        ],
        out_specs=[rows, rows, rows, pl.BlockSpec((8, D), lambda i: (0, 0))],
        compiler_params=params_of(),
        cost_estimate=cost(2 * tokens * D * D, 18 * tokens * D),
        name="middle_back",
    )(second_grad, middle, grad_out, gain, weight)


def first_back_kernel(steps, mixed_ref, w_ref, x_ref, mg_ref, gain_ref, out_ref, vec_ref, sum_ref):
    step = pl.program_id(0)
    part = nt(mixed_ref[...], w_ref[...])

    @pl.when(step == 0)
    def _():
        sum_ref[...] = part

    @pl.when(step > 0)
    def _():
        sum_ref[...] += part

    @pl.when(step == steps - 1)
    def _():
        block = row_blocks(x_ref.shape[0])
        vec_ref[...] = jnp.zeros(vec_ref.shape, F32)

        def body(i, _):
            rows = pl.ds(pl.multiple_of(i * block, 16), block)
            grad = sum_ref[rows, :]
            xhat, inverse = normalized(x_ref[rows, :].astype(F32))
            inner = normalized_back(grad * gain_ref[...], xhat, inverse)
            out_ref[rows, :] = (mg_ref[rows, :] + inner).astype(BF16)
            vec_ref[0:1, :] += jnp.sum(grad * xhat, axis=0, keepdims=True)
            vec_ref[1:2, :] += jnp.sum(grad, axis=0, keepdims=True)
            return 0

        lax.fori_loop(0, x_ref.shape[0] // block, body, 0)


def first_back(mixed_grad, weight, x, middle_grad, gain):
    tokens = x.shape[0]
    width = 768
    steps = 3 * D // width
    rows = pl.BlockSpec((tokens, D), lambda k: (0, 0), pipeline_mode=pl.Buffered(1))
    return pl.pallas_call(
        partial(first_back_kernel, steps),
        grid=(steps,),
        out_shape=[
            jax.ShapeDtypeStruct((tokens, D), BF16),
            jax.ShapeDtypeStruct((8, D), F32),
        ],
        in_specs=[
            pl.BlockSpec((tokens, width), lambda k: (0, k)),
            pl.BlockSpec((D, width), lambda k: (0, k)),
            rows,
            rows,
            pl.BlockSpec((1, D), lambda k: (0, 0)),
        ],
        out_specs=[
            pl.BlockSpec((tokens, D), lambda k: (0, 0)),
            pl.BlockSpec((8, D), lambda k: (0, 0)),
        ],
        scratch_shapes=[pltpu.VMEM((tokens, D), F32)],
        compiler_params=params_of(),
        cost_estimate=cost(6 * tokens * D * D, 6 * D * D + 14 * tokens * D),
        name="first_back",
    )(mixed_grad, weight, x, middle_grad, gain)


def local(
    patches,
    cotangent,
    window_rows,
    rel_index,
    params,
    first_moment,
    second_moment,
    learn_rate,
    step_count,
):
    arrivals = patches.shape[0]
    windows = arrivals // WT
    geo = Geometry(lax.axis_size("dp"), lax.axis_size("fsdp"), params.shape[0])
    dp_index = lax.axis_index("dp")
    fsdp_index = lax.axis_index("fsdp")
    me = jnp.stack(
        [lax.axis_index(AXES), dp_index // 2, dp_index % 2, fsdp_index // 2, fsdp_index % 2]
    ).astype(jnp.int32)

    shard = params.reshape(geo.rows, LANES)
    if geo.spill:
        spill = lax.ppermute(
            shard[: round_up(geo.spill, 8)], AXES, [(geo.spill_from, geo.spill_to)]
        )
    else:
        spill = jnp.zeros((8, LANES), F32)
    share = prepare(geo, me, shard, spill).reshape(4, geo.quarter, LANES)
    row_ids = jnp.pad(
        window_rows.reshape(windows, WT), ((0, 0), (0, WP - WT)), constant_values=-1
    ).reshape(windows * WP)
    stacked = jnp.stack(spread_quarters(geo, share, dp_index))
    gathers = []
    for groups in GATHER_PHASES:
        pieces = [
            lax.dynamic_index_in_dim(stacked, dp_index ^ group, 0, keepdims=True)
            for group in groups
        ]
        gathers.append(Gather(geo, jnp.concatenate(pieces, axis=0)))
    gathers[0].line()
    half = windows // 2
    ids_of = row_ids[:, None]
    x = permute_in(after(ids_of, gathers[0].held), patches, 0, half)
    held = gathers[0].joined(x)
    gathers[0].across()
    gathers[1].line(held)
    x = permute_in(after(ids_of, held), patches, half, windows, x)
    near = gathers[0].last(x)
    held = gathers[1].joined(x)
    gathers[2].line(held)
    grad_out = permute_in(after(ids_of, near, held), cotangent, 0, half)
    gathered = {0: gathers[0].finish(grad_out)}
    far = gathered[0][1]
    gathers[1].across(far)
    grad_out = permute_in(after(ids_of, far), cotangent, half, windows, grad_out)
    held = gathers[2].joined(grad_out)
    gathers[3].line(held)
    gathered[0] = gathered[0][:3] + [after(gathered[0][3], grad_out, held)]

    mix_matrix = (MIX_ROW, D, 3 * D // LANES)
    out_matrix = (OUT_ROW, D, D // LANES)
    expand_matrix = (EXPAND_ROW, D, FF // LANES)
    shrink_matrix = (SHRINK_ROW, FF, D // LANES)
    out_end = p_row(STARTS[6])
    expand_end = p_row(STARTS[10])
    shrink_end = p_row(STARTS[12])
    mix_vectors = [(0, 8), (8, 8), (TAIL_ROW, TABLE_ROW - TAIL_ROW), (TABLE_ROW, SPLIT_ROW - TABLE_ROW)]
    out_vectors = [(out_end + 8 * i, 8) for i in range(3)]
    expand_vectors = [(expand_end, FF // LANES)]
    shrink_vectors = [(shrink_end, 8)]

    first = Region(
        geo, 0, OUT_ROW, mix_matrix, mix_vectors, high=geo.spill_to if geo.spill else None
    )
    mix_weight, attn_gain, attn_shift, mix_bias, table_rows = unpack(geo, first, me, gathered)
    near = gathers[1].last(mix_weight)
    held = gathers[3].joined(mix_weight)
    gathers[2].across(near)
    table_rows = after(table_rows, near, held)

    def line_of(rows):
        return rows.reshape(1, -1)

    entries = round_up(TABLE_ROWS, 16)
    table = table_rows.reshape(-1)[: TABLE_ROWS * HEADS].reshape(TABLE_ROWS, HEADS).T
    table = jnp.pad(table, ((0, 0), (0, entries - TABLE_ROWS))).astype(BF16)
    ids = jnp.pad(rel_index.T, ((0, WP - WT), (0, LANES - WT)), constant_values=-1)
    bias = score_bias(ids, table)

    normed, mixed = mix(
        after(x, bias),
        line_of(attn_gain),
        line_of(attn_shift),
        mix_weight,
        line_of(mix_bias),
    )
    gathered[1] = gathers[1].finish(mixed)
    near = gathers[2].last(mixed)
    gathers[3].across(near)
    attended, logs = attention(after(mixed, near, gathered[1][1]), bias)
    out_weight, out_bias, mlp_gain, mlp_shift = unpack(
        geo, Region(geo, OUT_ROW, EXPAND_ROW, out_matrix, out_vectors), me, gathered
    )
    gathered[2] = gathers[2].finish(out_weight)
    near = gathers[3].last(out_weight)
    middle, second = middle_rows(
        x,
        after(attended, near, gathered[2][1]),
        out_weight,
        line_of(out_bias),
        line_of(mlp_gain),
        line_of(mlp_shift),
    )
    expand_weight, expand_bias = unpack(
        geo, Region(geo, EXPAND_ROW, SHRINK_ROW, expand_matrix, expand_vectors), me, gathered
    )
    gathered[3] = gathers[3].finish(expand_weight)
    second = after(second, gathered[3][1])

    shrink_region = Region(
        geo, SHRINK_ROW, END_ROW, shrink_matrix, shrink_vectors, high=geo.devices - 1
    )
    expand_region = Region(geo, EXPAND_ROW, SHRINK_ROW, expand_matrix, expand_vectors)
    out_region = Region(geo, OUT_ROW, EXPAND_ROW, out_matrix, out_vectors)
    mix_region = Region(geo, 0, TAIL_ROW, mix_matrix, [])
    slots = {}
    shrink_bias_grad = jnp.sum(grad_out.astype(F32), axis=0).reshape(-1, LANES)
    hidden, slope, slots = mlp_up(
        geo,
        shrink_region,
        me,
        second,
        grad_out,
        expand_weight,
        line_of(expand_bias),
        shrink_bias_grad,
        slots,
        False,
    )
    phase3 = Reduction(geo, slots[3], 3)
    shrink_weight, shrink_bias = unpack(
        geo, Region(geo, SHRINK_ROW, END_ROW, shrink_matrix, shrink_vectors), me, gathered
    )
    sent = phase3.last(shrink_weight)
    result, second_grad, slots = mlp_down(
        geo,
        expand_region,
        me,
        after(hidden, sent),
        slope,
        second,
        grad_out,
        expand_weight,
        shrink_weight,
        middle,
        line_of(shrink_bias),
        slots,
        expand_region.high == shrink_region.low,
    )
    phase2 = Reduction(geo, slots[2], 2)
    sent = phase3.across(second_grad)
    middle_grad, branch_grad, context_grad, middle_vec = middle_back(
        after(second_grad, sent), middle, grad_out, line_of(mlp_gain), out_weight
    )
    sent = [phase3.line(context_grad), phase2.last(context_grad)]
    slots = pack(
        geo,
        out_region,
        me,
        attended,
        after(branch_grad, *sent),
        [middle_vec[i].reshape(8, LANES) for i in range(3)],
        slots,
        out_region.high == expand_region.low,
    )
    phase1 = Reduction(geo, slots[1], 1)
    context_grad = after(context_grad, slots[1][0])
    parts = attention_back(mixed, context_grad, bias, logs, 0, half)
    sums = {3: phase3.total(parts[1])}
    sent = [phase2.across(parts[1]), phase1.last(parts[1]), sums[3]]
    mixed_grad, score_sums, column_sums = attention_back(
        mixed, after(context_grad, *sent), bias, logs, half, windows, parts
    )
    sent = [phase2.line(score_sums), phase1.across(score_sums)]
    slots = pack(
        geo,
        mix_region,
        me,
        normed,
        after(mixed_grad, *sent),
        [],
        slots,
        mix_region.high == out_region.low,
    )
    packed = slots[0][0]
    phase0 = Reduction(geo, slots[0], 0)
    sums[2] = phase2.total(packed)
    sent = [phase1.line(packed), sums[2]]
    activations = permute_out(row_ids[None], after(result, packed, *sent), arrivals)
    sent = phase0.last(activations)
    input_rows, first_vec = first_back(
        after(mixed_grad, sent), mix_weight, x, middle_grad, line_of(attn_gain)
    )
    sums[1] = phase1.total(input_rows)
    sent = [phase0.across(input_rows), sums[1]]
    table_grad = score_bias_back(ids, after(score_sums, *sent), entries)[:TABLE_ROWS]

    table_pad = (SPLIT_ROW - TABLE_ROW) * LANES - TABLE_ROWS * HEADS
    late = jnp.concatenate(
        [
            first_vec[:2].reshape(HEAD_ROWS, LANES),
            column_sums[0].reshape(-1, LANES),
            jnp.pad(table_grad.reshape(-1), (0, table_pad)).reshape(-1, LANES),
        ],
        axis=0,
    )
    sent = phase0.line(table_grad)
    late = after(jnp.pad(late, ((0, LATE_ROWS - late.shape[0]), (0, 0))), sent)
    late = sum_everywhere(geo, late)
    input_grad = permute_out(row_ids[None], after(input_rows, sent), arrivals)
    squares = square_sums(
        geo, me, REDUCE_PHASES[1:], [after(sums[1], sent), sums[2], sums[3]]
    )
    sums[0] = phase0.total(squares, input_grad)
    squares = squares + square_sums(geo, me, REDUCE_PHASES[:1], [sums[0]])
    collected = collect_quarters(geo, [sums[group][0] for group in range(4)], dp_index)
    scale = 1.0 / jnp.sqrt(F32(arrivals * geo.devices))
    squares = sum_everywhere(geo, jnp.sum(squares, axis=1)[None], 0, 3)
    collected[0] = after(collected[0], squares)
    step_float = step_count.astype(F32)
    coef = jnp.stack(
        [
            scale,
            1.0 - jnp.power(F32(0.9), step_float),
            1.0 - jnp.power(F32(0.999), step_float),
            learn_rate,
        ]
    )
    params_new, first_new, second_new = update_step(
        geo,
        me,
        coef,
        collected,
        late,
        shard,
        first_moment.reshape(geo.rows, LANES),
        second_moment.reshape(geo.rows, LANES),
    )
    squares = sum_everywhere(geo, after(squares, params_new), 3)
    tensor = lax.broadcasted_iota(jnp.int32, (LATE_ROWS, 16), 1)
    row = lax.broadcasted_iota(jnp.int32, (LATE_ROWS, 16), 0)
    inside = tensor < 0
    edges = [0, 8, HEAD_ROWS, HEAD_ROWS + TABLE_ROW - TAIL_ROW, LATE_ROWS]
    for t, start, stop in zip((0, 1, 3, 4), edges, edges[1:]):
        inside = inside | ((tensor == t) & (row >= start) & (row < stop))
    late_rows = jnp.sum(late * late, axis=1, keepdims=True)
    totals = squares[0] + jnp.sum(jnp.where(inside, late_rows, 0.0), axis=0)
    entry_counts = jnp.array([math.prod(shape) for shape in SHAPES], F32)
    group_rms = jnp.sqrt(totals[: len(SHAPES)] * (scale * scale) / entry_counts)

    return (
        activations,
        input_grad,
        group_rms,
        params_new.reshape(-1),
        first_new.reshape(-1),
        second_new.reshape(-1),
    )


def solution(mesh):
    placed = (
        P(AXES, None),
        P(AXES, None),
        P(AXES),
        P(),
        P(AXES),
        P(AXES),
        P(AXES),
        P(),
        P(),
    )
    return jax.shard_map(
        local,
        mesh=mesh,
        in_specs=placed,
        out_specs=(P(AXES, None), P(AXES, None), P(), P(AXES), P(AXES), P(AXES)),
        check_vma=False,
    )
```

```python
from functools import partial
import math

import jax
import jax.numpy as jnp
from jax import lax
from jax.experimental import pallas as pl
from jax.experimental.pallas import tpu as pltpu
from jax.sharding import PartitionSpec as P

D = 1024
HEADS = 32
HEAD_DIM = 32
FF = 4096
WT = 100
WP = 104
TABLE_ROWS = 361
RAW = 12607776
LANES = 128
QUAD = LANES // HEAD_DIM
AXES = ("dp", "fsdp")
BF16 = jnp.bfloat16
F32 = jnp.float32
VMEM_LIMIT = 62 << 20
BUFFERS = 4
FETCHES = 6

SHAPES = [
    (D,),
    (D,),
    (D, 3 * D),
    (3 * D,),
    (TABLE_ROWS, HEADS),
    (D, D),
    (D,),
    (D,),
    (D,),
    (D, FF),
    (FF,),
    (FF, D),
    (D,),
]
STARTS = [0]
for _shape in SHAPES:
    STARTS.append(STARTS[-1] + math.prod(_shape))

SPLIT = STARTS[5]
LIFT = (-SPLIT) % LANES


def p_row(position):
    lifted = position + (LIFT if position >= SPLIT else 0)
    assert lifted % LANES == 0
    return lifted // LANES


MIX_ROW, OUT_ROW, EXPAND_ROW, SHRINK_ROW = (p_row(STARTS[i]) for i in (2, 5, 9, 11))
SPLIT_ROW = p_row(SPLIT)
TAIL_ROW = p_row(STARTS[3])
TABLE_ROW = STARTS[4] // LANES
END_ROW = p_row(RAW)
HEAD_ROWS = MIX_ROW
LATE_TAIL = SPLIT_ROW - TAIL_ROW
LATE_ROWS = -(-(HEAD_ROWS + LATE_TAIL) // 8) * 8


def round_up(value, step):
    return -(-value // step) * step


def vmem():
    return pl.BlockSpec(memory_space=pltpu.VMEM)


def smem():
    return pl.BlockSpec(memory_space=pltpu.SMEM)


def anywhere():
    return pl.BlockSpec(memory_space=pl.ANY)


def params_of(**more):
    return pltpu.CompilerParams(vmem_limit_bytes=VMEM_LIMIT, **more)


COST_SCALE = 200


def cost(flops, bytes_accessed, transcendentals=0):
    return pl.CostEstimate(
        flops=int(COST_SCALE * flops),
        bytes_accessed=int(COST_SCALE * bytes_accessed),
        transcendentals=int(transcendentals),
    )


def nn(left, right):
    return jnp.dot(left, right, preferred_element_type=F32)


def nt(left, right):
    return lax.dot_general(left, right, (((1,), (1,)), ((), ())), preferred_element_type=F32)


class Geometry:
    def __init__(self, dp, fsdp, shard_len):
        assert dp == 4 and shard_len % LANES == 0 and fsdp % 2 == 0
        self.fsdp = fsdp
        self.devices = dp * fsdp
        self.line = fsdp // 2
        assert self.line & (self.line - 1) == 0
        self.rows = shard_len // LANES
        first, last = TABLE_ROW // self.rows, (SPLIT_ROW - 1) // self.rows
        assert last - first in (0, 1)
        self.spill_from, self.spill_to = last, first
        self.spill = SPLIT_ROW - self.rows * last if last != first else 0
        self.quarter = round_up(-(-(self.rows + 16 + self.spill) // 4), 8)
        self.slot = 4 * self.quarter
        assert self.slot % 16 == 0
        tiles = self.slot // 16
        self.chunk = max(t for t in range(1, 34) if tiles % t == 0)
        self.bit_x, self.bit_core, self.bit_y = 2 * fsdp, fsdp, 1

    def base(self, device):
        return (device * self.rows) // 16 * 16

    def permute(self, value, mask_core0, mask_core1):
        pairs = []
        for index in range(self.devices):
            core = (index // self.fsdp) % 2
            pairs.append((index, index ^ (mask_core1 if core else mask_core0)))
        return lax.ppermute(value, AXES, pairs)

    def core_swap(self, value):
        return self.permute(value, self.bit_core, self.bit_core)


def prepare_kernel(geo, me_ref, shard_ref, spill_ref, out_ref, pad_ref):
    rows, slot = geo.rows, geo.slot
    base = me_ref[0] * rows
    shift = lax.rem(base, 16)
    pad_ref[0:32, :] = jnp.zeros((32, LANES), F32)
    pad_ref[16 + rows : slot + 32, :] = jnp.zeros((slot + 16 - rows, LANES), F32)
    whole = rows // 64

    def place_body(i, _):
        r0 = i * 64
        pad_ref[pl.ds(16 + shift + r0, 64), :] = shard_ref[pl.ds(pl.multiple_of(r0, 64), 64), :]
        return 0

    lax.fori_loop(0, whole, place_body, 0)
    rest = rows - whole * 64
    if rest:
        pad_ref[pl.ds(16 + shift + whole * 64, rest), :] = shard_ref[whole * 64 : rows, :]
    if geo.spill:
        count = geo.spill

        @pl.when(me_ref[0] == geo.spill_to)
        def _():
            lane = lax.broadcasted_iota(jnp.int32, (count, LANES), 1)
            row = lax.broadcasted_iota(jnp.int32, (count, LANES), 0)
            flat = (rows * geo.spill_from + row) * LANES + lane
            at = 16 + rows * geo.spill_from - geo.base(geo.spill_to)
            pad_ref[at : at + count, :] = jnp.where(flat < SPLIT, spill_ref[0:count, :], 0.0)

    step = 16 * geo.chunk

    def body(i, _):
        r0 = pl.multiple_of(i * step, 16)
        here = pad_ref[pl.ds(r0 + 16, step), :]
        above = pad_ref[pl.ds(r0 + 15, step), :]
        lane = lax.broadcasted_iota(jnp.int32, (step, LANES), 1)
        row = lax.broadcasted_iota(jnp.int32, (step, LANES), 0)
        flat = (base - shift + r0 + row) * LANES + lane
        moved = jnp.where(lane >= LIFT, pltpu.roll(here, LIFT, 1), pltpu.roll(above, LIFT, 1))
        value = jnp.where(flat < SPLIT, here, jnp.where(flat >= SPLIT + LIFT, moved, 0.0))
        out_ref[pl.ds(r0, step), :] = value.astype(BF16)
        return 0

    lax.fori_loop(0, slot // step, body, 0)


def prepare(geo, me, shard, spill):
    return pl.pallas_call(
        partial(prepare_kernel, geo),
        out_shape=jax.ShapeDtypeStruct((geo.slot, LANES), BF16),
        in_specs=[smem(), vmem(), vmem()],
        out_specs=vmem(),
        scratch_shapes=[pltpu.VMEM((geo.slot + 32, LANES), F32)],
        compiler_params=params_of(),
        name="prepare_share",
    )(me, shard, spill)


GATHER_PHASES = ((0,), (1,), (2,), (3,))
REDUCE_PHASES = ((0,), (1,), (2,), (3,))


def phase_of(phases, group):
    return [number for number, groups in enumerate(phases) if group in groups][0]


def spot(geo, me_ref, device, own, quarter_x, groups):
    core = me_ref[2] if own else 1 - me_ref[2]
    rel_x = quarter_x ^ me_ref[1]
    rel_z = (lax.rem(device, geo.fsdp) // 2) ^ me_ref[3]
    rel_y = lax.rem(device, 2) ^ me_ref[4]
    straight = core == 0
    first = jnp.where(straight, rel_x, rel_y)
    late = jnp.where(straight, rel_y, rel_x)
    at = (first * geo.line + rel_z) * len(groups) + device // geo.fsdp - groups[0]
    return quarter_x * 2 + core, late, at


def by_phase(geo, phases, numbers, device, action):
    if len(numbers) == 1:
        action(0, phases[numbers[0]])
        return
    group = device // geo.fsdp
    for position, number in enumerate(numbers):
        groups = phases[number]
        pl.when((group >= groups[0]) & (group <= groups[-1]))(partial(action, position, groups))


class Region:
    def __init__(self, geo, row0, row1, matrix, vectors, span=None, high=None):
        self.row0, self.row1 = row0, row1
        self.mat_row, self.depth, self.cols = matrix
        self.start, self.stop = span or (0, self.depth)
        self.vectors = vectors
        self.low = max(row0 - 1, 0) // geo.rows
        self.high = (row1 - 1) // geo.rows if high is None else high
        self.slots = self.high - self.low + 1
        self.origin = geo.base(self.low)
        self.pitch = 17 if self.cols % 32 == 0 else 16
        self.stride = self.cols * self.pitch // 16
        self.scratch_tiles = (geo.base(self.high) + geo.slot - self.origin) // 16
        groups = {d // geo.fsdp for d in range(self.low, self.high + 1)}
        self.gather = sorted({phase_of(GATHER_PHASES, group) for group in groups})
        self.reduce = sorted({phase_of(REDUCE_PHASES, group) for group in groups})

    def address(self, row):
        rel = row - self.origin
        return rel if self.pitch == 16 else rel + rel // 16

    def scratch(self):
        return pltpu.VMEM((self.scratch_tiles * self.pitch, LANES), F32)


def copy_rows(region, ref, row, count, move):
    done = 0
    while done < count:
        size = min(count - done, 16 - (row + done - region.origin) % 16)
        if region.pitch == 16:
            size = count - done
        move(region.address(row + done), done, size)
        done += size


def unpack_kernel(geo, region, block, aliased, me_ref, *refs):
    arrays = 4 * len(region.gather)
    srcs, refs = refs[:arrays], refs[arrays:]
    if aliased:
        refs = refs[1:]
    weight_ref, refs = refs[0], refs[1:]
    vec_refs, refs = refs[: len(region.vectors)], refs[len(region.vectors) :]
    flat_ref, slot_ref, stage_ref, sems, out_sem = refs
    quarter, pitch, cols = geo.quarter, region.pitch, region.cols
    total = (region.stop - region.start) // block

    def fetch(step):
        device = region.low + step
        buf = lax.rem(step, FETCHES)

        def from_phase(position, groups):
            for own in range(2):
                for quarter_x in range(2):
                    q, late, at = spot(geo, me_ref, device, own, quarter_x, groups)
                    to = pl.ds(pl.multiple_of(q * quarter, 8), quarter)
                    for side in range(2):
                        src = srcs[position * 4 + (1 - own) * 2 + side]

                        @pl.when(late == side)
                        def _(src=src, at=at, to=to, own=own, quarter_x=quarter_x):
                            pltpu.make_async_copy(
                                src.at[at],
                                slot_ref.at[buf, to],
                                sems.at[buf, own * 2 + quarter_x],
                            ).start()

        by_phase(geo, GATHER_PHASES, region.gather, device, from_phase)

    ahead = min(FETCHES - 1, region.slots)

    def fetch_body(step, _):
        fetch(step)
        return 0

    lax.fori_loop(0, ahead, fetch_body, 0)

    def slot_body(step, carry):
        tile_carry, done = carry

        @pl.when(step + ahead < region.slots)
        def _():
            fetch(step + ahead)

        buf = lax.rem(step, FETCHES)
        for number in range(4):
            pltpu.make_async_copy(
                srcs[0].at[0], slot_ref.at[buf, pl.ds(0, quarter)], sems.at[buf, number]
            ).wait()
        device = region.low + step
        first_tile = geo.base(device) // 16 - region.origin // 16
        next_row = (device + 1) * geo.rows // 16 * 16
        next_tile = next_row // 16 - region.origin // 16

        def rows_body(i, _):
            t0 = i * geo.chunk
            r0 = pl.multiple_of(t0 * 16, 16)
            if pitch == 16:
                to = pl.multiple_of((first_tile + t0) * 16, 16)
                flat_ref[pl.ds(to, geo.chunk * 16), :] = slot_ref[
                    buf, pl.ds(r0, geo.chunk * 16), :
                ].astype(F32)
            else:
                for t in range(geo.chunk):
                    flat_ref[pl.ds((first_tile + t0 + t) * pitch, 16), :] = slot_ref[
                        buf, pl.ds(r0 + t * 16, 16), :
                    ].astype(F32)
            return 0

        lax.fori_loop(0, geo.slot // 16 // geo.chunk, rows_body, 0)
        seam = pl.ds(first_tile * pitch, 16)
        flat_ref[seam, :] = flat_ref[seam, :] + tile_carry
        complete = jnp.maximum(next_row - region.mat_row - region.start * cols, 0) // (block * cols)
        complete = jnp.where(step == region.slots - 1, total, jnp.minimum(complete, total))

        def mat_body(i, _):
            to = pl.multiple_of(i * block, block)
            row = i * (block * region.stride)
            for c in range(cols):
                at = region.address(region.mat_row + region.start * cols + c)
                stage_ref[pl.ds(to, block), c * LANES : (c + 1) * LANES] = flat_ref[
                    pl.ds(at + row, block, stride=region.stride), :
                ].astype(BF16)
            pltpu.make_async_copy(
                stage_ref.at[pl.ds(to, block)],
                weight_ref.at[pl.ds(region.start + to, block)],
                out_sem,
            ).start()
            return 0

        lax.fori_loop(done, complete, mat_body, 0)
        return flat_ref[pl.ds(next_tile * pitch, 16), :], complete

    lax.fori_loop(0, region.slots, slot_body, (jnp.zeros((16, LANES), F32), jnp.int32(0)))
    for (row, count), out_ref in zip(region.vectors, vec_refs):

        def move(at, done, size, out_ref=out_ref):
            out_ref[done : done + size, :] = flat_ref[at : at + size, :]

        copy_rows(region, flat_ref, row, count, move)
    pltpu.make_async_copy(
        stage_ref, weight_ref.at[pl.ds(region.start, region.stop - region.start)], out_sem
    ).wait()


def unpack(geo, region, me, gathered, weight=None):
    operands = [me] + [array for phase in region.gather for array in gathered[phase]]
    specs = [smem()] + [anywhere()] * (len(operands) - 1)
    aliases = {}
    if weight is not None:
        operands.append(weight)
        specs.append(anywhere())
        aliases = {len(operands) - 1: 0}
    height = region.stop - region.start
    return pl.pallas_call(
        partial(unpack_kernel, geo, region, 64 if region.cols <= 8 else 16, weight is not None),
        out_shape=[jax.ShapeDtypeStruct((region.depth, region.cols * LANES), BF16)]
        + [jax.ShapeDtypeStruct((count, LANES), F32) for _, count in region.vectors],
        in_specs=specs,
        out_specs=[anywhere()] + [vmem()] * len(region.vectors),
        scratch_shapes=[
            region.scratch(),
            pltpu.VMEM((FETCHES, geo.slot, LANES), BF16),
            pltpu.VMEM((height, region.cols * LANES), BF16),
            pltpu.SemaphoreType.DMA((FETCHES, 4)),
            pltpu.SemaphoreType.DMA(()),
        ],
        input_output_aliases=aliases,
        compiler_params=params_of(),
        cost_estimate=cost(0, 8 * LANES * height * region.cols),
        name="unpack_weights",
    )(*operands)


def clear_rows(region, flat_ref):
    filled = sorted(
        [(region.mat_row, region.mat_row + region.depth * region.cols)]
        + [(row, row + count) for row, count in region.vectors]
    )
    edges = [region.origin] + [edge for run in filled for edge in run]
    edges.append(region.origin + 16 * region.scratch_tiles)
    for start, stop in zip(edges[::2], edges[1::2]):
        if stop > start:

            def move(at, done, size):
                for r in range(0, size, 64):
                    span = min(64, size - r)
                    flat_ref[at + r : at + r + span, :] = jnp.zeros((span, LANES), F32)

            copy_rows(region, flat_ref, start, stop - start, move)


class Emitter:
    def __init__(self, geo, region, shared, me_ref, outs, flat_ref, slot_ref, old_ref, sems, old_sem):
        self.geo, self.region, self.shared, self.me_ref = geo, region, shared, me_ref
        self.outs, self.flat_ref, self.slot_ref, self.old_ref = outs, flat_ref, slot_ref, old_ref
        self.sems, self.old_sem = sems, old_sem

    def copies(self, device, action):
        geo = self.geo

        def to_phase(position, groups):
            count = 2 * geo.line * len(groups)
            for own in range(2):
                for quarter_x in range(2):
                    q, late, at = spot(geo, self.me_ref, device, own, quarter_x, groups)
                    rows = pl.ds(pl.multiple_of(q * geo.quarter, 8), geo.quarter)
                    action(
                        self.outs[position * 2 + 1 - own].at[late * count + at],
                        rows,
                        own * 2 + quarter_x,
                    )

        by_phase(geo, REDUCE_PHASES, self.region.reduce, device, to_phase)

    def begin(self):
        clear_rows(self.region, self.flat_ref)
        if self.shared:
            def action(place, rows, number):
                pltpu.make_async_copy(
                    place, self.old_ref.at[rows], self.old_sem.at[number]
                ).start()

            self.copies(self.region.high, action)

    def wait(self, parity):
        for number in range(4):
            pltpu.make_async_copy(
                self.slot_ref.at[parity, pl.ds(0, self.geo.quarter)],
                self.outs[0].at[0],
                self.sems.at[parity, number],
            ).wait()

    def slots_before(self, row):
        ready = (row - 1) // self.geo.rows - self.region.low
        return jnp.clip(ready, 0, self.region.slots)

    def emit(self, start, stop):
        geo, region, pitch = self.geo, self.region, self.region.pitch

        def slot_body(index, _):
            parity = lax.rem(index, BUFFERS)
            pl.when(index >= BUFFERS)(lambda: self.wait(parity))
            first_tile = geo.base(region.low + index) // 16 - region.origin // 16

            def convert(add):
                def rows_body(i, _):
                    t0 = i * geo.chunk
                    r0 = pl.multiple_of(t0 * 16, 16)
                    run = 1 if pitch > 16 else geo.chunk
                    for t in range(0, geo.chunk, run):
                        row = (first_tile + t0 + t) * pitch
                        row = pl.multiple_of(row, 16) if pitch == 16 else row
                        value = self.flat_ref[pl.ds(row, run * 16), :]
                        here = pl.ds(r0 + t * 16, run * 16)
                        if add:
                            value = value + self.old_ref[here, :].astype(F32)
                        self.slot_ref[parity, here, :] = value.astype(BF16)
                    return 0

                lax.fori_loop(0, geo.slot // 16 // geo.chunk, rows_body, 0)

            if self.shared:
                last = index == region.slots - 1

                @pl.when(last)
                def _():
                    for number in range(4):
                        pltpu.make_async_copy(
                            self.outs[0].at[0],
                            self.old_ref.at[pl.ds(0, geo.quarter)],
                            self.old_sem.at[number],
                        ).wait()
                    convert(True)

                pl.when(jnp.logical_not(last))(lambda: convert(False))
            else:
                convert(False)

            def action(place, rows, number):
                pltpu.make_async_copy(
                    self.slot_ref.at[parity, rows], place, self.sems.at[parity, number]
                ).start()

            self.copies(region.low + index, action)
            return 0

        lax.fori_loop(start, stop, slot_body, 0)

    def finish(self):
        for index in range(max(0, self.region.slots - BUFFERS), self.region.slots):
            self.wait(index % BUFFERS)


def emit_scratch(geo, region):
    return [
        region.scratch(),
        pltpu.VMEM((BUFFERS, geo.slot, LANES), BF16),
        pltpu.VMEM((geo.slot, LANES), BF16),
        pltpu.SemaphoreType.DMA((BUFFERS, 4)),
        pltpu.SemaphoreType.DMA((4,)),
    ]


def store_columns(region, flat_ref, row0, first_col, values):
    height = values.shape[0]
    for c in range(values.shape[1] // LANES):
        at = region.address(region.mat_row + first_col + c) + row0 * region.stride
        flat_ref[pl.ds(at, height, stride=region.stride), :] = values[
            :, c * LANES : (c + 1) * LANES
        ]


def with_slots(geo, region, slots, operands, specs):
    shapes = []
    aliases = {}
    for position, phase in enumerate(region.reduce):
        count = 4 * geo.line * len(REDUCE_PHASES[phase])
        for number in range(2):
            shapes.append(jax.ShapeDtypeStruct((count, geo.quarter, LANES), BF16))
            if phase in slots:
                operands.append(slots[phase][number])
                specs.append(anywhere())
                aliases[len(operands) - 1] = position * 2 + number
    return shapes, aliases, len(aliases)


def updated_slots(region, slots, results):
    merged = dict(slots)
    for position, phase in enumerate(region.reduce):
        merged[phase] = results[position * 2 : position * 2 + 2]
    return merged


def pack_kernel(geo, region, shared, grid_steps, skip, me_ref, a_ref, b_ref, *refs):
    vec_refs, refs = refs[: len(region.vectors)], refs[len(region.vectors) + skip :]
    arrays = 2 * len(region.reduce)
    *scratch, left_ref = refs[arrays:]
    emitter = Emitter(geo, region, shared, me_ref, refs[:arrays], *scratch)
    flat_ref = emitter.flat_ref
    step = pl.program_id(0)

    @pl.when(step == 0)
    def _():
        emitter.begin()
        for (row, count), vec_ref in zip(region.vectors, vec_refs):

            def move(at, done, size, vec_ref=vec_ref):
                flat_ref[at : at + size, :] = vec_ref[done : done + size, :]

            copy_rows(region, flat_ref, row, count, move)

        for r in range(0, region.depth, 256):
            left_ref[r : r + 256, :] = a_ref[:, r : r + 256].T

    width = b_ref.shape[1]
    store_columns(
        region, flat_ref, 0, step * (width // LANES), nn(left_ref[...], b_ref[...])
    )

    @pl.when(step == grid_steps - 1)
    def _():
        emitter.emit(0, region.slots)
        emitter.finish()


def emit_rows(emitter, step, grid_steps, height):
    region = emitter.region
    span = height * region.cols
    before = emitter.slots_before(region.mat_row + step * span)
    after = emitter.slots_before(region.mat_row + (step + 1) * span)
    last = step == grid_steps - 1
    emitter.emit(jnp.where(step == 0, 0, before), jnp.where(last, region.slots, after))
    pl.when(last)(emitter.finish)


def pack(geo, region, me, left, right, vectors, slots, shared):
    tokens = left.shape[0]
    width = 512
    steps = region.cols * LANES // width
    operands = [me, left, right] + vectors
    specs = [
        smem(),
        pl.BlockSpec((tokens, region.depth), lambda k: (0, 0), pipeline_mode=pl.Buffered(1)),
        pl.BlockSpec((tokens, width), lambda k: (0, k)),
    ] + [pl.BlockSpec(vector.shape, lambda k: (0, 0)) for vector in vectors]
    shapes, aliases, skip = with_slots(geo, region, slots, operands, specs)
    results = pl.pallas_call(
        partial(pack_kernel, geo, region, shared, steps, skip),
        grid=(steps,),
        out_shape=shapes,
        in_specs=specs,
        out_specs=[anywhere()] * len(shapes),
        scratch_shapes=emit_scratch(geo, region) + [pltpu.VMEM((region.depth, tokens), BF16)],
        input_output_aliases=aliases,
        compiler_params=params_of(),
        cost_estimate=cost(
            2 * tokens * region.depth * width * steps, 2 * region.depth * width * steps
        ),
        name="weight_grad_pack",
    )(*operands)
    return updated_slots(region, slots, results)


def line_masks(geo):
    if geo.line == 4:
        return [[2, 4, 6]]
    return [[2 << bit] for bit in range(geo.line.bit_length() - 1)]


def after(value, *others):
    return lax.optimization_barrier((value,) + others)[0]


def spread_quarters(geo, share, dp_index):
    pieces = [lax.dynamic_index_in_dim(share, dp_index, 0, keepdims=False)]
    for offset in (1, 2, 3):
        piece = lax.dynamic_index_in_dim(share, dp_index ^ offset, 0, keepdims=False)
        mask = offset * geo.fsdp
        pieces.append(geo.permute(piece, mask, mask))
    return pieces


def light():
    return pl.CostEstimate(flops=1024, bytes_accessed=1024, transcendentals=0)


def join_kernel(*refs):
    out_ref = refs[-1]
    start = 0
    for ref in refs[:-1]:
        out_ref[start : start + ref.shape[0]] = ref[...]
        start += ref.shape[0]


def join(parts):
    count = sum(part.shape[0] for part in parts)
    return pl.pallas_call(
        join_kernel,
        out_shape=jax.ShapeDtypeStruct((count,) + parts[0].shape[1:], parts[0].dtype),
        in_specs=[vmem()] * len(parts),
        out_specs=vmem(),
        compiler_params=params_of(),
        cost_estimate=light(),
        name="join",
    )(*parts)


class Gather:
    def __init__(self, geo, pieces):
        self.geo, self.held = geo, pieces

    def line(self, *deps):
        held = after(self.held, *deps)
        stages = line_masks(self.geo)
        for masks in stages[:-1]:
            moved = [self.geo.permute(held, mask, mask) for mask in masks]
            held = jnp.concatenate([held] + moved, axis=0)
        self.held = held
        self.moved = [self.geo.permute(held, mask, mask) for mask in stages[-1]]

    def joined(self, *deps):
        self.held = join([self.held] + [after(part, *deps) for part in self.moved])
        return self.held

    def across(self, *deps):
        self.moved = self.geo.permute(
            after(self.held, *deps), self.geo.bit_x, self.geo.bit_y
        )

    def last(self, *deps):
        self.near = join([self.held, after(self.moved, *deps)])
        self.moved = self.geo.permute(self.near, self.geo.bit_y, self.geo.bit_x)
        self.near_other = self.geo.core_swap(self.near)
        return self.near

    def finish(self, *deps):
        far = after(self.moved, *deps)
        return [self.near, far, after(self.near_other, *deps), self.geo.core_swap(far)]


def add_far_kernel(keep_ref, got_ref, out_ref):
    out_ref[...] = (keep_ref[...].astype(F32) + got_ref[...].astype(F32)).astype(BF16)


def add_near_kernel(keep_ref, got_ref, far_ref, kept_ref, moved_ref):
    total = keep_ref[...].astype(F32) + got_ref[...].astype(F32) + far_ref[...].astype(F32)
    half = kept_ref.shape[0]
    kept_ref[...] = total[:half]
    moved_ref[...] = total[half:].astype(BF16)


def add_line_kernel(near_ref, across_ref, own_ref, *moved_refs):
    own = own_ref.shape[0]
    own_ref[...] = near_ref[:own] + across_ref[:own].astype(F32)
    for number, ref in enumerate(moved_refs):
        rows = slice((number + 1) * own, (number + 2) * own)
        ref[...] = (near_ref[rows] + across_ref[rows].astype(F32)).astype(BF16)


def add_total_kernel(own_ref, *refs):
    total = own_ref[...]
    for ref in refs[:-1]:
        total = total + ref[...].astype(F32)
    refs[-1][...] = total


class Reduction:
    def __init__(self, geo, slots, phase):
        self.geo = geo
        self.count = geo.line * len(REDUCE_PHASES[phase])
        self.keep, send = slots
        self.got = geo.core_swap(send)
        self.block = (1, geo.quarter, LANES)

    def call(self, kernel, out_shape, **more):
        return pl.pallas_call(
            kernel,
            out_shape=out_shape,
            compiler_params=params_of(),
            cost_estimate=light(),
            name="add_terms",
            **more,
        )

    def shape(self, count, dtype):
        return jax.ShapeDtypeStruct((count,) + self.block[1:], dtype)

    def last(self, *deps):
        count = 2 * self.count
        got = after(self.got, *deps)
        later = pl.BlockSpec((count,) + self.block[1:], lambda i: (1, 0, 0))
        far = self.call(
            add_far_kernel,
            self.shape(count, BF16),
            grid=(1,),
            in_specs=[later, later],
            out_specs=vmem(),
        )(self.keep, got)
        self.from_far = self.geo.permute(far, self.geo.bit_y, self.geo.bit_x)
        self.got = got
        return far

    def across(self, *deps):
        count = self.count
        part = pl.BlockSpec((2 * count,) + self.block[1:], lambda i: (0, 0, 0))
        self.near, moved = self.call(
            add_near_kernel,
            [self.shape(count, F32), self.shape(count, BF16)],
            grid=(1,),
            in_specs=[part, part, part],
            out_specs=[vmem(), vmem()],
        )(self.keep, self.got, after(self.from_far, *deps))
        self.from_across = self.geo.permute(moved, self.geo.bit_x, self.geo.bit_y)
        return moved

    def line(self, *deps):
        near, received = self.near, after(self.from_across, *deps)
        stages = line_masks(self.geo)[::-1]
        for masks in stages:
            own = near.shape[0] // (len(masks) + 1)
            near, *parts = self.call(
                add_line_kernel,
                [self.shape(own, F32)] + [self.shape(own, BF16)] * len(masks),
                in_specs=[vmem(), vmem()],
                out_specs=[vmem()] * (len(masks) + 1),
            )(near, received)
            moved = [self.geo.permute(part, mask, mask) for part, mask in zip(parts, masks)]
            if masks is not stages[-1]:
                (received,) = moved
        self.near, self.parts = near, moved
        return near

    def total(self, *deps):
        parts = [after(part, *deps) for part in self.parts]
        return self.call(
            add_total_kernel,
            self.shape(self.near.shape[0], F32),
            in_specs=[vmem()] * (1 + len(parts)),
            out_specs=vmem(),
        )(self.near, *parts)


def collect_quarters(geo, sums, dp_index):
    def of_group(group):
        low = jnp.where(group == 0, sums[0], sums[1])
        return jnp.where(group < 2, low, jnp.where(group == 2, sums[2], sums[3]))

    pieces = [of_group(dp_index)]
    for offset in (1, 2, 3):
        mask = offset * geo.fsdp
        pieces.append(geo.permute(of_group(dp_index ^ offset).astype(BF16), mask, mask))
    return pieces


def sum_everywhere(geo, value, start=0, stop=None):
    bits = geo.devices.bit_length() - 1
    for bit in range(start, bits if stop is None else stop):
        value = value + geo.permute(value, 1 << bit, 1 << bit)
    return value


def tensor_sums(sums_ref, squares, flat, low, high, tensors):
    for t in tensors:

        @pl.when((low < STARTS[t + 1]) & (high > STARTS[t]))
        def _(t=t):
            inside = (flat >= STARTS[t]) & (flat < STARTS[t + 1])
            part = jnp.where(inside, squares, 0.0)
            sums_ref[t : t + 1, :] += jnp.sum(part, axis=0, keepdims=True)


def squares_kernel(geo, groups, me_ref, *refs):
    sums_ref = refs[-1]
    sums_ref[...] = jnp.zeros((16, LANES), F32)
    span = 8 * max(t for t in range(1, 13) if geo.quarter // 8 % t == 0)
    dp_index = me_ref[1] * 2 + me_ref[2]
    places = [(number, at, g) for number, part in enumerate(groups) for at, g in enumerate(part)]
    for number, at, group in places:
        device = group * geo.fsdp + me_ref[3] * 2 + me_ref[4]
        share = geo.rows * LANES
        base = device * geo.rows
        first = base - lax.rem(base, 16) + dp_index * geo.quarter

        def body(i, _, number=number, at=at, base=base, first=first):
            r0 = pl.multiple_of(i * span, 8)
            value = refs[number][at, pl.ds(r0, span), :]
            lane = lax.broadcasted_iota(jnp.int32, (span, LANES), 1)
            row = lax.broadcasted_iota(jnp.int32, (span, LANES), 0)
            lifted = (first + r0 + row) * LANES + lane
            flat = jnp.where(lifted < SPLIT, lifted, lifted - LIFT)
            owned = (flat >= base * LANES) & (flat < base * LANES + share)
            low = (first + r0) * LANES - LIFT
            high = (first + r0 + span) * LANES
            squares = jnp.where(owned, value * value, 0.0)
            tensor_sums(sums_ref, squares, flat, low, high, (2,) + tuple(range(5, 13)))
            return 0

        lax.fori_loop(0, geo.quarter // span, body, 0)


def square_sums(geo, me, groups, sums):
    return pl.pallas_call(
        partial(squares_kernel, geo, groups),
        out_shape=jax.ShapeDtypeStruct((16, LANES), F32),
        in_specs=[smem()] + [vmem()] * len(sums),
        out_specs=vmem(),
        compiler_params=params_of(),
        cost_estimate=light(),
        name="square_sums",
    )(me, *sums)


def update_kernel(geo, me_ref, coef_ref, *refs):
    quarters, (late_ref, p_ref, m_ref, v_ref), outs = refs[:4], refs[4:8], refs[8:]
    params_out, first_out, second_out, grad_ref = outs
    rows, quarter = geo.rows, geo.quarter
    base = me_ref[0] * rows
    shift = lax.rem(base, 16)
    dp_index = me_ref[1] * 2 + me_ref[2]
    margin = 128
    step = pl.program_id(0)

    @pl.when(step == 0)
    def _():
        for offset in range(4):
            to = pl.multiple_of(margin + (dp_index ^ offset) * quarter, 8)
            grad_ref[pl.ds(to, quarter), :] = quarters[offset][...].astype(F32)
        for row, count, at in ((0, HEAD_ROWS, 0), (TAIL_ROW, LATE_TAIL, HEAD_ROWS)):

            @pl.when((base < row + count) & (base + rows > row))
            def _(row=row, count=count, at=at):
                lane = lax.broadcasted_iota(jnp.int32, (count, LANES), 1)
                p_rows = lax.broadcasted_iota(jnp.int32, (count, LANES), 0) + row
                before = p_rows * LANES + lane < SPLIT
                to = jnp.clip(margin + shift + row - base, 0, margin + geo.slot)
                here = pl.ds(to, count)
                late = late_ref[at : at + count, :]
                grad_ref[here, :] = jnp.where(before, late, grad_ref[here, :])

    span = 64
    count = p_ref.shape[0]
    scale, first_fix, second_fix, rate = (coef_ref[i] for i in range(4))

    def body(i, _):
        r0 = pl.multiple_of(i * span, span)
        ahead = step * count + r0
        here = grad_ref[pl.ds(margin + shift + ahead, span), :]
        below = grad_ref[pl.ds(margin + shift + ahead + 1, span), :]
        lane = lax.broadcasted_iota(jnp.int32, (span, LANES), 1)
        row = lax.broadcasted_iota(jnp.int32, (span, LANES), 0)
        flat = (base + ahead + row) * LANES + lane
        back = LANES - LIFT
        moved = jnp.where(lane < back, pltpu.roll(here, back, 1), pltpu.roll(below, back, 1))
        scaled = jnp.where(flat < SPLIT, here, moved) * scale
        at = pl.ds(r0, span)
        first_new = 0.9 * m_ref[at, :] + 0.1 * scaled
        second_new = 0.999 * v_ref[at, :] + 0.001 * scaled * scaled
        params = p_ref[at, :]
        update = first_new / first_fix / (jnp.sqrt(second_new / second_fix) + 1e-08) + 0.05 * params
        params_out[at, :] = params - rate * update
        first_out[at, :] = first_new
        second_out[at, :] = second_new
        return 0

    lax.fori_loop(0, count // span, body, 0)


def update_step(geo, me, coef, quarters, late, params, first, second):
    rows = jax.ShapeDtypeStruct((geo.rows, LANES), F32)
    block = round_up(-(-geo.rows // 4), 64)
    part = pl.BlockSpec((block, LANES), lambda i: (i, 0))
    return pl.pallas_call(
        partial(update_kernel, geo),
        grid=(-(-geo.rows // block),),
        out_shape=[rows, rows, rows],
        in_specs=[smem(), smem()] + [vmem()] * 5 + [part] * 3,
        out_specs=[part] * 3,
        scratch_shapes=[pltpu.VMEM((geo.slot + 704, LANES), F32)],
        compiler_params=params_of(),
        name="moments_update",
    )(me, coef, *quarters, late, params, first, second)


def row_blocks(tokens):
    return tokens // 4 if tokens % 64 == 0 else tokens


def permute_in_kernel(rows_ref, values_ref, *refs):
    arrivals = values_ref.shape[0]
    lane = lax.broadcasted_iota(jnp.int32, (WP, arrivals), 1)
    pick = jnp.where(rows_ref[...] == lane, 1.0, 0.0).astype(BF16)
    refs[-1][...] = nn(pick, values_ref[...]).astype(BF16)


def permute_in(row_ids, values, start, stop, before=None):
    tokens = row_ids.shape[0]
    operands = [row_ids, values]
    specs = [
        pl.BlockSpec((WP, 1), lambda i: (i + start, 0)),
        pl.BlockSpec(values.shape, lambda i: (0, 0)),
    ]
    if before is not None:
        operands.append(before)
        specs.append(anywhere())
    return pl.pallas_call(
        permute_in_kernel,
        grid=(stop - start,),
        out_shape=jax.ShapeDtypeStruct((tokens, D), BF16),
        in_specs=specs,
        out_specs=pl.BlockSpec((WP, D), lambda i: (i + start, 0)),
        input_output_aliases={} if before is None else {2: 0},
        compiler_params=params_of(),
        cost_estimate=cost(tokens * tokens * D, 2 * tokens * D),
        name="window_order",
    )(*operands)


def permute_out_kernel(rows_ref, x_ref, out_ref):
    count = out_ref.shape[0]
    arrival = lax.broadcasted_iota(jnp.int32, (count, rows_ref.shape[1]), 0)
    pick = jnp.where(rows_ref[...] == arrival + pl.program_id(0) * count, 1.0, 0.0).astype(BF16)
    out_ref[...] = nn(pick, x_ref[...]).astype(BF16)


def permute_out(row_ids, values, arrivals):
    tokens = values.shape[0]
    block = 160 if arrivals % 160 == 0 else arrivals
    return pl.pallas_call(
        permute_out_kernel,
        grid=(arrivals // block,),
        out_shape=jax.ShapeDtypeStruct((arrivals, D), BF16),
        in_specs=[
            pl.BlockSpec((1, tokens), lambda i: (0, 0)),
            pl.BlockSpec((tokens, D), lambda i: (0, 0)),
        ],
        out_specs=pl.BlockSpec((block, D), lambda i: (i, 0)),
        compiler_params=params_of(),
        cost_estimate=cost(2 * tokens * arrivals * D, 4 * tokens * D),
        name="arrival_order",
    )(row_ids, values)


def normalized(x):
    center = x - jnp.mean(x, axis=-1, keepdims=True)
    spread = jnp.mean(center * center, axis=-1, keepdims=True)
    inverse = lax.rsqrt(spread + 1e-05)
    return center * inverse, inverse


def normalized_back(e, xhat, inverse):
    mean = jnp.mean(e, axis=-1, keepdims=True)
    along = jnp.mean(e * xhat, axis=-1, keepdims=True)
    return (e - mean - xhat * along) * inverse


def mix_kernel(x_ref, gain_ref, shift_ref, w_ref, b_ref, normed_ref, mixed_ref):
    step = pl.program_id(0)
    tokens = x_ref.shape[0]

    @pl.when(step == 0)
    def _():
        def body(i, _):
            rows = pl.ds(pl.multiple_of(i * 16, 16), 16)
            xhat, _ = normalized(x_ref[rows, :].astype(F32))
            normed_ref[rows, :] = (xhat * gain_ref[...] + shift_ref[...]).astype(BF16)
            return 0

        lax.fori_loop(0, tokens // 16, body, 0, unroll=4)

    mixed = nn(normed_ref[...], w_ref[...]) + b_ref[...]
    scale = jnp.where(step < D // w_ref.shape[1], F32(HEAD_DIM ** (-0.5)), F32(1.0))
    mixed_ref[...] = (mixed * scale).astype(BF16)


def mix(x, gain, shift, weight, bias):
    tokens = x.shape[0]
    width = 512
    rows = pl.BlockSpec((tokens, D), lambda j: (0, 0))
    vec = pl.BlockSpec((1, D), lambda j: (0, 0))
    return pl.pallas_call(
        mix_kernel,
        grid=(3 * D // width,),
        out_shape=[
            jax.ShapeDtypeStruct((tokens, D), BF16),
            jax.ShapeDtypeStruct((tokens, 3 * D), BF16),
        ],
        in_specs=[
            rows,
            vec,
            vec,
            pl.BlockSpec((D, width), lambda j: (0, j)),
            pl.BlockSpec((1, width), lambda j: (0, j)),
        ],
        out_specs=[rows, pl.BlockSpec((tokens, width), lambda j: (0, j))],
        compiler_params=params_of(),
        cost_estimate=cost(6 * tokens * D * D, 6 * D * D + 8 * tokens * D),
        name="mix_rows",
    )(x, gain, shift, weight, bias)


def bias_kernel(ids_ref, table_ref, out_ref):
    entries = table_ref.shape[1]

    def body(j, _):
        entry = lax.broadcasted_iota(jnp.int32, (entries, LANES), 0)
        pick = jnp.where(ids_ref[pl.ds(j, 1), :] == entry, 1.0, 0.0).astype(BF16)
        out_ref[:, pl.ds(j, 1), :] = nn(table_ref[...], pick).reshape(HEADS, 1, LANES)
        return 0

    lax.fori_loop(0, WT, body, 0, unroll=4)
    for j in range(WT, WP):
        out_ref[:, j : j + 1, :] = jnp.full((HEADS, 1, LANES), -1e30, F32)


def score_bias(ids, table):
    return pl.pallas_call(
        bias_kernel,
        out_shape=jax.ShapeDtypeStruct((HEADS, WP, LANES), F32),
        in_specs=[vmem(), vmem()],
        out_specs=vmem(),
        compiler_params=params_of(),
        cost_estimate=cost(2 * HEADS * WP * LANES * 384, 4 * HEADS * WP * LANES),
        name="score_bias",
    )(ids, table)


def bias_back_kernel(ids_ref, sums_ref, out_ref):
    entries = out_ref.shape[0]
    out_ref[...] = jnp.zeros(out_ref.shape, F32)
    lane = lax.broadcasted_iota(jnp.int32, (HEADS, LANES), 1)
    entry = lax.broadcasted_iota(jnp.int32, (entries, LANES), 0)
    together = 4

    def body(i, _):
        rows, picks = [], []
        for number in range(together):
            j = i * together + number
            row = sums_ref[:, pl.ds(j, 1), :].reshape(HEADS, LANES)
            rows.append(jnp.where(lane < WT, row, 0.0))
            picks.append(jnp.where(ids_ref[pl.ds(j, 1), :] == entry, 1.0, 0.0).astype(BF16))
        row = jnp.concatenate(rows, axis=1)
        high = row.astype(BF16)
        rest = row - high.astype(F32)
        middle = rest.astype(BF16)
        low = (rest - middle.astype(F32)).astype(BF16)
        parts = jnp.concatenate([high, middle, low], axis=0)
        out_ref[...] += nt(jnp.concatenate(picks, axis=1), parts)
        return 0

    lax.fori_loop(0, WT // together, body, 0)


def score_bias_back(ids, sums, entries):
    parts = pl.pallas_call(
        bias_back_kernel,
        out_shape=jax.ShapeDtypeStruct((entries, 3 * HEADS), F32),
        in_specs=[vmem(), vmem()],
        out_specs=vmem(),
        compiler_params=params_of(),
        cost_estimate=cost(6 * HEADS * WP * LANES * 384, 4 * HEADS * WP * LANES),
        name="score_bias_back",
    )(ids, sums)
    return parts[:, :HEADS] + parts[:, HEADS : 2 * HEADS] + parts[:, 2 * HEADS :]


def pad_rows(x, rows):
    return jnp.concatenate([x, jnp.zeros((rows - x.shape[0], x.shape[1]), x.dtype)], axis=0)


def one_head(x, head):
    lane = lax.broadcasted_iota(jnp.int32, x.shape, 1)
    return jnp.where(lane // HEAD_DIM == head, x, jnp.zeros_like(x))


def by_head(x):
    return jnp.concatenate([one_head(x, head) for head in range(QUAD)], axis=0)


def attention_kernel(q_ref, k_ref, v_ref, bias_ref, out_ref, log_ref):
    def block(b, _):
        lanes = pl.ds(pl.multiple_of(b * LANES, LANES), LANES)
        queries = pad_rows(q_ref[:, lanes], LANES)
        scores = nt(by_head(k_ref[:, lanes]), queries)
        values = v_ref[:, lanes].astype(F32).T.astype(BF16)
        parts = []
        for head in range(QUAD):
            s = scores[head * WP : (head + 1) * WP] + bias_ref[b * QUAD + head]
            top = jnp.max(s, axis=0, keepdims=True)
            e = jnp.exp(s - top)
            total = jnp.sum(e, axis=0, keepdims=True)
            probs = (e * (1.0 / total)).astype(BF16)
            log_ref[0, pl.ds(b * QUAD + head, 1), :] = top + jnp.log(total)
            parts.append(nn(values[head * HEAD_DIM : (head + 1) * HEAD_DIM], probs))
        context = jnp.concatenate(parts, axis=0).T
        out_ref[:, lanes] = context[:WP].astype(BF16)
        return 0

    lax.fori_loop(0, HEADS // QUAD, block, 0, unroll=8)


def attention(mixed, bias):
    windows = mixed.shape[0] // WP

    def third(c):
        return pl.BlockSpec((WP, D), lambda i, c=c: (i, c))

    return pl.pallas_call(
        attention_kernel,
        grid=(windows,),
        out_shape=[
            jax.ShapeDtypeStruct((windows * WP, D), BF16),
            jax.ShapeDtypeStruct((windows, HEADS, LANES), F32),
        ],
        in_specs=[third(0), third(1), third(2), pl.BlockSpec(bias.shape, lambda i: (0, 0, 0))],
        out_specs=[third(0), pl.BlockSpec((1, HEADS, LANES), lambda i: (i, 0, 0))],
        compiler_params=params_of(),
        cost_estimate=cost(12e9, 8 * windows * WP * D, windows * HEADS * WP * LANES),
        name="attention",
    )(mixed, mixed, mixed, bias)


def attention_back_kernel(
    more, q_ref, k_ref, v_ref, g_ref, bias_ref, log_ref, *refs
):
    out_ref, acc_ref, column_ref = refs[-3:]

    @pl.when(pl.program_id(0) == 0)
    def _():
        if more:
            acc_ref[...] = refs[0][...]
            column_ref[...] = refs[1][...]
        else:
            acc_ref[...] = jnp.zeros(acc_ref.shape, F32)
            column_ref[...] = jnp.zeros(column_ref.shape, F32)

    def put(third, b, value):
        lanes = pl.ds(pl.multiple_of(third * D + b * LANES, LANES), LANES)
        low = value.astype(BF16)
        out_ref[:, lanes] = low
        column_ref[0:1, lanes] += jnp.sum(low.astype(F32), axis=0, keepdims=True)

    def block(b, _):
        lanes = pl.ds(pl.multiple_of(b * LANES, LANES), LANES)
        queries = pad_rows(q_ref[:, lanes], LANES)
        grads = pad_rows(g_ref[:, lanes], LANES)
        keys = k_ref[:, lanes]
        scores = nt(by_head(keys), queries)
        probs_grads = nt(by_head(v_ref[:, lanes]), grads)
        keys_t = keys.astype(F32).T.astype(BF16)
        query_parts, probs_parts, score_parts = [], [], []
        for head in range(QUAD):
            span = slice(head * WP, (head + 1) * WP)
            s = scores[span] + bias_ref[b * QUAD + head]
            probs = jnp.exp(s - log_ref[0, pl.ds(b * QUAD + head, 1), :])
            probs_grad = probs_grads[span]
            along = jnp.sum(probs * probs_grad, axis=0, keepdims=True)
            score_grad = (probs * (probs_grad - along)).astype(BF16)
            acc_ref[b * QUAD + head] += score_grad.astype(F32)
            probs_parts.append(probs.astype(BF16))
            score_parts.append(score_grad)
            query_parts.append(nn(keys_t[head * HEAD_DIM : (head + 1) * HEAD_DIM], score_grad))
        put(2, b, nn(jnp.concatenate(probs_parts, axis=1), by_head(grads)))
        put(1, b, nn(jnp.concatenate(score_parts, axis=1), by_head(queries)))
        put(0, b, jnp.concatenate(query_parts, axis=0).T[:WP] * HEAD_DIM ** (-0.5))
        return 0

    lax.fori_loop(0, HEADS // QUAD, block, 0, unroll=4)


def attention_back(mixed, grads, bias, logs, start, stop, before=None):
    rows = mixed.shape[0]

    def third(c):
        return pl.BlockSpec((WP, D), lambda i, c=c: (i + start, c))

    fixed = pl.BlockSpec(bias.shape, lambda i: (0, 0, 0))
    columns = pl.BlockSpec((8, 3 * D), lambda i: (0, 0))
    operands = [mixed, mixed, mixed, grads, bias, logs]
    specs = [
        third(0),
        third(1),
        third(2),
        third(0),
        fixed,
        pl.BlockSpec((1, HEADS, LANES), lambda i: (i + start, 0, 0)),
    ]
    aliases = {}
    if before is not None:
        operands += [before[1], before[2], before[0]]
        specs += [fixed, columns, anywhere()]
        aliases = {8: 0}
    return pl.pallas_call(
        partial(attention_back_kernel, before is not None),
        grid=(stop - start,),
        out_shape=[
            jax.ShapeDtypeStruct((rows, 3 * D), BF16),
            jax.ShapeDtypeStruct(bias.shape, F32),
            jax.ShapeDtypeStruct((8, 3 * D), F32),
        ],
        in_specs=specs,
        out_specs=[pl.BlockSpec((WP, 3 * D), lambda i: (i + start, 0)), fixed, columns],
        input_output_aliases=aliases,
        compiler_params=params_of(),
        cost_estimate=cost(
            3e9 * (stop - start), 16 * (stop - start) * WP * D, HEADS * WP * LANES
        ),
        name="attention_back",
    )(*operands)


def middle_kernel(x_ref, a_ref, w_ref, b_ref, gain_ref, shift_ref, middle_ref, second_ref):
    middle = x_ref[...].astype(F32) + nn(a_ref[...], w_ref[...]) + b_ref[...]
    middle_ref[...] = middle
    xhat, _ = normalized(middle)
    second_ref[...] = (xhat * gain_ref[...] + shift_ref[...]).astype(BF16)


def middle_rows(x, attended, weight, bias, gain, shift):
    tokens = x.shape[0]
    block = row_blocks(tokens)
    rows = pl.BlockSpec((block, D), lambda i: (i, 0))
    vec = pl.BlockSpec((1, D), lambda i: (0, 0))
    return pl.pallas_call(
        middle_kernel,
        grid=(tokens // block,),
        out_shape=[
            jax.ShapeDtypeStruct((tokens, D), F32),
            jax.ShapeDtypeStruct((tokens, D), BF16),
        ],
        in_specs=[rows, rows, pl.BlockSpec((D, D), lambda i: (0, 0)), vec, vec, vec],
        out_specs=[rows, rows],
        compiler_params=params_of(),
        cost_estimate=cost(2 * tokens * D * D, 10 * tokens * D),
        name="middle_rows",
    )(x, attended, weight, bias, gain, shift)


def mlp_up_kernel(geo, region, shared, steps, skip, me_ref, s_ref, g_ref, w_ref, b_ref, *refs):
    vec_ref, refs = refs[0], refs[1 + skip :]
    hidden_ref, slope_ref, refs = refs[0], refs[1], refs[2:]
    arrays = 2 * len(region.reduce)
    *scratch, held_ref = refs[arrays:]
    emitter = Emitter(geo, region, shared, me_ref, refs[:arrays], *scratch)
    flat_ref = emitter.flat_ref
    step = pl.program_id(0)
    height = w_ref.shape[1]

    @pl.when(step == 0)
    def _():
        emitter.begin()
        ((row, count),) = region.vectors

        def move(at, done, size):
            flat_ref[at : at + size, :] = vec_ref[done : done + size, :]

        copy_rows(region, flat_ref, row, count, move)

    block = jnp.maximum(step - 1, 0)
    left = held_ref[lax.rem(step + 1, 2)].T
    u = nn(s_ref[...], w_ref[...]) + b_ref[...]
    below = 0.5 * (1.0 + lax.erf(u * F32(math.sqrt(0.5))))
    density = jnp.exp(-0.5 * u * u) * F32(1.0 / math.sqrt(2.0 * math.pi))
    hidden = (u * below).astype(BF16)
    for j in range(0, D, 512):
        store_columns(
            region, flat_ref, block * height, j // LANES, nn(left, g_ref[:, j : j + 512])
        )
    hidden_ref[...] = hidden
    slope_ref[...] = below + u * density
    held_ref[lax.rem(step, 2)] = hidden
    pl.when(step > 0)(lambda: emit_rows(emitter, step - 1, steps, height))


def mlp_up(geo, region, me, second, grad_out, weight, bias, vector, slots, shared):
    tokens = second.shape[0]
    height = 512
    steps = FF // height
    last = steps - 1
    rows = pl.BlockSpec((tokens, D), lambda k: (0, 0), pipeline_mode=pl.Buffered(1))
    columns = pl.BlockSpec((tokens, height), lambda k: (0, jnp.minimum(k, last)))
    operands = [me, second, grad_out, weight, bias, vector]
    specs = [
        smem(),
        rows,
        rows,
        pl.BlockSpec((D, height), lambda k: (0, jnp.minimum(k, last))),
        pl.BlockSpec((1, height), lambda k: (0, jnp.minimum(k, last))),
        pl.BlockSpec(vector.shape, lambda k: (0, 0)),
    ]
    shapes, aliases, skip = with_slots(geo, region, slots, operands, specs)
    results = pl.pallas_call(
        partial(mlp_up_kernel, geo, region, shared, steps, skip),
        grid=(steps + 1,),
        out_shape=[
            jax.ShapeDtypeStruct((tokens, FF), BF16),
            jax.ShapeDtypeStruct((tokens, FF), F32),
        ]
        + shapes,
        in_specs=specs,
        out_specs=[columns, columns] + [anywhere()] * len(shapes),
        scratch_shapes=emit_scratch(geo, region) + [pltpu.VMEM((2, tokens, height), BF16)],
        input_output_aliases={key: value + 2 for key, value in aliases.items()},
        compiler_params=params_of(),
        cost_estimate=cost(4 * tokens * D * FF, 4 * D * FF + 6 * tokens * FF),
        name="mlp_up",
    )(*operands)
    return results[0], results[1], updated_slots(region, slots, results[2:])


def mlp_down_kernel(geo, region, shared, steps, skip, me_ref, *refs):
    (h_ref, slope_ref, s_ref, g_ref, up_ref, down_ref, m_ref, b_ref) = refs[:8]
    refs = refs[8 + skip :]
    result_ref, grad_ref, refs = refs[0], refs[1], refs[2:]
    arrays = 2 * len(region.reduce)
    *scratch, left_ref, sum_ref = refs[arrays:]
    emitter = Emitter(geo, region, shared, me_ref, refs[:arrays], *scratch)
    flat_ref = emitter.flat_ref
    step = pl.program_id(0)
    width = h_ref.shape[1]

    @pl.when(step == 0)
    def _():
        emitter.begin()
        left_ref[...] = s_ref[...].T
        sum_ref[...] = jnp.zeros(sum_ref.shape, F32)
        grad_ref[...] = jnp.zeros(grad_ref.shape, F32)

    pre = (nt(g_ref[...], down_ref[...]) * slope_ref[...]).astype(BF16)
    column = jnp.sum(pre.astype(F32), axis=0, keepdims=True)
    sum_ref[...] += nn(h_ref[...], down_ref[...])
    grad_ref[...] += nt(pre, up_ref[...])
    cols = width // LANES
    ((vec_row, _),) = region.vectors
    for c in range(cols):
        at = region.address(vec_row + step * cols + c)
        flat_ref[pl.ds(at, 1), :] = column[:, c * LANES : (c + 1) * LANES]
    store_columns(region, flat_ref, 0, step * cols, nn(left_ref[...], pre))

    @pl.when(step == steps - 1)
    def _():
        result_ref[...] = (sum_ref[...] + m_ref[...] + b_ref[...]).astype(BF16)
        emitter.emit(0, region.slots)
        emitter.finish()


def mlp_down(geo, region, me, hidden, slope, second, grad_out, up, down, middle, bias, slots, shared):
    tokens = second.shape[0]
    width = 512
    steps = FF // width
    rows = pl.BlockSpec((tokens, D), lambda k: (0, 0), pipeline_mode=pl.Buffered(1))
    columns = pl.BlockSpec((tokens, width), lambda k: (0, k))
    operands = [me, hidden, slope, second, grad_out, up, down, middle, bias]
    specs = [
        smem(),
        columns,
        columns,
        rows,
        rows,
        pl.BlockSpec((D, width), lambda k: (0, k)),
        pl.BlockSpec((width, D), lambda k: (k, 0)),
        rows,
        pl.BlockSpec((1, D), lambda k: (0, 0)),
    ]
    shapes, aliases, skip = with_slots(geo, region, slots, operands, specs)
    whole = pl.BlockSpec((tokens, D), lambda k: (0, 0))
    results = pl.pallas_call(
        partial(mlp_down_kernel, geo, region, shared, steps, skip),
        grid=(steps,),
        out_shape=[
            jax.ShapeDtypeStruct((tokens, D), BF16),
            jax.ShapeDtypeStruct((tokens, D), F32),
        ]
        + shapes,
        in_specs=specs,
        out_specs=[whole, whole] + [anywhere()] * len(shapes),
        scratch_shapes=emit_scratch(geo, region)
        + [
            pltpu.VMEM((D, tokens), BF16),
            pltpu.VMEM((tokens, D), F32),
        ],
        input_output_aliases={key: value + 2 for key, value in aliases.items()},
        compiler_params=params_of(),
        cost_estimate=cost(8 * tokens * D * FF, 6 * D * FF + 6 * tokens * FF),
        name="mlp_down",
    )(*operands)
    return results[0], results[1], updated_slots(region, slots, results[2:])


def middle_back_kernel(s_ref, m_ref, g_ref, gain_ref, w_ref, mg_ref, bg_ref, cg_ref, vec_ref):
    @pl.when(pl.program_id(0) == 0)
    def _():
        vec_ref[...] = jnp.zeros(vec_ref.shape, F32)

    grad = s_ref[...]
    xhat, inverse = normalized(m_ref[...])
    middle_grad = g_ref[...].astype(F32) + normalized_back(grad * gain_ref[...], xhat, inverse)
    branch = middle_grad.astype(BF16)
    mg_ref[...] = middle_grad
    bg_ref[...] = branch
    cg_ref[...] = nt(branch, w_ref[...]).astype(BF16)
    vec_ref[0:1, :] += jnp.sum(branch.astype(F32), axis=0, keepdims=True)
    vec_ref[1:2, :] += jnp.sum(grad * xhat, axis=0, keepdims=True)
    vec_ref[2:3, :] += jnp.sum(grad, axis=0, keepdims=True)


def middle_back(second_grad, middle, grad_out, gain, weight):
    tokens = middle.shape[0]
    block = row_blocks(tokens)
    rows = pl.BlockSpec((block, D), lambda i: (i, 0))
    low = jax.ShapeDtypeStruct((tokens, D), BF16)
    return pl.pallas_call(
        middle_back_kernel,
        grid=(tokens // block,),
        out_shape=[
            jax.ShapeDtypeStruct((tokens, D), F32),
            low,
            low,
            jax.ShapeDtypeStruct((8, D), F32),
        ],
        in_specs=[
            rows,
            rows,
            rows,
            pl.BlockSpec((1, D), lambda i: (0, 0)),
            pl.BlockSpec((D, D), lambda i: (0, 0)),
        ],
        out_specs=[rows, rows, rows, pl.BlockSpec((8, D), lambda i: (0, 0))],
        compiler_params=params_of(),
        cost_estimate=cost(2 * tokens * D * D, 18 * tokens * D),
        name="middle_back",
    )(second_grad, middle, grad_out, gain, weight)


def first_back_kernel(steps, mixed_ref, w_ref, x_ref, mg_ref, gain_ref, out_ref, vec_ref, sum_ref):
    step = pl.program_id(0)
    width = w_ref.shape[0]
    lanes = pl.ds(pl.multiple_of(step * width, width), width)
    sum_ref[:, lanes] = nt(mixed_ref[...], w_ref[...])

    @pl.when(step == steps - 1)
    def _():
        block = row_blocks(x_ref.shape[0])
        vec_ref[...] = jnp.zeros(vec_ref.shape, F32)

        def body(i, _):
            rows = pl.ds(pl.multiple_of(i * block, 16), block)
            grad = sum_ref[rows, :]
            xhat, inverse = normalized(x_ref[rows, :].astype(F32))
            inner = normalized_back(grad * gain_ref[...], xhat, inverse)
            out_ref[rows, :] = (mg_ref[rows, :] + inner).astype(BF16)
            vec_ref[0:1, :] += jnp.sum(grad * xhat, axis=0, keepdims=True)
            vec_ref[1:2, :] += jnp.sum(grad, axis=0, keepdims=True)
            return 0

        lax.fori_loop(0, x_ref.shape[0] // block, body, 0)


def first_back(mixed_grad, weight, x, middle_grad, gain):
    tokens = x.shape[0]
    width = 256
    steps = D // width
    rows = pl.BlockSpec((tokens, D), lambda k: (0, 0), pipeline_mode=pl.Buffered(1))
    return pl.pallas_call(
        partial(first_back_kernel, steps),
        grid=(steps,),
        out_shape=[
            jax.ShapeDtypeStruct((tokens, D), BF16),
            jax.ShapeDtypeStruct((8, D), F32),
        ],
        in_specs=[
            pl.BlockSpec((tokens, 3 * D), lambda k: (0, 0), pipeline_mode=pl.Buffered(1)),
            pl.BlockSpec((width, 3 * D), lambda k: (k, 0)),
            rows,
            rows,
            pl.BlockSpec((1, D), lambda k: (0, 0)),
        ],
        out_specs=[
            pl.BlockSpec((tokens, D), lambda k: (0, 0)),
            pl.BlockSpec((8, D), lambda k: (0, 0)),
        ],
        scratch_shapes=[pltpu.VMEM((tokens, D), F32)],
        compiler_params=params_of(),
        cost_estimate=cost(6 * tokens * D * D, 6 * D * D + 14 * tokens * D),
        name="first_back",
    )(mixed_grad, weight, x, middle_grad, gain)


def local(
    patches,
    cotangent,
    window_rows,
    rel_index,
    params,
    first_moment,
    second_moment,
    learn_rate,
    step_count,
):
    arrivals = patches.shape[0]
    windows = arrivals // WT
    geo = Geometry(lax.axis_size("dp"), lax.axis_size("fsdp"), params.shape[0])
    dp_index = lax.axis_index("dp")
    fsdp_index = lax.axis_index("fsdp")
    me = jnp.stack(
        [lax.axis_index(AXES), dp_index // 2, dp_index % 2, fsdp_index // 2, fsdp_index % 2]
    ).astype(jnp.int32)

    shard = params.reshape(geo.rows, LANES)
    if geo.spill:
        spill = lax.ppermute(
            shard[: round_up(geo.spill, 8)], AXES, [(geo.spill_from, geo.spill_to)]
        )
    else:
        spill = jnp.zeros((8, LANES), F32)
    share = prepare(geo, me, shard, spill).reshape(4, geo.quarter, LANES)
    row_ids = jnp.pad(
        window_rows.reshape(windows, WT), ((0, 0), (0, WP - WT)), constant_values=-1
    ).reshape(windows * WP)
    stacked = jnp.stack(spread_quarters(geo, share, dp_index))
    gathers = []
    for groups in GATHER_PHASES:
        pieces = [
            lax.dynamic_index_in_dim(stacked, dp_index ^ group, 0, keepdims=True)
            for group in groups
        ]
        gathers.append(Gather(geo, jnp.concatenate(pieces, axis=0)))
    gathers[0].line()
    half = windows // 2
    ids_of = row_ids[:, None]
    x = permute_in(after(ids_of, gathers[0].held), patches, 0, half)
    held = gathers[0].joined(x)
    gathers[0].across()
    gathers[1].line(held)
    x = permute_in(after(ids_of, held), patches, half, windows, x)
    near = gathers[0].last(x)
    grad_out = permute_in(after(ids_of, near), cotangent, 0, half)
    gathered = {0: gathers[0].finish(grad_out)}
    far = gathered[0][1]
    held = gathers[1].joined(far)
    gathers[1].across()
    gathers[2].line(held)
    grad_out = permute_in(after(ids_of, far), cotangent, half, windows, grad_out)
    gathered[0] = gathered[0][:3] + [after(gathered[0][3], grad_out)]

    mix_matrix = (MIX_ROW, D, 3 * D // LANES)
    out_matrix = (OUT_ROW, D, D // LANES)
    expand_matrix = (EXPAND_ROW, D, FF // LANES)
    shrink_matrix = (SHRINK_ROW, FF, D // LANES)
    out_end = p_row(STARTS[6])
    expand_end = p_row(STARTS[10])
    shrink_end = p_row(STARTS[12])
    mix_vectors = [(0, 8), (8, 8), (TAIL_ROW, TABLE_ROW - TAIL_ROW), (TABLE_ROW, SPLIT_ROW - TABLE_ROW)]
    out_vectors = [(out_end + 8 * i, 8) for i in range(3)]
    expand_vectors = [(expand_end, FF // LANES)]
    shrink_vectors = [(shrink_end, 8)]

    first = Region(
        geo, 0, OUT_ROW, mix_matrix, mix_vectors, high=geo.spill_to if geo.spill else None
    )
    mix_weight, attn_gain, attn_shift, mix_bias, table_rows = unpack(geo, first, me, gathered)
    near = gathers[1].last(mix_weight)
    held = gathers[2].joined(mix_weight)
    gathers[2].across(near)
    gathers[3].line(held)
    table_rows = after(table_rows, near, held)

    def line_of(rows):
        return rows.reshape(1, -1)

    entries = round_up(TABLE_ROWS, 16)
    table = table_rows.reshape(-1)[: TABLE_ROWS * HEADS].reshape(TABLE_ROWS, HEADS).T
    table = jnp.pad(table, ((0, 0), (0, entries - TABLE_ROWS))).astype(BF16)
    ids = jnp.pad(rel_index.T, ((0, WP - WT), (0, LANES - WT)), constant_values=-1)
    bias = score_bias(ids, table)

    normed, mixed = mix(
        after(x, bias),
        line_of(attn_gain),
        line_of(attn_shift),
        mix_weight,
        line_of(mix_bias),
    )
    gathered[1] = gathers[1].finish(mixed)
    near = gathers[2].last(mixed)
    held = gathers[3].joined(mixed)
    gathers[3].across(near)
    attended, logs = attention(after(mixed, near, held, gathered[1][1]), bias)
    out_weight, out_bias, mlp_gain, mlp_shift = unpack(
        geo, Region(geo, OUT_ROW, EXPAND_ROW, out_matrix, out_vectors), me, gathered
    )
    gathered[2] = gathers[2].finish(out_weight)
    near = gathers[3].last(out_weight)
    middle, second = middle_rows(
        x,
        after(attended, near, gathered[2][1]),
        out_weight,
        line_of(out_bias),
        line_of(mlp_gain),
        line_of(mlp_shift),
    )
    expand_weight, expand_bias = unpack(
        geo, Region(geo, EXPAND_ROW, SHRINK_ROW, expand_matrix, expand_vectors), me, gathered
    )
    gathered[3] = gathers[3].finish(expand_weight)
    second = after(second, gathered[3][1])

    shrink_region = Region(
        geo, SHRINK_ROW, END_ROW, shrink_matrix, shrink_vectors, high=geo.devices - 1
    )
    expand_region = Region(geo, EXPAND_ROW, SHRINK_ROW, expand_matrix, expand_vectors)
    out_region = Region(geo, OUT_ROW, EXPAND_ROW, out_matrix, out_vectors)
    mix_region = Region(geo, 0, TAIL_ROW, mix_matrix, [])
    slots = {}
    shrink_bias_grad = jnp.sum(grad_out.astype(F32), axis=0).reshape(-1, LANES)
    hidden, slope, slots = mlp_up(
        geo,
        shrink_region,
        me,
        second,
        grad_out,
        expand_weight,
        line_of(expand_bias),
        shrink_bias_grad,
        slots,
        False,
    )
    phase3 = Reduction(geo, slots[3], 3)
    shrink_weight, shrink_bias = unpack(
        geo, Region(geo, SHRINK_ROW, END_ROW, shrink_matrix, shrink_vectors), me, gathered
    )
    sent = phase3.last(shrink_weight)
    result, second_grad, slots = mlp_down(
        geo,
        expand_region,
        me,
        after(hidden, sent),
        slope,
        second,
        grad_out,
        expand_weight,
        shrink_weight,
        middle,
        line_of(shrink_bias),
        slots,
        expand_region.high == shrink_region.low,
    )
    phase2 = Reduction(geo, slots[2], 2)
    sent = phase3.across(second_grad)
    middle_grad, branch_grad, context_grad, middle_vec = middle_back(
        after(second_grad, sent), middle, grad_out, line_of(mlp_gain), out_weight
    )
    sent = [phase3.line(context_grad), phase2.last(context_grad)]
    slots = pack(
        geo,
        out_region,
        me,
        attended,
        after(branch_grad, *sent),
        [middle_vec[i].reshape(8, LANES) for i in range(3)],
        slots,
        out_region.high == expand_region.low,
    )
    phase1 = Reduction(geo, slots[1], 1)
    context_grad = after(context_grad, slots[1][0])
    parts = attention_back(mixed, context_grad, bias, logs, 0, half)
    sums = {3: phase3.total(parts[1])}
    sent = [phase2.across(parts[1]), phase1.last(parts[1]), sums[3]]
    mixed_grad, score_sums, column_sums = attention_back(
        mixed, after(context_grad, *sent), bias, logs, half, windows, parts
    )
    sent = [phase2.line(score_sums), phase1.across(score_sums)]
    slots = pack(
        geo,
        mix_region,
        me,
        normed,
        after(mixed_grad, *sent),
        [],
        slots,
        mix_region.high == out_region.low,
    )
    packed = slots[0][0]
    phase0 = Reduction(geo, slots[0], 0)
    activations = permute_out(row_ids[None], after(result, packed), arrivals)
    far = phase0.last(activations)
    sums[2] = phase2.total(packed, far)
    sent = [phase1.line(packed, far), sums[2]]
    input_rows, first_vec = first_back(
        after(mixed_grad, far, *sent), mix_weight, x, middle_grad, line_of(attn_gain)
    )
    sent = phase0.across(input_rows)
    table_grad = score_bias_back(ids, after(score_sums, sent), entries)[:TABLE_ROWS]

    table_pad = (SPLIT_ROW - TABLE_ROW) * LANES - TABLE_ROWS * HEADS
    late = jnp.concatenate(
        [
            first_vec[:2].reshape(HEAD_ROWS, LANES),
            column_sums[0].reshape(-1, LANES),
            jnp.pad(table_grad.reshape(-1), (0, table_pad)).reshape(-1, LANES),
        ],
        axis=0,
    )
    sent = phase0.line(table_grad)
    sums[1] = phase1.total(sent)
    late = after(jnp.pad(late, ((0, LATE_ROWS - late.shape[0]), (0, 0))), sent)
    late = sum_everywhere(geo, late)
    input_grad = permute_out(row_ids[None], after(input_rows, sent), arrivals)
    squares = square_sums(
        geo, me, REDUCE_PHASES[1:], [after(sums[1], sent), sums[2], sums[3]]
    )
    sums[0] = phase0.total(squares, input_grad)
    squares = squares + square_sums(geo, me, REDUCE_PHASES[:1], [sums[0]])
    collected = collect_quarters(geo, [sums[group][0] for group in range(4)], dp_index)
    scale = 1.0 / jnp.sqrt(F32(arrivals * geo.devices))
    squares = sum_everywhere(geo, jnp.sum(squares, axis=1)[None], 0, 3)
    collected[0] = after(collected[0], squares)
    step_float = step_count.astype(F32)
    coef = jnp.stack(
        [
            scale,
            1.0 - jnp.power(F32(0.9), step_float),
            1.0 - jnp.power(F32(0.999), step_float),
            learn_rate,
        ]
    )
    params_new, first_new, second_new = update_step(
        geo,
        me,
        coef,
        collected,
        late,
        shard,
        first_moment.reshape(geo.rows, LANES),
        second_moment.reshape(geo.rows, LANES),
    )
    squares = sum_everywhere(geo, after(squares, params_new), 3)
    tensor = lax.broadcasted_iota(jnp.int32, (LATE_ROWS, 16), 1)
    row = lax.broadcasted_iota(jnp.int32, (LATE_ROWS, 16), 0)
    inside = tensor < 0
    edges = [0, 8, HEAD_ROWS, HEAD_ROWS + TABLE_ROW - TAIL_ROW, LATE_ROWS]
    for t, start, stop in zip((0, 1, 3, 4), edges, edges[1:]):
        inside = inside | ((tensor == t) & (row >= start) & (row < stop))
    late_rows = jnp.sum(late * late, axis=1, keepdims=True)
    totals = squares[0] + jnp.sum(jnp.where(inside, late_rows, 0.0), axis=0)
    entry_counts = jnp.array([math.prod(shape) for shape in SHAPES], F32)
    group_rms = jnp.sqrt(totals[: len(SHAPES)] * (scale * scale) / entry_counts)

    return (
        activations,
        input_grad,
        group_rms,
        params_new.reshape(-1),
        first_new.reshape(-1),
        second_new.reshape(-1),
    )


def solution(mesh):
    placed = (
        P(AXES, None),
        P(AXES, None),
        P(AXES),
        P(),
        P(AXES),
        P(AXES),
        P(AXES),
        P(),
        P(),
    )
    return jax.shard_map(
        local,
        mesh=mesh,
        in_specs=placed,
        out_specs=(P(AXES, None), P(AXES, None), P(), P(AXES), P(AXES), P(AXES)),
        check_vma=False,
    )
```

```python
from functools import partial
import math

import jax
import jax.numpy as jnp
from jax import lax
from jax.experimental import pallas as pl
from jax.experimental.pallas import tpu as pltpu
from jax.sharding import PartitionSpec as P

D = 1024
HEADS = 32
HEAD_DIM = 32
FF = 4096
WT = 100
WP = 104
TABLE_ROWS = 361
RAW = 12607776
LANES = 128
QUAD = LANES // HEAD_DIM
AXES = ("dp", "fsdp")
BF16 = jnp.bfloat16
F32 = jnp.float32
VMEM_LIMIT = 62 << 20
BUFFERS = 4
FETCHES = 6

SHAPES = [
    (D,),
    (D,),
    (D, 3 * D),
    (3 * D,),
    (TABLE_ROWS, HEADS),
    (D, D),
    (D,),
    (D,),
    (D,),
    (D, FF),
    (FF,),
    (FF, D),
    (D,),
]
STARTS = [0]
for _shape in SHAPES:
    STARTS.append(STARTS[-1] + math.prod(_shape))

SPLIT = STARTS[5]
LIFT = (-SPLIT) % LANES


def p_row(position):
    lifted = position + (LIFT if position >= SPLIT else 0)
    assert lifted % LANES == 0
    return lifted // LANES


MIX_ROW, OUT_ROW, EXPAND_ROW, SHRINK_ROW = (p_row(STARTS[i]) for i in (2, 5, 9, 11))
SPLIT_ROW = p_row(SPLIT)
TAIL_ROW = p_row(STARTS[3])
TABLE_ROW = STARTS[4] // LANES
END_ROW = p_row(RAW)
HEAD_ROWS = MIX_ROW
LATE_TAIL = SPLIT_ROW - TAIL_ROW
LATE_ROWS = -(-(HEAD_ROWS + LATE_TAIL) // 8) * 8


def round_up(value, step):
    return -(-value // step) * step


def vmem():
    return pl.BlockSpec(memory_space=pltpu.VMEM)


def smem():
    return pl.BlockSpec(memory_space=pltpu.SMEM)


def anywhere():
    return pl.BlockSpec(memory_space=pl.ANY)


def params_of(**more):
    return pltpu.CompilerParams(vmem_limit_bytes=VMEM_LIMIT, **more)


COST_SCALE = 200


def cost(flops, bytes_accessed, transcendentals=0):
    return pl.CostEstimate(
        flops=int(COST_SCALE * flops),
        bytes_accessed=int(COST_SCALE * bytes_accessed),
        transcendentals=int(transcendentals),
    )


def nn(left, right):
    return jnp.dot(left, right, preferred_element_type=F32)


def nt(left, right):
    return lax.dot_general(left, right, (((1,), (1,)), ((), ())), preferred_element_type=F32)


class Geometry:
    def __init__(self, dp, fsdp, shard_len):
        assert dp == 4 and shard_len % LANES == 0 and fsdp % 2 == 0
        self.fsdp = fsdp
        self.devices = dp * fsdp
        self.line = fsdp // 2
        assert self.line & (self.line - 1) == 0
        self.rows = shard_len // LANES
        first, last = TABLE_ROW // self.rows, (SPLIT_ROW - 1) // self.rows
        assert last - first in (0, 1)
        self.spill_from, self.spill_to = last, first
        self.spill = SPLIT_ROW - self.rows * last if last != first else 0
        self.quarter = round_up(-(-(self.rows + 16 + self.spill) // 4), 8)
        self.slot = 4 * self.quarter
        assert self.slot % 16 == 0
        tiles = self.slot // 16
        self.chunk = max(t for t in range(1, 19) if tiles % t == 0)
        self.bit_x, self.bit_core, self.bit_y = 2 * fsdp, fsdp, 1

    def base(self, device):
        return (device * self.rows) // 16 * 16

    def permute(self, value, mask_core0, mask_core1):
        pairs = []
        for index in range(self.devices):
            core = (index // self.fsdp) % 2
            pairs.append((index, index ^ (mask_core1 if core else mask_core0)))
        return lax.ppermute(value, AXES, pairs)

    def core_swap(self, value):
        return self.permute(value, self.bit_core, self.bit_core)


def prepare_kernel(geo, me_ref, shard_ref, spill_ref, out_ref, pad_ref):
    rows, slot = geo.rows, geo.slot
    base = me_ref[0] * rows
    shift = lax.rem(base, 16)
    pad_ref[0:32, :] = jnp.zeros((32, LANES), F32)
    pad_ref[16 + rows : slot + 32, :] = jnp.zeros((slot + 16 - rows, LANES), F32)
    whole = rows // 64

    def place_body(i, _):
        r0 = i * 64
        pad_ref[pl.ds(16 + shift + r0, 64), :] = shard_ref[pl.ds(pl.multiple_of(r0, 64), 64), :]
        return 0

    lax.fori_loop(0, whole, place_body, 0)
    rest = rows - whole * 64
    if rest:
        pad_ref[pl.ds(16 + shift + whole * 64, rest), :] = shard_ref[whole * 64 : rows, :]
    if geo.spill:
        count = geo.spill

        @pl.when(me_ref[0] == geo.spill_to)
        def _():
            lane = lax.broadcasted_iota(jnp.int32, (count, LANES), 1)
            row = lax.broadcasted_iota(jnp.int32, (count, LANES), 0)
            flat = (rows * geo.spill_from + row) * LANES + lane
            at = 16 + rows * geo.spill_from - geo.base(geo.spill_to)
            pad_ref[at : at + count, :] = jnp.where(flat < SPLIT, spill_ref[0:count, :], 0.0)

    step = 16 * geo.chunk

    def body(i, _):
        r0 = pl.multiple_of(i * step, 16)
        here = pad_ref[pl.ds(r0 + 16, step), :]
        above = pad_ref[pl.ds(r0 + 15, step), :]
        lane = lax.broadcasted_iota(jnp.int32, (step, LANES), 1)
        row = lax.broadcasted_iota(jnp.int32, (step, LANES), 0)
        flat = (base - shift + r0 + row) * LANES + lane
        moved = jnp.where(lane >= LIFT, pltpu.roll(here, LIFT, 1), pltpu.roll(above, LIFT, 1))
        value = jnp.where(flat < SPLIT, here, jnp.where(flat >= SPLIT + LIFT, moved, 0.0))
        out_ref[pl.ds(r0, step), :] = value.astype(BF16)
        return 0

    lax.fori_loop(0, slot // step, body, 0)


def prepare(geo, me, shard, spill):
    return pl.pallas_call(
        partial(prepare_kernel, geo),
        out_shape=jax.ShapeDtypeStruct((geo.slot, LANES), BF16),
        in_specs=[smem(), vmem(), vmem()],
        out_specs=vmem(),
        scratch_shapes=[pltpu.VMEM((geo.slot + 32, LANES), F32)],
        compiler_params=params_of(),
        name="prepare_share",
    )(me, shard, spill)


GATHER_PHASES = ((0,), (1,), (2,), (3,))
REDUCE_PHASES = ((0,), (1,), (2,), (3,))


def phase_of(phases, group):
    return [number for number, groups in enumerate(phases) if group in groups][0]


def spot(geo, me_ref, device, own, quarter_x, groups):
    core = me_ref[2] if own else 1 - me_ref[2]
    rel_x = quarter_x ^ me_ref[1]
    rel_z = (lax.rem(device, geo.fsdp) // 2) ^ me_ref[3]
    rel_y = lax.rem(device, 2) ^ me_ref[4]
    straight = core == 0
    first = jnp.where(straight, rel_x, rel_y)
    late = jnp.where(straight, rel_y, rel_x)
    at = (first * geo.line + rel_z) * len(groups) + device // geo.fsdp - groups[0]
    return quarter_x * 2 + core, late, at


def by_phase(geo, phases, numbers, device, action):
    if len(numbers) == 1:
        action(0, phases[numbers[0]])
        return
    group = device // geo.fsdp
    for position, number in enumerate(numbers):
        groups = phases[number]
        pl.when((group >= groups[0]) & (group <= groups[-1]))(partial(action, position, groups))


class Region:
    def __init__(self, geo, row0, row1, matrix, vectors, span=None, high=None):
        self.row0, self.row1 = row0, row1
        self.mat_row, self.depth, self.cols = matrix
        self.start, self.stop = span or (0, self.depth)
        self.vectors = vectors
        self.low = max(row0 - 1, 0) // geo.rows
        self.high = (row1 - 1) // geo.rows if high is None else high
        self.slots = self.high - self.low + 1
        self.origin = geo.base(self.low)
        self.pitch = 17 if self.cols % 32 == 0 else 16
        self.stride = self.cols * self.pitch // 16
        self.scratch_tiles = (geo.base(self.high) + geo.slot - self.origin) // 16
        groups = {d // geo.fsdp for d in range(self.low, self.high + 1)}
        self.gather = sorted({phase_of(GATHER_PHASES, group) for group in groups})
        self.reduce = sorted({phase_of(REDUCE_PHASES, group) for group in groups})

    def address(self, row):
        rel = row - self.origin
        return rel if self.pitch == 16 else rel + rel // 16

    def scratch(self):
        return pltpu.VMEM((self.scratch_tiles * self.pitch, LANES), F32)


def copy_rows(region, ref, row, count, move):
    done = 0
    while done < count:
        size = min(count - done, 16 - (row + done - region.origin) % 16)
        if region.pitch == 16:
            size = count - done
        move(region.address(row + done), done, size)
        done += size


def unpack_kernel(geo, region, block, aliased, me_ref, *refs):
    arrays = 4 * len(region.gather)
    srcs, refs = refs[:arrays], refs[arrays:]
    if aliased:
        refs = refs[1:]
    weight_ref, refs = refs[0], refs[1:]
    vec_refs, refs = refs[: len(region.vectors)], refs[len(region.vectors) :]
    flat_ref, slot_ref, stage_ref, sems, out_sem = refs
    quarter, pitch, cols = geo.quarter, region.pitch, region.cols
    total = (region.stop - region.start) // block

    def fetch(step):
        device = region.low + step
        buf = lax.rem(step, FETCHES)

        def from_phase(position, groups):
            for own in range(2):
                for quarter_x in range(2):
                    q, late, at = spot(geo, me_ref, device, own, quarter_x, groups)
                    to = pl.ds(pl.multiple_of(q * quarter, 8), quarter)
                    for side in range(2):
                        src = srcs[position * 4 + (1 - own) * 2 + side]

                        @pl.when(late == side)
                        def _(src=src, at=at, to=to, own=own, quarter_x=quarter_x):
                            pltpu.make_async_copy(
                                src.at[at],
                                slot_ref.at[buf, to],
                                sems.at[buf, own * 2 + quarter_x],
                            ).start()

        by_phase(geo, GATHER_PHASES, region.gather, device, from_phase)

    ahead = min(FETCHES - 1, region.slots)

    def fetch_body(step, _):
        fetch(step)
        return 0

    lax.fori_loop(0, ahead, fetch_body, 0)

    def slot_body(step, carry):
        tile_carry, done = carry

        @pl.when(step + ahead < region.slots)
        def _():
            fetch(step + ahead)

        buf = lax.rem(step, FETCHES)
        for number in range(4):
            pltpu.make_async_copy(
                srcs[0].at[0], slot_ref.at[buf, pl.ds(0, quarter)], sems.at[buf, number]
            ).wait()
        device = region.low + step
        first_tile = geo.base(device) // 16 - region.origin // 16
        next_row = (device + 1) * geo.rows // 16 * 16
        next_tile = next_row // 16 - region.origin // 16

        def rows_body(i, _):
            t0 = i * geo.chunk
            r0 = pl.multiple_of(t0 * 16, 16)
            if pitch == 16:
                to = pl.multiple_of((first_tile + t0) * 16, 16)
                flat_ref[pl.ds(to, geo.chunk * 16), :] = slot_ref[
                    buf, pl.ds(r0, geo.chunk * 16), :
                ].astype(F32)
            else:
                for t in range(geo.chunk):
                    flat_ref[pl.ds((first_tile + t0 + t) * pitch, 16), :] = slot_ref[
                        buf, pl.ds(r0 + t * 16, 16), :
                    ].astype(F32)
            return 0

        lax.fori_loop(0, geo.slot // 16 // geo.chunk, rows_body, 0)
        seam = pl.ds(first_tile * pitch, 16)
        flat_ref[seam, :] = flat_ref[seam, :] + tile_carry
        complete = jnp.maximum(next_row - region.mat_row - region.start * cols, 0) // (block * cols)
        complete = jnp.where(step == region.slots - 1, total, jnp.minimum(complete, total))

        def mat_body(i, _):
            to = pl.multiple_of(i * block, block)
            row = i * (block * region.stride)
            for c in range(cols):
                at = region.address(region.mat_row + region.start * cols + c)
                stage_ref[pl.ds(to, block), c * LANES : (c + 1) * LANES] = flat_ref[
                    pl.ds(at + row, block, stride=region.stride), :
                ].astype(BF16)
            pltpu.make_async_copy(
                stage_ref.at[pl.ds(to, block)],
                weight_ref.at[pl.ds(region.start + to, block)],
                out_sem,
            ).start()
            return 0

        lax.fori_loop(done, complete, mat_body, 0)
        return flat_ref[pl.ds(next_tile * pitch, 16), :], complete

    lax.fori_loop(0, region.slots, slot_body, (jnp.zeros((16, LANES), F32), jnp.int32(0)))
    for (row, count), out_ref in zip(region.vectors, vec_refs):

        def move(at, done, size, out_ref=out_ref):
            out_ref[done : done + size, :] = flat_ref[at : at + size, :]

        copy_rows(region, flat_ref, row, count, move)
    pltpu.make_async_copy(
        stage_ref, weight_ref.at[pl.ds(region.start, region.stop - region.start)], out_sem
    ).wait()


def unpack(geo, region, me, gathered, weight=None):
    operands = [me] + [array for phase in region.gather for array in gathered[phase]]
    specs = [smem()] + [anywhere()] * (len(operands) - 1)
    aliases = {}
    if weight is not None:
        operands.append(weight)
        specs.append(anywhere())
        aliases = {len(operands) - 1: 0}
    height = region.stop - region.start
    return pl.pallas_call(
        partial(unpack_kernel, geo, region, 64 if region.cols <= 8 else 16, weight is not None),
        out_shape=[jax.ShapeDtypeStruct((region.depth, region.cols * LANES), BF16)]
        + [jax.ShapeDtypeStruct((count, LANES), F32) for _, count in region.vectors],
        in_specs=specs,
        out_specs=[anywhere()] + [vmem()] * len(region.vectors),
        scratch_shapes=[
            region.scratch(),
            pltpu.VMEM((FETCHES, geo.slot, LANES), BF16),
            pltpu.VMEM((height, region.cols * LANES), BF16),
            pltpu.SemaphoreType.DMA((FETCHES, 4)),
            pltpu.SemaphoreType.DMA(()),
        ],
        input_output_aliases=aliases,
        compiler_params=params_of(),
        cost_estimate=cost(0, 8 * LANES * height * region.cols),
        name="unpack_weights",
    )(*operands)


def clear_rows(region, flat_ref):
    filled = sorted(
        [(region.mat_row, region.mat_row + region.depth * region.cols)]
        + [(row, row + count) for row, count in region.vectors]
    )
    edges = [region.origin] + [edge for run in filled for edge in run]
    edges.append(region.origin + 16 * region.scratch_tiles)
    for start, stop in zip(edges[::2], edges[1::2]):
        if stop > start:

            def move(at, done, size):
                for r in range(0, size, 64):
                    span = min(64, size - r)
                    flat_ref[at + r : at + r + span, :] = jnp.zeros((span, LANES), F32)

            copy_rows(region, flat_ref, start, stop - start, move)


class Emitter:
    def __init__(self, geo, region, shared, me_ref, outs, flat_ref, slot_ref, old_ref, sems, old_sem):
        self.geo, self.region, self.shared, self.me_ref = geo, region, shared, me_ref
        self.outs, self.flat_ref, self.slot_ref, self.old_ref = outs, flat_ref, slot_ref, old_ref
        self.sems, self.old_sem = sems, old_sem

    def copies(self, device, action):
        geo = self.geo

        def to_phase(position, groups):
            count = 2 * geo.line * len(groups)
            for own in range(2):
                for quarter_x in range(2):
                    q, late, at = spot(geo, self.me_ref, device, own, quarter_x, groups)
                    rows = pl.ds(pl.multiple_of(q * geo.quarter, 8), geo.quarter)
                    action(
                        self.outs[position * 2 + 1 - own].at[late * count + at],
                        rows,
                        own * 2 + quarter_x,
                    )

        by_phase(geo, REDUCE_PHASES, self.region.reduce, device, to_phase)

    def begin(self):
        clear_rows(self.region, self.flat_ref)
        if self.shared:
            def action(place, rows, number):
                pltpu.make_async_copy(
                    place, self.old_ref.at[rows], self.old_sem.at[number]
                ).start()

            self.copies(self.region.high, action)

    def wait(self, parity):
        for number in range(4):
            pltpu.make_async_copy(
                self.slot_ref.at[parity, pl.ds(0, self.geo.quarter)],
                self.outs[0].at[0],
                self.sems.at[parity, number],
            ).wait()

    def slots_before(self, row):
        ready = (row - 1) // self.geo.rows - self.region.low
        return jnp.clip(ready, 0, self.region.slots)

    def emit(self, start, stop):
        geo, region, pitch = self.geo, self.region, self.region.pitch

        def slot_body(index, _):
            parity = lax.rem(index, BUFFERS)
            pl.when(index >= BUFFERS)(lambda: self.wait(parity))
            first_tile = geo.base(region.low + index) // 16 - region.origin // 16

            def convert(add):
                def rows_body(i, _):
                    t0 = i * geo.chunk
                    r0 = pl.multiple_of(t0 * 16, 16)
                    run = 1 if pitch > 16 else geo.chunk
                    for t in range(0, geo.chunk, run):
                        row = (first_tile + t0 + t) * pitch
                        row = pl.multiple_of(row, 16) if pitch == 16 else row
                        value = self.flat_ref[pl.ds(row, run * 16), :]
                        here = pl.ds(r0 + t * 16, run * 16)
                        if add:
                            value = value + self.old_ref[here, :].astype(F32)
                        self.slot_ref[parity, here, :] = value.astype(BF16)
                    return 0

                lax.fori_loop(0, geo.slot // 16 // geo.chunk, rows_body, 0)

            if self.shared:
                last = index == region.slots - 1

                @pl.when(last)
                def _():
                    for number in range(4):
                        pltpu.make_async_copy(
                            self.outs[0].at[0],
                            self.old_ref.at[pl.ds(0, geo.quarter)],
                            self.old_sem.at[number],
                        ).wait()
                    convert(True)

                pl.when(jnp.logical_not(last))(lambda: convert(False))
            else:
                convert(False)

            def action(place, rows, number):
                pltpu.make_async_copy(
                    self.slot_ref.at[parity, rows], place, self.sems.at[parity, number]
                ).start()

            self.copies(region.low + index, action)
            return 0

        lax.fori_loop(start, stop, slot_body, 0)

    def finish(self):
        for index in range(max(0, self.region.slots - BUFFERS), self.region.slots):
            self.wait(index % BUFFERS)


def emit_scratch(geo, region):
    return [
        region.scratch(),
        pltpu.VMEM((BUFFERS, geo.slot, LANES), BF16),
        pltpu.VMEM((geo.slot, LANES), BF16),
        pltpu.SemaphoreType.DMA((BUFFERS, 4)),
        pltpu.SemaphoreType.DMA((4,)),
    ]


def store_columns(region, flat_ref, row0, first_col, values):
    height = values.shape[0]
    for c in range(values.shape[1] // LANES):
        at = region.address(region.mat_row + first_col + c) + row0 * region.stride
        flat_ref[pl.ds(at, height, stride=region.stride), :] = values[
            :, c * LANES : (c + 1) * LANES
        ]


def with_slots(geo, region, slots, operands, specs):
    shapes = []
    aliases = {}
    for position, phase in enumerate(region.reduce):
        count = 4 * geo.line * len(REDUCE_PHASES[phase])
        for number in range(2):
            shapes.append(jax.ShapeDtypeStruct((count, geo.quarter, LANES), BF16))
            if phase in slots:
                operands.append(slots[phase][number])
                specs.append(anywhere())
                aliases[len(operands) - 1] = position * 2 + number
    return shapes, aliases, len(aliases)


def updated_slots(region, slots, results):
    merged = dict(slots)
    for position, phase in enumerate(region.reduce):
        merged[phase] = results[position * 2 : position * 2 + 2]
    return merged


def pack_kernel(geo, region, shared, grid_steps, skip, me_ref, a_ref, b_ref, *refs):
    vec_refs, refs = refs[: len(region.vectors)], refs[len(region.vectors) + skip :]
    arrays = 2 * len(region.reduce)
    *scratch, left_ref = refs[arrays:]
    emitter = Emitter(geo, region, shared, me_ref, refs[:arrays], *scratch)
    flat_ref = emitter.flat_ref
    step = pl.program_id(0)

    @pl.when(step == 0)
    def _():
        emitter.begin()
        for (row, count), vec_ref in zip(region.vectors, vec_refs):

            def move(at, done, size, vec_ref=vec_ref):
                flat_ref[at : at + size, :] = vec_ref[done : done + size, :]

            copy_rows(region, flat_ref, row, count, move)

        for r in range(0, region.depth, 256):
            left_ref[r : r + 256, :] = a_ref[:, r : r + 256].T

    width = b_ref.shape[1]
    def rows_body(i, _):
        r0 = pl.multiple_of(i * 512, 512)
        store_columns(
            region,
            flat_ref,
            r0,
            step * (width // LANES),
            nn(left_ref[pl.ds(r0, 512), :], b_ref[...]),
        )
        return 0

    lax.fori_loop(0, region.depth // 512, rows_body, 0)

    @pl.when(step == grid_steps - 1)
    def _():
        emitter.emit(0, region.slots)
        emitter.finish()


def emit_rows(emitter, step, grid_steps, height):
    region = emitter.region
    span = height * region.cols
    before = emitter.slots_before(region.mat_row + step * span)
    after = emitter.slots_before(region.mat_row + (step + 1) * span)
    last = step == grid_steps - 1
    emitter.emit(jnp.where(step == 0, 0, before), jnp.where(last, region.slots, after))
    pl.when(last)(emitter.finish)


def pack(geo, region, me, left, right, vectors, slots, shared):
    tokens = left.shape[0]
    width = 512
    steps = region.cols * LANES // width
    operands = [me, left, right] + vectors
    specs = [
        smem(),
        pl.BlockSpec((tokens, region.depth), lambda k: (0, 0), pipeline_mode=pl.Buffered(1)),
        pl.BlockSpec((tokens, width), lambda k: (0, k)),
    ] + [pl.BlockSpec(vector.shape, lambda k: (0, 0)) for vector in vectors]
    shapes, aliases, skip = with_slots(geo, region, slots, operands, specs)
    results = pl.pallas_call(
        partial(pack_kernel, geo, region, shared, steps, skip),
        grid=(steps,),
        out_shape=shapes,
        in_specs=specs,
        out_specs=[anywhere()] * len(shapes),
        scratch_shapes=emit_scratch(geo, region) + [pltpu.VMEM((region.depth, tokens), BF16)],
        input_output_aliases=aliases,
        compiler_params=params_of(),
        cost_estimate=cost(
            2 * tokens * region.depth * width * steps, 2 * region.depth * width * steps
        ),
        name="weight_grad_pack",
    )(*operands)
    return updated_slots(region, slots, results)


def line_masks(geo):
    if geo.line == 4:
        return [[2, 4, 6]]
    return [[2 << bit] for bit in range(geo.line.bit_length() - 1)]


def after(value, *others):
    return lax.optimization_barrier((value,) + others)[0]


def spread_quarters(geo, share, dp_index):
    pieces = [lax.dynamic_index_in_dim(share, dp_index, 0, keepdims=False)]
    for offset in (1, 2, 3):
        piece = lax.dynamic_index_in_dim(share, dp_index ^ offset, 0, keepdims=False)
        mask = offset * geo.fsdp
        pieces.append(geo.permute(piece, mask, mask))
    return pieces


def light():
    return pl.CostEstimate(flops=1024, bytes_accessed=1024, transcendentals=0)


def join_kernel(*refs):
    out_ref = refs[-1]
    start = 0
    for ref in refs[:-1]:
        out_ref[start : start + ref.shape[0]] = ref[...]
        start += ref.shape[0]


def join(parts):
    count = sum(part.shape[0] for part in parts)
    return pl.pallas_call(
        join_kernel,
        out_shape=jax.ShapeDtypeStruct((count,) + parts[0].shape[1:], parts[0].dtype),
        in_specs=[vmem()] * len(parts),
        out_specs=vmem(),
        compiler_params=params_of(),
        cost_estimate=light(),
        name="join",
    )(*parts)


class Gather:
    def __init__(self, geo, pieces):
        self.geo, self.held = geo, pieces

    def line(self, *deps):
        held = after(self.held, *deps)
        stages = line_masks(self.geo)
        for masks in stages[:-1]:
            moved = [self.geo.permute(held, mask, mask) for mask in masks]
            held = jnp.concatenate([held] + moved, axis=0)
        self.held = held
        self.moved = [self.geo.permute(held, mask, mask) for mask in stages[-1]]

    def joined(self, *deps):
        self.held = join([self.held] + [after(part, *deps) for part in self.moved])
        return self.held

    def across(self, *deps):
        self.moved = self.geo.permute(
            after(self.held, *deps), self.geo.bit_x, self.geo.bit_y
        )

    def last(self, *deps):
        self.near = join([self.held, after(self.moved, *deps)])
        self.moved = self.geo.permute(self.near, self.geo.bit_y, self.geo.bit_x)
        self.near_other = self.geo.core_swap(self.near)
        return self.near

    def finish(self, *deps):
        far = after(self.moved, *deps)
        return [self.near, far, after(self.near_other, *deps), self.geo.core_swap(far)]


def add_far_kernel(keep_ref, got_ref, out_ref):
    out_ref[...] = (keep_ref[...].astype(F32) + got_ref[...].astype(F32)).astype(BF16)


def add_near_kernel(keep_ref, got_ref, far_ref, kept_ref, moved_ref):
    total = keep_ref[...].astype(F32) + got_ref[...].astype(F32) + far_ref[...].astype(F32)
    half = kept_ref.shape[0]
    kept_ref[...] = total[:half]
    moved_ref[...] = total[half:].astype(BF16)


def add_line_kernel(near_ref, across_ref, own_ref, *moved_refs):
    own = own_ref.shape[0]
    own_ref[...] = near_ref[:own] + across_ref[:own].astype(F32)
    for number, ref in enumerate(moved_refs):
        rows = slice((number + 1) * own, (number + 2) * own)
        ref[...] = (near_ref[rows] + across_ref[rows].astype(F32)).astype(BF16)


def add_total_kernel(own_ref, *refs):
    total = own_ref[...]
    for ref in refs[:-1]:
        total = total + ref[...].astype(F32)
    refs[-1][...] = total


class Reduction:
    def __init__(self, geo, slots, phase):
        self.geo = geo
        self.count = geo.line * len(REDUCE_PHASES[phase])
        self.keep, send = slots
        self.got = geo.core_swap(send)
        self.block = (1, geo.quarter, LANES)

    def call(self, kernel, out_shape, **more):
        return pl.pallas_call(
            kernel,
            out_shape=out_shape,
            compiler_params=params_of(),
            cost_estimate=light(),
            name="add_terms",
            **more,
        )

    def shape(self, count, dtype):
        return jax.ShapeDtypeStruct((count,) + self.block[1:], dtype)

    def last(self, *deps):
        count = 2 * self.count
        got = after(self.got, *deps)
        later = pl.BlockSpec((count,) + self.block[1:], lambda i: (1, 0, 0))
        far = self.call(
            add_far_kernel,
            self.shape(count, BF16),
            grid=(1,),
            in_specs=[later, later],
            out_specs=vmem(),
        )(self.keep, got)
        self.from_far = self.geo.permute(far, self.geo.bit_y, self.geo.bit_x)
        self.got = got
        return far

    def across(self, *deps):
        count = self.count
        part = pl.BlockSpec((2 * count,) + self.block[1:], lambda i: (0, 0, 0))
        self.near, moved = self.call(
            add_near_kernel,
            [self.shape(count, F32), self.shape(count, BF16)],
            grid=(1,),
            in_specs=[part, part, part],
            out_specs=[vmem(), vmem()],
        )(self.keep, self.got, after(self.from_far, *deps))
        self.from_across = self.geo.permute(moved, self.geo.bit_x, self.geo.bit_y)
        return moved

    def line(self, *deps):
        near, received = self.near, after(self.from_across, *deps)
        stages = line_masks(self.geo)[::-1]
        for masks in stages:
            own = near.shape[0] // (len(masks) + 1)
            near, *parts = self.call(
                add_line_kernel,
                [self.shape(own, F32)] + [self.shape(own, BF16)] * len(masks),
                in_specs=[vmem(), vmem()],
                out_specs=[vmem()] * (len(masks) + 1),
            )(near, received)
            moved = [self.geo.permute(part, mask, mask) for part, mask in zip(parts, masks)]
            if masks is not stages[-1]:
                (received,) = moved
        self.near, self.parts = near, moved
        return near

    def total(self, *deps):
        parts = [after(part, *deps) for part in self.parts]
        return self.call(
            add_total_kernel,
            self.shape(self.near.shape[0], F32),
            in_specs=[vmem()] * (1 + len(parts)),
            out_specs=vmem(),
        )(self.near, *parts)


def collect_quarters(geo, sums, dp_index):
    def of_group(group):
        low = jnp.where(group == 0, sums[0], sums[1])
        return jnp.where(group < 2, low, jnp.where(group == 2, sums[2], sums[3]))

    pieces = [of_group(dp_index)]
    for offset in (1, 2, 3):
        mask = offset * geo.fsdp
        pieces.append(geo.permute(of_group(dp_index ^ offset).astype(BF16), mask, mask))
    return pieces


def sum_everywhere(geo, value, start=0, stop=None):
    bits = geo.devices.bit_length() - 1
    for bit in range(start, bits if stop is None else stop):
        value = value + geo.permute(value, 1 << bit, 1 << bit)
    return value


def tensor_sums(sums_ref, squares, flat, low, high, tensors):
    for t in tensors:

        @pl.when((low < STARTS[t + 1]) & (high > STARTS[t]))
        def _(t=t):
            inside = (flat >= STARTS[t]) & (flat < STARTS[t + 1])
            part = jnp.where(inside, squares, 0.0)
            sums_ref[t : t + 1, :] += jnp.sum(part, axis=0, keepdims=True)


def squares_kernel(geo, groups, me_ref, *refs):
    sums_ref = refs[-1]
    sums_ref[...] = jnp.zeros((16, LANES), F32)
    span = 8 * max(t for t in range(1, 13) if geo.quarter // 8 % t == 0)
    dp_index = me_ref[1] * 2 + me_ref[2]
    places = [(number, at, g) for number, part in enumerate(groups) for at, g in enumerate(part)]
    for number, at, group in places:
        device = group * geo.fsdp + me_ref[3] * 2 + me_ref[4]
        share = geo.rows * LANES
        base = device * geo.rows
        first = base - lax.rem(base, 16) + dp_index * geo.quarter

        def body(i, _, number=number, at=at, base=base, first=first):
            r0 = pl.multiple_of(i * span, 8)
            value = refs[number][at, pl.ds(r0, span), :]
            lane = lax.broadcasted_iota(jnp.int32, (span, LANES), 1)
            row = lax.broadcasted_iota(jnp.int32, (span, LANES), 0)
            lifted = (first + r0 + row) * LANES + lane
            flat = jnp.where(lifted < SPLIT, lifted, lifted - LIFT)
            owned = (flat >= base * LANES) & (flat < base * LANES + share)
            low = (first + r0) * LANES - LIFT
            high = (first + r0 + span) * LANES
            squares = jnp.where(owned, value * value, 0.0)
            tensor_sums(sums_ref, squares, flat, low, high, (2,) + tuple(range(5, 13)))
            return 0

        lax.fori_loop(0, geo.quarter // span, body, 0)


def square_sums(geo, me, groups, sums):
    return pl.pallas_call(
        partial(squares_kernel, geo, groups),
        out_shape=jax.ShapeDtypeStruct((16, LANES), F32),
        in_specs=[smem()] + [vmem()] * len(sums),
        out_specs=vmem(),
        compiler_params=params_of(),
        cost_estimate=light(),
        name="square_sums",
    )(me, *sums)


def update_kernel(geo, me_ref, coef_ref, *refs):
    quarters, (late_ref, p_ref, m_ref, v_ref), outs = refs[:4], refs[4:8], refs[8:]
    params_out, first_out, second_out, grad_ref = outs
    rows, quarter = geo.rows, geo.quarter
    base = me_ref[0] * rows
    shift = lax.rem(base, 16)
    dp_index = me_ref[1] * 2 + me_ref[2]
    margin = 128
    step = pl.program_id(0)

    @pl.when(step == 0)
    def _():
        for offset in range(4):
            to = pl.multiple_of(margin + (dp_index ^ offset) * quarter, 8)
            grad_ref[pl.ds(to, quarter), :] = quarters[offset][...].astype(F32)
        for row, count, at in ((0, HEAD_ROWS, 0), (TAIL_ROW, LATE_TAIL, HEAD_ROWS)):

            @pl.when((base < row + count) & (base + rows > row))
            def _(row=row, count=count, at=at):
                lane = lax.broadcasted_iota(jnp.int32, (count, LANES), 1)
                p_rows = lax.broadcasted_iota(jnp.int32, (count, LANES), 0) + row
                before = p_rows * LANES + lane < SPLIT
                to = jnp.clip(margin + shift + row - base, 0, margin + geo.slot)
                here = pl.ds(to, count)
                late = late_ref[at : at + count, :]
                grad_ref[here, :] = jnp.where(before, late, grad_ref[here, :])

    span = 64
    count = p_ref.shape[0]
    scale, first_fix, second_fix, rate = (coef_ref[i] for i in range(4))

    def body(i, _):
        r0 = pl.multiple_of(i * span, span)
        ahead = step * count + r0
        here = grad_ref[pl.ds(margin + shift + ahead, span), :]
        below = grad_ref[pl.ds(margin + shift + ahead + 1, span), :]
        lane = lax.broadcasted_iota(jnp.int32, (span, LANES), 1)
        row = lax.broadcasted_iota(jnp.int32, (span, LANES), 0)
        flat = (base + ahead + row) * LANES + lane
        back = LANES - LIFT
        moved = jnp.where(lane < back, pltpu.roll(here, back, 1), pltpu.roll(below, back, 1))
        scaled = jnp.where(flat < SPLIT, here, moved) * scale
        at = pl.ds(r0, span)
        first_new = 0.9 * m_ref[at, :] + 0.1 * scaled
        second_new = 0.999 * v_ref[at, :] + 0.001 * scaled * scaled
        params = p_ref[at, :]
        update = first_new / first_fix / (jnp.sqrt(second_new / second_fix) + 1e-08) + 0.05 * params
        params_out[at, :] = params - rate * update
        first_out[at, :] = first_new
        second_out[at, :] = second_new
        return 0

    lax.fori_loop(0, count // span, body, 0)


def update_step(geo, me, coef, quarters, late, params, first, second):
    rows = jax.ShapeDtypeStruct((geo.rows, LANES), F32)
    block = round_up(-(-geo.rows // 4), 64)
    part = pl.BlockSpec((block, LANES), lambda i: (i, 0))
    return pl.pallas_call(
        partial(update_kernel, geo),
        grid=(-(-geo.rows // block),),
        out_shape=[rows, rows, rows],
        in_specs=[smem(), smem()] + [vmem()] * 5 + [part] * 3,
        out_specs=[part] * 3,
        scratch_shapes=[pltpu.VMEM((geo.slot + 704, LANES), F32)],
        compiler_params=params_of(),
        name="moments_update",
    )(me, coef, *quarters, late, params, first, second)


def row_blocks(tokens):
    return tokens // 4 if tokens % 64 == 0 else tokens


def permute_in_kernel(rows_ref, values_ref, *refs):
    arrivals = values_ref.shape[0]
    lane = lax.broadcasted_iota(jnp.int32, (WP, arrivals), 1)
    pick = jnp.where(rows_ref[...] == lane, 1.0, 0.0).astype(BF16)
    out_ref = refs[-1]

    def body(i, _):
        lanes = pl.ds(pl.multiple_of(i * 512, 512), 512)
        out_ref[:, lanes] = nn(pick, values_ref[:, lanes]).astype(BF16)
        return 0

    lax.fori_loop(0, D // 512, body, 0)


def permute_in(row_ids, values, start, stop, before=None):
    tokens = row_ids.shape[0]
    operands = [row_ids, values]
    specs = [
        pl.BlockSpec((WP, 1), lambda i: (i + start, 0)),
        pl.BlockSpec(values.shape, lambda i: (0, 0)),
    ]
    if before is not None:
        operands.append(before)
        specs.append(anywhere())
    return pl.pallas_call(
        permute_in_kernel,
        grid=(stop - start,),
        out_shape=jax.ShapeDtypeStruct((tokens, D), BF16),
        in_specs=specs,
        out_specs=pl.BlockSpec((WP, D), lambda i: (i + start, 0)),
        input_output_aliases={} if before is None else {2: 0},
        compiler_params=params_of(),
        cost_estimate=cost(tokens * tokens * D, 2 * tokens * D),
        name="window_order",
    )(*operands)


def permute_out_kernel(rows_ref, x_ref, out_ref):
    count = out_ref.shape[0]
    arrival = lax.broadcasted_iota(jnp.int32, (count, rows_ref.shape[1]), 0)
    pick = jnp.where(rows_ref[...] == arrival + pl.program_id(0) * count, 1.0, 0.0).astype(BF16)

    def body(i, _):
        lanes = pl.ds(pl.multiple_of(i * 512, 512), 512)
        out_ref[:, lanes] = nn(pick, x_ref[:, lanes]).astype(BF16)
        return 0

    lax.fori_loop(0, D // 512, body, 0)


def permute_out(row_ids, values, arrivals):
    tokens = values.shape[0]
    block = 160 if arrivals % 160 == 0 else arrivals
    return pl.pallas_call(
        permute_out_kernel,
        grid=(arrivals // block,),
        out_shape=jax.ShapeDtypeStruct((arrivals, D), BF16),
        in_specs=[
            pl.BlockSpec((1, tokens), lambda i: (0, 0)),
            pl.BlockSpec((tokens, D), lambda i: (0, 0)),
        ],
        out_specs=pl.BlockSpec((block, D), lambda i: (i, 0)),
        compiler_params=params_of(),
        cost_estimate=cost(2 * tokens * arrivals * D, 4 * tokens * D),
        name="arrival_order",
    )(row_ids, values)


def normalized(x):
    center = x - jnp.mean(x, axis=-1, keepdims=True)
    spread = jnp.mean(center * center, axis=-1, keepdims=True)
    inverse = lax.rsqrt(spread + 1e-05)
    return center * inverse, inverse


def normalized_back(e, xhat, inverse):
    mean = jnp.mean(e, axis=-1, keepdims=True)
    along = jnp.mean(e * xhat, axis=-1, keepdims=True)
    return (e - mean - xhat * along) * inverse


def mix_kernel(x_ref, gain_ref, shift_ref, w_ref, b_ref, normed_ref, mixed_ref):
    step = pl.program_id(0)
    tokens = x_ref.shape[0]

    @pl.when(step == 0)
    def _():
        def body(i, _):
            rows = pl.ds(pl.multiple_of(i * 16, 16), 16)
            xhat, _ = normalized(x_ref[rows, :].astype(F32))
            normed_ref[rows, :] = (xhat * gain_ref[...] + shift_ref[...]).astype(BF16)
            return 0

        lax.fori_loop(0, tokens // 16, body, 0, unroll=4)

    mixed = nn(normed_ref[...], w_ref[...]) + b_ref[...]
    scale = jnp.where(step < D // w_ref.shape[1], F32(HEAD_DIM ** (-0.5)), F32(1.0))
    mixed_ref[...] = (mixed * scale).astype(BF16)


def mix(x, gain, shift, weight, bias):
    tokens = x.shape[0]
    width = 512
    rows = pl.BlockSpec((tokens, D), lambda j: (0, 0))
    vec = pl.BlockSpec((1, D), lambda j: (0, 0))
    return pl.pallas_call(
        mix_kernel,
        grid=(3 * D // width,),
        out_shape=[
            jax.ShapeDtypeStruct((tokens, D), BF16),
            jax.ShapeDtypeStruct((tokens, 3 * D), BF16),
        ],
        in_specs=[
            rows,
            vec,
            vec,
            pl.BlockSpec((D, width), lambda j: (0, j)),
            pl.BlockSpec((1, width), lambda j: (0, j)),
        ],
        out_specs=[rows, pl.BlockSpec((tokens, width), lambda j: (0, j))],
        compiler_params=params_of(),
        cost_estimate=cost(6 * tokens * D * D, 6 * D * D + 8 * tokens * D),
        name="mix_rows",
    )(x, gain, shift, weight, bias)


def bias_kernel(ids_ref, table_ref, out_ref):
    entries = table_ref.shape[1]

    def body(j, _):
        entry = lax.broadcasted_iota(jnp.int32, (entries, LANES), 0)
        pick = jnp.where(ids_ref[pl.ds(j, 1), :] == entry, 1.0, 0.0).astype(BF16)
        out_ref[:, pl.ds(j, 1), :] = nn(table_ref[...], pick).reshape(HEADS, 1, LANES)
        return 0

    lax.fori_loop(0, WT, body, 0, unroll=4)
    for j in range(WT, WP):
        out_ref[:, j : j + 1, :] = jnp.full((HEADS, 1, LANES), -1e30, F32)


def score_bias(ids, table):
    return pl.pallas_call(
        bias_kernel,
        out_shape=jax.ShapeDtypeStruct((HEADS, WP, LANES), F32),
        in_specs=[vmem(), vmem()],
        out_specs=vmem(),
        compiler_params=params_of(),
        cost_estimate=cost(2 * HEADS * WP * LANES * 384, 4 * HEADS * WP * LANES),
        name="score_bias",
    )(ids, table)


def bias_back_kernel(ids_ref, sums_ref, out_ref):
    entries = out_ref.shape[0]
    out_ref[...] = jnp.zeros(out_ref.shape, F32)
    lane = lax.broadcasted_iota(jnp.int32, (HEADS, LANES), 1)
    entry = lax.broadcasted_iota(jnp.int32, (entries, LANES), 0)
    together = 4

    def body(i, _):
        rows, picks = [], []
        for number in range(together):
            j = i * together + number
            row = sums_ref[:, pl.ds(j, 1), :].reshape(HEADS, LANES)
            rows.append(jnp.where(lane < WT, row, 0.0))
            picks.append(jnp.where(ids_ref[pl.ds(j, 1), :] == entry, 1.0, 0.0).astype(BF16))
        row = jnp.concatenate(rows, axis=1)
        high = row.astype(BF16)
        rest = row - high.astype(F32)
        middle = rest.astype(BF16)
        low = (rest - middle.astype(F32)).astype(BF16)
        parts = jnp.concatenate([high, middle, low], axis=0)
        out_ref[...] += nt(jnp.concatenate(picks, axis=1), parts)
        return 0

    lax.fori_loop(0, WT // together, body, 0)


def score_bias_back(ids, sums, entries):
    parts = pl.pallas_call(
        bias_back_kernel,
        out_shape=jax.ShapeDtypeStruct((entries, 3 * HEADS), F32),
        in_specs=[vmem(), vmem()],
        out_specs=vmem(),
        compiler_params=params_of(),
        cost_estimate=cost(6 * HEADS * WP * LANES * 384, 4 * HEADS * WP * LANES),
        name="score_bias_back",
    )(ids, sums)
    return parts[:, :HEADS] + parts[:, HEADS : 2 * HEADS] + parts[:, 2 * HEADS :]


def pad_rows(x, rows):
    return jnp.concatenate([x, jnp.zeros((rows - x.shape[0], x.shape[1]), x.dtype)], axis=0)


def one_head(x, head):
    lane = lax.broadcasted_iota(jnp.int32, x.shape, 1)
    return jnp.where(lane // HEAD_DIM == head, x, jnp.zeros_like(x))


def by_head(x):
    return jnp.concatenate([one_head(x, head) for head in range(QUAD)], axis=0)


def attention_kernel(q_ref, k_ref, v_ref, bias_ref, out_ref, log_ref):
    def block(b, _):
        lanes = pl.ds(pl.multiple_of(b * LANES, LANES), LANES)
        queries = pad_rows(q_ref[:, lanes], LANES)
        scores = nt(by_head(k_ref[:, lanes]), queries)
        values = v_ref[:, lanes].astype(F32).T.astype(BF16)
        parts = []
        for head in range(QUAD):
            s = scores[head * WP : (head + 1) * WP] + bias_ref[b * QUAD + head]
            top = jnp.max(s, axis=0, keepdims=True)
            e = jnp.exp(s - top)
            total = jnp.sum(e, axis=0, keepdims=True)
            probs = (e * (1.0 / total)).astype(BF16)
            log_ref[0, pl.ds(b * QUAD + head, 1), :] = top + jnp.log(total)
            parts.append(nn(values[head * HEAD_DIM : (head + 1) * HEAD_DIM], probs))
        context = jnp.concatenate(parts, axis=0).T
        out_ref[:, lanes] = context[:WP].astype(BF16)
        return 0

    lax.fori_loop(0, HEADS // QUAD, block, 0, unroll=8)


def attention(mixed, bias):
    windows = mixed.shape[0] // WP

    def third(c):
        return pl.BlockSpec((WP, D), lambda i, c=c: (i, c))

    return pl.pallas_call(
        attention_kernel,
        grid=(windows,),
        out_shape=[
            jax.ShapeDtypeStruct((windows * WP, D), BF16),
            jax.ShapeDtypeStruct((windows, HEADS, LANES), F32),
        ],
        in_specs=[third(0), third(1), third(2), pl.BlockSpec(bias.shape, lambda i: (0, 0, 0))],
        out_specs=[third(0), pl.BlockSpec((1, HEADS, LANES), lambda i: (i, 0, 0))],
        compiler_params=params_of(),
        cost_estimate=cost(12e9, 8 * windows * WP * D, windows * HEADS * WP * LANES),
        name="attention",
    )(mixed, mixed, mixed, bias)


def attention_back_kernel(
    more, q_ref, k_ref, v_ref, g_ref, bias_ref, log_ref, *refs
):
    out_ref, acc_ref, column_ref = refs[-3:]

    @pl.when(pl.program_id(0) == 0)
    def _():
        if more:
            acc_ref[...] = refs[0][...]
            column_ref[...] = refs[1][...]
        else:
            acc_ref[...] = jnp.zeros(acc_ref.shape, F32)
            column_ref[...] = jnp.zeros(column_ref.shape, F32)

    def put(third, b, value):
        lanes = pl.ds(pl.multiple_of(third * D + b * LANES, LANES), LANES)
        low = value.astype(BF16)
        out_ref[:, lanes] = low
        column_ref[0:1, lanes] += jnp.sum(low.astype(F32), axis=0, keepdims=True)

    def block(b, _):
        lanes = pl.ds(pl.multiple_of(b * LANES, LANES), LANES)
        queries = pad_rows(q_ref[:, lanes], LANES)
        grads = pad_rows(g_ref[:, lanes], LANES)
        keys = k_ref[:, lanes]
        scores = nt(by_head(keys), queries)
        probs_grads = nt(by_head(v_ref[:, lanes]), grads)
        keys_t = keys.astype(F32).T.astype(BF16)
        query_parts, probs_parts, score_parts = [], [], []
        for head in range(QUAD):
            span = slice(head * WP, (head + 1) * WP)
            s = scores[span] + bias_ref[b * QUAD + head]
            probs = jnp.exp(s - log_ref[0, pl.ds(b * QUAD + head, 1), :])
            probs_grad = probs_grads[span]
            along = jnp.sum(probs * probs_grad, axis=0, keepdims=True)
            score_grad = (probs * (probs_grad - along)).astype(BF16)
            acc_ref[b * QUAD + head] += score_grad.astype(F32)
            probs_parts.append(probs.astype(BF16))
            score_parts.append(score_grad)
            query_parts.append(nn(keys_t[head * HEAD_DIM : (head + 1) * HEAD_DIM], score_grad))
        put(2, b, nn(jnp.concatenate(probs_parts, axis=1), by_head(grads)))
        put(1, b, nn(jnp.concatenate(score_parts, axis=1), by_head(queries)))
        put(0, b, jnp.concatenate(query_parts, axis=0).T[:WP] * HEAD_DIM ** (-0.5))
        return 0

    lax.fori_loop(0, HEADS // QUAD, block, 0, unroll=4)


def attention_back(mixed, grads, bias, logs, start, stop, before=None):
    rows = mixed.shape[0]

    def third(c):
        return pl.BlockSpec((WP, D), lambda i, c=c: (i + start, c))

    fixed = pl.BlockSpec(bias.shape, lambda i: (0, 0, 0))
    columns = pl.BlockSpec((8, 3 * D), lambda i: (0, 0))
    operands = [mixed, mixed, mixed, grads, bias, logs]
    specs = [
        third(0),
        third(1),
        third(2),
        third(0),
        fixed,
        pl.BlockSpec((1, HEADS, LANES), lambda i: (i + start, 0, 0)),
    ]
    aliases = {}
    if before is not None:
        operands += [before[1], before[2], before[0]]
        specs += [fixed, columns, anywhere()]
        aliases = {8: 0}
    return pl.pallas_call(
        partial(attention_back_kernel, before is not None),
        grid=(stop - start,),
        out_shape=[
            jax.ShapeDtypeStruct((rows, 3 * D), BF16),
            jax.ShapeDtypeStruct(bias.shape, F32),
            jax.ShapeDtypeStruct((8, 3 * D), F32),
        ],
        in_specs=specs,
        out_specs=[pl.BlockSpec((WP, 3 * D), lambda i: (i + start, 0)), fixed, columns],
        input_output_aliases=aliases,
        compiler_params=params_of(),
        cost_estimate=cost(
            3e9 * (stop - start), 16 * (stop - start) * WP * D, HEADS * WP * LANES
        ),
        name="attention_back",
    )(*operands)


def middle_kernel(x_ref, a_ref, w_ref, b_ref, gain_ref, shift_ref, middle_ref, second_ref):
    middle = x_ref[...].astype(F32) + nn(a_ref[...], w_ref[...]) + b_ref[...]
    middle_ref[...] = middle
    xhat, _ = normalized(middle)
    second_ref[...] = (xhat * gain_ref[...] + shift_ref[...]).astype(BF16)


def middle_rows(x, attended, weight, bias, gain, shift):
    tokens = x.shape[0]
    block = row_blocks(tokens)
    rows = pl.BlockSpec((block, D), lambda i: (i, 0))
    vec = pl.BlockSpec((1, D), lambda i: (0, 0))
    return pl.pallas_call(
        middle_kernel,
        grid=(tokens // block,),
        out_shape=[
            jax.ShapeDtypeStruct((tokens, D), F32),
            jax.ShapeDtypeStruct((tokens, D), BF16),
        ],
        in_specs=[rows, rows, pl.BlockSpec((D, D), lambda i: (0, 0)), vec, vec, vec],
        out_specs=[rows, rows],
        compiler_params=params_of(),
        cost_estimate=cost(2 * tokens * D * D, 10 * tokens * D),
        name="middle_rows",
    )(x, attended, weight, bias, gain, shift)


def mlp_up_kernel(geo, region, shared, steps, skip, me_ref, s_ref, g_ref, w_ref, b_ref, *refs):
    vec_ref, refs = refs[0], refs[1 + skip :]
    hidden_ref, slope_ref, refs = refs[0], refs[1], refs[2:]
    arrays = 2 * len(region.reduce)
    *scratch, held_ref = refs[arrays:]
    emitter = Emitter(geo, region, shared, me_ref, refs[:arrays], *scratch)
    flat_ref = emitter.flat_ref
    step = pl.program_id(0)
    height = w_ref.shape[1]

    @pl.when(step == 0)
    def _():
        emitter.begin()
        ((row, count),) = region.vectors

        def move(at, done, size):
            flat_ref[at : at + size, :] = vec_ref[done : done + size, :]

        copy_rows(region, flat_ref, row, count, move)

    block = jnp.maximum(step - 1, 0)
    left = held_ref[lax.rem(step + 1, 2)].T
    u = nn(s_ref[...], w_ref[...]) + b_ref[...]
    below = 0.5 * (1.0 + lax.erf(u * F32(math.sqrt(0.5))))
    density = jnp.exp(-0.5 * u * u) * F32(1.0 / math.sqrt(2.0 * math.pi))
    hidden = (u * below).astype(BF16)
    for j in range(0, D, 512):
        store_columns(
            region, flat_ref, block * height, j // LANES, nn(left, g_ref[:, j : j + 512])
        )
    hidden_ref[...] = hidden
    slope_ref[...] = below + u * density
    held_ref[lax.rem(step, 2)] = hidden
    pl.when(step > 0)(lambda: emit_rows(emitter, step - 1, steps, height))


def mlp_up(geo, region, me, second, grad_out, weight, bias, vector, slots, shared):
    tokens = second.shape[0]
    height = 512
    steps = FF // height
    last = steps - 1
    rows = pl.BlockSpec((tokens, D), lambda k: (0, 0), pipeline_mode=pl.Buffered(1))
    columns = pl.BlockSpec((tokens, height), lambda k: (0, jnp.minimum(k, last)))
    operands = [me, second, grad_out, weight, bias, vector]
    specs = [
        smem(),
        rows,
        rows,
        pl.BlockSpec((D, height), lambda k: (0, jnp.minimum(k, last))),
        pl.BlockSpec((1, height), lambda k: (0, jnp.minimum(k, last))),
        pl.BlockSpec(vector.shape, lambda k: (0, 0)),
    ]
    shapes, aliases, skip = with_slots(geo, region, slots, operands, specs)
    results = pl.pallas_call(
        partial(mlp_up_kernel, geo, region, shared, steps, skip),
        grid=(steps + 1,),
        out_shape=[
            jax.ShapeDtypeStruct((tokens, FF), BF16),
            jax.ShapeDtypeStruct((tokens, FF), F32),
        ]
        + shapes,
        in_specs=specs,
        out_specs=[columns, columns] + [anywhere()] * len(shapes),
        scratch_shapes=emit_scratch(geo, region) + [pltpu.VMEM((2, tokens, height), BF16)],
        input_output_aliases={key: value + 2 for key, value in aliases.items()},
        compiler_params=params_of(),
        cost_estimate=cost(4 * tokens * D * FF, 4 * D * FF + 6 * tokens * FF),
        name="mlp_up",
    )(*operands)
    return results[0], results[1], updated_slots(region, slots, results[2:])


def mlp_down_kernel(geo, region, shared, steps, skip, me_ref, *refs):
    (h_ref, slope_ref, s_ref, g_ref, up_ref, down_ref, m_ref, b_ref) = refs[:8]
    refs = refs[8 + skip :]
    result_ref, grad_ref, refs = refs[0], refs[1], refs[2:]
    arrays = 2 * len(region.reduce)
    *scratch, left_ref, sum_ref = refs[arrays:]
    emitter = Emitter(geo, region, shared, me_ref, refs[:arrays], *scratch)
    flat_ref = emitter.flat_ref
    step = pl.program_id(0)
    width = h_ref.shape[1]

    @pl.when(step == 0)
    def _():
        emitter.begin()
        left_ref[...] = s_ref[...].T
        sum_ref[...] = jnp.zeros(sum_ref.shape, F32)
        grad_ref[...] = jnp.zeros(grad_ref.shape, F32)

    pre = (nt(g_ref[...], down_ref[...]) * slope_ref[...]).astype(BF16)
    column = jnp.sum(pre.astype(F32), axis=0, keepdims=True)
    sum_ref[...] += nn(h_ref[...], down_ref[...])
    grad_ref[...] += nt(pre, up_ref[...])
    cols = width // LANES
    ((vec_row, _),) = region.vectors
    for c in range(cols):
        at = region.address(vec_row + step * cols + c)
        flat_ref[pl.ds(at, 1), :] = column[:, c * LANES : (c + 1) * LANES]
    store_columns(region, flat_ref, 0, step * cols, nn(left_ref[...], pre))

    @pl.when(step == steps - 1)
    def _():
        result_ref[...] = (sum_ref[...] + m_ref[...] + b_ref[...]).astype(BF16)
        emitter.emit(0, region.slots)
        emitter.finish()


def mlp_down(geo, region, me, hidden, slope, second, grad_out, up, down, middle, bias, slots, shared):
    tokens = second.shape[0]
    width = 512
    steps = FF // width
    rows = pl.BlockSpec((tokens, D), lambda k: (0, 0), pipeline_mode=pl.Buffered(1))
    columns = pl.BlockSpec((tokens, width), lambda k: (0, k))
    operands = [me, hidden, slope, second, grad_out, up, down, middle, bias]
    specs = [
        smem(),
        columns,
        columns,
        rows,
        rows,
        pl.BlockSpec((D, width), lambda k: (0, k)),
        pl.BlockSpec((width, D), lambda k: (k, 0)),
        rows,
        pl.BlockSpec((1, D), lambda k: (0, 0)),
    ]
    shapes, aliases, skip = with_slots(geo, region, slots, operands, specs)
    whole = pl.BlockSpec((tokens, D), lambda k: (0, 0))
    results = pl.pallas_call(
        partial(mlp_down_kernel, geo, region, shared, steps, skip),
        grid=(steps,),
        out_shape=[
            jax.ShapeDtypeStruct((tokens, D), BF16),
            jax.ShapeDtypeStruct((tokens, D), F32),
        ]
        + shapes,
        in_specs=specs,
        out_specs=[whole, whole] + [anywhere()] * len(shapes),
        scratch_shapes=emit_scratch(geo, region)
        + [
            pltpu.VMEM((D, tokens), BF16),
            pltpu.VMEM((tokens, D), F32),
        ],
        input_output_aliases={key: value + 2 for key, value in aliases.items()},
        compiler_params=params_of(),
        cost_estimate=cost(8 * tokens * D * FF, 6 * D * FF + 6 * tokens * FF),
        name="mlp_down",
    )(*operands)
    return results[0], results[1], updated_slots(region, slots, results[2:])


def middle_back_kernel(s_ref, m_ref, g_ref, gain_ref, w_ref, mg_ref, bg_ref, cg_ref, vec_ref):
    @pl.when(pl.program_id(0) == 0)
    def _():
        vec_ref[...] = jnp.zeros(vec_ref.shape, F32)

    grad = s_ref[...]
    xhat, inverse = normalized(m_ref[...])
    middle_grad = g_ref[...].astype(F32) + normalized_back(grad * gain_ref[...], xhat, inverse)
    branch = middle_grad.astype(BF16)
    mg_ref[...] = middle_grad
    bg_ref[...] = branch
    cg_ref[...] = nt(branch, w_ref[...]).astype(BF16)
    vec_ref[0:1, :] += jnp.sum(branch.astype(F32), axis=0, keepdims=True)
    vec_ref[1:2, :] += jnp.sum(grad * xhat, axis=0, keepdims=True)
    vec_ref[2:3, :] += jnp.sum(grad, axis=0, keepdims=True)


def middle_back(second_grad, middle, grad_out, gain, weight):
    tokens = middle.shape[0]
    block = row_blocks(tokens)
    rows = pl.BlockSpec((block, D), lambda i: (i, 0))
    low = jax.ShapeDtypeStruct((tokens, D), BF16)
    return pl.pallas_call(
        middle_back_kernel,
        grid=(tokens // block,),
        out_shape=[
            jax.ShapeDtypeStruct((tokens, D), F32),
            low,
            low,
            jax.ShapeDtypeStruct((8, D), F32),
        ],
        in_specs=[
            rows,
            rows,
            rows,
            pl.BlockSpec((1, D), lambda i: (0, 0)),
            pl.BlockSpec((D, D), lambda i: (0, 0)),
        ],
        out_specs=[rows, rows, rows, pl.BlockSpec((8, D), lambda i: (0, 0))],
        compiler_params=params_of(),
        cost_estimate=cost(2 * tokens * D * D, 18 * tokens * D),
        name="middle_back",
    )(second_grad, middle, grad_out, gain, weight)


def first_back_kernel(steps, mixed_ref, w_ref, x_ref, mg_ref, gain_ref, out_ref, vec_ref, sum_ref):
    step = pl.program_id(0)
    width = w_ref.shape[0]
    lanes = pl.ds(pl.multiple_of(step * width, width), width)
    sum_ref[:, lanes] = nt(mixed_ref[...], w_ref[...])

    @pl.when(step == steps - 1)
    def _():
        block = row_blocks(x_ref.shape[0])
        vec_ref[...] = jnp.zeros(vec_ref.shape, F32)

        def body(i, _):
            rows = pl.ds(pl.multiple_of(i * block, 16), block)
            grad = sum_ref[rows, :]
            xhat, inverse = normalized(x_ref[rows, :].astype(F32))
            inner = normalized_back(grad * gain_ref[...], xhat, inverse)
            out_ref[rows, :] = (mg_ref[rows, :] + inner).astype(BF16)
            vec_ref[0:1, :] += jnp.sum(grad * xhat, axis=0, keepdims=True)
            vec_ref[1:2, :] += jnp.sum(grad, axis=0, keepdims=True)
            return 0

        lax.fori_loop(0, x_ref.shape[0] // block, body, 0)


def first_back(mixed_grad, weight, x, middle_grad, gain):
    tokens = x.shape[0]
    width = 256
    steps = D // width
    rows = pl.BlockSpec((tokens, D), lambda k: (0, 0), pipeline_mode=pl.Buffered(1))
    return pl.pallas_call(
        partial(first_back_kernel, steps),
        grid=(steps,),
        out_shape=[
            jax.ShapeDtypeStruct((tokens, D), BF16),
            jax.ShapeDtypeStruct((8, D), F32),
        ],
        in_specs=[
            pl.BlockSpec((tokens, 3 * D), lambda k: (0, 0), pipeline_mode=pl.Buffered(1)),
            pl.BlockSpec((width, 3 * D), lambda k: (k, 0)),
            rows,
            rows,
            pl.BlockSpec((1, D), lambda k: (0, 0)),
        ],
        out_specs=[
            pl.BlockSpec((tokens, D), lambda k: (0, 0)),
            pl.BlockSpec((8, D), lambda k: (0, 0)),
        ],
        scratch_shapes=[pltpu.VMEM((tokens, D), F32)],
        compiler_params=params_of(),
        cost_estimate=cost(6 * tokens * D * D, 6 * D * D + 14 * tokens * D),
        name="first_back",
    )(mixed_grad, weight, x, middle_grad, gain)


def local(
    patches,
    cotangent,
    window_rows,
    rel_index,
    params,
    first_moment,
    second_moment,
    learn_rate,
    step_count,
):
    arrivals = patches.shape[0]
    windows = arrivals // WT
    geo = Geometry(lax.axis_size("dp"), lax.axis_size("fsdp"), params.shape[0])
    dp_index = lax.axis_index("dp")
    fsdp_index = lax.axis_index("fsdp")
    me = jnp.stack(
        [lax.axis_index(AXES), dp_index // 2, dp_index % 2, fsdp_index // 2, fsdp_index % 2]
    ).astype(jnp.int32)

    shard = params.reshape(geo.rows, LANES)
    if geo.spill:
        spill = lax.ppermute(
            shard[: round_up(geo.spill, 8)], AXES, [(geo.spill_from, geo.spill_to)]
        )
    else:
        spill = jnp.zeros((8, LANES), F32)
    share = prepare(geo, me, shard, spill).reshape(4, geo.quarter, LANES)
    row_ids = jnp.pad(
        window_rows.reshape(windows, WT), ((0, 0), (0, WP - WT)), constant_values=-1
    ).reshape(windows * WP)
    stacked = jnp.stack(spread_quarters(geo, share, dp_index))
    gathers = []
    for groups in GATHER_PHASES:
        pieces = [
            lax.dynamic_index_in_dim(stacked, dp_index ^ group, 0, keepdims=True)
            for group in groups
        ]
        gathers.append(Gather(geo, jnp.concatenate(pieces, axis=0)))
    gathers[0].line()
    half = windows // 2
    ids_of = row_ids[:, None]
    x = permute_in(after(ids_of, gathers[0].held), patches, 0, half)
    held = gathers[0].joined(x)
    gathers[0].across()
    gathers[1].line(held)
    x = permute_in(after(ids_of, held), patches, half, windows, x)
    near = gathers[0].last(x)
    grad_out = permute_in(after(ids_of, near), cotangent, 0, half)
    gathered = {0: gathers[0].finish(grad_out)}
    far = gathered[0][1]
    held = gathers[1].joined(far)
    gathers[1].across()
    gathers[2].line(held)
    grad_out = permute_in(after(ids_of, far), cotangent, half, windows, grad_out)
    gathered[0] = gathered[0][:3] + [after(gathered[0][3], grad_out)]

    mix_matrix = (MIX_ROW, D, 3 * D // LANES)
    out_matrix = (OUT_ROW, D, D // LANES)
    expand_matrix = (EXPAND_ROW, D, FF // LANES)
    shrink_matrix = (SHRINK_ROW, FF, D // LANES)
    out_end = p_row(STARTS[6])
    expand_end = p_row(STARTS[10])
    shrink_end = p_row(STARTS[12])
    mix_vectors = [(0, 8), (8, 8), (TAIL_ROW, TABLE_ROW - TAIL_ROW), (TABLE_ROW, SPLIT_ROW - TABLE_ROW)]
    out_vectors = [(out_end + 8 * i, 8) for i in range(3)]
    expand_vectors = [(expand_end, FF // LANES)]
    shrink_vectors = [(shrink_end, 8)]

    first = Region(
        geo, 0, OUT_ROW, mix_matrix, mix_vectors, high=geo.spill_to if geo.spill else None
    )
    mix_weight, attn_gain, attn_shift, mix_bias, table_rows = unpack(geo, first, me, gathered)
    near = gathers[1].last(mix_weight)
    held = gathers[2].joined(mix_weight)
    gathers[2].across(near)
    gathers[3].line(held)
    table_rows = after(table_rows, near, held)

    def line_of(rows):
        return rows.reshape(1, -1)

    entries = round_up(TABLE_ROWS, 16)
    table = table_rows.reshape(-1)[: TABLE_ROWS * HEADS].reshape(TABLE_ROWS, HEADS).T
    table = jnp.pad(table, ((0, 0), (0, entries - TABLE_ROWS))).astype(BF16)
    ids = jnp.pad(rel_index.T, ((0, WP - WT), (0, LANES - WT)), constant_values=-1)
    bias = score_bias(ids, table)

    normed, mixed = mix(
        after(x, bias),
        line_of(attn_gain),
        line_of(attn_shift),
        mix_weight,
        line_of(mix_bias),
    )
    gathered[1] = gathers[1].finish(mixed)
    near = gathers[2].last(mixed)
    held = gathers[3].joined(mixed)
    gathers[3].across(near)
    attended, logs = attention(after(mixed, near, held, gathered[1][1]), bias)
    out_weight, out_bias, mlp_gain, mlp_shift = unpack(
        geo, Region(geo, OUT_ROW, EXPAND_ROW, out_matrix, out_vectors), me, gathered
    )
    gathered[2] = gathers[2].finish(out_weight)
    near = gathers[3].last(out_weight)
    middle, second = middle_rows(
        x,
        after(attended, near, gathered[2][1]),
        out_weight,
        line_of(out_bias),
        line_of(mlp_gain),
        line_of(mlp_shift),
    )
    expand_weight, expand_bias = unpack(
        geo, Region(geo, EXPAND_ROW, SHRINK_ROW, expand_matrix, expand_vectors), me, gathered
    )
    gathered[3] = gathers[3].finish(expand_weight)
    second = after(second, gathered[3][1])

    shrink_region = Region(
        geo, SHRINK_ROW, END_ROW, shrink_matrix, shrink_vectors, high=geo.devices - 1
    )
    expand_region = Region(geo, EXPAND_ROW, SHRINK_ROW, expand_matrix, expand_vectors)
    out_region = Region(geo, OUT_ROW, EXPAND_ROW, out_matrix, out_vectors)
    mix_region = Region(geo, 0, TAIL_ROW, mix_matrix, [])
    slots = {}
    shrink_bias_grad = jnp.sum(grad_out.astype(F32), axis=0).reshape(-1, LANES)
    hidden, slope, slots = mlp_up(
        geo,
        shrink_region,
        me,
        second,
        grad_out,
        expand_weight,
        line_of(expand_bias),
        shrink_bias_grad,
        slots,
        False,
    )
    phase3 = Reduction(geo, slots[3], 3)
    shrink_weight, shrink_bias = unpack(
        geo, Region(geo, SHRINK_ROW, END_ROW, shrink_matrix, shrink_vectors), me, gathered
    )
    sent = phase3.last(shrink_weight)
    result, second_grad, slots = mlp_down(
        geo,
        expand_region,
        me,
        after(hidden, sent),
        slope,
        second,
        grad_out,
        expand_weight,
        shrink_weight,
        middle,
        line_of(shrink_bias),
        slots,
        expand_region.high == shrink_region.low,
    )
    phase2 = Reduction(geo, slots[2], 2)
    sent = phase3.across(second_grad)
    middle_grad, branch_grad, context_grad, middle_vec = middle_back(
        after(second_grad, sent), middle, grad_out, line_of(mlp_gain), out_weight
    )
    sent = [phase3.line(context_grad), phase2.last(context_grad)]
    slots = pack(
        geo,
        out_region,
        me,
        attended,
        after(branch_grad, *sent),
        [middle_vec[i].reshape(8, LANES) for i in range(3)],
        slots,
        out_region.high == expand_region.low,
    )
    phase1 = Reduction(geo, slots[1], 1)
    context_grad = after(context_grad, slots[1][0])
    parts = attention_back(mixed, context_grad, bias, logs, 0, half)
    sums = {3: phase3.total(parts[1])}
    sent = [phase2.across(parts[1]), phase1.last(parts[1]), sums[3]]
    mixed_grad, score_sums, column_sums = attention_back(
        mixed, after(context_grad, *sent), bias, logs, half, windows, parts
    )
    sent = [phase2.line(score_sums), phase1.across(score_sums)]
    slots = pack(
        geo,
        mix_region,
        me,
        normed,
        after(mixed_grad, *sent),
        [],
        slots,
        mix_region.high == out_region.low,
    )
    packed = slots[0][0]
    phase0 = Reduction(geo, slots[0], 0)
    activations = permute_out(row_ids[None], after(result, packed), arrivals)
    far = phase0.last(activations)
    sums[2] = phase2.total(packed, far)
    sent = [phase1.line(packed, far), sums[2]]
    input_rows, first_vec = first_back(
        after(mixed_grad, far, *sent), mix_weight, x, middle_grad, line_of(attn_gain)
    )
    sent = phase0.across(input_rows)
    table_grad = score_bias_back(ids, after(score_sums, sent), entries)[:TABLE_ROWS]

    table_pad = (SPLIT_ROW - TABLE_ROW) * LANES - TABLE_ROWS * HEADS
    late = jnp.concatenate(
        [
            first_vec[:2].reshape(HEAD_ROWS, LANES),
            column_sums[0].reshape(-1, LANES),
            jnp.pad(table_grad.reshape(-1), (0, table_pad)).reshape(-1, LANES),
        ],
        axis=0,
    )
    sent = phase0.line(table_grad)
    sums[1] = phase1.total(sent)
    late = after(jnp.pad(late, ((0, LATE_ROWS - late.shape[0]), (0, 0))), sent)
    late = sum_everywhere(geo, late)
    input_grad = permute_out(row_ids[None], after(input_rows, sent), arrivals)
    squares = square_sums(
        geo, me, REDUCE_PHASES[1:], [after(sums[1], sent), sums[2], sums[3]]
    )
    sums[0] = phase0.total(squares, input_grad)
    squares = squares + square_sums(geo, me, REDUCE_PHASES[:1], [sums[0]])
    collected = collect_quarters(geo, [sums[group][0] for group in range(4)], dp_index)
    scale = 1.0 / jnp.sqrt(F32(arrivals * geo.devices))
    squares = sum_everywhere(geo, jnp.sum(squares, axis=1)[None], 0, 3)
    collected[0] = after(collected[0], squares)
    step_float = step_count.astype(F32)
    coef = jnp.stack(
        [
            scale,
            1.0 - jnp.power(F32(0.9), step_float),
            1.0 - jnp.power(F32(0.999), step_float),
            learn_rate,
        ]
    )
    params_new, first_new, second_new = update_step(
        geo,
        me,
        coef,
        collected,
        late,
        shard,
        first_moment.reshape(geo.rows, LANES),
        second_moment.reshape(geo.rows, LANES),
    )
    squares = sum_everywhere(geo, after(squares, params_new), 3)
    tensor = lax.broadcasted_iota(jnp.int32, (LATE_ROWS, 16), 1)
    row = lax.broadcasted_iota(jnp.int32, (LATE_ROWS, 16), 0)
    inside = tensor < 0
    edges = [0, 8, HEAD_ROWS, HEAD_ROWS + TABLE_ROW - TAIL_ROW, LATE_ROWS]
    for t, start, stop in zip((0, 1, 3, 4), edges, edges[1:]):
        inside = inside | ((tensor == t) & (row >= start) & (row < stop))
    late_rows = jnp.sum(late * late, axis=1, keepdims=True)
    totals = squares[0] + jnp.sum(jnp.where(inside, late_rows, 0.0), axis=0)
    entry_counts = jnp.array([math.prod(shape) for shape in SHAPES], F32)
    group_rms = jnp.sqrt(totals[: len(SHAPES)] * (scale * scale) / entry_counts)

    return (
        activations,
        input_grad,
        group_rms,
        params_new.reshape(-1),
        first_new.reshape(-1),
        second_new.reshape(-1),
    )


def solution(mesh):
    placed = (
        P(AXES, None),
        P(AXES, None),
        P(AXES),
        P(),
        P(AXES),
        P(AXES),
        P(AXES),
        P(),
        P(),
    )
    return jax.shard_map(
        local,
        mesh=mesh,
        in_specs=placed,
        out_specs=(P(AXES, None), P(AXES, None), P(), P(AXES), P(AXES), P(AXES)),
        check_vma=False,
    )
```

```python
from functools import partial
import math

import jax
import jax.numpy as jnp
from jax import lax
from jax.experimental import pallas as pl
from jax.experimental.pallas import tpu as pltpu
from jax.sharding import PartitionSpec as P

D = 1024
HEADS = 32
HEAD_DIM = 32
FF = 4096
WT = 100
WP = 104
TABLE_ROWS = 361
RAW = 12607776
LANES = 128
QUAD = LANES // HEAD_DIM
AXES = ("dp", "fsdp")
BF16 = jnp.bfloat16
F32 = jnp.float32
VMEM_LIMIT = 62 << 20
BUFFERS = 4
FETCHES = 6

SHAPES = [
    (D,),
    (D,),
    (D, 3 * D),
    (3 * D,),
    (TABLE_ROWS, HEADS),
    (D, D),
    (D,),
    (D,),
    (D,),
    (D, FF),
    (FF,),
    (FF, D),
    (D,),
]
STARTS = [0]
for _shape in SHAPES:
    STARTS.append(STARTS[-1] + math.prod(_shape))

SPLIT = STARTS[5]
LIFT = (-SPLIT) % LANES


def p_row(position):
    lifted = position + (LIFT if position >= SPLIT else 0)
    assert lifted % LANES == 0
    return lifted // LANES


MIX_ROW, OUT_ROW, EXPAND_ROW, SHRINK_ROW = (p_row(STARTS[i]) for i in (2, 5, 9, 11))
SPLIT_ROW = p_row(SPLIT)
TAIL_ROW = p_row(STARTS[3])
TABLE_ROW = STARTS[4] // LANES
END_ROW = p_row(RAW)
HEAD_ROWS = MIX_ROW
LATE_TAIL = SPLIT_ROW - TAIL_ROW
LATE_ROWS = -(-(HEAD_ROWS + LATE_TAIL) // 8) * 8


def round_up(value, step):
    return -(-value // step) * step


def vmem():
    return pl.BlockSpec(memory_space=pltpu.VMEM)


def smem():
    return pl.BlockSpec(memory_space=pltpu.SMEM)


def anywhere():
    return pl.BlockSpec(memory_space=pl.ANY)


def params_of(**more):
    return pltpu.CompilerParams(vmem_limit_bytes=VMEM_LIMIT, **more)


COST_SCALE = 2000


def cost(flops, bytes_accessed, transcendentals=0):
    return pl.CostEstimate(
        flops=int(COST_SCALE * flops),
        bytes_accessed=int(COST_SCALE * bytes_accessed),
        transcendentals=int(transcendentals),
    )


def nn(left, right):
    return jnp.dot(left, right, preferred_element_type=F32)


def nt(left, right):
    return lax.dot_general(left, right, (((1,), (1,)), ((), ())), preferred_element_type=F32)


class Geometry:
    def __init__(self, dp, fsdp, shard_len):
        assert dp == 4 and shard_len % LANES == 0 and fsdp % 2 == 0
        self.fsdp = fsdp
        self.devices = dp * fsdp
        self.line = fsdp // 2
        assert self.line & (self.line - 1) == 0
        self.rows = shard_len // LANES
        first, last = TABLE_ROW // self.rows, (SPLIT_ROW - 1) // self.rows
        assert last - first in (0, 1)
        self.spill_from, self.spill_to = last, first
        self.spill = SPLIT_ROW - self.rows * last if last != first else 0
        self.quarter = round_up(-(-(self.rows + 16 + self.spill) // 4), 8)
        self.slot = 4 * self.quarter
        assert self.slot % 16 == 0
        tiles = self.slot // 16
        self.chunk = max(t for t in range(1, 19) if tiles % t == 0)
        self.bit_x, self.bit_core, self.bit_y = 2 * fsdp, fsdp, 1

    def base(self, device):
        return (device * self.rows) // 16 * 16

    def permute(self, value, mask_core0, mask_core1):
        pairs = []
        for index in range(self.devices):
            core = (index // self.fsdp) % 2
            pairs.append((index, index ^ (mask_core1 if core else mask_core0)))
        return lax.ppermute(value, AXES, pairs)

    def core_swap(self, value):
        return self.permute(value, self.bit_core, self.bit_core)


def prepare_kernel(geo, me_ref, shard_ref, spill_ref, out_ref, pad_ref):
    rows, slot = geo.rows, geo.slot
    base = me_ref[0] * rows
    shift = lax.rem(base, 16)
    pad_ref[0:32, :] = jnp.zeros((32, LANES), F32)
    pad_ref[16 + rows : slot + 32, :] = jnp.zeros((slot + 16 - rows, LANES), F32)
    whole = rows // 64

    def place_body(i, _):
        r0 = i * 64
        pad_ref[pl.ds(16 + shift + r0, 64), :] = shard_ref[pl.ds(pl.multiple_of(r0, 64), 64), :]
        return 0

    lax.fori_loop(0, whole, place_body, 0)
    rest = rows - whole * 64
    if rest:
        pad_ref[pl.ds(16 + shift + whole * 64, rest), :] = shard_ref[whole * 64 : rows, :]
    if geo.spill:
        count = geo.spill

        @pl.when(me_ref[0] == geo.spill_to)
        def _():
            lane = lax.broadcasted_iota(jnp.int32, (count, LANES), 1)
            row = lax.broadcasted_iota(jnp.int32, (count, LANES), 0)
            flat = (rows * geo.spill_from + row) * LANES + lane
            at = 16 + rows * geo.spill_from - geo.base(geo.spill_to)
            pad_ref[at : at + count, :] = jnp.where(flat < SPLIT, spill_ref[0:count, :], 0.0)

    step = 16 * geo.chunk

    def body(i, _):
        r0 = pl.multiple_of(i * step, 16)
        here = pad_ref[pl.ds(r0 + 16, step), :]
        above = pad_ref[pl.ds(r0 + 15, step), :]
        lane = lax.broadcasted_iota(jnp.int32, (step, LANES), 1)
        row = lax.broadcasted_iota(jnp.int32, (step, LANES), 0)
        flat = (base - shift + r0 + row) * LANES + lane
        moved = jnp.where(lane >= LIFT, pltpu.roll(here, LIFT, 1), pltpu.roll(above, LIFT, 1))
        value = jnp.where(flat < SPLIT, here, jnp.where(flat >= SPLIT + LIFT, moved, 0.0))
        out_ref[pl.ds(r0, step), :] = value.astype(BF16)
        return 0

    lax.fori_loop(0, slot // step, body, 0)


def prepare(geo, me, shard, spill):
    return pl.pallas_call(
        partial(prepare_kernel, geo),
        out_shape=jax.ShapeDtypeStruct((geo.slot, LANES), BF16),
        in_specs=[smem(), vmem(), vmem()],
        out_specs=vmem(),
        scratch_shapes=[pltpu.VMEM((geo.slot + 32, LANES), F32)],
        compiler_params=params_of(),
        name="prepare_share",
    )(me, shard, spill)


GATHER_PHASES = ((0,), (1,), (2,), (3,))
REDUCE_PHASES = ((0,), (1,), (2,), (3,))


def phase_of(phases, group):
    return [number for number, groups in enumerate(phases) if group in groups][0]


def spot(geo, me_ref, device, own, quarter_x, groups):
    core = me_ref[2] if own else 1 - me_ref[2]
    rel_x = quarter_x ^ me_ref[1]
    rel_z = (lax.rem(device, geo.fsdp) // 2) ^ me_ref[3]
    rel_y = lax.rem(device, 2) ^ me_ref[4]
    straight = core == 0
    first = jnp.where(straight, rel_x, rel_y)
    late = jnp.where(straight, rel_y, rel_x)
    at = (first * geo.line + rel_z) * len(groups) + device // geo.fsdp - groups[0]
    return quarter_x * 2 + core, late, at


def by_phase(geo, phases, numbers, device, action):
    if len(numbers) == 1:
        action(0, phases[numbers[0]])
        return
    group = device // geo.fsdp
    for position, number in enumerate(numbers):
        groups = phases[number]
        pl.when((group >= groups[0]) & (group <= groups[-1]))(partial(action, position, groups))


class Region:
    def __init__(self, geo, row0, row1, matrix, vectors, span=None, high=None):
        self.row0, self.row1 = row0, row1
        self.mat_row, self.depth, self.cols = matrix
        self.start, self.stop = span or (0, self.depth)
        self.vectors = vectors
        self.low = max(row0 - 1, 0) // geo.rows
        self.high = (row1 - 1) // geo.rows if high is None else high
        self.slots = self.high - self.low + 1
        self.origin = geo.base(self.low)
        self.pitch = 17 if self.cols % 32 == 0 else 16
        self.stride = self.cols * self.pitch // 16
        self.scratch_tiles = (geo.base(self.high) + geo.slot - self.origin) // 16
        groups = {d // geo.fsdp for d in range(self.low, self.high + 1)}
        self.gather = sorted({phase_of(GATHER_PHASES, group) for group in groups})
        self.reduce = sorted({phase_of(REDUCE_PHASES, group) for group in groups})

    def address(self, row):
        rel = row - self.origin
        return rel if self.pitch == 16 else rel + rel // 16

    def scratch(self):
        return pltpu.VMEM((self.scratch_tiles * self.pitch, LANES), F32)


def copy_rows(region, ref, row, count, move):
    done = 0
    while done < count:
        size = min(count - done, 16 - (row + done - region.origin) % 16)
        if region.pitch == 16:
            size = count - done
        move(region.address(row + done), done, size)
        done += size


def unpack_kernel(geo, region, block, aliased, me_ref, *refs):
    arrays = 4 * len(region.gather)
    srcs, refs = refs[:arrays], refs[arrays:]
    if aliased:
        refs = refs[1:]
    weight_ref, refs = refs[0], refs[1:]
    vec_refs, refs = refs[: len(region.vectors)], refs[len(region.vectors) :]
    flat_ref, slot_ref, stage_ref, sems, out_sem = refs
    quarter, pitch, cols = geo.quarter, region.pitch, region.cols
    total = (region.stop - region.start) // block

    def fetch(step):
        device = region.low + step
        buf = lax.rem(step, FETCHES)

        def from_phase(position, groups):
            for own in range(2):
                for quarter_x in range(2):
                    q, late, at = spot(geo, me_ref, device, own, quarter_x, groups)
                    to = pl.ds(pl.multiple_of(q * quarter, 8), quarter)
                    for side in range(2):
                        src = srcs[position * 4 + (1 - own) * 2 + side]

                        @pl.when(late == side)
                        def _(src=src, at=at, to=to, own=own, quarter_x=quarter_x):
                            pltpu.make_async_copy(
                                src.at[at],
                                slot_ref.at[buf, to],
                                sems.at[buf, own * 2 + quarter_x],
                            ).start()

        by_phase(geo, GATHER_PHASES, region.gather, device, from_phase)

    ahead = min(FETCHES - 1, region.slots)

    def fetch_body(step, _):
        fetch(step)
        return 0

    lax.fori_loop(0, ahead, fetch_body, 0)

    def slot_body(step, carry):
        tile_carry, done = carry

        @pl.when(step + ahead < region.slots)
        def _():
            fetch(step + ahead)

        buf = lax.rem(step, FETCHES)
        for number in range(4):
            pltpu.make_async_copy(
                srcs[0].at[0], slot_ref.at[buf, pl.ds(0, quarter)], sems.at[buf, number]
            ).wait()
        device = region.low + step
        first_tile = geo.base(device) // 16 - region.origin // 16
        next_row = (device + 1) * geo.rows // 16 * 16
        next_tile = next_row // 16 - region.origin // 16

        def rows_body(i, _):
            t0 = i * geo.chunk
            r0 = pl.multiple_of(t0 * 16, 16)
            if pitch == 16:
                to = pl.multiple_of((first_tile + t0) * 16, 16)
                flat_ref[pl.ds(to, geo.chunk * 16), :] = slot_ref[
                    buf, pl.ds(r0, geo.chunk * 16), :
                ].astype(F32)
            else:
                for t in range(geo.chunk):
                    flat_ref[pl.ds((first_tile + t0 + t) * pitch, 16), :] = slot_ref[
                        buf, pl.ds(r0 + t * 16, 16), :
                    ].astype(F32)
            return 0

        lax.fori_loop(0, geo.slot // 16 // geo.chunk, rows_body, 0)
        seam = pl.ds(first_tile * pitch, 16)
        flat_ref[seam, :] = flat_ref[seam, :] + tile_carry
        complete = jnp.maximum(next_row - region.mat_row - region.start * cols, 0) // (block * cols)
        complete = jnp.where(step == region.slots - 1, total, jnp.minimum(complete, total))

        def mat_body(i, _):
            to = pl.multiple_of(i * block, block)
            row = i * (block * region.stride)
            for c in range(cols):
                at = region.address(region.mat_row + region.start * cols + c)
                stage_ref[pl.ds(to, block), c * LANES : (c + 1) * LANES] = flat_ref[
                    pl.ds(at + row, block, stride=region.stride), :
                ].astype(BF16)
            pltpu.make_async_copy(
                stage_ref.at[pl.ds(to, block)],
                weight_ref.at[pl.ds(region.start + to, block)],
                out_sem,
            ).start()
            return 0

        lax.fori_loop(done, complete, mat_body, 0)
        return flat_ref[pl.ds(next_tile * pitch, 16), :], complete

    lax.fori_loop(0, region.slots, slot_body, (jnp.zeros((16, LANES), F32), jnp.int32(0)))
    for (row, count), out_ref in zip(region.vectors, vec_refs):

        def move(at, done, size, out_ref=out_ref):
            out_ref[done : done + size, :] = flat_ref[at : at + size, :]

        copy_rows(region, flat_ref, row, count, move)
    pltpu.make_async_copy(
        stage_ref, weight_ref.at[pl.ds(region.start, region.stop - region.start)], out_sem
    ).wait()


def unpack(geo, region, me, gathered, weight=None):
    operands = [me] + [array for phase in region.gather for array in gathered[phase]]
    specs = [smem()] + [anywhere()] * (len(operands) - 1)
    aliases = {}
    if weight is not None:
        operands.append(weight)
        specs.append(anywhere())
        aliases = {len(operands) - 1: 0}
    height = region.stop - region.start
    return pl.pallas_call(
        partial(unpack_kernel, geo, region, 64 if region.cols <= 8 else 16, weight is not None),
        out_shape=[jax.ShapeDtypeStruct((region.depth, region.cols * LANES), BF16)]
        + [jax.ShapeDtypeStruct((count, LANES), F32) for _, count in region.vectors],
        in_specs=specs,
        out_specs=[anywhere()] + [vmem()] * len(region.vectors),
        scratch_shapes=[
            region.scratch(),
            pltpu.VMEM((FETCHES, geo.slot, LANES), BF16),
            pltpu.VMEM((height, region.cols * LANES), BF16),
            pltpu.SemaphoreType.DMA((FETCHES, 4)),
            pltpu.SemaphoreType.DMA(()),
        ],
        input_output_aliases=aliases,
        compiler_params=params_of(),
        cost_estimate=cost(0, 8 * LANES * height * region.cols),
        name="unpack_weights",
    )(*operands)


def clear_rows(region, flat_ref):
    filled = sorted(
        [(region.mat_row, region.mat_row + region.depth * region.cols)]
        + [(row, row + count) for row, count in region.vectors]
    )
    edges = [region.origin] + [edge for run in filled for edge in run]
    edges.append(region.origin + 16 * region.scratch_tiles)
    for start, stop in zip(edges[::2], edges[1::2]):
        if stop > start:

            def move(at, done, size):
                for r in range(0, size, 64):
                    span = min(64, size - r)
                    flat_ref[at + r : at + r + span, :] = jnp.zeros((span, LANES), F32)

            copy_rows(region, flat_ref, start, stop - start, move)


class Emitter:
    def __init__(self, geo, region, shared, me_ref, outs, flat_ref, slot_ref, old_ref, sems, old_sem):
        self.geo, self.region, self.shared, self.me_ref = geo, region, shared, me_ref
        self.outs, self.flat_ref, self.slot_ref, self.old_ref = outs, flat_ref, slot_ref, old_ref
        self.sems, self.old_sem = sems, old_sem

    def copies(self, device, action):
        geo = self.geo

        def to_phase(position, groups):
            count = 2 * geo.line * len(groups)
            for own in range(2):
                for quarter_x in range(2):
                    q, late, at = spot(geo, self.me_ref, device, own, quarter_x, groups)
                    rows = pl.ds(pl.multiple_of(q * geo.quarter, 8), geo.quarter)
                    action(
                        self.outs[position * 2 + 1 - own].at[late * count + at],
                        rows,
                        own * 2 + quarter_x,
                    )

        by_phase(geo, REDUCE_PHASES, self.region.reduce, device, to_phase)

    def begin(self):
        clear_rows(self.region, self.flat_ref)
        if self.shared:
            def action(place, rows, number):
                pltpu.make_async_copy(
                    place, self.old_ref.at[rows], self.old_sem.at[number]
                ).start()

            self.copies(self.region.high, action)

    def wait(self, parity):
        for number in range(4):
            pltpu.make_async_copy(
                self.slot_ref.at[parity, pl.ds(0, self.geo.quarter)],
                self.outs[0].at[0],
                self.sems.at[parity, number],
            ).wait()

    def slots_before(self, row):
        ready = (row - 1) // self.geo.rows - self.region.low
        return jnp.clip(ready, 0, self.region.slots)

    def emit(self, start, stop):
        geo, region, pitch = self.geo, self.region, self.region.pitch

        def slot_body(index, _):
            parity = lax.rem(index, BUFFERS)
            pl.when(index >= BUFFERS)(lambda: self.wait(parity))
            first_tile = geo.base(region.low + index) // 16 - region.origin // 16

            def convert(add):
                def rows_body(i, _):
                    t0 = i * geo.chunk
                    r0 = pl.multiple_of(t0 * 16, 16)
                    run = 1 if pitch > 16 else geo.chunk
                    for t in range(0, geo.chunk, run):
                        row = (first_tile + t0 + t) * pitch
                        row = pl.multiple_of(row, 16) if pitch == 16 else row
                        value = self.flat_ref[pl.ds(row, run * 16), :]
                        here = pl.ds(r0 + t * 16, run * 16)
                        if add:
                            value = value + self.old_ref[here, :].astype(F32)
                        self.slot_ref[parity, here, :] = value.astype(BF16)
                    return 0

                lax.fori_loop(0, geo.slot // 16 // geo.chunk, rows_body, 0)

            if self.shared:
                last = index == region.slots - 1

                @pl.when(last)
                def _():
                    for number in range(4):
                        pltpu.make_async_copy(
                            self.outs[0].at[0],
                            self.old_ref.at[pl.ds(0, geo.quarter)],
                            self.old_sem.at[number],
                        ).wait()
                    convert(True)

                pl.when(jnp.logical_not(last))(lambda: convert(False))
            else:
                convert(False)

            def action(place, rows, number):
                pltpu.make_async_copy(
                    self.slot_ref.at[parity, rows], place, self.sems.at[parity, number]
                ).start()

            self.copies(region.low + index, action)
            return 0

        lax.fori_loop(start, stop, slot_body, 0)

    def finish(self):
        for index in range(max(0, self.region.slots - BUFFERS), self.region.slots):
            self.wait(index % BUFFERS)


def emit_scratch(geo, region):
    return [
        region.scratch(),
        pltpu.VMEM((BUFFERS, geo.slot, LANES), BF16),
        pltpu.VMEM((geo.slot, LANES), BF16),
        pltpu.SemaphoreType.DMA((BUFFERS, 4)),
        pltpu.SemaphoreType.DMA((4,)),
    ]


def store_columns(region, flat_ref, row0, first_col, values):
    height = values.shape[0]
    for c in range(values.shape[1] // LANES):
        at = region.address(region.mat_row + first_col + c) + row0 * region.stride
        flat_ref[pl.ds(at, height, stride=region.stride), :] = values[
            :, c * LANES : (c + 1) * LANES
        ]


def with_slots(geo, region, slots, operands, specs):
    shapes = []
    aliases = {}
    for position, phase in enumerate(region.reduce):
        count = 4 * geo.line * len(REDUCE_PHASES[phase])
        for number in range(2):
            shapes.append(jax.ShapeDtypeStruct((count, geo.quarter, LANES), BF16))
            if phase in slots:
                operands.append(slots[phase][number])
                specs.append(anywhere())
                aliases[len(operands) - 1] = position * 2 + number
    return shapes, aliases, len(aliases)


def updated_slots(region, slots, results):
    merged = dict(slots)
    for position, phase in enumerate(region.reduce):
        merged[phase] = results[position * 2 : position * 2 + 2]
    return merged


def pack_kernel(geo, region, shared, grid_steps, skip, me_ref, a_ref, b_ref, *refs):
    vec_refs, refs = refs[: len(region.vectors)], refs[len(region.vectors) + skip :]
    arrays = 2 * len(region.reduce)
    *scratch, left_ref = refs[arrays:]
    emitter = Emitter(geo, region, shared, me_ref, refs[:arrays], *scratch)
    flat_ref = emitter.flat_ref
    step = pl.program_id(0)

    @pl.when(step == 0)
    def _():
        emitter.begin()
        for (row, count), vec_ref in zip(region.vectors, vec_refs):

            def move(at, done, size, vec_ref=vec_ref):
                flat_ref[at : at + size, :] = vec_ref[done : done + size, :]

            copy_rows(region, flat_ref, row, count, move)

        for r in range(0, region.depth, 256):
            left_ref[r : r + 256, :] = a_ref[:, r : r + 256].T

    width = b_ref.shape[1]
    def rows_body(i, _):
        r0 = pl.multiple_of(i * 512, 512)
        store_columns(
            region,
            flat_ref,
            r0,
            step * (width // LANES),
            nn(left_ref[pl.ds(r0, 512), :], b_ref[...]),
        )
        return 0

    lax.fori_loop(0, region.depth // 512, rows_body, 0)

    @pl.when(step == grid_steps - 1)
    def _():
        emitter.emit(0, region.slots)
        emitter.finish()


def emit_rows(emitter, step, grid_steps, height):
    region = emitter.region
    span = height * region.cols
    before = emitter.slots_before(region.mat_row + step * span)
    after = emitter.slots_before(region.mat_row + (step + 1) * span)
    last = step == grid_steps - 1
    emitter.emit(jnp.where(step == 0, 0, before), jnp.where(last, region.slots, after))
    pl.when(last)(emitter.finish)


def pack(geo, region, me, left, right, vectors, slots, shared):
    tokens = left.shape[0]
    width = 512
    steps = region.cols * LANES // width
    operands = [me, left, right] + vectors
    specs = [
        smem(),
        pl.BlockSpec((tokens, region.depth), lambda k: (0, 0), pipeline_mode=pl.Buffered(1)),
        pl.BlockSpec((tokens, width), lambda k: (0, k)),
    ] + [pl.BlockSpec(vector.shape, lambda k: (0, 0)) for vector in vectors]
    shapes, aliases, skip = with_slots(geo, region, slots, operands, specs)
    results = pl.pallas_call(
        partial(pack_kernel, geo, region, shared, steps, skip),
        grid=(steps,),
        out_shape=shapes,
        in_specs=specs,
        out_specs=[anywhere()] * len(shapes),
        scratch_shapes=emit_scratch(geo, region) + [pltpu.VMEM((region.depth, tokens), BF16)],
        input_output_aliases=aliases,
        compiler_params=params_of(),
        cost_estimate=cost(
            2 * tokens * region.depth * width * steps, 2 * region.depth * width * steps
        ),
        name="weight_grad_pack",
    )(*operands)
    return updated_slots(region, slots, results)


def line_masks(geo):
    if geo.line == 4:
        return [[2, 4, 6]]
    return [[2 << bit] for bit in range(geo.line.bit_length() - 1)]


def after(value, *others):
    return lax.optimization_barrier((value,) + others)[0]


def spread_quarters(geo, share, dp_index):
    pieces = [lax.dynamic_index_in_dim(share, dp_index, 0, keepdims=False)]
    for offset in (1, 2, 3):
        piece = lax.dynamic_index_in_dim(share, dp_index ^ offset, 0, keepdims=False)
        mask = offset * geo.fsdp
        pieces.append(geo.permute(piece, mask, mask))
    return pieces


def light():
    return pl.CostEstimate(flops=1024, bytes_accessed=1024, transcendentals=0)


def join_kernel(*refs):
    out_ref = refs[-1]
    start = 0
    for ref in refs[:-1]:
        out_ref[start : start + ref.shape[0]] = ref[...]
        start += ref.shape[0]


def join(parts):
    count = sum(part.shape[0] for part in parts)
    return pl.pallas_call(
        join_kernel,
        out_shape=jax.ShapeDtypeStruct((count,) + parts[0].shape[1:], parts[0].dtype),
        in_specs=[vmem()] * len(parts),
        out_specs=vmem(),
        compiler_params=params_of(),
        cost_estimate=light(),
        name="join",
    )(*parts)


class Gather:
    def __init__(self, geo, pieces):
        self.geo, self.held = geo, pieces

    def line(self, *deps):
        held = after(self.held, *deps)
        stages = line_masks(self.geo)
        for masks in stages[:-1]:
            moved = [self.geo.permute(held, mask, mask) for mask in masks]
            held = jnp.concatenate([held] + moved, axis=0)
        self.held = held
        self.moved = [self.geo.permute(held, mask, mask) for mask in stages[-1]]

    def joined(self, *deps):
        self.held = join([self.held] + [after(part, *deps) for part in self.moved])
        return self.held

    def across(self, *deps):
        self.moved = self.geo.permute(
            after(self.held, *deps), self.geo.bit_x, self.geo.bit_y
        )

    def last(self, *deps):
        self.near = join([self.held, after(self.moved, *deps)])
        self.moved = self.geo.permute(self.near, self.geo.bit_y, self.geo.bit_x)
        self.near_other = self.geo.core_swap(self.near)
        return self.near

    def finish(self, *deps):
        far = after(self.moved, *deps)
        return [self.near, far, after(self.near_other, *deps), self.geo.core_swap(far)]


def add_far_kernel(keep_ref, got_ref, out_ref):
    out_ref[...] = (keep_ref[...].astype(F32) + got_ref[...].astype(F32)).astype(BF16)


def add_near_kernel(keep_ref, got_ref, far_ref, kept_ref, moved_ref):
    total = keep_ref[...].astype(F32) + got_ref[...].astype(F32) + far_ref[...].astype(F32)
    half = kept_ref.shape[0]
    kept_ref[...] = total[:half]
    moved_ref[...] = total[half:].astype(BF16)


def add_line_kernel(near_ref, across_ref, own_ref, *moved_refs):
    own = own_ref.shape[0]
    own_ref[...] = near_ref[:own] + across_ref[:own].astype(F32)
    for number, ref in enumerate(moved_refs):
        rows = slice((number + 1) * own, (number + 2) * own)
        ref[...] = (near_ref[rows] + across_ref[rows].astype(F32)).astype(BF16)


def add_total_kernel(own_ref, *refs):
    total = own_ref[...]
    for ref in refs[:-1]:
        total = total + ref[...].astype(F32)
    refs[-1][...] = total


class Reduction:
    def __init__(self, geo, slots, phase):
        self.geo = geo
        self.count = geo.line * len(REDUCE_PHASES[phase])
        self.keep, send = slots
        self.got = geo.core_swap(send)
        self.block = (1, geo.quarter, LANES)

    def call(self, kernel, out_shape, **more):
        return pl.pallas_call(
            kernel,
            out_shape=out_shape,
            compiler_params=params_of(),
            cost_estimate=light(),
            name="add_terms",
            **more,
        )

    def shape(self, count, dtype):
        return jax.ShapeDtypeStruct((count,) + self.block[1:], dtype)

    def last(self, *deps):
        count = 2 * self.count
        got = after(self.got, *deps)
        later = pl.BlockSpec((count,) + self.block[1:], lambda i: (1, 0, 0))
        far = self.call(
            add_far_kernel,
            self.shape(count, BF16),
            grid=(1,),
            in_specs=[later, later],
            out_specs=vmem(),
        )(self.keep, got)
        self.from_far = self.geo.permute(far, self.geo.bit_y, self.geo.bit_x)
        self.got = got
        return far

    def across(self, *deps):
        count = self.count
        part = pl.BlockSpec((2 * count,) + self.block[1:], lambda i: (0, 0, 0))
        self.near, moved = self.call(
            add_near_kernel,
            [self.shape(count, F32), self.shape(count, BF16)],
            grid=(1,),
            in_specs=[part, part, part],
            out_specs=[vmem(), vmem()],
        )(self.keep, self.got, after(self.from_far, *deps))
        self.from_across = self.geo.permute(moved, self.geo.bit_x, self.geo.bit_y)
        return moved

    def line(self, *deps):
        near, received = self.near, after(self.from_across, *deps)
        stages = line_masks(self.geo)[::-1]
        for masks in stages:
            own = near.shape[0] // (len(masks) + 1)
            near, *parts = self.call(
                add_line_kernel,
                [self.shape(own, F32)] + [self.shape(own, BF16)] * len(masks),
                in_specs=[vmem(), vmem()],
                out_specs=[vmem()] * (len(masks) + 1),
            )(near, received)
            moved = [self.geo.permute(part, mask, mask) for part, mask in zip(parts, masks)]
            if masks is not stages[-1]:
                (received,) = moved
        self.near, self.parts = near, moved
        return near

    def total(self, *deps):
        parts = [after(part, *deps) for part in self.parts]
        return self.call(
            add_total_kernel,
            self.shape(self.near.shape[0], F32),
            in_specs=[vmem()] * (1 + len(parts)),
            out_specs=vmem(),
        )(self.near, *parts)


def collect_quarters(geo, sums, dp_index):
    def of_group(group):
        low = jnp.where(group == 0, sums[0], sums[1])
        return jnp.where(group < 2, low, jnp.where(group == 2, sums[2], sums[3]))

    pieces = [of_group(dp_index)]
    for offset in (1, 2, 3):
        mask = offset * geo.fsdp
        pieces.append(geo.permute(of_group(dp_index ^ offset).astype(BF16), mask, mask))
    return pieces


def sum_everywhere(geo, value, start=0, stop=None):
    bits = geo.devices.bit_length() - 1
    for bit in range(start, bits if stop is None else stop):
        value = value + geo.permute(value, 1 << bit, 1 << bit)
    return value


def tensor_sums(sums_ref, squares, flat, low, high, tensors):
    for t in tensors:

        @pl.when((low < STARTS[t + 1]) & (high > STARTS[t]))
        def _(t=t):
            inside = (flat >= STARTS[t]) & (flat < STARTS[t + 1])
            part = jnp.where(inside, squares, 0.0)
            sums_ref[t : t + 1, :] += jnp.sum(part, axis=0, keepdims=True)


def squares_kernel(geo, groups, me_ref, *refs):
    sums_ref = refs[-1]
    sums_ref[...] = jnp.zeros((16, LANES), F32)
    span = 8 * max(t for t in range(1, 13) if geo.quarter // 8 % t == 0)
    dp_index = me_ref[1] * 2 + me_ref[2]
    places = [(number, at, g) for number, part in enumerate(groups) for at, g in enumerate(part)]
    for number, at, group in places:
        device = group * geo.fsdp + me_ref[3] * 2 + me_ref[4]
        share = geo.rows * LANES
        base = device * geo.rows
        first = base - lax.rem(base, 16) + dp_index * geo.quarter

        def body(i, _, number=number, at=at, base=base, first=first):
            r0 = pl.multiple_of(i * span, 8)
            value = refs[number][at, pl.ds(r0, span), :]
            lane = lax.broadcasted_iota(jnp.int32, (span, LANES), 1)
            row = lax.broadcasted_iota(jnp.int32, (span, LANES), 0)
            lifted = (first + r0 + row) * LANES + lane
            flat = jnp.where(lifted < SPLIT, lifted, lifted - LIFT)
            owned = (flat >= base * LANES) & (flat < base * LANES + share)
            low = (first + r0) * LANES - LIFT
            high = (first + r0 + span) * LANES
            squares = jnp.where(owned, value * value, 0.0)
            tensor_sums(sums_ref, squares, flat, low, high, (2,) + tuple(range(5, 13)))
            return 0

        lax.fori_loop(0, geo.quarter // span, body, 0)


def square_sums(geo, me, groups, sums):
    return pl.pallas_call(
        partial(squares_kernel, geo, groups),
        out_shape=jax.ShapeDtypeStruct((16, LANES), F32),
        in_specs=[smem()] + [vmem()] * len(sums),
        out_specs=vmem(),
        compiler_params=params_of(),
        cost_estimate=light(),
        name="square_sums",
    )(me, *sums)


def update_kernel(geo, me_ref, coef_ref, *refs):
    quarters, (late_ref, p_ref, m_ref, v_ref), outs = refs[:4], refs[4:8], refs[8:]
    params_out, first_out, second_out, grad_ref = outs
    rows, quarter = geo.rows, geo.quarter
    base = me_ref[0] * rows
    shift = lax.rem(base, 16)
    dp_index = me_ref[1] * 2 + me_ref[2]
    margin = 128
    step = pl.program_id(0)

    @pl.when(step == 0)
    def _():
        for offset in range(4):
            to = pl.multiple_of(margin + (dp_index ^ offset) * quarter, 8)
            grad_ref[pl.ds(to, quarter), :] = quarters[offset][...].astype(F32)
        for row, count, at in ((0, HEAD_ROWS, 0), (TAIL_ROW, LATE_TAIL, HEAD_ROWS)):

            @pl.when((base < row + count) & (base + rows > row))
            def _(row=row, count=count, at=at):
                lane = lax.broadcasted_iota(jnp.int32, (count, LANES), 1)
                p_rows = lax.broadcasted_iota(jnp.int32, (count, LANES), 0) + row
                before = p_rows * LANES + lane < SPLIT
                to = jnp.clip(margin + shift + row - base, 0, margin + geo.slot)
                here = pl.ds(to, count)
                late = late_ref[at : at + count, :]
                grad_ref[here, :] = jnp.where(before, late, grad_ref[here, :])

    span = 64
    count = p_ref.shape[0]
    scale, first_fix, second_fix, rate = (coef_ref[i] for i in range(4))

    def body(i, _):
        r0 = pl.multiple_of(i * span, span)
        ahead = step * count + r0
        here = grad_ref[pl.ds(margin + shift + ahead, span), :]
        below = grad_ref[pl.ds(margin + shift + ahead + 1, span), :]
        lane = lax.broadcasted_iota(jnp.int32, (span, LANES), 1)
        row = lax.broadcasted_iota(jnp.int32, (span, LANES), 0)
        flat = (base + ahead + row) * LANES + lane
        back = LANES - LIFT
        moved = jnp.where(lane < back, pltpu.roll(here, back, 1), pltpu.roll(below, back, 1))
        scaled = jnp.where(flat < SPLIT, here, moved) * scale
        at = pl.ds(r0, span)
        first_new = 0.9 * m_ref[at, :] + 0.1 * scaled
        second_new = 0.999 * v_ref[at, :] + 0.001 * scaled * scaled
        params = p_ref[at, :]
        update = first_new / first_fix / (jnp.sqrt(second_new / second_fix) + 1e-08) + 0.05 * params
        params_out[at, :] = params - rate * update
        first_out[at, :] = first_new
        second_out[at, :] = second_new
        return 0

    lax.fori_loop(0, count // span, body, 0)


def update_step(geo, me, coef, quarters, late, params, first, second):
    rows = jax.ShapeDtypeStruct((geo.rows, LANES), F32)
    block = round_up(-(-geo.rows // 4), 64)
    part = pl.BlockSpec((block, LANES), lambda i: (i, 0))
    return pl.pallas_call(
        partial(update_kernel, geo),
        grid=(-(-geo.rows // block),),
        out_shape=[rows, rows, rows],
        in_specs=[smem(), smem()] + [vmem()] * 5 + [part] * 3,
        out_specs=[part] * 3,
        scratch_shapes=[pltpu.VMEM((geo.slot + 704, LANES), F32)],
        compiler_params=params_of(),
        name="moments_update",
    )(me, coef, *quarters, late, params, first, second)


def row_blocks(tokens):
    return tokens // 4 if tokens % 64 == 0 else tokens


def permute_in_kernel(rows_ref, values_ref, *refs):
    arrivals = values_ref.shape[0]
    lane = lax.broadcasted_iota(jnp.int32, (WP, arrivals), 1)
    pick = jnp.where(rows_ref[...] == lane, 1.0, 0.0).astype(BF16)
    out_ref = refs[-1]

    def body(i, _):
        lanes = pl.ds(pl.multiple_of(i * 512, 512), 512)
        out_ref[:, lanes] = nn(pick, values_ref[:, lanes]).astype(BF16)
        return 0

    lax.fori_loop(0, D // 512, body, 0)


def permute_in(row_ids, values, start, stop, before=None):
    tokens = row_ids.shape[0]
    operands = [row_ids, values]
    specs = [
        pl.BlockSpec((WP, 1), lambda i: (i + start, 0)),
        pl.BlockSpec(values.shape, lambda i: (0, 0)),
    ]
    if before is not None:
        operands.append(before)
        specs.append(anywhere())
    return pl.pallas_call(
        permute_in_kernel,
        grid=(stop - start,),
        out_shape=jax.ShapeDtypeStruct((tokens, D), BF16),
        in_specs=specs,
        out_specs=pl.BlockSpec((WP, D), lambda i: (i + start, 0)),
        input_output_aliases={} if before is None else {2: 0},
        compiler_params=params_of(),
        cost_estimate=cost(tokens * tokens * D, 2 * tokens * D),
        name="window_order",
    )(*operands)


def permute_out_kernel(rows_ref, x_ref, out_ref):
    count = out_ref.shape[0]
    arrival = lax.broadcasted_iota(jnp.int32, (count, rows_ref.shape[1]), 0)
    pick = jnp.where(rows_ref[...] == arrival + pl.program_id(0) * count, 1.0, 0.0).astype(BF16)

    def body(i, _):
        lanes = pl.ds(pl.multiple_of(i * 512, 512), 512)
        out_ref[:, lanes] = nn(pick, x_ref[:, lanes]).astype(BF16)
        return 0

    lax.fori_loop(0, D // 512, body, 0)


def permute_out(row_ids, values, arrivals):
    tokens = values.shape[0]
    block = 160 if arrivals % 160 == 0 else arrivals
    return pl.pallas_call(
        permute_out_kernel,
        grid=(arrivals // block,),
        out_shape=jax.ShapeDtypeStruct((arrivals, D), BF16),
        in_specs=[
            pl.BlockSpec((1, tokens), lambda i: (0, 0)),
            pl.BlockSpec((tokens, D), lambda i: (0, 0)),
        ],
        out_specs=pl.BlockSpec((block, D), lambda i: (i, 0)),
        compiler_params=params_of(),
        cost_estimate=cost(2 * tokens * arrivals * D, 4 * tokens * D),
        name="arrival_order",
    )(row_ids, values)


def normalized(x):
    center = x - jnp.mean(x, axis=-1, keepdims=True)
    spread = jnp.mean(center * center, axis=-1, keepdims=True)
    inverse = lax.rsqrt(spread + 1e-05)
    return center * inverse, inverse


def normalized_back(e, xhat, inverse):
    mean = jnp.mean(e, axis=-1, keepdims=True)
    along = jnp.mean(e * xhat, axis=-1, keepdims=True)
    return (e - mean - xhat * along) * inverse


def mix_kernel(x_ref, gain_ref, shift_ref, w_ref, b_ref, normed_ref, mixed_ref):
    step = pl.program_id(0)
    tokens = x_ref.shape[0]

    @pl.when(step == 0)
    def _():
        def body(i, _):
            rows = pl.ds(pl.multiple_of(i * 16, 16), 16)
            xhat, _ = normalized(x_ref[rows, :].astype(F32))
            normed_ref[rows, :] = (xhat * gain_ref[...] + shift_ref[...]).astype(BF16)
            return 0

        lax.fori_loop(0, tokens // 16, body, 0, unroll=4)

    mixed = nn(normed_ref[...], w_ref[...]) + b_ref[...]
    scale = jnp.where(step < D // w_ref.shape[1], F32(HEAD_DIM ** (-0.5)), F32(1.0))
    mixed_ref[...] = (mixed * scale).astype(BF16)


def mix(x, gain, shift, weight, bias):
    tokens = x.shape[0]
    width = 512
    rows = pl.BlockSpec((tokens, D), lambda j: (0, 0))
    vec = pl.BlockSpec((1, D), lambda j: (0, 0))
    return pl.pallas_call(
        mix_kernel,
        grid=(3 * D // width,),
        out_shape=[
            jax.ShapeDtypeStruct((tokens, D), BF16),
            jax.ShapeDtypeStruct((tokens, 3 * D), BF16),
        ],
        in_specs=[
            rows,
            vec,
            vec,
            pl.BlockSpec((D, width), lambda j: (0, j)),
            pl.BlockSpec((1, width), lambda j: (0, j)),
        ],
        out_specs=[rows, pl.BlockSpec((tokens, width), lambda j: (0, j))],
        compiler_params=params_of(),
        cost_estimate=cost(6 * tokens * D * D, 6 * D * D + 8 * tokens * D),
        name="mix_rows",
    )(x, gain, shift, weight, bias)


def bias_kernel(ids_ref, table_ref, out_ref):
    entries = table_ref.shape[1]

    def body(j, _):
        entry = lax.broadcasted_iota(jnp.int32, (entries, LANES), 0)
        pick = jnp.where(ids_ref[pl.ds(j, 1), :] == entry, 1.0, 0.0).astype(BF16)
        out_ref[:, pl.ds(j, 1), :] = nn(table_ref[...], pick).reshape(HEADS, 1, LANES)
        return 0

    lax.fori_loop(0, WT, body, 0, unroll=4)
    for j in range(WT, WP):
        out_ref[:, j : j + 1, :] = jnp.full((HEADS, 1, LANES), -1e30, F32)


def score_bias(ids, table):
    return pl.pallas_call(
        bias_kernel,
        out_shape=jax.ShapeDtypeStruct((HEADS, WP, LANES), F32),
        in_specs=[vmem(), vmem()],
        out_specs=vmem(),
        compiler_params=params_of(),
        cost_estimate=cost(2 * HEADS * WP * LANES * 384, 4 * HEADS * WP * LANES),
        name="score_bias",
    )(ids, table)


def bias_back_kernel(ids_ref, sums_ref, out_ref):
    entries = out_ref.shape[0]
    out_ref[...] = jnp.zeros(out_ref.shape, F32)
    lane = lax.broadcasted_iota(jnp.int32, (HEADS, LANES), 1)
    entry = lax.broadcasted_iota(jnp.int32, (entries, LANES), 0)
    together = 4

    def body(i, _):
        rows, picks = [], []
        for number in range(together):
            j = i * together + number
            row = sums_ref[:, pl.ds(j, 1), :].reshape(HEADS, LANES)
            rows.append(jnp.where(lane < WT, row, 0.0))
            picks.append(jnp.where(ids_ref[pl.ds(j, 1), :] == entry, 1.0, 0.0).astype(BF16))
        row = jnp.concatenate(rows, axis=1)
        high = row.astype(BF16)
        rest = row - high.astype(F32)
        middle = rest.astype(BF16)
        low = (rest - middle.astype(F32)).astype(BF16)
        parts = jnp.concatenate([high, middle, low], axis=0)
        out_ref[...] += nt(jnp.concatenate(picks, axis=1), parts)
        return 0

    lax.fori_loop(0, WT // together, body, 0)


def score_bias_back(ids, sums, entries):
    parts = pl.pallas_call(
        bias_back_kernel,
        out_shape=jax.ShapeDtypeStruct((entries, 3 * HEADS), F32),
        in_specs=[vmem(), vmem()],
        out_specs=vmem(),
        compiler_params=params_of(),
        cost_estimate=cost(6 * HEADS * WP * LANES * 384, 4 * HEADS * WP * LANES),
        name="score_bias_back",
    )(ids, sums)
    return parts[:, :HEADS] + parts[:, HEADS : 2 * HEADS] + parts[:, 2 * HEADS :]


def pad_rows(x, rows):
    return jnp.concatenate([x, jnp.zeros((rows - x.shape[0], x.shape[1]), x.dtype)], axis=0)


def one_head(x, head):
    lane = lax.broadcasted_iota(jnp.int32, x.shape, 1)
    return jnp.where(lane // HEAD_DIM == head, x, jnp.zeros_like(x))


def by_head(x):
    return jnp.concatenate([one_head(x, head) for head in range(QUAD)], axis=0)


def attention_kernel(q_ref, k_ref, v_ref, bias_ref, out_ref, log_ref):
    def block(b, _):
        lanes = pl.ds(pl.multiple_of(b * LANES, LANES), LANES)
        queries = pad_rows(q_ref[:, lanes], LANES)
        scores = nt(by_head(k_ref[:, lanes]), queries)
        values = v_ref[:, lanes].astype(F32).T.astype(BF16)
        parts = []
        for head in range(QUAD):
            s = scores[head * WP : (head + 1) * WP] + bias_ref[b * QUAD + head]
            top = jnp.max(s, axis=0, keepdims=True)
            e = jnp.exp(s - top)
            total = jnp.sum(e, axis=0, keepdims=True)
            probs = (e * (1.0 / total)).astype(BF16)
            log_ref[0, pl.ds(b * QUAD + head, 1), :] = top + jnp.log(total)
            parts.append(nn(values[head * HEAD_DIM : (head + 1) * HEAD_DIM], probs))
        context = jnp.concatenate(parts, axis=0).T
        out_ref[:, lanes] = context[:WP].astype(BF16)
        return 0

    lax.fori_loop(0, HEADS // QUAD, block, 0, unroll=8)


def attention(mixed, bias):
    windows = mixed.shape[0] // WP

    def third(c):
        return pl.BlockSpec((WP, D), lambda i, c=c: (i, c))

    return pl.pallas_call(
        attention_kernel,
        grid=(windows,),
        out_shape=[
            jax.ShapeDtypeStruct((windows * WP, D), BF16),
            jax.ShapeDtypeStruct((windows, HEADS, LANES), F32),
        ],
        in_specs=[third(0), third(1), third(2), pl.BlockSpec(bias.shape, lambda i: (0, 0, 0))],
        out_specs=[third(0), pl.BlockSpec((1, HEADS, LANES), lambda i: (i, 0, 0))],
        compiler_params=params_of(),
        cost_estimate=cost(12e9, 8 * windows * WP * D, windows * HEADS * WP * LANES),
        name="attention",
    )(mixed, mixed, mixed, bias)


def attention_back_kernel(
    more, q_ref, k_ref, v_ref, g_ref, bias_ref, log_ref, *refs
):
    out_ref, acc_ref, column_ref = refs[-3:]

    @pl.when(pl.program_id(0) == 0)
    def _():
        if more:
            acc_ref[...] = refs[0][...]
            column_ref[...] = refs[1][...]
        else:
            acc_ref[...] = jnp.zeros(acc_ref.shape, F32)
            column_ref[...] = jnp.zeros(column_ref.shape, F32)

    def put(third, b, value):
        lanes = pl.ds(pl.multiple_of(third * D + b * LANES, LANES), LANES)
        low = value.astype(BF16)
        out_ref[:, lanes] = low
        column_ref[0:1, lanes] += jnp.sum(low.astype(F32), axis=0, keepdims=True)

    def block(b, _):
        lanes = pl.ds(pl.multiple_of(b * LANES, LANES), LANES)
        queries = pad_rows(q_ref[:, lanes], LANES)
        grads = pad_rows(g_ref[:, lanes], LANES)
        keys = k_ref[:, lanes]
        scores = nt(by_head(keys), queries)
        probs_grads = nt(by_head(v_ref[:, lanes]), grads)
        keys_t = keys.astype(F32).T.astype(BF16)
        query_parts, probs_parts, score_parts = [], [], []
        for head in range(QUAD):
            span = slice(head * WP, (head + 1) * WP)
            s = scores[span] + bias_ref[b * QUAD + head]
            probs = jnp.exp(s - log_ref[0, pl.ds(b * QUAD + head, 1), :])
            probs_grad = probs_grads[span]
            along = jnp.sum(probs * probs_grad, axis=0, keepdims=True)
            score_grad = (probs * (probs_grad - along)).astype(BF16)
            acc_ref[b * QUAD + head] += score_grad.astype(F32)
            probs_parts.append(probs.astype(BF16))
            score_parts.append(score_grad)
            query_parts.append(nn(keys_t[head * HEAD_DIM : (head + 1) * HEAD_DIM], score_grad))
        put(2, b, nn(jnp.concatenate(probs_parts, axis=1), by_head(grads)))
        put(1, b, nn(jnp.concatenate(score_parts, axis=1), by_head(queries)))
        put(0, b, jnp.concatenate(query_parts, axis=0).T[:WP] * HEAD_DIM ** (-0.5))
        return 0

    lax.fori_loop(0, HEADS // QUAD, block, 0, unroll=4)


def attention_back(mixed, grads, bias, logs, start, stop, before=None):
    rows = mixed.shape[0]

    def third(c):
        return pl.BlockSpec((WP, D), lambda i, c=c: (i + start, c))

    fixed = pl.BlockSpec(bias.shape, lambda i: (0, 0, 0))
    columns = pl.BlockSpec((8, 3 * D), lambda i: (0, 0))
    operands = [mixed, mixed, mixed, grads, bias, logs]
    specs = [
        third(0),
        third(1),
        third(2),
        third(0),
        fixed,
        pl.BlockSpec((1, HEADS, LANES), lambda i: (i + start, 0, 0)),
    ]
    aliases = {}
    if before is not None:
        operands += [before[1], before[2], before[0]]
        specs += [fixed, columns, anywhere()]
        aliases = {8: 0}
    return pl.pallas_call(
        partial(attention_back_kernel, before is not None),
        grid=(stop - start,),
        out_shape=[
            jax.ShapeDtypeStruct((rows, 3 * D), BF16),
            jax.ShapeDtypeStruct(bias.shape, F32),
            jax.ShapeDtypeStruct((8, 3 * D), F32),
        ],
        in_specs=specs,
        out_specs=[pl.BlockSpec((WP, 3 * D), lambda i: (i + start, 0)), fixed, columns],
        input_output_aliases=aliases,
        compiler_params=params_of(),
        cost_estimate=cost(
            3e9 * (stop - start), 16 * (stop - start) * WP * D, HEADS * WP * LANES
        ),
        name="attention_back",
    )(*operands)


def middle_kernel(x_ref, a_ref, w_ref, b_ref, gain_ref, shift_ref, middle_ref, second_ref):
    middle = x_ref[...].astype(F32) + nn(a_ref[...], w_ref[...]) + b_ref[...]
    middle_ref[...] = middle
    xhat, _ = normalized(middle)
    second_ref[...] = (xhat * gain_ref[...] + shift_ref[...]).astype(BF16)


def middle_rows(x, attended, weight, bias, gain, shift):
    tokens = x.shape[0]
    block = row_blocks(tokens)
    rows = pl.BlockSpec((block, D), lambda i: (i, 0))
    vec = pl.BlockSpec((1, D), lambda i: (0, 0))
    return pl.pallas_call(
        middle_kernel,
        grid=(tokens // block,),
        out_shape=[
            jax.ShapeDtypeStruct((tokens, D), F32),
            jax.ShapeDtypeStruct((tokens, D), BF16),
        ],
        in_specs=[rows, rows, pl.BlockSpec((D, D), lambda i: (0, 0)), vec, vec, vec],
        out_specs=[rows, rows],
        compiler_params=params_of(),
        cost_estimate=cost(2 * tokens * D * D, 10 * tokens * D),
        name="middle_rows",
    )(x, attended, weight, bias, gain, shift)


def mlp_up_kernel(geo, region, shared, steps, skip, me_ref, s_ref, g_ref, w_ref, b_ref, *refs):
    vec_ref, refs = refs[0], refs[1 + skip :]
    hidden_ref, slope_ref, refs = refs[0], refs[1], refs[2:]
    arrays = 2 * len(region.reduce)
    *scratch, held_ref = refs[arrays:]
    emitter = Emitter(geo, region, shared, me_ref, refs[:arrays], *scratch)
    flat_ref = emitter.flat_ref
    step = pl.program_id(0)
    height = w_ref.shape[1]

    @pl.when(step == 0)
    def _():
        emitter.begin()
        ((row, count),) = region.vectors

        def move(at, done, size):
            flat_ref[at : at + size, :] = vec_ref[done : done + size, :]

        copy_rows(region, flat_ref, row, count, move)

    block = jnp.maximum(step - 1, 0)
    left = held_ref[lax.rem(step + 1, 2)].T
    u = nn(s_ref[...], w_ref[...]) + b_ref[...]
    below = 0.5 * (1.0 + lax.erf(u * F32(math.sqrt(0.5))))
    density = jnp.exp(-0.5 * u * u) * F32(1.0 / math.sqrt(2.0 * math.pi))
    hidden = (u * below).astype(BF16)
    for j in range(0, D, 512):
        store_columns(
            region, flat_ref, block * height, j // LANES, nn(left, g_ref[:, j : j + 512])
        )
    hidden_ref[...] = hidden
    slope_ref[...] = below + u * density
    held_ref[lax.rem(step, 2)] = hidden
    pl.when(step > 0)(lambda: emit_rows(emitter, step - 1, steps, height))


def mlp_up(geo, region, me, second, grad_out, weight, bias, vector, slots, shared):
    tokens = second.shape[0]
    height = 512
    steps = FF // height
    last = steps - 1
    rows = pl.BlockSpec((tokens, D), lambda k: (0, 0), pipeline_mode=pl.Buffered(1))
    columns = pl.BlockSpec((tokens, height), lambda k: (0, jnp.minimum(k, last)))
    operands = [me, second, grad_out, weight, bias, vector]
    specs = [
        smem(),
        rows,
        rows,
        pl.BlockSpec((D, height), lambda k: (0, jnp.minimum(k, last))),
        pl.BlockSpec((1, height), lambda k: (0, jnp.minimum(k, last))),
        pl.BlockSpec(vector.shape, lambda k: (0, 0)),
    ]
    shapes, aliases, skip = with_slots(geo, region, slots, operands, specs)
    results = pl.pallas_call(
        partial(mlp_up_kernel, geo, region, shared, steps, skip),
        grid=(steps + 1,),
        out_shape=[
            jax.ShapeDtypeStruct((tokens, FF), BF16),
            jax.ShapeDtypeStruct((tokens, FF), F32),
        ]
        + shapes,
        in_specs=specs,
        out_specs=[columns, columns] + [anywhere()] * len(shapes),
        scratch_shapes=emit_scratch(geo, region) + [pltpu.VMEM((2, tokens, height), BF16)],
        input_output_aliases={key: value + 2 for key, value in aliases.items()},
        compiler_params=params_of(),
        cost_estimate=cost(4 * tokens * D * FF, 4 * D * FF + 6 * tokens * FF),
        name="mlp_up",
    )(*operands)
    return results[0], results[1], updated_slots(region, slots, results[2:])


def mlp_down_kernel(geo, region, shared, steps, skip, me_ref, *refs):
    (h_ref, slope_ref, s_ref, g_ref, up_ref, down_ref, m_ref, b_ref) = refs[:8]
    refs = refs[8 + skip :]
    result_ref, grad_ref, refs = refs[0], refs[1], refs[2:]
    arrays = 2 * len(region.reduce)
    *scratch, left_ref, sum_ref = refs[arrays:]
    emitter = Emitter(geo, region, shared, me_ref, refs[:arrays], *scratch)
    flat_ref = emitter.flat_ref
    step = pl.program_id(0)
    width = h_ref.shape[1]

    @pl.when(step == 0)
    def _():
        emitter.begin()
        left_ref[...] = s_ref[...].T
        sum_ref[...] = jnp.zeros(sum_ref.shape, F32)
        grad_ref[...] = jnp.zeros(grad_ref.shape, F32)

    pre = (nt(g_ref[...], down_ref[...]) * slope_ref[...]).astype(BF16)
    column = jnp.sum(pre.astype(F32), axis=0, keepdims=True)
    sum_ref[...] += nn(h_ref[...], down_ref[...])
    grad_ref[...] += nt(pre, up_ref[...])
    cols = width // LANES
    ((vec_row, _),) = region.vectors
    for c in range(cols):
        at = region.address(vec_row + step * cols + c)
        flat_ref[pl.ds(at, 1), :] = column[:, c * LANES : (c + 1) * LANES]
    store_columns(region, flat_ref, 0, step * cols, nn(left_ref[...], pre))

    @pl.when(step == steps - 1)
    def _():
        result_ref[...] = (sum_ref[...] + m_ref[...] + b_ref[...]).astype(BF16)
        emitter.emit(0, region.slots)
        emitter.finish()


def mlp_down(geo, region, me, hidden, slope, second, grad_out, up, down, middle, bias, slots, shared):
    tokens = second.shape[0]
    width = 512
    steps = FF // width
    rows = pl.BlockSpec((tokens, D), lambda k: (0, 0), pipeline_mode=pl.Buffered(1))
    columns = pl.BlockSpec((tokens, width), lambda k: (0, k))
    operands = [me, hidden, slope, second, grad_out, up, down, middle, bias]
    specs = [
        smem(),
        columns,
        columns,
        rows,
        rows,
        pl.BlockSpec((D, width), lambda k: (0, k)),
        pl.BlockSpec((width, D), lambda k: (k, 0)),
        rows,
        pl.BlockSpec((1, D), lambda k: (0, 0)),
    ]
    shapes, aliases, skip = with_slots(geo, region, slots, operands, specs)
    whole = pl.BlockSpec((tokens, D), lambda k: (0, 0))
    results = pl.pallas_call(
        partial(mlp_down_kernel, geo, region, shared, steps, skip),
        grid=(steps,),
        out_shape=[
            jax.ShapeDtypeStruct((tokens, D), BF16),
            jax.ShapeDtypeStruct((tokens, D), F32),
        ]
        + shapes,
        in_specs=specs,
        out_specs=[whole, whole] + [anywhere()] * len(shapes),
        scratch_shapes=emit_scratch(geo, region)
        + [
            pltpu.VMEM((D, tokens), BF16),
            pltpu.VMEM((tokens, D), F32),
        ],
        input_output_aliases={key: value + 2 for key, value in aliases.items()},
        compiler_params=params_of(),
        cost_estimate=cost(8 * tokens * D * FF, 6 * D * FF + 6 * tokens * FF),
        name="mlp_down",
    )(*operands)
    return results[0], results[1], updated_slots(region, slots, results[2:])


def middle_back_kernel(s_ref, m_ref, g_ref, gain_ref, w_ref, mg_ref, bg_ref, cg_ref, vec_ref):
    @pl.when(pl.program_id(0) == 0)
    def _():
        vec_ref[...] = jnp.zeros(vec_ref.shape, F32)

    grad = s_ref[...]
    xhat, inverse = normalized(m_ref[...])
    middle_grad = g_ref[...].astype(F32) + normalized_back(grad * gain_ref[...], xhat, inverse)
    branch = middle_grad.astype(BF16)
    mg_ref[...] = middle_grad
    bg_ref[...] = branch
    cg_ref[...] = nt(branch, w_ref[...]).astype(BF16)
    vec_ref[0:1, :] += jnp.sum(branch.astype(F32), axis=0, keepdims=True)
    vec_ref[1:2, :] += jnp.sum(grad * xhat, axis=0, keepdims=True)
    vec_ref[2:3, :] += jnp.sum(grad, axis=0, keepdims=True)


def middle_back(second_grad, middle, grad_out, gain, weight):
    tokens = middle.shape[0]
    block = row_blocks(tokens)
    rows = pl.BlockSpec((block, D), lambda i: (i, 0))
    low = jax.ShapeDtypeStruct((tokens, D), BF16)
    return pl.pallas_call(
        middle_back_kernel,
        grid=(tokens // block,),
        out_shape=[
            jax.ShapeDtypeStruct((tokens, D), F32),
            low,
            low,
            jax.ShapeDtypeStruct((8, D), F32),
        ],
        in_specs=[
            rows,
            rows,
            rows,
            pl.BlockSpec((1, D), lambda i: (0, 0)),
            pl.BlockSpec((D, D), lambda i: (0, 0)),
        ],
        out_specs=[rows, rows, rows, pl.BlockSpec((8, D), lambda i: (0, 0))],
        compiler_params=params_of(),
        cost_estimate=cost(2 * tokens * D * D, 18 * tokens * D),
        name="middle_back",
    )(second_grad, middle, grad_out, gain, weight)


def first_back_kernel(steps, mixed_ref, w_ref, x_ref, mg_ref, gain_ref, out_ref, vec_ref, sum_ref):
    step = pl.program_id(0)
    width = w_ref.shape[0]
    lanes = pl.ds(pl.multiple_of(step * width, width), width)
    sum_ref[:, lanes] = nt(mixed_ref[...], w_ref[...])

    @pl.when(step == steps - 1)
    def _():
        block = row_blocks(x_ref.shape[0])
        vec_ref[...] = jnp.zeros(vec_ref.shape, F32)

        def body(i, _):
            rows = pl.ds(pl.multiple_of(i * block, 16), block)
            grad = sum_ref[rows, :]
            xhat, inverse = normalized(x_ref[rows, :].astype(F32))
            inner = normalized_back(grad * gain_ref[...], xhat, inverse)
            out_ref[rows, :] = (mg_ref[rows, :] + inner).astype(BF16)
            vec_ref[0:1, :] += jnp.sum(grad * xhat, axis=0, keepdims=True)
            vec_ref[1:2, :] += jnp.sum(grad, axis=0, keepdims=True)
            return 0

        lax.fori_loop(0, x_ref.shape[0] // block, body, 0)


def first_back(mixed_grad, weight, x, middle_grad, gain):
    tokens = x.shape[0]
    width = 256
    steps = D // width
    rows = pl.BlockSpec((tokens, D), lambda k: (0, 0), pipeline_mode=pl.Buffered(1))
    return pl.pallas_call(
        partial(first_back_kernel, steps),
        grid=(steps,),
        out_shape=[
            jax.ShapeDtypeStruct((tokens, D), BF16),
            jax.ShapeDtypeStruct((8, D), F32),
        ],
        in_specs=[
            pl.BlockSpec((tokens, 3 * D), lambda k: (0, 0), pipeline_mode=pl.Buffered(1)),
            pl.BlockSpec((width, 3 * D), lambda k: (k, 0)),
            rows,
            rows,
            pl.BlockSpec((1, D), lambda k: (0, 0)),
        ],
        out_specs=[
            pl.BlockSpec((tokens, D), lambda k: (0, 0)),
            pl.BlockSpec((8, D), lambda k: (0, 0)),
        ],
        scratch_shapes=[pltpu.VMEM((tokens, D), F32)],
        compiler_params=params_of(),
        cost_estimate=cost(6 * tokens * D * D, 6 * D * D + 14 * tokens * D),
        name="first_back",
    )(mixed_grad, weight, x, middle_grad, gain)


def local(
    patches,
    cotangent,
    window_rows,
    rel_index,
    params,
    first_moment,
    second_moment,
    learn_rate,
    step_count,
):
    arrivals = patches.shape[0]
    windows = arrivals // WT
    geo = Geometry(lax.axis_size("dp"), lax.axis_size("fsdp"), params.shape[0])
    dp_index = lax.axis_index("dp")
    fsdp_index = lax.axis_index("fsdp")
    me = jnp.stack(
        [lax.axis_index(AXES), dp_index // 2, dp_index % 2, fsdp_index // 2, fsdp_index % 2]
    ).astype(jnp.int32)

    shard = params.reshape(geo.rows, LANES)
    if geo.spill:
        spill = lax.ppermute(
            shard[: round_up(geo.spill, 8)], AXES, [(geo.spill_from, geo.spill_to)]
        )
    else:
        spill = jnp.zeros((8, LANES), F32)
    share = prepare(geo, me, shard, spill).reshape(4, geo.quarter, LANES)
    row_ids = jnp.pad(
        window_rows.reshape(windows, WT), ((0, 0), (0, WP - WT)), constant_values=-1
    ).reshape(windows * WP)
    stacked = jnp.stack(spread_quarters(geo, share, dp_index))
    gathers = []
    for groups in GATHER_PHASES:
        pieces = [
            lax.dynamic_index_in_dim(stacked, dp_index ^ group, 0, keepdims=True)
            for group in groups
        ]
        gathers.append(Gather(geo, jnp.concatenate(pieces, axis=0)))
    gathers[0].line()
    half = windows // 2
    ids_of = row_ids[:, None]
    x = permute_in(after(ids_of, gathers[0].held), patches, 0, half)
    held = gathers[0].joined(x)
    gathers[0].across()
    gathers[1].line(held)
    x = permute_in(after(ids_of, held), patches, half, windows, x)
    near = gathers[0].last(x)
    grad_out = permute_in(after(ids_of, near), cotangent, 0, half)
    gathered = {0: gathers[0].finish(grad_out)}
    far = gathered[0][1]
    held = gathers[1].joined(far)
    gathers[1].across()
    gathers[2].line(held)
    grad_out = permute_in(after(ids_of, far), cotangent, half, windows, grad_out)
    gathered[0] = gathered[0][:3] + [after(gathered[0][3], grad_out)]

    mix_matrix = (MIX_ROW, D, 3 * D // LANES)
    out_matrix = (OUT_ROW, D, D // LANES)
    expand_matrix = (EXPAND_ROW, D, FF // LANES)
    shrink_matrix = (SHRINK_ROW, FF, D // LANES)
    out_end = p_row(STARTS[6])
    expand_end = p_row(STARTS[10])
    shrink_end = p_row(STARTS[12])
    mix_vectors = [(0, 8), (8, 8), (TAIL_ROW, TABLE_ROW - TAIL_ROW), (TABLE_ROW, SPLIT_ROW - TABLE_ROW)]
    out_vectors = [(out_end + 8 * i, 8) for i in range(3)]
    expand_vectors = [(expand_end, FF // LANES)]
    shrink_vectors = [(shrink_end, 8)]

    first = Region(
        geo, 0, OUT_ROW, mix_matrix, mix_vectors, high=geo.spill_to if geo.spill else None
    )
    mix_weight, attn_gain, attn_shift, mix_bias, table_rows = unpack(geo, first, me, gathered)
    near = gathers[1].last(mix_weight)
    held = gathers[2].joined(mix_weight)
    gathers[2].across(near)
    gathers[3].line(held)
    table_rows = after(table_rows, near, held)

    def line_of(rows):
        return rows.reshape(1, -1)

    entries = round_up(TABLE_ROWS, 16)
    table = table_rows.reshape(-1)[: TABLE_ROWS * HEADS].reshape(TABLE_ROWS, HEADS).T
    table = jnp.pad(table, ((0, 0), (0, entries - TABLE_ROWS))).astype(BF16)
    ids = jnp.pad(rel_index.T, ((0, WP - WT), (0, LANES - WT)), constant_values=-1)
    bias = score_bias(ids, table)

    normed, mixed = mix(
        after(x, bias),
        line_of(attn_gain),
        line_of(attn_shift),
        mix_weight,
        line_of(mix_bias),
    )
    gathered[1] = gathers[1].finish(mixed)
    near = gathers[2].last(mixed)
    held = gathers[3].joined(mixed)
    gathers[3].across(near)
    attended, logs = attention(after(mixed, near, held, gathered[1][1]), bias)
    out_weight, out_bias, mlp_gain, mlp_shift = unpack(
        geo, Region(geo, OUT_ROW, EXPAND_ROW, out_matrix, out_vectors), me, gathered
    )
    gathered[2] = gathers[2].finish(out_weight)
    near = gathers[3].last(out_weight)
    middle, second = middle_rows(
        x,
        after(attended, near, gathered[2][1]),
        out_weight,
        line_of(out_bias),
        line_of(mlp_gain),
        line_of(mlp_shift),
    )
    expand_weight, expand_bias = unpack(
        geo, Region(geo, EXPAND_ROW, SHRINK_ROW, expand_matrix, expand_vectors), me, gathered
    )
    gathered[3] = gathers[3].finish(expand_weight)
    second = after(second, gathered[3][1])

    shrink_region = Region(
        geo, SHRINK_ROW, END_ROW, shrink_matrix, shrink_vectors, high=geo.devices - 1
    )
    expand_region = Region(geo, EXPAND_ROW, SHRINK_ROW, expand_matrix, expand_vectors)
    out_region = Region(geo, OUT_ROW, EXPAND_ROW, out_matrix, out_vectors)
    mix_region = Region(geo, 0, TAIL_ROW, mix_matrix, [])
    slots = {}
    shrink_bias_grad = jnp.sum(grad_out.astype(F32), axis=0).reshape(-1, LANES)
    hidden, slope, slots = mlp_up(
        geo,
        shrink_region,
        me,
        second,
        grad_out,
        expand_weight,
        line_of(expand_bias),
        shrink_bias_grad,
        slots,
        False,
    )
    phase3 = Reduction(geo, slots[3], 3)
    shrink_weight, shrink_bias = unpack(
        geo, Region(geo, SHRINK_ROW, END_ROW, shrink_matrix, shrink_vectors), me, gathered
    )
    sent = phase3.last(shrink_weight)
    result, second_grad, slots = mlp_down(
        geo,
        expand_region,
        me,
        after(hidden, sent),
        slope,
        second,
        grad_out,
        expand_weight,
        shrink_weight,
        middle,
        line_of(shrink_bias),
        slots,
        expand_region.high == shrink_region.low,
    )
    phase2 = Reduction(geo, slots[2], 2)
    sent = phase3.across(second_grad)
    middle_grad, branch_grad, context_grad, middle_vec = middle_back(
        after(second_grad, sent), middle, grad_out, line_of(mlp_gain), out_weight
    )
    sent = [phase3.line(context_grad), phase2.last(context_grad)]
    slots = pack(
        geo,
        out_region,
        me,
        attended,
        after(branch_grad, *sent),
        [middle_vec[i].reshape(8, LANES) for i in range(3)],
        slots,
        out_region.high == expand_region.low,
    )
    phase1 = Reduction(geo, slots[1], 1)
    context_grad = after(context_grad, slots[1][0])
    parts = attention_back(mixed, context_grad, bias, logs, 0, half)
    sums = {3: phase3.total(parts[1])}
    sent = [phase2.across(parts[1]), phase1.last(parts[1]), sums[3]]
    mixed_grad, score_sums, column_sums = attention_back(
        mixed, after(context_grad, *sent), bias, logs, half, windows, parts
    )
    sent = [phase2.line(score_sums), phase1.across(score_sums)]
    slots = pack(
        geo,
        mix_region,
        me,
        normed,
        after(mixed_grad, *sent),
        [],
        slots,
        mix_region.high == out_region.low,
    )
    packed = slots[0][0]
    phase0 = Reduction(geo, slots[0], 0)
    activations = permute_out(row_ids[None], after(result, packed), arrivals)
    far = phase0.last(activations)
    sums[2] = phase2.total(packed, far)
    sent = [phase1.line(packed, far), sums[2]]
    input_rows, first_vec = first_back(
        after(mixed_grad, far, *sent), mix_weight, x, middle_grad, line_of(attn_gain)
    )
    sent = phase0.across(input_rows)
    table_grad = score_bias_back(ids, after(score_sums, sent), entries)[:TABLE_ROWS]

    table_pad = (SPLIT_ROW - TABLE_ROW) * LANES - TABLE_ROWS * HEADS
    late = jnp.concatenate(
        [
            first_vec[:2].reshape(HEAD_ROWS, LANES),
            column_sums[0].reshape(-1, LANES),
            jnp.pad(table_grad.reshape(-1), (0, table_pad)).reshape(-1, LANES),
        ],
        axis=0,
    )
    sent = phase0.line(table_grad)
    sums[1] = phase1.total(sent)
    late = after(jnp.pad(late, ((0, LATE_ROWS - late.shape[0]), (0, 0))), sent)
    late = sum_everywhere(geo, late)
    input_grad = permute_out(row_ids[None], after(input_rows, sent), arrivals)
    squares = square_sums(
        geo, me, REDUCE_PHASES[1:], [after(sums[1], sent), sums[2], sums[3]]
    )
    sums[0] = phase0.total(squares, input_grad)
    squares = squares + square_sums(geo, me, REDUCE_PHASES[:1], [sums[0]])
    collected = collect_quarters(geo, [sums[group][0] for group in range(4)], dp_index)
    scale = 1.0 / jnp.sqrt(F32(arrivals * geo.devices))
    squares = sum_everywhere(geo, jnp.sum(squares, axis=1)[None], 0, 4)
    collected[0] = after(collected[0], squares)
    step_float = step_count.astype(F32)
    coef = jnp.stack(
        [
            scale,
            1.0 - jnp.power(F32(0.9), step_float),
            1.0 - jnp.power(F32(0.999), step_float),
            learn_rate,
        ]
    )
    params_new, first_new, second_new = update_step(
        geo,
        me,
        coef,
        collected,
        late,
        shard,
        first_moment.reshape(geo.rows, LANES),
        second_moment.reshape(geo.rows, LANES),
    )
    squares = sum_everywhere(geo, after(squares, params_new), 4)
    tensor = lax.broadcasted_iota(jnp.int32, (LATE_ROWS, 16), 1)
    row = lax.broadcasted_iota(jnp.int32, (LATE_ROWS, 16), 0)
    inside = tensor < 0
    edges = [0, 8, HEAD_ROWS, HEAD_ROWS + TABLE_ROW - TAIL_ROW, LATE_ROWS]
    for t, start, stop in zip((0, 1, 3, 4), edges, edges[1:]):
        inside = inside | ((tensor == t) & (row >= start) & (row < stop))
    late_rows = jnp.sum(late * late, axis=1, keepdims=True)
    totals = squares[0] + jnp.sum(jnp.where(inside, late_rows, 0.0), axis=0)
    entry_counts = jnp.array([math.prod(shape) for shape in SHAPES], F32)
    group_rms = jnp.sqrt(totals[: len(SHAPES)] * (scale * scale) / entry_counts)

    return (
        activations,
        input_grad,
        group_rms,
        params_new.reshape(-1),
        first_new.reshape(-1),
        second_new.reshape(-1),
    )


def solution(mesh):
    placed = (
        P(AXES, None),
        P(AXES, None),
        P(AXES),
        P(),
        P(AXES),
        P(AXES),
        P(AXES),
        P(),
        P(),
    )
    return jax.shard_map(
        local,
        mesh=mesh,
        in_specs=placed,
        out_specs=(P(AXES, None), P(AXES, None), P(), P(AXES), P(AXES), P(AXES)),
        check_vma=False,
    )
```
